32 devices in a mesh: dp: 8 (over y, x, core), seq: 4 (over z).
Axes of the slice: x: 2, y: 2, z: 4, core: 2. Of those that a mesh axis runs over, the one named last changes fastest.
Arguments:
- tokens: bfloat16 [32, 256, 1536], P('dp', 'seq'), may hold values from -6 to 6
- lengths: int32 [32], P('dp'), may hold values from 64 to 256, as said below
- routes: int32 [32, 256, 6], P('dp', 'seq'), may hold values from 0 to 15, all different within a row; in each aligned block of 64 rows (0 to 63, 64 to 127, ..., all dimensions but the last counted through in order) at most 30 rows name the same one
- cotangent: bfloat16 [32, 256, 1536], P('dp', 'seq'), may hold values from -6 to 6
- norm_gain: float32 [1536], replicated, may hold values from 0.5 to 1.5
- in_weight: bfloat16 [1536, 6448], P(('dp', 'seq')), may hold values from -0.15625 to 0.15625
- conv_weight: float32 [4, 3328], replicated, may hold values from -3 to 3
- conv_bias: float32 [3328], replicated, may hold values from -3 to 3
- dt_bias: float32 [48], replicated, may hold values from -4 to -1
- a_log: float32 [48], replicated, may hold values from -4 to 1
- d_skip: float32 [48], replicated, may hold values from 0.5 to 1.5
- mix_gain: float32 [3072], replicated, may hold values from 0.5 to 1.5
- out_weight: bfloat16 [3072, 1536], P(('dp', 'seq')), may hold values from -0.109375 to 0.109375
- ffn_gain: float32 [1536], replicated, may hold values from 0.5 to 1.5
- router_weight: bfloat16 [1536, 16], P(('dp', 'seq')), may hold values from -0.078125 to 0.078125
- shared_up: bfloat16 [1536, 2048], P(('dp', 'seq')), may hold values from -0.15625 to 0.15625
- shared_down: bfloat16 [1024, 1536], P(('dp', 'seq')), may hold values from -0.1875 to 0.1875
- expert_up: bfloat16 [16, 1536, 1024], P('dp'), may hold values from -0.15625 to 0.15625
- expert_down: bfloat16 [16, 512, 1536], P('dp'), may hold values from -0.25 to 0.25
Outputs:
- output: bfloat16 [32, 256, 1536], P('dp', 'seq')
- input_grad: bfloat16 [32, 256, 1536], P('dp', 'seq')
- norm_gain_grad: float32 [1536], replicated
- in_weight_grad: float32 [1536, 6448], P(('dp', 'seq'))
- conv_weight_grad: float32 [4, 3328], replicated
- conv_bias_grad: float32 [3328], replicated
- dt_bias_grad: float32 [48], replicated
- a_log_grad: float32 [48], replicated
- d_skip_grad: float32 [48], replicated
- mix_gain_grad: float32 [3072], replicated
- out_weight_grad: float32 [3072, 1536], P(('dp', 'seq'))
- ffn_gain_grad: float32 [1536], replicated
- router_grad: float32 [1536, 16], P(('dp', 'seq'))
- shared_up_grad: float32 [1536, 2048], P(('dp', 'seq'))
- shared_down_grad: float32 [1024, 1536], P(('dp', 'seq'))
- expert_up_grad: float32 [16, 1536, 1024], P('dp', 'seq')
- expert_down_grad: float32 [16, 512, 1536], P('dp', 'seq')
The draws below stay inside these ranges and needn't reach their ends.
Inputs may be any that keep to these rules, and one draw needn't show every extreme that they name: `lengths`: one sequence has exactly 256 used slots and one exactly 64. `routes`: each slot names 6 different experts; in the 64 slots of one sequence on one device (aligned blocks) no expert is named more than 30 times, a bound that some block reaches.
All inputs are finite; a program needn't handle non-finite values.
Results may differ from the reference program's by a relative error of at most 0.023.
Values may be sent and summed in bfloat16 or wider, within the bound.
A program may use at most 640 MiB of HBM per device.

```python
import math
import jax
import jax.numpy as jnp
import numpy as np
from jax import lax

MODEL_WIDTH = 1536
INNER = 3072
HEADS = 48
HDIM = 64
STATE = 128
KCONV = 4
EXPERT_HIDDEN = 512
SFF = 1024
TOP = 6
L_DEV = 64
CONV = 3328
PROJ = 6448
EXPERTS = 16
SEQS = 32
L_SEQ = 256
CAP = 30


def draw_lengths(key, part):
    key_len, key_pick = jax.random.split(jax.random.fold_in(key, 17))
    values = jax.random.randint(key_len, (SEQS,), L_SEQ // 4, L_SEQ + 1)
    shuffle = jax.random.permutation(key_pick, SEQS)
    values = values.at[shuffle[0]].set(L_SEQ)
    values = values.at[shuffle[1]].set(L_SEQ // 4)
    return values.astype(jnp.int32)


def shard_levels(stream_key, extent, cuts, smallest, high):
    def one(axis_at, parts):
        steps = jax.random.uniform(jax.random.fold_in(jax.random.fold_in(stream_key, 6), axis_at), (parts,), jnp.float32, smallest / len(cuts), high / len(cuts))
        return jnp.repeat(jnp.exp(steps), extent[axis_at] // parts).reshape((-1,) + (1,) * (len(extent) - axis_at - 1))

    level = one(*cuts[0])
    for cut in cuts[1:]:
        level = level * one(*cut)
    return level


def shared_out(own_key, own, number, rows, amount, top, limit, lean):
    ranking = jax.random.permutation(own_key, amount)
    crowded, common = portions_of(amount, rows * top, limit, lean, True), portions_of(amount, rows * top, limit, lean, False)
    places = jnp.arange(amount)

    def named(sizes, offset_by):
        used = int((sizes > 0).sum())
        fixed = max(1, used // 4)
        moved = fixed + (places - fixed + offset_by * (used - fixed)) % max(1, amount - fixed)
        return jnp.zeros((amount,), jnp.int32).at[ranking[jnp.where(places < fixed, places, moved)]].set(jnp.asarray(sizes, jnp.int32))

    sizes = jnp.where(number % 4 == 0, named(crowded, number // 4), named(common, number - number // 4 - 1))
    mixed = jax.random.permutation(jax.random.fold_in(own, 3), amount)
    giver, sink = mixed[0:amount // 2 * 2:2], mixed[1:amount // 2 * 2:2]
    margin = jnp.minimum(sizes[giver] - 1, limit - sizes[sink]) // 2
    margin = jnp.where((giver == ranking[0]) | (sink == ranking[0]) | (sizes[sink] == 0), 0, jnp.maximum(margin, 0))
    moved = jax.random.randint(jax.random.fold_in(own, 4), (amount // 2,), 0, 1 << 20) % (margin + 1)
    sizes = sizes.at[giver].add(-moved).at[sink].add(moved)
    members = jnp.searchsorted(jnp.cumsum(sizes), jnp.arange(rows * top), side="right").astype(jnp.int32)
    listing = members.reshape(top, rows).T
    listing = listing[jax.random.permutation(jax.random.fold_in(own, 1), rows)]
    offset_by = jax.random.randint(jax.random.fold_in(own, 2), (rows, 1), 0, top)
    return jnp.take_along_axis(listing, (jnp.arange(top)[None, :] + offset_by) % top, axis=1)


def portions_of(number_of, total, most, lean, full):
    loads = [(1 << 20) // math.isqrt(standing ** lean) + 1 for standing in range(1, number_of + 1)]
    largest = most if full else min(most, max(-(-total // number_of), total * loads[0] // sum(loads)))
    least = 1 if total - largest >= number_of - 1 else 0
    holding, surplus = [largest] + [least] * (number_of - 1), total - largest - least * (number_of - 1)
    while surplus > 0:
        movable = [i for i in range(1, number_of) if holding[i] < largest] or [i for i in range(1, number_of) if holding[i] < most]
        whole, left = sum([loads[i] for i in movable]), surplus
        for i in movable:
            addition = min(most - holding[i], max(1, left * loads[i] // whole), surplus)
            holding[i] = holding[i] + addition
            surplus = surplus - addition
    return np.array(holding)


def scatter_about(rng, shape, width, limit, cuts=(), dtype=jnp.bfloat16):
    values = jax.random.normal(rng, shape, jnp.float32) * width
    if len(cuts) > 0:
        values = shard_levels(rng, shape, cuts, -0.22, 0.18) * values
    return jnp.clip(values, min=-limit, max=limit).astype(dtype)


def setup_inputs(seed: int = 0) -> dict:
    seeds = jax.random.split(jax.random.key(seed), 20)
    tokens = scatter_about(seeds[0], (SEQS, L_SEQ, MODEL_WIDTH), 1.0, 6.0, ((0, 8), (1, 4)))
    lengths = draw_lengths(jax.random.fold_in(seeds[19], 71), 0)
    routes_keys = jax.random.split(jax.random.fold_in(seeds[2], 1), SEQS * L_SEQ // L_DEV)
    routes_turns = jax.random.permutation(jax.random.fold_in(seeds[2], 3), SEQS * L_SEQ // L_DEV)
    routes = jax.vmap(lambda own, number: shared_out(jax.random.fold_in(seeds[2], 2), own, number, L_DEV, EXPERTS, TOP, CAP, 2))(routes_keys, routes_turns).reshape((SEQS, L_SEQ, TOP))
    cotangent = scatter_about(seeds[3], (SEQS, L_SEQ, MODEL_WIDTH), 1.0, 6.0, ((0, 8), (1, 4)))
    norm_gain = jnp.clip(1.0 + 0.1 * jax.random.normal(seeds[4], (MODEL_WIDTH,), jnp.float32), 0.5, 1.5)
    in_weight = scatter_about(seeds[5], (MODEL_WIDTH, PROJ), MODEL_WIDTH ** -0.5, 0.15625, ((0, 32),))
    conv_weight = scatter_about(seeds[6], (KCONV, CONV), 0.5, 3.0, (), jnp.float32)
    conv_bias = scatter_about(seeds[7], (CONV,), 0.3, 3.0, (), jnp.float32)
    dt_bias = jnp.clip(jax.random.uniform(seeds[8], (HEADS,), jnp.float32, -4.0, -1.0), -4.0, -1.0)
    a_log = jnp.clip(jax.random.uniform(seeds[9], (HEADS,), jnp.float32, -4.0, 1.0), -4.0, 1.0)
    d_skip = jnp.clip(jax.random.uniform(seeds[10], (HEADS,), jnp.float32, 0.5, 1.5), 0.5, 1.5)
    mix_gain = jnp.clip(1.0 + 0.1 * jax.random.normal(seeds[11], (INNER,), jnp.float32), 0.5, 1.5)
    out_weight = scatter_about(seeds[12], (INNER, MODEL_WIDTH), INNER ** -0.5, 0.109375, ((0, 32),))
    ffn_gain = jnp.clip(1.0 + 0.1 * jax.random.normal(seeds[13], (MODEL_WIDTH,), jnp.float32), 0.5, 1.5)
    router_weight = scatter_about(seeds[14], (MODEL_WIDTH, EXPERTS), (4 * MODEL_WIDTH) ** -0.5, 0.078125, ((0, 32),))
    shared_up = scatter_about(seeds[15], (MODEL_WIDTH, 2 * SFF), MODEL_WIDTH ** -0.5, 0.15625, ((0, 32),))
    shared_down = scatter_about(seeds[16], (SFF, MODEL_WIDTH), SFF ** -0.5, 0.1875, ((0, 32),))
    expert_up = scatter_about(seeds[17], (EXPERTS, MODEL_WIDTH, 2 * EXPERT_HIDDEN), MODEL_WIDTH ** -0.5, 0.15625, ((0, 8),))
    expert_down = scatter_about(seeds[18], (EXPERTS, EXPERT_HIDDEN, MODEL_WIDTH), EXPERT_HIDDEN ** -0.5, 0.25, ((0, 8),))
    return dict(tokens=tokens, lengths=lengths, routes=routes, cotangent=cotangent, norm_gain=norm_gain, in_weight=in_weight, conv_weight=conv_weight, conv_bias=conv_bias, dt_bias=dt_bias, a_log=a_log, d_skip=d_skip, mix_gain=mix_gain, out_weight=out_weight, ffn_gain=ffn_gain, router_weight=router_weight, shared_up=shared_up, shared_down=shared_down, expert_up=expert_up, expert_down=expert_down)


EPSILON = 1e-05
PRECISE = lax.Precision.HIGHEST

@jax.custom_vjp
def low(v):
    return lax.optimization_barrier(v.astype(jnp.bfloat16)).astype(jnp.float32)

@jax.custom_vjp
def low_back(v):
    return v

def low_keep(v):
    return (low(v), None)

def low_pass(kept, grad):
    return (grad,)

def back_keep(v):
    return (v, None)

def back_low(kept, grad):
    return (low(grad),)
low.defvjp(low_keep, low_pass)
low_back.defvjp(back_keep, back_low)

def matmul(left_mat, right_mat):
    return jnp.dot(left_mat, right_mat, precision=PRECISE)

def rms_norm(values, gain_vec):
    return values * lax.rsqrt(lax.optimization_barrier(jnp.mean(values * values, axis=-1, keepdims=True)) + EPSILON) * gain_vec

def swiglu(values, half_width):
    return jax.nn.silu(values[..., :half_width]) * values[..., half_width:]

def block_terms(head_in, b_rows, c_rows, step_sizes, a_log):
    log_rates = -step_sizes * jnp.exp(a_log)
    cumulative = jnp.cumsum(log_rates, axis=0)
    block_len = head_in.shape[0]
    lower_tri = jnp.arange(block_len)[:, None] >= jnp.arange(block_len)[None, :]
    spread = jnp.where(lower_tri[:, :, None], cumulative[:, None, :] - cumulative[None, :, :], -jnp.inf)
    scores = jnp.dot(c_rows, b_rows.T, precision=PRECISE)
    weights = jnp.exp(spread) * scores[:, :, None] * step_sizes[None, :, :]
    local_out = jnp.einsum('tih,ihp->thp', weights, head_in, precision=PRECISE)
    tail_weight = jnp.exp(cumulative[-1][None, :] - cumulative) * step_sizes
    local_state = jnp.einsum('ih,ihp,in->hpn', tail_weight, head_in, b_rows, precision=PRECISE)
    return (cumulative, local_out, local_state, jnp.exp(cumulative[-1]))

def carried_out(c_rows, cumulative, state_in):
    return jnp.einsum('tn,hpn->thp', c_rows, state_in, precision=PRECISE) * jnp.exp(cumulative)[:, :, None]

def sequence_out(params, x_row, length, route_row):
    norm_gain, in_weight, conv_weight, conv_bias, dt_bias, a_log, d_skip, mix_gain, out_weight, ffn_gain, router_weight, shared_up, shared_down, expert_up, expert_down = params
    valid_rows = (jnp.arange(L_SEQ) < length).astype(jnp.float32)[:, None]
    normed = low(rms_norm(x_row, norm_gain))
    projected = low(low_back(matmul(normed, in_weight)))
    gate_z = projected[:, :INNER]
    conv_in = projected[:, INNER:INNER + CONV]
    raw_steps = projected[:, INNER + CONV:]
    padded = jnp.concatenate([jnp.zeros((KCONV - 1, CONV), jnp.float32), conv_in], axis=0)
    conv_sum = conv_bias + conv_weight[0] * padded[0:L_SEQ]
    for tap_idx in range(1, KCONV):
        conv_sum = conv_sum + conv_weight[tap_idx] * padded[tap_idx:tap_idx + L_SEQ]
    activated = jax.nn.silu(conv_sum) * valid_rows
    head_in = activated[:, :INNER].reshape(L_SEQ, HEADS, HDIM)
    b_rows = activated[:, INNER:INNER + STATE]
    c_rows = activated[:, INNER + STATE:]
    step_sizes = jax.nn.softplus(raw_steps + dt_bias)
    blocks = L_SEQ // L_DEV

    def advance(state_in, pieces):
        head_block, b_block, c_block, step_block = pieces
        cumulative, local_out, local_state, decay_total = block_terms(head_block, b_block, c_block, step_block, a_log)
        block_out = local_out + carried_out(c_block, cumulative, state_in)
        return (decay_total[:, None, None] * state_in + local_state, block_out)
    _, scanned = lax.scan(jax.checkpoint(advance), jnp.zeros((HEADS, HDIM, STATE), jnp.float32), (head_in.reshape(blocks, L_DEV, HEADS, HDIM), b_rows.reshape(blocks, L_DEV, STATE), c_rows.reshape(blocks, L_DEV, STATE), step_sizes.reshape(blocks, L_DEV, HEADS)))
    mixed_out = scanned.reshape(L_SEQ, HEADS, HDIM) + d_skip[:, None] * head_in
    gated_out = mixed_out.reshape(L_SEQ, INNER) * jax.nn.silu(gate_z)
    normed_mix = low(rms_norm(gated_out, mix_gain))
    hidden = x_row + low_back(matmul(normed_mix, out_weight)) * valid_rows
    normed_ffn = low(rms_norm(hidden, ffn_gain))
    logits = low_back(matmul(normed_ffn, router_weight))
    picked = jnp.take_along_axis(logits, route_row, axis=1)
    gate_probs = jax.nn.softmax(picked, axis=-1)
    onehot = (route_row[:, :, None] == jnp.arange(EXPERTS)[None, None, :]).astype(jnp.float32)
    combine_rows = jnp.einsum('lk,lke->el', gate_probs, onehot, precision=PRECISE)
    shared_gu = low_back(matmul(normed_ffn, shared_up))
    shared_h = low(swiglu(shared_gu, SFF))
    shared_y = low_back(matmul(shared_h, shared_down))

    def expert_term(pieces):
        up_mat, down_mat, weight_row = pieces
        expert_in = low_back(normed_ffn)
        expert_gu = low_back(matmul(expert_in, up_mat))
        expert_h = low(swiglu(expert_gu, EXPERT_HIDDEN))
        expert_y = low(low_back(matmul(expert_h, down_mat)))
        return weight_row[:, None] * expert_y
    routed = lax.optimization_barrier(jnp.sum(lax.map(jax.checkpoint(expert_term), (expert_up, expert_down, combine_rows)), axis=0))
    return hidden + valid_rows * (shared_y + routed)

def reference(tokens, lengths, routes, cotangent, norm_gain, in_weight, conv_weight, conv_bias, dt_bias, a_log, d_skip, mix_gain, out_weight, ffn_gain, router_weight, shared_up, shared_down, expert_up, expert_down):
    params = tuple((value.astype(jnp.float32) for value in (norm_gain, in_weight, conv_weight, conv_bias, dt_bias, a_log, d_skip, mix_gain, out_weight, ffn_gain, router_weight, shared_up, shared_down, expert_up, expert_down)))

    def forward(x_all, weights_all):

        def one_sequence(pieces):
            return sequence_out(weights_all, pieces[0], pieces[1], pieces[2])
        return lax.map(jax.checkpoint(one_sequence), (x_all, lengths, routes))
    result, pullback = jax.vjp(forward, tokens.astype(jnp.float32), params)
    grad_x, grad_params = pullback(cotangent.astype(jnp.float32))
    return (result.astype(jnp.bfloat16), grad_x.astype(jnp.bfloat16), grad_params[0], grad_params[1], grad_params[2], grad_params[3], grad_params[4], grad_params[5], grad_params[6], grad_params[7], grad_params[8], grad_params[9], grad_params[10], grad_params[11], grad_params[12], grad_params[13], grad_params[14])
```

```python
from functools import partial

import jax
import jax.numpy as jnp
from jax import lax
from jax.sharding import PartitionSpec as P

MODEL_WIDTH = 1536
INNER = 3072
HEADS = 48
HDIM = 64
STATE = 128
KCONV = 4
EXPERT_HIDDEN = 512
SFF = 1024
MB = 4
CONV = 3328
PROJ = 6448


EPSILON = 1e-05
PRECISE = lax.Precision.HIGHEST


def from_behind(x, axis, by):
    size = lax.axis_size(axis)
    pairs = [(i, i + by) for i in range(size) if 0 <= i + by < size]
    return lax.ppermute(x, axis, pairs)


def prefix(x, axis, join, neutral):
    place = lax.axis_index(axis)
    gathered = jax.tree.map(
        lambda a, kind: lax.all_gather(a.astype(kind), axis), x, (jnp.bfloat16, jnp.bfloat16)
    )
    state = jax.tree.map(lambda a, e: jnp.zeros_like(a) + jnp.asarray(e, a.dtype), x, neutral)

    def one(step, state):
        return join(
            state,
            jax.tree.map(
                lambda a, own: lax.dynamic_index_in_dim(a, step, 0, False).astype(own.dtype),
                gathered,
                x,
            ),
        )

    return lax.fori_loop(0, place, one, state)


def prefix_2(x, axis, join, neutral):
    count = lax.axis_size(axis)
    place = lax.axis_index(axis)
    ahead = count - 1 - place
    gathered = jax.tree.map(
        lambda a, kind: lax.all_gather(a.astype(kind), axis),
        x,
        jax.tree.map(lambda a: jnp.bfloat16 if a.dtype == jnp.float32 else a.dtype, x),
    )
    state = jax.tree.map(lambda a, e: jnp.zeros_like(a) + jnp.asarray(e, a.dtype), x, neutral)

    def one(step, state):
        source = count - 1 - step
        return join(
            state,
            jax.tree.map(
                lambda a, own: lax.dynamic_index_in_dim(a, source, 0, False).astype(own.dtype),
                gathered,
                x,
            ),
        )

    return lax.fori_loop(0, ahead, one, state)


def rms_norm(values, gain_vec):
    return (
        values * lax.rsqrt(jnp.mean(values * values, axis=-1, keepdims=True) + EPSILON) * gain_vec
    )


def swiglu(values, half_width):
    return jax.nn.silu(values[..., :half_width]) * values[..., half_width:]


def contract_rows(left_mat, right_mat):
    return lax.dot_general(
        left_mat, right_mat, (((0,), (0,)), ((), ())), preferred_element_type=jnp.float32
    )


def contract_cols(left_mat, right_mat):
    return lax.dot_general(
        left_mat, right_mat, (((1,), (1,)), ((), ())), preferred_element_type=jnp.float32
    )


def block_terms(head_in, b_rows, c_rows, step_sizes, a_log):
    log_rates = -step_sizes * jnp.exp(a_log)
    cumulative = jnp.cumsum(log_rates, axis=0)
    block_len = head_in.shape[0]
    lower_tri = jnp.arange(block_len)[:, None] >= jnp.arange(block_len)[None, :]
    spread = jnp.where(
        lower_tri[:, :, None], cumulative[:, None, :] - cumulative[None, :, :], -jnp.inf
    )
    scores = jnp.dot(c_rows, b_rows.T, precision=PRECISE)
    weights = jnp.exp(spread) * scores[:, :, None] * step_sizes[None, :, :]
    local_out = jnp.einsum("tih,ihp->thp", weights, head_in, precision=PRECISE)
    tail_weight = jnp.exp(cumulative[-1][None, :] - cumulative) * step_sizes
    local_state = jnp.einsum("ih,ihp,in->hpn", tail_weight, head_in, b_rows, precision=PRECISE)
    return (cumulative, local_out, local_state, jnp.exp(cumulative[-1]))


def carried_out(c_rows, cumulative, state_in):
    return (
        jnp.einsum("tn,hpn->thp", c_rows, state_in, precision=PRECISE)
        * jnp.exp(cumulative)[:, :, None]
    )


def mixer_front(valid_rows, projected, previous, conv_weight, conv_bias, dt_bias, a_log):
    row_count = projected.shape[0]
    conv_in = projected[:, INNER : INNER + CONV]
    padded = jnp.concatenate([previous, conv_in], axis=0)
    conv_sum = conv_bias + conv_weight[0] * padded[0:row_count]
    for tap_idx in range(1, KCONV):
        conv_sum = conv_sum + conv_weight[tap_idx] * padded[tap_idx : tap_idx + row_count]
    activated = jax.nn.silu(conv_sum) * valid_rows
    head_in = activated[:, :INNER].reshape(row_count, HEADS, HDIM)
    b_rows = activated[:, INNER : INNER + STATE]
    c_rows = activated[:, INNER + STATE :]
    step_sizes = jax.nn.softplus(projected[:, INNER + CONV :] + dt_bias)
    cumulative, local_out, local_state, decay_total = block_terms(
        head_in, b_rows, c_rows, step_sizes, a_log
    )
    return (projected[:, :INNER], head_in, c_rows, cumulative, local_out, local_state, decay_total)


def mixer_tail(gate_z, head_in, c_rows, cumulative, local_out, state_in, d_skip, mix_gain):
    mixed_out = local_out + carried_out(c_rows, cumulative, state_in) + d_skip[:, None] * head_in
    gated_out = mixed_out.reshape(head_in.shape[0], INNER) * jax.nn.silu(gate_z)
    return rms_norm(gated_out, mix_gain)


def link_states(earlier, latter):
    return (earlier[0] * latter[0], latter[1] + latter[0][:, None, None] * earlier[1])


def local(
    tokens,
    lengths,
    routes,
    cotangent,
    norm_gain,
    in_weight,
    conv_weight,
    conv_bias,
    dt_bias,
    a_log,
    d_skip,
    mix_gain,
    out_weight,
    ffn_gain,
    router_weight,
    shared_up,
    shared_down,
    expert_up,
    expert_down,
):
    row_count = tokens.shape[1]
    resident_experts = expert_up.shape[0]
    groups = lax.axis_size("dp")
    experts = resident_experts * groups
    top_count = routes.shape[2]
    capacity = row_count * top_count * 5 // (4 * experts)
    shards = (in_weight, out_weight, router_weight, shared_up, shared_down)
    kept_full = (
        lax.all_gather(shards[0], ("dp", "seq"), axis=0, tiled=True),
        lax.all_gather(shards[1], ("dp", "seq"), axis=0, tiled=True),
        lax.all_gather(shards[2], ("dp", "seq"), axis=0, tiled=True),
        lax.all_gather(shards[3], ("dp", "seq"), axis=0, tiled=True),
        lax.all_gather(shards[4], ("dp", "seq"), axis=0, tiled=True),
    )
    grad_inw = jnp.zeros((MODEL_WIDTH, PROJ), jnp.float32)
    grad_outw = jnp.zeros((INNER, MODEL_WIDTH), jnp.float32)
    grad_router = jnp.zeros((MODEL_WIDTH, experts), jnp.float32)
    grad_sup = jnp.zeros((MODEL_WIDTH, 2 * SFF), jnp.float32)
    grad_sdown = jnp.zeros((SFF, MODEL_WIDTH), jnp.float32)
    expert_upward_grad = jnp.zeros((resident_experts, MODEL_WIDTH, 2 * EXPERT_HIDDEN), jnp.float32)
    grad_edown = jnp.zeros((resident_experts, EXPERT_HIDDEN, MODEL_WIDTH), jnp.float32)
    grad_ngain = jnp.zeros_like(norm_gain)
    grad_cw = jnp.zeros_like(conv_weight)
    grad_cb = jnp.zeros_like(conv_bias)
    grad_db = jnp.zeros_like(dt_bias)
    grad_al = jnp.zeros_like(a_log)
    grad_skip = jnp.zeros_like(d_skip)
    grad_mgain = jnp.zeros_like(mix_gain)
    grad_fgain = jnp.zeros_like(ffn_gain)
    outputs = []
    input_grads = []
    for micro_idx in range(MB):
        in_full, out_full, router_full, up_full, down_full = kept_full
        x_rows = tokens[micro_idx].astype(jnp.float32)
        position = lax.axis_index("seq") * row_count + jnp.arange(row_count)
        valid_rows = (position < lengths[micro_idx]).astype(jnp.float32)[:, None]
        normed, norm_pull = jax.vjp(rms_norm, x_rows, norm_gain)
        normed_low = normed.astype(jnp.bfloat16)
        projected = jnp.dot(normed_low, in_full, preferred_element_type=jnp.float32).astype(
            jnp.bfloat16
        )
        previous = from_behind(projected[row_count - (KCONV - 1) :, INNER : INNER + CONV], "seq", 1)
        front_out, front_pull = jax.vjp(
            partial(mixer_front, valid_rows),
            projected.astype(jnp.float32),
            previous.astype(jnp.float32),
            conv_weight,
            conv_bias,
            dt_bias,
            a_log,
        )
        gate_z, head_in, c_rows, cumulative, local_out, local_state, decay_total = front_out
        identity = (jnp.ones_like(decay_total), jnp.zeros_like(local_state))
        _, state_in = prefix((decay_total, local_state), "seq", link_states, identity)
        normed_mix, tail_pull = jax.vjp(
            mixer_tail, gate_z, head_in, c_rows, cumulative, local_out, state_in, d_skip, mix_gain
        )
        mix_low = normed_mix.astype(jnp.bfloat16)
        mixer_out = jnp.dot(mix_low, out_full, preferred_element_type=jnp.float32)
        hidden = x_rows + mixer_out * valid_rows
        normed_ffn, ffn_pull = jax.vjp(rms_norm, hidden, ffn_gain)
        ffn_low = normed_ffn.astype(jnp.bfloat16)
        logits = jnp.dot(ffn_low, router_full, preferred_element_type=jnp.float32)
        route_row = routes[micro_idx]
        picked = jnp.take_along_axis(logits, route_row, axis=1)
        gate_probs = jax.nn.softmax(picked, axis=-1)
        shared_gu = jnp.dot(ffn_low, up_full, preferred_element_type=jnp.float32)
        shared_act, shared_pull = jax.vjp(partial(swiglu, half_width=SFF), shared_gu)
        shared_h = shared_act.astype(jnp.bfloat16)
        shared_y = jnp.dot(shared_h, down_full, preferred_element_type=jnp.float32)
        flat_route = route_row.reshape(-1)
        member = (flat_route[:, None] == jnp.arange(experts)[None, :]).astype(jnp.int32)
        slot_pos = jnp.sum((jnp.cumsum(member, axis=0) - member) * member, axis=1)
        target = flat_route * capacity + slot_pos
        source = (
            jnp.zeros((experts * capacity,), jnp.int32)
            .at[target]
            .set(jnp.arange(row_count * top_count, dtype=jnp.int32))
        )
        filled = jnp.zeros((experts * capacity, 1), jnp.bfloat16).at[target].set(jnp.bfloat16(1))
        outgoing = (jnp.take(ffn_low, source // top_count, axis=0) * filled).reshape(
            groups, resident_experts, capacity, MODEL_WIDTH
        )
        received_rows = lax.all_to_all(outgoing, "dp", split_axis=0, concat_axis=2, tiled=True)[0]
        expert_gu = jnp.einsum(
            "erd,edf->erf", received_rows, expert_up, preferred_element_type=jnp.float32
        )
        expert_act, expert_pull = jax.vjp(partial(swiglu, half_width=EXPERT_HIDDEN), expert_gu)
        expert_h = expert_act.astype(jnp.bfloat16)
        expert_y = jnp.einsum(
            "erf,efd->erd", expert_h, expert_down, preferred_element_type=jnp.float32
        ).astype(jnp.bfloat16)
        returned = lax.all_to_all(expert_y[None], "dp", split_axis=2, concat_axis=0, tiled=True)
        per_choice = (
            jnp.take(returned.reshape(experts * capacity, MODEL_WIDTH), target, axis=0)
            .reshape(row_count, top_count, MODEL_WIDTH)
            .astype(jnp.float32)
        )
        routed = jnp.einsum("lk,lkd->ld", gate_probs, per_choice, precision=PRECISE)
        outputs.append((hidden + valid_rows * (shared_y + routed)).astype(jnp.bfloat16))
        in_back, out_back, router_back, up_back, down_back = kept_full
        grad_out = cotangent[micro_idx].astype(jnp.float32)
        branch = valid_rows * grad_out
        shared_g = branch.astype(jnp.bfloat16)
        grad_sdown = grad_sdown + contract_rows(shared_h, shared_g)
        grad_sgu = shared_pull(contract_cols(shared_g, down_back))[0].astype(jnp.bfloat16)
        grad_sup = grad_sup + contract_rows(ffn_low, grad_sgu)
        grad_ffn = contract_cols(grad_sgu, up_back)
        grad_choice = (gate_probs[:, :, None] * branch[:, None, :]).astype(jnp.bfloat16)
        grad_gate = jnp.sum(branch[:, None, :] * per_choice, axis=-1)
        grad_pick = gate_probs * (
            grad_gate - jnp.sum(gate_probs * grad_gate, axis=-1, keepdims=True)
        )
        onehot = (route_row[:, :, None] == jnp.arange(experts)[None, None, :]).astype(jnp.float32)
        grad_logit = jnp.einsum("lk,lke->le", grad_pick, onehot, precision=PRECISE).astype(
            jnp.bfloat16
        )
        grad_router = grad_router + contract_rows(ffn_low, grad_logit)
        grad_ffn = grad_ffn + contract_cols(grad_logit, router_back)
        back_out = (
            jnp.take(grad_choice.reshape(row_count * top_count, MODEL_WIDTH), source, axis=0)
            * filled
        ).reshape(groups, resident_experts, capacity, MODEL_WIDTH)
        grad_arrived = lax.all_to_all(back_out, "dp", split_axis=0, concat_axis=2, tiled=True)[0]
        step_edown = jnp.einsum(
            "erf,erd->efd", expert_h, grad_arrived, preferred_element_type=jnp.float32
        )
        grad_eh = jnp.einsum(
            "erd,efd->erf", grad_arrived, expert_down, preferred_element_type=jnp.float32
        )
        expert_gate_up_grad = expert_pull(grad_eh)[0].astype(jnp.bfloat16)
        expert_upward_step = jnp.einsum(
            "tbw,tbj->twj", received_rows, expert_gate_up_grad, preferred_element_type=jnp.float32
        )
        grad_ein = jnp.einsum(
            "erf,edf->erd", expert_gate_up_grad, expert_up, preferred_element_type=jnp.float32
        ).astype(jnp.bfloat16)
        expert_upward_grad = expert_upward_grad + expert_upward_step
        grad_edown = grad_edown + step_edown
        came_back = lax.all_to_all(grad_ein[None], "dp", split_axis=2, concat_axis=0, tiled=True)
        grad_ffn = grad_ffn + jnp.sum(
            jnp.take(came_back.reshape(experts * capacity, MODEL_WIDTH), target, axis=0)
            .reshape(row_count, top_count, MODEL_WIDTH)
            .astype(jnp.float32),
            axis=1,
        )
        grad_hidden, step_fgain = ffn_pull(grad_ffn)
        grad_fgain = grad_fgain + step_fgain
        grad_hidden = grad_hidden + grad_out
        grad_mix_out = (grad_hidden * valid_rows).astype(jnp.bfloat16)
        grad_outw = grad_outw + contract_rows(mix_low, grad_mix_out)
        grad_mix = contract_cols(grad_mix_out, out_back)
        grad_z, grad_head, grad_c, grad_cum, grad_local, grad_state, step_skip, step_mgain = (
            tail_pull(grad_mix)
        )
        grad_skip = grad_skip + step_skip
        grad_mgain = grad_mgain + step_mgain
        _, grad_carry = prefix_2((decay_total, grad_state), "seq", link_states, identity)
        grad_decay = jnp.sum(grad_carry * state_in, axis=(1, 2))
        grad_proj, grad_prev, step_cw, step_cb, step_db, step_al = front_pull(
            (grad_z, grad_head, grad_c, grad_cum, grad_local, grad_carry, grad_decay)
        )
        grad_cw = grad_cw + step_cw
        grad_cb = grad_cb + step_cb
        grad_db = grad_db + step_db
        grad_al = grad_al + step_al
        from_next = from_behind(grad_prev.astype(jnp.bfloat16), "seq", -1).astype(grad_prev.dtype)
        grad_proj = (
            grad_proj.at[row_count - (KCONV - 1) :, INNER : INNER + CONV]
            .add(from_next)
            .astype(jnp.bfloat16)
        )
        grad_inw = grad_inw + contract_rows(normed_low, grad_proj)
        grad_normed = contract_cols(grad_proj, in_back)
        grad_x, step_ngain = norm_pull(grad_normed)
        grad_ngain = grad_ngain + step_ngain
        input_grads.append((grad_x + grad_hidden).astype(jnp.bfloat16))
    weight_grads = (
        lax.psum_scatter(grad_inw, ("dp", "seq"), scatter_dimension=0, tiled=True),
        lax.psum_scatter(grad_outw, ("dp", "seq"), scatter_dimension=0, tiled=True),
        lax.psum_scatter(grad_router, ("dp", "seq"), scatter_dimension=0, tiled=True),
        lax.psum_scatter(grad_sup, ("dp", "seq"), scatter_dimension=0, tiled=True),
        lax.psum_scatter(grad_sdown, ("dp", "seq"), scatter_dimension=0, tiled=True),
    )
    small_sums = lax.psum(
        (grad_ngain, grad_cw, grad_cb, grad_db, grad_al, grad_skip, grad_mgain, grad_fgain),
        ("dp", "seq"),
    )
    expert_sums = (
        lax.psum_scatter(
            expert_upward_grad.astype(jnp.bfloat16), "seq", scatter_dimension=1, tiled=True
        ).astype(jnp.float32),
        lax.psum_scatter(
            grad_edown.astype(jnp.bfloat16), "seq", scatter_dimension=1, tiled=True
        ).astype(jnp.float32),
    )
    return (
        jnp.stack(outputs),
        jnp.stack(input_grads),
        small_sums[0],
        weight_grads[0],
        small_sums[1],
        small_sums[2],
        small_sums[3],
        small_sums[4],
        small_sums[5],
        small_sums[6],
        weight_grads[1],
        small_sums[7],
        weight_grads[2],
        weight_grads[3],
        weight_grads[4],
        expert_sums[0],
        expert_sums[1],
    )


def ssd_sequence(head_in, b_rows, c_rows, step_sizes, a_log, block):
    count = head_in.shape[0] // block
    split = lambda a: a.reshape((count, block) + a.shape[1:])
    cumulative, local_out, local_state, decay_total = jax.vmap(
        block_terms, in_axes=(0, 0, 0, 0, None)
    )(split(head_in), split(b_rows), split(c_rows), split(step_sizes), a_log)
    state = jnp.zeros_like(local_state[0])
    pieces = []
    c_blocks = split(c_rows)
    for i in range(count):
        pieces.append(local_out[i] + carried_out(c_blocks[i], cumulative[i], state))
        state = decay_total[i][:, None, None] * state + local_state[i]
    return jnp.concatenate(pieces, axis=0)


def mixer(valid_rows, projected, conv_weight, conv_bias, dt_bias, a_log, d_skip, mix_gain, block):
    row_count = projected.shape[0]
    conv_in = projected[:, INNER : INNER + CONV]
    padded = jnp.concatenate([jnp.zeros((KCONV - 1, CONV), jnp.float32), conv_in], axis=0)
    conv_sum = conv_bias + conv_weight[0] * padded[0:row_count]
    for tap_idx in range(1, KCONV):
        conv_sum = conv_sum + conv_weight[tap_idx] * padded[tap_idx : tap_idx + row_count]
    activated = jax.nn.silu(conv_sum) * valid_rows
    head_in = activated[:, :INNER].reshape(row_count, HEADS, HDIM)
    b_rows = activated[:, INNER : INNER + STATE]
    c_rows = activated[:, INNER + STATE :]
    step_sizes = jax.nn.softplus(projected[:, INNER + CONV :] + dt_bias)
    mixed = ssd_sequence(head_in, b_rows, c_rows, step_sizes, a_log, block)
    mixed = mixed + d_skip[:, None] * head_in
    gated = mixed.reshape(row_count, INNER) * jax.nn.silu(projected[:, :INNER])
    return rms_norm(gated, mix_gain)


def local_fast(
    tokens, lengths, routes, cotangent, norm_gain, in_weight, conv_weight, conv_bias, dt_bias,
    a_log, d_skip, mix_gain, out_weight, ffn_gain, router_weight, shared_up, shared_down,
    expert_up, expert_down,
):
    bf, f32 = jnp.bfloat16, jnp.float32
    block = tokens.shape[1]
    parts = tokens.shape[0]
    rows = block * parts
    groups = lax.axis_size("dp")
    lines = lax.axis_size("seq")
    held = expert_up.shape[0]
    experts = held * groups
    top = routes.shape[2]
    slots = block * top * 5 // (4 * experts) * parts
    slots = -(-slots // 128) * 128
    place = lax.axis_index("seq")
    group = lax.axis_index("dp")

    def to_sequence(a):
        return lax.all_to_all(a, "seq", split_axis=0, concat_axis=1, tiled=True)[0]

    def to_blocks(a):
        return lax.all_to_all(a[None], "seq", split_axis=1, concat_axis=0, tiled=True)

    in_full = lax.all_gather(in_weight, ("dp", "seq"), axis=0, tiled=True)
    out_full = lax.all_gather(out_weight, ("dp", "seq"), axis=0, tiled=True)
    router_full = lax.all_gather(router_weight, ("dp", "seq"), axis=0, tiled=True)
    width = SFF // groups
    up_cols = shared_up.reshape(-1, 2, groups, width).transpose(2, 0, 1, 3).reshape(groups, -1, 2 * width)
    up_cols = lax.all_to_all(up_cols, "dp", split_axis=0, concat_axis=0, tiled=True)
    up_part = lax.all_gather(up_cols, "seq", axis=1).reshape(MODEL_WIDTH, 2 * width)
    down_part = lax.all_gather(shared_down, "seq", axis=0, tiled=True)

    length = lax.dynamic_index_in_dim(lengths, place, 0, False)
    x_low = to_sequence(tokens)
    route = to_sequence(routes)
    cot_low = to_sequence(cotangent)
    valid = (jnp.arange(rows) < length).astype(f32)[:, None]
    x_rows = x_low.astype(f32)
    normed, norm_pull = jax.vjp(rms_norm, x_rows, norm_gain)
    normed_low = normed.astype(bf)
    projected = jnp.dot(normed_low, in_full, preferred_element_type=f32).astype(bf)
    normed_mix, mixer_pull = jax.vjp(
        partial(mixer, valid, block=block),
        projected.astype(f32), conv_weight, conv_bias, dt_bias, a_log, d_skip, mix_gain,
    )
    mix_low = normed_mix.astype(bf)
    hidden = x_rows + jnp.dot(mix_low, out_full, preferred_element_type=f32) * valid
    normed_ffn, ffn_pull = jax.vjp(rms_norm, hidden, ffn_gain)
    ffn_low = normed_ffn.astype(bf)
    logits = jnp.dot(ffn_low, router_full, preferred_element_type=f32)
    onehot = (route[:, :, None] == jnp.arange(experts)[None, None, :]).astype(f32)
    chosen = jnp.sum(onehot, axis=1)
    peak = jnp.max(jnp.where(chosen > 0, logits, -jnp.inf), axis=1, keepdims=True)
    raised = jnp.exp(jnp.where(chosen > 0, logits - peak, -jnp.inf))
    probs = raised / jnp.sum(raised, axis=1, keepdims=True)

    all_rows = lax.all_gather(ffn_low, "dp")
    all_cot = lax.all_gather(cot_low * valid.astype(bf), "dp")
    all_probs = lax.all_gather(probs, "dp")
    all_route = lax.all_gather(route, "dp")
    mine = group * held + jnp.arange(held)
    member = jnp.any(all_route[:, :, :, None] == mine, axis=2).astype(f32)
    before = jnp.cumsum(member, axis=1) - member
    pick = (
        (before.transpose(2, 0, 1)[:, :, None, :] == jnp.arange(slots)[None, None, :, None].astype(f32))
        & (member.transpose(2, 0, 1)[:, :, None, :] > 0)
    ).astype(bf)
    gate = lax.dynamic_slice_in_dim(all_probs, group * held, held, 2)
    ein = partial(jnp.einsum, preferred_element_type=f32)
    slot_rows = ein("egst,gtd->egsd", pick, all_rows).astype(bf).reshape(held, groups * slots, MODEL_WIDTH)
    slot_cot = ein("egst,gtd->egsd", pick, all_cot).reshape(held, groups * slots, MODEL_WIDTH)
    slot_gate = jnp.einsum("egst,gte->egs", pick.astype(f32), gate, precision=PRECISE).reshape(held, groups * slots, 1)
    expert_gu = ein("erd,edf->erf", slot_rows, expert_up)
    expert_act, expert_pull = jax.vjp(partial(swiglu, half_width=EXPERT_HIDDEN), expert_gu)
    expert_h = expert_act.astype(bf)
    expert_y = ein("erf,efd->erd", expert_h, expert_down).astype(bf).astype(f32)
    slot_dot = jnp.sum(expert_y * slot_cot, axis=-1)
    grad_ey = (slot_gate * slot_cot).astype(bf)
    grad_edown = ein("erf,erd->efd", expert_h, grad_ey)
    grad_eu = expert_pull(ein("erd,efd->erf", grad_ey, expert_down))[0].astype(bf)
    grad_eup = ein("erd,erf->edf", slot_rows, grad_eu)
    grad_ein = ein("erf,edf->erd", grad_eu, expert_up).astype(bf)
    spread = lambda a: ein("egst,egsd->gtd", pick, a.reshape(held, groups, slots, MODEL_WIDTH))
    flat_rows = all_rows.reshape(-1, MODEL_WIDTH)
    flat_cot = all_cot.reshape(-1, MODEL_WIDTH)
    shared_gu = jnp.dot(flat_rows, up_part, preferred_element_type=f32)
    shared_act, shared_pull = jax.vjp(partial(swiglu, half_width=width), shared_gu)
    shared_h = shared_act.astype(bf)
    grad_sdown = contract_rows(shared_h, flat_cot)
    grad_sgu = shared_pull(contract_cols(flat_cot, down_part))[0].astype(bf)
    grad_sup = contract_rows(flat_rows, grad_sgu)
    y_part = spread((slot_gate * expert_y).astype(bf)) + jnp.dot(
        shared_h, down_part, preferred_element_type=f32
    ).reshape(groups, rows, MODEL_WIDTH)
    g_part = spread(grad_ein) + contract_cols(grad_sgu, up_part).reshape(groups, rows, MODEL_WIDTH)
    dots = jnp.einsum("egst,egs->gte", pick.astype(f32), slot_dot.reshape(held, groups, slots), precision=PRECISE)
    dots = lax.all_to_all(dots, "dp", split_axis=0, concat_axis=2, tiled=True)[0]
    scatter = lambda a: lax.psum_scatter(a.astype(bf), "dp", scatter_dimension=0, tiled=False).astype(f32)
    y_sum = scatter(y_part)
    g_sum = scatter(g_part)
    output = (hidden + valid * y_sum).astype(bf)

    grad_out = cot_low.astype(f32)
    grad_logit = (probs * (dots - jnp.sum(probs * dots, axis=1, keepdims=True))).astype(bf)
    grad_router = contract_rows(ffn_low, grad_logit)
    grad_ffn = g_sum + contract_cols(grad_logit, router_full)
    grad_hidden, grad_fgain = ffn_pull(grad_ffn)
    grad_hidden = grad_hidden + grad_out
    grad_mo = (grad_hidden * valid).astype(bf)
    grad_outw = contract_rows(mix_low, grad_mo)
    grad_mix = contract_cols(grad_mo, out_full)
    grad_proj, grad_cw, grad_cb, grad_db, grad_al, grad_skip, grad_mgain = mixer_pull(grad_mix)
    grad_proj = grad_proj.astype(bf)
    grad_inw = contract_rows(normed_low, grad_proj)
    grad_x, grad_ngain = norm_pull(contract_cols(grad_proj, in_full))
    input_grad = (grad_x + grad_hidden).astype(bf)

    def owners(g):
        g = lax.psum_scatter(g.astype(bf), "dp", scatter_dimension=0, tiled=True)
        return lax.psum_scatter(g, "seq", scatter_dimension=0, tiled=True).astype(f32)

    pieces = (
        grad_router, grad_ngain, grad_cw, grad_cb, grad_db, grad_al, grad_skip, grad_mgain, grad_fgain,
    )
    flat = jnp.concatenate([p.reshape(-1) for p in pieces])
    flat = jnp.pad(flat, (0, -flat.shape[0] % 1024)).reshape(-1, 1024)
    flat = lax.psum(flat, ("dp", "seq")).reshape(-1)
    small = []
    start = 0
    for p in pieces:
        small.append(flat[start : start + p.size].reshape(p.shape))
        start += p.size
    own_router = lax.dynamic_slice_in_dim(
        small.pop(0), (group * lines + place) * router_weight.shape[0], router_weight.shape[0], 0
    )
    along = lambda g, d: lax.psum_scatter(g.astype(bf), "seq", scatter_dimension=d, tiled=True)
    sup = grad_sup.astype(bf).reshape(groups, lines, -1, 2 * width).transpose(1, 0, 2, 3)
    sup = along(sup.reshape(MODEL_WIDTH, 2 * width), 0).reshape(groups, -1, 2 * width)
    sup = lax.all_to_all(sup, "dp", split_axis=0, concat_axis=0, tiled=True).astype(f32)
    sup = sup.reshape(groups, -1, 2, width).transpose(1, 2, 0, 3).reshape(-1, 2 * SFF)
    sdown = along(grad_sdown, 0).astype(f32)
    return (
        to_blocks(output), to_blocks(input_grad), small[0], owners(grad_inw), small[1], small[2],
        small[3], small[4], small[5], small[6], owners(grad_outw), small[7], own_router, sup, sdown,
        along(grad_eup, 1).astype(f32), along(grad_edown, 1).astype(f32),
    )


def solution(mesh):
    def program(*arrays):
        each = arrays[0].shape[0] == lax.axis_size("seq")
        return (local_fast if each else local)(*arrays)

    return jax.shard_map(
        program,
        mesh=mesh,
        in_specs=(
            P("dp", "seq", None),
            P("dp"),
            P("dp", "seq", None),
            P("dp", "seq", None),
            P(),
            P(("dp", "seq"), None),
            P(),
            P(),
            P(),
            P(),
            P(),
            P(),
            P(("dp", "seq"), None),
            P(),
            P(("dp", "seq"), None),
            P(("dp", "seq"), None),
            P(("dp", "seq"), None),
            P("dp", None, None),
            P("dp", None, None),
        ),
        out_specs=(
            P("dp", "seq", None),
            P("dp", "seq", None),
            P(),
            P(("dp", "seq"), None),
            P(),
            P(),
            P(),
            P(),
            P(),
            P(),
            P(("dp", "seq"), None),
            P(),
            P(("dp", "seq"), None),
            P(("dp", "seq"), None),
            P(("dp", "seq"), None),
            P("dp", "seq", None),
            P("dp", "seq", None),
        ),
        check_vma=False,
    )
```

```python
from functools import partial

import jax
import jax.numpy as jnp
from jax import lax
from jax.experimental import pallas as pl
from jax.experimental.pallas import tpu as pltpu
from jax.sharding import PartitionSpec as P

MODEL_WIDTH = 1536
INNER = 3072
HEADS = 48
HDIM = 64
STATE = 128
KCONV = 4
EXPERT_HIDDEN = 512
SFF = 1024
MB = 4
CONV = 3328
PROJ = 6448


EPSILON = 1e-05
PRECISE = lax.Precision.HIGHEST
MESH = pl.DeviceIdType.MESH


def from_behind(x, axis, by):
    size = lax.axis_size(axis)
    pairs = [(i, i + by) for i in range(size) if 0 <= i + by < size]
    return lax.ppermute(x, axis, pairs)


def prefix(x, axis, join, neutral):
    place = lax.axis_index(axis)
    gathered = jax.tree.map(
        lambda a, kind: lax.all_gather(a.astype(kind), axis), x, (jnp.bfloat16, jnp.bfloat16)
    )
    state = jax.tree.map(lambda a, e: jnp.zeros_like(a) + jnp.asarray(e, a.dtype), x, neutral)

    def one(step, state):
        return join(
            state,
            jax.tree.map(
                lambda a, own: lax.dynamic_index_in_dim(a, step, 0, False).astype(own.dtype),
                gathered,
                x,
            ),
        )

    return lax.fori_loop(0, place, one, state)


def prefix_2(x, axis, join, neutral):
    count = lax.axis_size(axis)
    place = lax.axis_index(axis)
    ahead = count - 1 - place
    gathered = jax.tree.map(
        lambda a, kind: lax.all_gather(a.astype(kind), axis),
        x,
        jax.tree.map(lambda a: jnp.bfloat16 if a.dtype == jnp.float32 else a.dtype, x),
    )
    state = jax.tree.map(lambda a, e: jnp.zeros_like(a) + jnp.asarray(e, a.dtype), x, neutral)

    def one(step, state):
        source = count - 1 - step
        return join(
            state,
            jax.tree.map(
                lambda a, own: lax.dynamic_index_in_dim(a, source, 0, False).astype(own.dtype),
                gathered,
                x,
            ),
        )

    return lax.fori_loop(0, ahead, one, state)


def rms_norm(values, gain_vec):
    return (
        values * lax.rsqrt(jnp.mean(values * values, axis=-1, keepdims=True) + EPSILON) * gain_vec
    )


def swiglu(values, half_width):
    return jax.nn.silu(values[..., :half_width]) * values[..., half_width:]


def contract_rows(left_mat, right_mat):
    return lax.dot_general(
        left_mat, right_mat, (((0,), (0,)), ((), ())), preferred_element_type=jnp.float32
    )


def contract_cols(left_mat, right_mat):
    return lax.dot_general(
        left_mat, right_mat, (((1,), (1,)), ((), ())), preferred_element_type=jnp.float32
    )


def block_terms(head_in, b_rows, c_rows, step_sizes, a_log):
    log_rates = -step_sizes * jnp.exp(a_log)
    cumulative = jnp.cumsum(log_rates, axis=0)
    block_len = head_in.shape[0]
    lower_tri = jnp.arange(block_len)[:, None] >= jnp.arange(block_len)[None, :]
    spread = jnp.where(
        lower_tri[:, :, None], cumulative[:, None, :] - cumulative[None, :, :], -jnp.inf
    )
    scores = jnp.dot(c_rows, b_rows.T, precision=PRECISE)
    weights = jnp.exp(spread) * scores[:, :, None] * step_sizes[None, :, :]
    local_out = jnp.einsum("tih,ihp->thp", weights, head_in, precision=PRECISE)
    tail_weight = jnp.exp(cumulative[-1][None, :] - cumulative) * step_sizes
    local_state = jnp.einsum("ih,ihp,in->hpn", tail_weight, head_in, b_rows, precision=PRECISE)
    return (cumulative, local_out, local_state, jnp.exp(cumulative[-1]))


def carried_out(c_rows, cumulative, state_in):
    return (
        jnp.einsum("tn,hpn->thp", c_rows, state_in, precision=PRECISE)
        * jnp.exp(cumulative)[:, :, None]
    )


def mixer_front(valid_rows, projected, previous, conv_weight, conv_bias, dt_bias, a_log):
    row_count = projected.shape[0]
    conv_in = projected[:, INNER : INNER + CONV]
    padded = jnp.concatenate([previous, conv_in], axis=0)
    conv_sum = conv_bias + conv_weight[0] * padded[0:row_count]
    for tap_idx in range(1, KCONV):
        conv_sum = conv_sum + conv_weight[tap_idx] * padded[tap_idx : tap_idx + row_count]
    activated = jax.nn.silu(conv_sum) * valid_rows
    head_in = activated[:, :INNER].reshape(row_count, HEADS, HDIM)
    b_rows = activated[:, INNER : INNER + STATE]
    c_rows = activated[:, INNER + STATE :]
    step_sizes = jax.nn.softplus(projected[:, INNER + CONV :] + dt_bias)
    cumulative, local_out, local_state, decay_total = block_terms(
        head_in, b_rows, c_rows, step_sizes, a_log
    )
    return (projected[:, :INNER], head_in, c_rows, cumulative, local_out, local_state, decay_total)


def mixer_tail(gate_z, head_in, c_rows, cumulative, local_out, state_in, d_skip, mix_gain):
    mixed_out = local_out + carried_out(c_rows, cumulative, state_in) + d_skip[:, None] * head_in
    gated_out = mixed_out.reshape(head_in.shape[0], INNER) * jax.nn.silu(gate_z)
    return rms_norm(gated_out, mix_gain)


def link_states(earlier, latter):
    return (earlier[0] * latter[0], latter[1] + latter[0][:, None, None] * earlier[1])


def local(
    tokens,
    lengths,
    routes,
    cotangent,
    norm_gain,
    in_weight,
    conv_weight,
    conv_bias,
    dt_bias,
    a_log,
    d_skip,
    mix_gain,
    out_weight,
    ffn_gain,
    router_weight,
    shared_up,
    shared_down,
    expert_up,
    expert_down,
):
    row_count = tokens.shape[1]
    resident_experts = expert_up.shape[0]
    groups = lax.axis_size("dp")
    experts = resident_experts * groups
    top_count = routes.shape[2]
    capacity = row_count * top_count * 5 // (4 * experts)
    shards = (in_weight, out_weight, router_weight, shared_up, shared_down)
    kept_full = (
        lax.all_gather(shards[0], ("dp", "seq"), axis=0, tiled=True),
        lax.all_gather(shards[1], ("dp", "seq"), axis=0, tiled=True),
        lax.all_gather(shards[2], ("dp", "seq"), axis=0, tiled=True),
        lax.all_gather(shards[3], ("dp", "seq"), axis=0, tiled=True),
        lax.all_gather(shards[4], ("dp", "seq"), axis=0, tiled=True),
    )
    grad_inw = jnp.zeros((MODEL_WIDTH, PROJ), jnp.float32)
    grad_outw = jnp.zeros((INNER, MODEL_WIDTH), jnp.float32)
    grad_router = jnp.zeros((MODEL_WIDTH, experts), jnp.float32)
    grad_sup = jnp.zeros((MODEL_WIDTH, 2 * SFF), jnp.float32)
    grad_sdown = jnp.zeros((SFF, MODEL_WIDTH), jnp.float32)
    expert_upward_grad = jnp.zeros((resident_experts, MODEL_WIDTH, 2 * EXPERT_HIDDEN), jnp.float32)
    grad_edown = jnp.zeros((resident_experts, EXPERT_HIDDEN, MODEL_WIDTH), jnp.float32)
    grad_ngain = jnp.zeros_like(norm_gain)
    grad_cw = jnp.zeros_like(conv_weight)
    grad_cb = jnp.zeros_like(conv_bias)
    grad_db = jnp.zeros_like(dt_bias)
    grad_al = jnp.zeros_like(a_log)
    grad_skip = jnp.zeros_like(d_skip)
    grad_mgain = jnp.zeros_like(mix_gain)
    grad_fgain = jnp.zeros_like(ffn_gain)
    outputs = []
    input_grads = []
    for micro_idx in range(MB):
        in_full, out_full, router_full, up_full, down_full = kept_full
        x_rows = tokens[micro_idx].astype(jnp.float32)
        position = lax.axis_index("seq") * row_count + jnp.arange(row_count)
        valid_rows = (position < lengths[micro_idx]).astype(jnp.float32)[:, None]
        normed, norm_pull = jax.vjp(rms_norm, x_rows, norm_gain)
        normed_low = normed.astype(jnp.bfloat16)
        projected = jnp.dot(normed_low, in_full, preferred_element_type=jnp.float32).astype(
            jnp.bfloat16
        )
        previous = from_behind(projected[row_count - (KCONV - 1) :, INNER : INNER + CONV], "seq", 1)
        front_out, front_pull = jax.vjp(
            partial(mixer_front, valid_rows),
            projected.astype(jnp.float32),
            previous.astype(jnp.float32),
            conv_weight,
            conv_bias,
            dt_bias,
            a_log,
        )
        gate_z, head_in, c_rows, cumulative, local_out, local_state, decay_total = front_out
        identity = (jnp.ones_like(decay_total), jnp.zeros_like(local_state))
        _, state_in = prefix((decay_total, local_state), "seq", link_states, identity)
        normed_mix, tail_pull = jax.vjp(
            mixer_tail, gate_z, head_in, c_rows, cumulative, local_out, state_in, d_skip, mix_gain
        )
        mix_low = normed_mix.astype(jnp.bfloat16)
        mixer_out = jnp.dot(mix_low, out_full, preferred_element_type=jnp.float32)
        hidden = x_rows + mixer_out * valid_rows
        normed_ffn, ffn_pull = jax.vjp(rms_norm, hidden, ffn_gain)
        ffn_low = normed_ffn.astype(jnp.bfloat16)
        logits = jnp.dot(ffn_low, router_full, preferred_element_type=jnp.float32)
        route_row = routes[micro_idx]
        picked = jnp.take_along_axis(logits, route_row, axis=1)
        gate_probs = jax.nn.softmax(picked, axis=-1)
        shared_gu = jnp.dot(ffn_low, up_full, preferred_element_type=jnp.float32)
        shared_act, shared_pull = jax.vjp(partial(swiglu, half_width=SFF), shared_gu)
        shared_h = shared_act.astype(jnp.bfloat16)
        shared_y = jnp.dot(shared_h, down_full, preferred_element_type=jnp.float32)
        flat_route = route_row.reshape(-1)
        member = (flat_route[:, None] == jnp.arange(experts)[None, :]).astype(jnp.int32)
        slot_pos = jnp.sum((jnp.cumsum(member, axis=0) - member) * member, axis=1)
        target = flat_route * capacity + slot_pos
        source = (
            jnp.zeros((experts * capacity,), jnp.int32)
            .at[target]
            .set(jnp.arange(row_count * top_count, dtype=jnp.int32))
        )
        filled = jnp.zeros((experts * capacity, 1), jnp.bfloat16).at[target].set(jnp.bfloat16(1))
        outgoing = (jnp.take(ffn_low, source // top_count, axis=0) * filled).reshape(
            groups, resident_experts, capacity, MODEL_WIDTH
        )
        received_rows = lax.all_to_all(outgoing, "dp", split_axis=0, concat_axis=2, tiled=True)[0]
        expert_gu = jnp.einsum(
            "erd,edf->erf", received_rows, expert_up, preferred_element_type=jnp.float32
        )
        expert_act, expert_pull = jax.vjp(partial(swiglu, half_width=EXPERT_HIDDEN), expert_gu)
        expert_h = expert_act.astype(jnp.bfloat16)
        expert_y = jnp.einsum(
            "erf,efd->erd", expert_h, expert_down, preferred_element_type=jnp.float32
        ).astype(jnp.bfloat16)
        returned = lax.all_to_all(expert_y[None], "dp", split_axis=2, concat_axis=0, tiled=True)
        per_choice = (
            jnp.take(returned.reshape(experts * capacity, MODEL_WIDTH), target, axis=0)
            .reshape(row_count, top_count, MODEL_WIDTH)
            .astype(jnp.float32)
        )
        routed = jnp.einsum("lk,lkd->ld", gate_probs, per_choice, precision=PRECISE)
        outputs.append((hidden + valid_rows * (shared_y + routed)).astype(jnp.bfloat16))
        in_back, out_back, router_back, up_back, down_back = kept_full
        grad_out = cotangent[micro_idx].astype(jnp.float32)
        branch = valid_rows * grad_out
        shared_g = branch.astype(jnp.bfloat16)
        grad_sdown = grad_sdown + contract_rows(shared_h, shared_g)
        grad_sgu = shared_pull(contract_cols(shared_g, down_back))[0].astype(jnp.bfloat16)
        grad_sup = grad_sup + contract_rows(ffn_low, grad_sgu)
        grad_ffn = contract_cols(grad_sgu, up_back)
        grad_choice = (gate_probs[:, :, None] * branch[:, None, :]).astype(jnp.bfloat16)
        grad_gate = jnp.sum(branch[:, None, :] * per_choice, axis=-1)
        grad_pick = gate_probs * (
            grad_gate - jnp.sum(gate_probs * grad_gate, axis=-1, keepdims=True)
        )
        onehot = (route_row[:, :, None] == jnp.arange(experts)[None, None, :]).astype(jnp.float32)
        grad_logit = jnp.einsum("lk,lke->le", grad_pick, onehot, precision=PRECISE).astype(
            jnp.bfloat16
        )
        grad_router = grad_router + contract_rows(ffn_low, grad_logit)
        grad_ffn = grad_ffn + contract_cols(grad_logit, router_back)
        back_out = (
            jnp.take(grad_choice.reshape(row_count * top_count, MODEL_WIDTH), source, axis=0)
            * filled
        ).reshape(groups, resident_experts, capacity, MODEL_WIDTH)
        grad_arrived = lax.all_to_all(back_out, "dp", split_axis=0, concat_axis=2, tiled=True)[0]
        step_edown = jnp.einsum(
            "erf,erd->efd", expert_h, grad_arrived, preferred_element_type=jnp.float32
        )
        grad_eh = jnp.einsum(
            "erd,efd->erf", grad_arrived, expert_down, preferred_element_type=jnp.float32
        )
        expert_gate_up_grad = expert_pull(grad_eh)[0].astype(jnp.bfloat16)
        expert_upward_step = jnp.einsum(
            "tbw,tbj->twj", received_rows, expert_gate_up_grad, preferred_element_type=jnp.float32
        )
        grad_ein = jnp.einsum(
            "erf,edf->erd", expert_gate_up_grad, expert_up, preferred_element_type=jnp.float32
        ).astype(jnp.bfloat16)
        expert_upward_grad = expert_upward_grad + expert_upward_step
        grad_edown = grad_edown + step_edown
        came_back = lax.all_to_all(grad_ein[None], "dp", split_axis=2, concat_axis=0, tiled=True)
        grad_ffn = grad_ffn + jnp.sum(
            jnp.take(came_back.reshape(experts * capacity, MODEL_WIDTH), target, axis=0)
            .reshape(row_count, top_count, MODEL_WIDTH)
            .astype(jnp.float32),
            axis=1,
        )
        grad_hidden, step_fgain = ffn_pull(grad_ffn)
        grad_fgain = grad_fgain + step_fgain
        grad_hidden = grad_hidden + grad_out
        grad_mix_out = (grad_hidden * valid_rows).astype(jnp.bfloat16)
        grad_outw = grad_outw + contract_rows(mix_low, grad_mix_out)
        grad_mix = contract_cols(grad_mix_out, out_back)
        grad_z, grad_head, grad_c, grad_cum, grad_local, grad_state, step_skip, step_mgain = (
            tail_pull(grad_mix)
        )
        grad_skip = grad_skip + step_skip
        grad_mgain = grad_mgain + step_mgain
        _, grad_carry = prefix_2((decay_total, grad_state), "seq", link_states, identity)
        grad_decay = jnp.sum(grad_carry * state_in, axis=(1, 2))
        grad_proj, grad_prev, step_cw, step_cb, step_db, step_al = front_pull(
            (grad_z, grad_head, grad_c, grad_cum, grad_local, grad_carry, grad_decay)
        )
        grad_cw = grad_cw + step_cw
        grad_cb = grad_cb + step_cb
        grad_db = grad_db + step_db
        grad_al = grad_al + step_al
        from_next = from_behind(grad_prev.astype(jnp.bfloat16), "seq", -1).astype(grad_prev.dtype)
        grad_proj = (
            grad_proj.at[row_count - (KCONV - 1) :, INNER : INNER + CONV]
            .add(from_next)
            .astype(jnp.bfloat16)
        )
        grad_inw = grad_inw + contract_rows(normed_low, grad_proj)
        grad_normed = contract_cols(grad_proj, in_back)
        grad_x, step_ngain = norm_pull(grad_normed)
        grad_ngain = grad_ngain + step_ngain
        input_grads.append((grad_x + grad_hidden).astype(jnp.bfloat16))
    weight_grads = (
        lax.psum_scatter(grad_inw, ("dp", "seq"), scatter_dimension=0, tiled=True),
        lax.psum_scatter(grad_outw, ("dp", "seq"), scatter_dimension=0, tiled=True),
        lax.psum_scatter(grad_router, ("dp", "seq"), scatter_dimension=0, tiled=True),
        lax.psum_scatter(grad_sup, ("dp", "seq"), scatter_dimension=0, tiled=True),
        lax.psum_scatter(grad_sdown, ("dp", "seq"), scatter_dimension=0, tiled=True),
    )
    small_sums = lax.psum(
        (grad_ngain, grad_cw, grad_cb, grad_db, grad_al, grad_skip, grad_mgain, grad_fgain),
        ("dp", "seq"),
    )
    expert_sums = (
        lax.psum_scatter(
            expert_upward_grad.astype(jnp.bfloat16), "seq", scatter_dimension=1, tiled=True
        ).astype(jnp.float32),
        lax.psum_scatter(
            grad_edown.astype(jnp.bfloat16), "seq", scatter_dimension=1, tiled=True
        ).astype(jnp.float32),
    )
    return (
        jnp.stack(outputs),
        jnp.stack(input_grads),
        small_sums[0],
        weight_grads[0],
        small_sums[1],
        small_sums[2],
        small_sums[3],
        small_sums[4],
        small_sums[5],
        small_sums[6],
        weight_grads[1],
        small_sums[7],
        weight_grads[2],
        weight_grads[3],
        weight_grads[4],
        expert_sums[0],
        expert_sums[1],
    )


def at_neighbours():
    d = lax.axis_index("dp")
    core, x, y = d % 2, (d // 2) % 2, d // 4
    return d, core, x, y, d + 1 - 2 * core, d + 2 - 4 * x, d + 4 - 8 * y


def meet(devices):
    barrier = pltpu.get_barrier_semaphore()
    for there in devices:
        pl.semaphore_signal(barrier, inc=1, device_id=there, device_id_type=MESH)
    pl.semaphore_wait(barrier, len(devices))


def send(source, target, send_sem, recv_sem, there):
    copy = pltpu.make_async_remote_copy(
        src_ref=source, dst_ref=target, send_sem=send_sem, recv_sem=recv_sem,
        device_id=there, device_id_type=MESH,
    )
    copy.start()
    return copy


def add_into(target, source, high):
    step = 16
    for s in (64, 48, 32):
        if high % s == 0:
            step = s
            break

    @pl.loop(0, high // step)
    def _(i):
        rows = pl.ds(pl.multiple_of(i * step, step), step)
        target[rows, :] = target[rows, :] + source[rows, :]


def swap_start(swaps, landed, line, lines, local_sem, send_sem, recv_sem):
    copies = []
    for n, (a, b) in enumerate(zip(swaps, landed)):
        keep = pltpu.make_async_copy(a.at[line], b.at[line], local_sem.at[n])
        keep.start()
        away = [
            send(a.at[o], b.at[line], send_sem.at[n, k], recv_sem.at[n, k], {"seq": o})
            for k, o in enumerate(lax.rem(line + k, lines) for k in range(1, lines))
        ]
        copies.append((keep, away))
    return copies


def swap_end(copies):
    for keep, away in copies:
        for copy in away:
            copy.wait_recv()
    for keep, away in copies:
        for copy in away:
            copy.wait_send()
        keep.wait()


def swap_sems(count, lines):
    dma = pltpu.SemaphoreType.DMA
    return [dma((count,)), dma((count, lines - 1)), dma((count, lines - 1))]


def sum_body(items, arrays, lines, tiny, moved, *refs):
    count = len(items)
    grads, refs = refs[:arrays], refs[arrays:]
    swaps, refs = refs[:moved], refs[moved:]
    if tiny:
        small_in, refs = refs[0], refs[1:]
    outs, refs = refs[:arrays], refs[arrays:]
    landed, refs = refs[:moved], refs[moved:]
    if tiny:
        small_out, refs = refs[0], refs[1:]
    own, refs = refs[:count], refs[count:]
    got, refs = refs[:count], refs[count:]
    from_x, refs = refs[:count], refs[count:]
    from_y, refs = refs[:count], refs[count:]
    last_x, refs = refs[:count], refs[count:]
    last_y, refs = refs[:count], refs[count:]
    if lines > 1:
        from_z, refs = refs[:count], refs[count:]
    (load_sem, send_sem, recv_sem), refs = refs[:3], refs[3:]
    if moved:
        swap_sem, refs = refs[:3], refs[3:]
    if tiny:
        half, t_core, t_x, t_y, t_z, t_back, t_send, t_recv = refs
    d, core, x, y, at_core, at_x, at_y = at_neighbours()
    line = lax.axis_index("seq")
    others = [lax.rem(line + k, lines) for k in range(1, lines)]
    meet([{"dp": at_core}, {"dp": at_x}, {"dp": at_y}] + [{"seq": o} for o in others])
    sent = [[] for _ in items]
    stage = [None] * count
    cross = [None] * count
    close = [None] * count
    along = [None] * count
    loads = [None] * count

    def begin(t):
        a, c0, wide, high = items[t]
        cols = pl.ds(c0, wide)
        loads[t] = pltpu.make_async_copy(grads[a].at[:, :, core, :, cols], own[t], load_sem.at[t])
        loads[t].start()
        stage[t] = send(
            grads[a].at[:, :, 1 - core, :, cols], got[t], send_sem.at[t, 0], recv_sem.at[t, 0], {"dp": at_core}
        )

    def fold(t):
        a, c0, wide, high = items[t]
        loads[t].wait()
        stage[t].wait_recv()
        for i in range(2):
            for j in range(2):
                add_into(got[t].at[i, j], own[t].at[i, j], high)
        top, low = pl.ds(0, high // 2), pl.ds(high // 2, high // 2)
        cross[t] = (
            send(got[t].at[:, 1 - x, top, :], from_x[t], send_sem.at[t, 1], recv_sem.at[t, 1], {"dp": at_x}),
            send(got[t].at[1 - y, :, low, :], from_y[t], send_sem.at[t, 2], recv_sem.at[t, 2], {"dp": at_y}),
        )

    def turn(t):
        a, c0, wide, high = items[t]
        top, low = pl.ds(0, high // 2), pl.ds(high // 2, high // 2)
        cross[t][0].wait_recv()
        for i in range(2):
            add_into(got[t].at[i, x, top, :], from_x[t].at[i], high // 2)
        close_y = send(got[t].at[1 - y, x, top, :], last_y[t], send_sem.at[t, 3], recv_sem.at[t, 3], {"dp": at_y})
        cross[t][1].wait_recv()
        for j in range(2):
            add_into(got[t].at[y, j, low, :], from_y[t].at[j], high // 2)
        close_x = send(got[t].at[y, 1 - x, low, :], last_x[t], send_sem.at[t, 4], recv_sem.at[t, 4], {"dp": at_x})
        close[t] = (close_y, close_x)

    def settle(t):
        a, c0, wide, high = items[t]
        top, low = pl.ds(0, high // 2), pl.ds(high // 2, high // 2)
        cols = pl.ds(c0, wide)
        close[t][0].wait_recv()
        add_into(got[t].at[y, x, top, :], last_y[t], high // 2)
        close[t][1].wait_recv()
        add_into(got[t].at[y, x, low, :], last_x[t], high // 2)
        if lines == 1:
            outs[a][:, cols] = got[t][y, x].astype(outs[a].dtype)
            return
        each = high // lines
        along[t] = [
            send(
                got[t].at[y, x, pl.ds(pl.multiple_of(o * each, 16), each), :], from_z[t].at[k],
                send_sem.at[t, 5 + k], recv_sem.at[t, 5 + k], {"seq": o},
            )
            for k, o in enumerate(others)
        ]

    def finish(t):
        a, c0, wide, high = items[t]
        each = high // lines
        total = got[t][y, x, pl.ds(pl.multiple_of(line * each, 16), each), :].astype(jnp.float32)
        for k in range(lines - 1):
            along[t][k].wait_recv()
            total = total + from_z[t][k].astype(jnp.float32)
        outs[a][:, pl.ds(c0, wide)] = total

    little = []

    def tiny_step(n):
        rows = half.shape[1]
        if n == 0:
            there = pl.ds(pl.multiple_of((1 - core) * rows, 8), rows)
            little.append(send(small_in.at[there, :], t_core, t_send.at[0], t_recv.at[0], {"dp": at_core}))
        elif n == 1:
            little[0].wait_recv()
            here = pl.ds(pl.multiple_of(core * rows, 8), rows)
            half[0] = small_in[here, :] + t_core[...]
            little.append(send(half.at[0], t_x, t_send.at[1], t_recv.at[1], {"dp": at_x}))
        elif n == 2:
            little[1].wait_recv()
            half[1] = half[0] + t_x[...]
            little.append(send(half.at[1], t_y, t_send.at[2], t_recv.at[2], {"dp": at_y}))
        elif n == 3:
            little[2].wait_recv()
            half[2] = half[1] + t_y[...]
            t_z[line] = half[2]
            for k, o in enumerate(others):
                little.append(send(half.at[2], t_z.at[line], t_send.at[3 + k], t_recv.at[3 + k], {"seq": o}))
        elif n == 4:
            for k in range(lines - 1):
                little[3 + k].wait_recv()
            total = t_z[0]
            for k in range(1, lines):
                total = total + t_z[k]
            half[3] = total
            small_out[pl.ds(pl.multiple_of(core * rows, 8), rows), :] = total
            little.append(send(half.at[3], t_back, t_send.at[7], t_recv.at[7], {"dp": at_core}))
        elif n == 5:
            little[-1].wait_recv()
            small_out[pl.ds(pl.multiple_of((1 - core) * rows, 8), rows), :] = t_back[...]
            for copy in little:
                copy.wait_send()

    begin(0)
    if tiny:
        tiny_step(0)
    moves = swap_start(swaps, landed, line, lines, *swap_sem) if moved else ()
    for t in range(max(count + 3, 5 if tiny else 0)):
        if t + 1 < count:
            begin(t + 1)
        if t < count:
            fold(t)
        if 0 <= t - 1 < count:
            turn(t - 1)
        if 0 <= t - 2 < count:
            settle(t - 2)
        if lines > 1 and 0 <= t - 3 < count:
            finish(t - 3)
        if tiny and t < 5:
            tiny_step(t + 1)
    swap_end(moves)
    for t in range(count):
        stage[t].wait_send()
        for copy in cross[t] + close[t] + tuple(along[t] or ()):
            copy.wait_send()


def sum_to_owners(grads, widths, lines, kinds, small, swaps, identity):
    items, views = [], []
    for a, (g, wide) in enumerate(zip(grads, widths)):
        high, cols = g.shape[0] // 8, g.shape[1]
        views.append(g.reshape(2, 2, 2, high, cols))
        start = 0
        while start < cols:
            w = min(wide, cols - start)
            items.append((a, start, w, high))
            start += w
    tiny = small is not None
    bf = jnp.bfloat16
    scratch = [pltpu.VMEM((2, 2, h, w), bf) for _, _, w, h in items]
    scratch += [pltpu.VMEM((2, 2, h, w), bf) for _, _, w, h in items]
    scratch += [pltpu.VMEM((2, h // 2, w), bf) for _, _, w, h in items] * 2
    scratch += [pltpu.VMEM((h // 2, w), bf) for _, _, w, h in items] * 2
    if lines > 1:
        scratch += [pltpu.VMEM((lines - 1, h // lines, w), bf) for _, _, w, h in items]
    ways = 4 + lines
    scratch += [
        pltpu.SemaphoreType.DMA((len(items),)),
        pltpu.SemaphoreType.DMA((len(items), ways)),
        pltpu.SemaphoreType.DMA((len(items), ways)),
    ]
    out_shape = [
        jax.ShapeDtypeStruct((g.shape[0] // 8 // lines, g.shape[1]), kind) for g, kind in zip(grads, kinds)
    ]
    ins = list(views)
    in_specs = [pl.BlockSpec(memory_space=pl.ANY)] * len(views)
    out_specs = [pl.BlockSpec(memory_space=pltpu.VMEM)] * len(views)
    if swaps:
        scratch += swap_sems(len(swaps), lines)
        ins += swaps
        in_specs += [pl.BlockSpec(memory_space=pl.ANY)] * len(swaps)
        out_specs += [pl.BlockSpec(memory_space=pl.ANY)] * len(swaps)
        out_shape += [jax.ShapeDtypeStruct(a.shape, a.dtype) for a in swaps]
    if tiny:
        rows = small.shape[0] // 2
        part = lambda *lead: pltpu.VMEM(lead + (rows, 128), jnp.float32)
        scratch += [part(4), part(), part(), part(), part(lines), part()]
        scratch += [pltpu.SemaphoreType.DMA((8,)), pltpu.SemaphoreType.DMA((8,))]
        out_shape.append(jax.ShapeDtypeStruct(small.shape, jnp.float32))
        ins.append(small)
        in_specs.append(pl.BlockSpec(memory_space=pltpu.VMEM))
        out_specs.append(pl.BlockSpec(memory_space=pltpu.VMEM))
    return pl.pallas_call(
        partial(sum_body, items, len(views), lines, tiny, len(swaps)),
        out_shape=out_shape,
        in_specs=in_specs,
        out_specs=out_specs,
        scratch_shapes=scratch,
        name="sum_to_owners_%d" % identity,
        compiler_params=pltpu.CompilerParams(
            collective_id=identity, has_side_effects=True, vmem_limit_bytes=60 << 20
        ),
    )(*ins)


def gather_body(pieces, arrays, lines, ahead, moved, *refs):
    mine, refs = refs[:arrays], refs[arrays:]
    swaps, refs = refs[:moved], refs[moved:]
    full, refs = refs[:arrays], refs[arrays:]
    landed, refs = refs[:moved], refs[moved:]
    keep_sem, send_sem, recv_sem, z_send, z_recv = refs[:5]
    swap_sem = refs[5:]
    d, core, x, y, at_core, at_x, at_y = at_neighbours()
    at_far = at_x + at_y - d
    line = lax.rem(lax.axis_index("seq"), lines)
    hops = [line]
    if lines > 1:
        upper = line // 2
        hops += [line + 1 - 2 * (line % 2), 2 - upper, 3 - 3 * upper]
    meet([{"dp": at_core}, {"dp": at_x}, {"dp": at_y}] + [{"seq": o} for o in hops[1:]])
    keep = []
    for a in range(arrays):
        keep.append(pltpu.make_async_copy(mine[a], full[a].at[d, line], keep_sem.at[a]))
        keep[a].start()
    order = [(j, p) for j in range(lines) for p in range(len(pieces))]
    total = len(order)
    out = [[None] * 7 for _ in order]
    z_copies = []

    def place(j, p, block):
        a, r0, high = pieces[p]
        return full[a].at[block, hops[j], pl.ds(r0, high), :]

    def z_copy(j, p, slot):
        a, r0, high = pieces[p]
        return pltpu.make_async_remote_copy(
            src_ref=mine[a].at[pl.ds(r0, high), :], dst_ref=full[a].at[d, line, pl.ds(r0, high), :],
            send_sem=z_send.at[p, j - 1], recv_sem=z_recv.at[p, slot],
            device_id={"seq": hops[j]}, device_id_type=MESH,
        )

    def z_round(j):
        for p in range(len(pieces)):
            z_copies.append(z_copy(j, p, line))
            z_copies[-1].start()

    def first(i):
        j, p = order[i]
        a, r0, high = pieces[p]
        if j == 0:
            block = mine[a].at[pl.ds(r0, high), :]
        else:
            z_copy(j, p, hops[j]).wait_recv()
            block = place(j, p, d)
        for n, there in enumerate((at_x, at_y, at_core)):
            out[i][n] = send(block, place(j, p, d), send_sem.at[i, n], recv_sem.at[i, n], {"dp": there})

    def pass_on(i, n, block, there):
        j, p = order[i]
        out[i][n] = send(
            place(j, p, block), place(j, p, block), send_sem.at[i, n], recv_sem.at[i, n], {"dp": there}
        )

    def second(i):
        out[i][0].wait_recv()
        if i % 2 == 0:
            pass_on(i, 5, at_x, at_y)
        pass_on(i, 3, at_x, at_core)
        out[i][1].wait_recv()
        if i % 2 == 1:
            pass_on(i, 5, at_y, at_x)
        pass_on(i, 4, at_y, at_core)

    def third(i):
        out[i][5].wait_recv()
        pass_on(i, 6, at_far, at_core)

    moves = swap_start(swaps, landed, line, lines, *swap_sem) if moved else ()
    if lines > 1:
        z_round(1)
    for i in range(min(ahead, total)):
        first(i)
    if lines > 1:
        z_round(2)
    for i in range(total):
        if i + ahead < total:
            first(i + ahead)
            if lines > 1 and order[i + ahead] == (2, 0):
                z_round(3)
        second(i)
        if i:
            third(i - 1)
    third(total - 1)
    for i in range(total):
        for n in (2, 3, 4, 6):
            out[i][n].wait_recv()
        for copy in out[i]:
            copy.wait_send()
    swap_end(moves)
    for copy in z_copies:
        copy.wait_send()
    for copy in keep:
        copy.wait()


def gather_rows(arrays, chunks, lines, ahead, swaps, identity):
    pieces = []
    for a, (w, chunk) in enumerate(zip(arrays, chunks)):
        for r0 in range(0, w.shape[0], chunk):
            pieces.append((a, r0, chunk))
    total = lines * len(pieces)
    anywhere = pl.BlockSpec(memory_space=pl.ANY)
    return pl.pallas_call(
        partial(gather_body, pieces, len(arrays), lines, ahead, len(swaps)),
        out_shape=[jax.ShapeDtypeStruct((8, lines) + w.shape, w.dtype) for w in arrays]
        + [jax.ShapeDtypeStruct(a.shape, a.dtype) for a in swaps],
        in_specs=[anywhere] * (len(arrays) + len(swaps)),
        out_specs=[anywhere] * (len(arrays) + len(swaps)),
        scratch_shapes=[
            pltpu.SemaphoreType.DMA((len(arrays),)),
            pltpu.SemaphoreType.DMA((total, 7)),
            pltpu.SemaphoreType.DMA((total, 7)),
            pltpu.SemaphoreType.DMA((len(pieces), max(1, lines - 1))),
            pltpu.SemaphoreType.DMA((len(pieces), lines)),
        ]
        + (swap_sems(len(swaps), lines) if swaps else []),
        name="gather_rows_%d" % identity,
        compiler_params=pltpu.CompilerParams(collective_id=identity, has_side_effects=True),
    )(*arrays, *swaps)


def ssd_sequence(head_in, b_rows, c_rows, step_sizes, a_log, block):
    count = head_in.shape[0] // block
    split = lambda a: a.reshape((count, block) + a.shape[1:])
    cumulative, local_out, local_state, decay_total = jax.vmap(
        block_terms, in_axes=(0, 0, 0, 0, None)
    )(split(head_in), split(b_rows), split(c_rows), split(step_sizes), a_log)
    state = jnp.zeros_like(local_state[0])
    pieces = []
    c_blocks = split(c_rows)
    for i in range(count):
        pieces.append(local_out[i] + carried_out(c_blocks[i], cumulative[i], state))
        state = decay_total[i][:, None, None] * state + local_state[i]
    return jnp.concatenate(pieces, axis=0)


def mixer(valid_rows, projected, conv_weight, conv_bias, dt_bias, a_log, d_skip, mix_gain, block):
    row_count = projected.shape[0]
    conv_in = projected[:, INNER : INNER + CONV]
    padded = jnp.concatenate([jnp.zeros((KCONV - 1, CONV), jnp.float32), conv_in], axis=0)
    conv_sum = conv_bias + conv_weight[0] * padded[0:row_count]
    for tap_idx in range(1, KCONV):
        conv_sum = conv_sum + conv_weight[tap_idx] * padded[tap_idx : tap_idx + row_count]
    activated = jax.nn.silu(conv_sum) * valid_rows
    head_in = activated[:, :INNER].reshape(row_count, HEADS, HDIM)
    b_rows = activated[:, INNER : INNER + STATE]
    c_rows = activated[:, INNER + STATE :]
    step_sizes = jax.nn.softplus(projected[:, INNER + CONV :] + dt_bias)
    mixed = ssd_sequence(head_in, b_rows, c_rows, step_sizes, a_log, block)
    mixed = mixed + d_skip[:, None] * head_in
    gated = mixed.reshape(row_count, INNER) * jax.nn.silu(projected[:, :INNER])
    return rms_norm(gated, mix_gain)


def local_fast(
    tokens, lengths, routes, cotangent, norm_gain, in_weight, conv_weight, conv_bias, dt_bias,
    a_log, d_skip, mix_gain, out_weight, ffn_gain, router_weight, shared_up, shared_down,
    expert_up, expert_down,
):
    bf, f32 = jnp.bfloat16, jnp.float32
    block = tokens.shape[1]
    parts = tokens.shape[0]
    rows = block * parts
    groups = lax.axis_size("dp")
    lines = lax.axis_size("seq")
    held = expert_up.shape[0]
    experts = held * groups
    top = routes.shape[2]
    slots = block * top * 5 // (4 * experts) * parts
    slots = -(-slots // 128) * 128
    place = lax.axis_index("seq")
    group = lax.axis_index("dp")

    in_blocks, x_low, cot_low, route = gather_rows(
        [in_weight], [in_weight.shape[0] // 3], lines, 2, [tokens, cotangent, routes], 1
    )
    in_full = in_blocks.reshape(MODEL_WIDTH, -1)
    in_full, late_out = lax.optimization_barrier((in_full, out_weight))
    out_full = lax.all_gather(late_out, ("dp", "seq"), axis=0, tiled=True)
    router_full = lax.all_gather(router_weight, ("dp", "seq"), axis=0, tiled=True)
    width = SFF // groups
    up_cols = shared_up.reshape(-1, 2, groups, width).transpose(2, 0, 1, 3).reshape(groups, -1, 2 * width)
    up_cols = lax.all_to_all(up_cols, "dp", split_axis=0, concat_axis=0, tiled=True)
    up_part = lax.all_gather(up_cols, "seq", axis=1).reshape(MODEL_WIDTH, 2 * width)
    down_part = lax.all_gather(shared_down, "seq", axis=0, tiled=True)

    length = lax.dynamic_index_in_dim(lengths, place, 0, False)
    x_low = x_low.reshape(rows, MODEL_WIDTH)
    cot_low = cot_low.reshape(rows, MODEL_WIDTH)
    route = route.reshape(rows, top)
    valid = (jnp.arange(rows) < length).astype(f32)[:, None]
    x_rows = x_low.astype(f32)
    normed, norm_pull = jax.vjp(rms_norm, x_rows, norm_gain)
    normed_low = normed.astype(bf)
    projected = jnp.dot(normed_low, in_full, preferred_element_type=f32).astype(bf)
    normed_mix, mixer_pull = jax.vjp(
        partial(mixer, valid, block=block),
        projected.astype(f32), conv_weight, conv_bias, dt_bias, a_log, d_skip, mix_gain,
    )
    mix_low = normed_mix.astype(bf)
    hidden = x_rows + jnp.dot(mix_low, out_full, preferred_element_type=f32) * valid
    normed_ffn, ffn_pull = jax.vjp(rms_norm, hidden, ffn_gain)
    ffn_low = normed_ffn.astype(bf)
    logits = jnp.dot(ffn_low, router_full, preferred_element_type=f32)
    onehot = (route[:, :, None] == jnp.arange(experts)[None, None, :]).astype(f32)
    chosen = jnp.sum(onehot, axis=1)
    peak = jnp.max(jnp.where(chosen > 0, logits, -jnp.inf), axis=1, keepdims=True)
    raised = jnp.exp(jnp.where(chosen > 0, logits - peak, -jnp.inf))
    probs = raised / jnp.sum(raised, axis=1, keepdims=True)

    all_cot = lax.all_gather(cot_low * valid.astype(bf), "dp")
    all_route = lax.all_gather(route, "dp")
    all_rows, all_probs = gather_rows(
        [ffn_low, jnp.pad(probs, ((0, 0), (0, 128 - experts)))], [64, rows], 1, 2, [], 2
    )
    all_rows, all_probs = all_rows[:, 0], all_probs[:, 0]
    mine = group * held + jnp.arange(held)
    member = jnp.any(all_route[:, :, :, None] == mine, axis=2).astype(f32)
    before = jnp.cumsum(member, axis=1) - member
    pick = (
        (before.transpose(2, 0, 1)[:, :, None, :] == jnp.arange(slots)[None, None, :, None].astype(f32))
        & (member.transpose(2, 0, 1)[:, :, None, :] > 0)
    ).astype(bf)
    gate = lax.dynamic_slice_in_dim(all_probs, group * held, held, 2)
    ein = partial(jnp.einsum, preferred_element_type=f32)
    slot_rows = ein("egst,gtd->egsd", pick, all_rows).astype(bf).reshape(held, groups * slots, MODEL_WIDTH)
    slot_cot = ein("egst,gtd->egsd", pick, all_cot).reshape(held, groups * slots, MODEL_WIDTH)
    slot_gate = jnp.einsum("egst,gte->egs", pick.astype(f32), gate, precision=PRECISE).reshape(held, groups * slots, 1)
    expert_gu = ein("erd,edf->erf", slot_rows, expert_up)
    expert_act, expert_pull = jax.vjp(partial(swiglu, half_width=EXPERT_HIDDEN), expert_gu)
    expert_h = expert_act.astype(bf)
    expert_y = ein("erf,efd->erd", expert_h, expert_down).astype(bf).astype(f32)
    slot_dot = jnp.sum(expert_y * slot_cot, axis=-1)
    grad_ey = (slot_gate * slot_cot).astype(bf)
    grad_edown = ein("erf,erd->efd", expert_h, grad_ey)
    grad_eu = expert_pull(ein("erd,efd->erf", grad_ey, expert_down))[0].astype(bf)
    grad_eup = ein("erd,erf->edf", slot_rows, grad_eu)
    grad_ein = ein("erf,edf->erd", grad_eu, expert_up).astype(bf)
    spread = lambda a: ein("egst,egsd->gtd", pick, a.reshape(held, groups, slots, MODEL_WIDTH))
    flat_rows = all_rows.reshape(-1, MODEL_WIDTH)
    flat_cot = all_cot.reshape(-1, MODEL_WIDTH)
    shared_gu = jnp.dot(flat_rows, up_part, preferred_element_type=f32)
    shared_act, shared_pull = jax.vjp(partial(swiglu, half_width=width), shared_gu)
    shared_h = shared_act.astype(bf)
    grad_sdown = contract_rows(shared_h, flat_cot)
    grad_sgu = shared_pull(contract_cols(flat_cot, down_part))[0].astype(bf)
    grad_sup = contract_rows(flat_rows, grad_sgu)
    y_part = spread((slot_gate * expert_y).astype(bf)) + jnp.dot(
        shared_h, down_part, preferred_element_type=f32
    ).reshape(groups, rows, MODEL_WIDTH)
    g_part = spread(grad_ein) + contract_cols(grad_sgu, up_part).reshape(groups, rows, MODEL_WIDTH)
    dots = jnp.einsum("egst,egs->gte", pick.astype(f32), slot_dot.reshape(held, groups, slots), precision=PRECISE)
    at_own = jnp.arange(128) == mine[:, None]
    dots = jnp.einsum("gte,ef->gtf", dots, at_own.astype(f32), precision=PRECISE)
    dots_hi = dots.astype(bf)
    dots_lo = jnp.roll((dots - dots_hi.astype(f32)).astype(bf), experts, axis=-1)
    g_sum, dots = sum_to_owners(
        [g_part.astype(bf).reshape(-1, MODEL_WIDTH), (dots_hi + dots_lo).reshape(-1, 128)],
        [384, 128], 1, [f32, f32], None, [], 3,
    )
    dots = dots[:, :experts] + dots[:, experts : 2 * experts]
    y_sum = lax.psum_scatter(y_part.astype(bf), "dp", scatter_dimension=0, tiled=False).astype(f32)
    output = (hidden + valid * y_sum).astype(bf)

    grad_out = cot_low.astype(f32)
    grad_logit = (probs * (dots - jnp.sum(probs * dots, axis=1, keepdims=True))).astype(bf)
    grad_router = contract_rows(ffn_low, grad_logit)
    grad_ffn = g_sum + contract_cols(grad_logit, router_full)
    grad_hidden, grad_fgain = ffn_pull(grad_ffn)
    grad_hidden = grad_hidden + grad_out
    grad_mo = (grad_hidden * valid).astype(bf)
    grad_outw = contract_rows(mix_low, grad_mo)
    grad_mix = contract_cols(grad_mo, out_full)
    grad_proj, grad_cw, grad_cb, grad_db, grad_al, grad_skip, grad_mgain = mixer_pull(grad_mix)
    grad_proj = grad_proj.astype(bf)
    spare = -PROJ % 128
    grad_inw = contract_rows(normed_low, jnp.pad(grad_proj, ((0, 0), (0, spare)))).astype(bf)
    grad_x, grad_ngain = norm_pull(contract_cols(grad_proj, in_full))
    input_grad = (grad_x + grad_hidden).astype(bf)
    grad_router = contract_rows(ffn_low, jnp.pad(grad_logit, ((0, 0), (0, 128 - experts)))).astype(bf)

    pieces = (grad_ngain, grad_cw, grad_cb, grad_db, grad_al, grad_skip, grad_mgain, grad_fgain)
    flat = jnp.concatenate([p.reshape(-1) for p in pieces])
    flat = jnp.pad(flat, (0, -flat.shape[0] % 2048)).reshape(-1, 128)
    own_out, own_in, own_router, output, input_grad, flat = sum_to_owners(
        [grad_outw.astype(bf), grad_inw, grad_router], [512, 768, 128], lines, [f32] * 3, flat,
        [a.reshape(tokens.shape) for a in (output, input_grad)], 4,
    )
    flat = flat.reshape(-1)
    small = []
    start = 0
    for p in pieces:
        small.append(flat[start : start + p.size].reshape(p.shape))
        start += p.size
    along = lambda g, d: lax.psum_scatter(g.astype(bf), "seq", scatter_dimension=d, tiled=True)
    sup = grad_sup.astype(bf).reshape(groups, lines, -1, 2 * width).transpose(1, 0, 2, 3)
    sup = along(sup.reshape(MODEL_WIDTH, 2 * width), 0).reshape(groups, -1, 2 * width)
    sup = lax.all_to_all(sup, "dp", split_axis=0, concat_axis=0, tiled=True).astype(f32)
    sup = sup.reshape(groups, -1, 2, width).transpose(1, 2, 0, 3).reshape(-1, 2 * SFF)
    sdown = along(grad_sdown, 0).astype(f32)
    return (
        output, input_grad, small[0], own_in[:, :PROJ], small[1], small[2],
        small[3], small[4], small[5], small[6], own_out, small[7], own_router[:, :experts], sup, sdown,
        along(grad_eup, 1).astype(f32), along(grad_edown, 1).astype(f32),
    )


def solution(mesh):
    def program(*arrays):
        each = arrays[0].shape[0] == lax.axis_size("seq") == 4 and lax.axis_size("dp") == 8
        return (local_fast if each else local)(*arrays)

    return jax.shard_map(
        program,
        mesh=mesh,
        in_specs=(
            P("dp", "seq", None),
            P("dp"),
            P("dp", "seq", None),
            P("dp", "seq", None),
            P(),
            P(("dp", "seq"), None),
            P(),
            P(),
            P(),
            P(),
            P(),
            P(),
            P(("dp", "seq"), None),
            P(),
            P(("dp", "seq"), None),
            P(("dp", "seq"), None),
            P(("dp", "seq"), None),
            P("dp", None, None),
            P("dp", None, None),
        ),
        out_specs=(
            P("dp", "seq", None),
            P("dp", "seq", None),
            P(),
            P(("dp", "seq"), None),
            P(),
            P(),
            P(),
            P(),
            P(),
            P(),
            P(("dp", "seq"), None),
            P(),
            P(("dp", "seq"), None),
            P(("dp", "seq"), None),
            P(("dp", "seq"), None),
            P("dp", "seq", None),
            P("dp", "seq", None),
        ),
        check_vma=False,
    )
```

```python
from functools import partial

import jax
import jax.numpy as jnp
from jax import lax
from jax.experimental import pallas as pl
from jax.experimental.pallas import tpu as pltpu
from jax.sharding import PartitionSpec as P

MODEL_WIDTH = 1536
INNER = 3072
HEADS = 48
HDIM = 64
STATE = 128
KCONV = 4
EXPERT_HIDDEN = 512
SFF = 1024
MB = 4
CONV = 3328
PROJ = 6448


EPSILON = 1e-05
PRECISE = lax.Precision.HIGHEST
MESH = pl.DeviceIdType.MESH


def from_behind(x, axis, by):
    size = lax.axis_size(axis)
    pairs = [(i, i + by) for i in range(size) if 0 <= i + by < size]
    return lax.ppermute(x, axis, pairs)


def prefix(x, axis, join, neutral):
    place = lax.axis_index(axis)
    gathered = jax.tree.map(
        lambda a, kind: lax.all_gather(a.astype(kind), axis), x, (jnp.bfloat16, jnp.bfloat16)
    )
    state = jax.tree.map(lambda a, e: jnp.zeros_like(a) + jnp.asarray(e, a.dtype), x, neutral)

    def one(step, state):
        return join(
            state,
            jax.tree.map(
                lambda a, own: lax.dynamic_index_in_dim(a, step, 0, False).astype(own.dtype),
                gathered,
                x,
            ),
        )

    return lax.fori_loop(0, place, one, state)


def prefix_2(x, axis, join, neutral):
    count = lax.axis_size(axis)
    place = lax.axis_index(axis)
    ahead = count - 1 - place
    gathered = jax.tree.map(
        lambda a, kind: lax.all_gather(a.astype(kind), axis),
        x,
        jax.tree.map(lambda a: jnp.bfloat16 if a.dtype == jnp.float32 else a.dtype, x),
    )
    state = jax.tree.map(lambda a, e: jnp.zeros_like(a) + jnp.asarray(e, a.dtype), x, neutral)

    def one(step, state):
        source = count - 1 - step
        return join(
            state,
            jax.tree.map(
                lambda a, own: lax.dynamic_index_in_dim(a, source, 0, False).astype(own.dtype),
                gathered,
                x,
            ),
        )

    return lax.fori_loop(0, ahead, one, state)


def rms_norm(values, gain_vec):
    return (
        values * lax.rsqrt(jnp.mean(values * values, axis=-1, keepdims=True) + EPSILON) * gain_vec
    )


def swiglu(values, half_width):
    return jax.nn.silu(values[..., :half_width]) * values[..., half_width:]


def contract_rows(left_mat, right_mat):
    return lax.dot_general(
        left_mat, right_mat, (((0,), (0,)), ((), ())), preferred_element_type=jnp.float32
    )


def contract_cols(left_mat, right_mat):
    return lax.dot_general(
        left_mat, right_mat, (((1,), (1,)), ((), ())), preferred_element_type=jnp.float32
    )


def block_terms(head_in, b_rows, c_rows, step_sizes, a_log):
    log_rates = -step_sizes * jnp.exp(a_log)
    cumulative = jnp.cumsum(log_rates, axis=0)
    block_len = head_in.shape[0]
    lower_tri = jnp.arange(block_len)[:, None] >= jnp.arange(block_len)[None, :]
    spread = jnp.where(
        lower_tri[:, :, None], cumulative[:, None, :] - cumulative[None, :, :], -jnp.inf
    )
    scores = jnp.dot(c_rows, b_rows.T, precision=PRECISE)
    weights = jnp.exp(spread) * scores[:, :, None] * step_sizes[None, :, :]
    local_out = jnp.einsum("tih,ihp->thp", weights, head_in, precision=PRECISE)
    tail_weight = jnp.exp(cumulative[-1][None, :] - cumulative) * step_sizes
    local_state = jnp.einsum("ih,ihp,in->hpn", tail_weight, head_in, b_rows, precision=PRECISE)
    return (cumulative, local_out, local_state, jnp.exp(cumulative[-1]))


def carried_out(c_rows, cumulative, state_in):
    return (
        jnp.einsum("tn,hpn->thp", c_rows, state_in, precision=PRECISE)
        * jnp.exp(cumulative)[:, :, None]
    )


def mixer_front(valid_rows, projected, previous, conv_weight, conv_bias, dt_bias, a_log):
    row_count = projected.shape[0]
    conv_in = projected[:, INNER : INNER + CONV]
    padded = jnp.concatenate([previous, conv_in], axis=0)
    conv_sum = conv_bias + conv_weight[0] * padded[0:row_count]
    for tap_idx in range(1, KCONV):
        conv_sum = conv_sum + conv_weight[tap_idx] * padded[tap_idx : tap_idx + row_count]
    activated = jax.nn.silu(conv_sum) * valid_rows
    head_in = activated[:, :INNER].reshape(row_count, HEADS, HDIM)
    b_rows = activated[:, INNER : INNER + STATE]
    c_rows = activated[:, INNER + STATE :]
    step_sizes = jax.nn.softplus(projected[:, INNER + CONV :] + dt_bias)
    cumulative, local_out, local_state, decay_total = block_terms(
        head_in, b_rows, c_rows, step_sizes, a_log
    )
    return (projected[:, :INNER], head_in, c_rows, cumulative, local_out, local_state, decay_total)


def mixer_tail(gate_z, head_in, c_rows, cumulative, local_out, state_in, d_skip, mix_gain):
    mixed_out = local_out + carried_out(c_rows, cumulative, state_in) + d_skip[:, None] * head_in
    gated_out = mixed_out.reshape(head_in.shape[0], INNER) * jax.nn.silu(gate_z)
    return rms_norm(gated_out, mix_gain)


def link_states(earlier, latter):
    return (earlier[0] * latter[0], latter[1] + latter[0][:, None, None] * earlier[1])


def local(
    tokens,
    lengths,
    routes,
    cotangent,
    norm_gain,
    in_weight,
    conv_weight,
    conv_bias,
    dt_bias,
    a_log,
    d_skip,
    mix_gain,
    out_weight,
    ffn_gain,
    router_weight,
    shared_up,
    shared_down,
    expert_up,
    expert_down,
):
    row_count = tokens.shape[1]
    resident_experts = expert_up.shape[0]
    groups = lax.axis_size("dp")
    experts = resident_experts * groups
    top_count = routes.shape[2]
    capacity = row_count * top_count * 5 // (4 * experts)
    shards = (in_weight, out_weight, router_weight, shared_up, shared_down)
    kept_full = (
        lax.all_gather(shards[0], ("dp", "seq"), axis=0, tiled=True),
        lax.all_gather(shards[1], ("dp", "seq"), axis=0, tiled=True),
        lax.all_gather(shards[2], ("dp", "seq"), axis=0, tiled=True),
        lax.all_gather(shards[3], ("dp", "seq"), axis=0, tiled=True),
        lax.all_gather(shards[4], ("dp", "seq"), axis=0, tiled=True),
    )
    grad_inw = jnp.zeros((MODEL_WIDTH, PROJ), jnp.float32)
    grad_outw = jnp.zeros((INNER, MODEL_WIDTH), jnp.float32)
    grad_router = jnp.zeros((MODEL_WIDTH, experts), jnp.float32)
    grad_sup = jnp.zeros((MODEL_WIDTH, 2 * SFF), jnp.float32)
    grad_sdown = jnp.zeros((SFF, MODEL_WIDTH), jnp.float32)
    expert_upward_grad = jnp.zeros((resident_experts, MODEL_WIDTH, 2 * EXPERT_HIDDEN), jnp.float32)
    grad_edown = jnp.zeros((resident_experts, EXPERT_HIDDEN, MODEL_WIDTH), jnp.float32)
    grad_ngain = jnp.zeros_like(norm_gain)
    grad_cw = jnp.zeros_like(conv_weight)
    grad_cb = jnp.zeros_like(conv_bias)
    grad_db = jnp.zeros_like(dt_bias)
    grad_al = jnp.zeros_like(a_log)
    grad_skip = jnp.zeros_like(d_skip)
    grad_mgain = jnp.zeros_like(mix_gain)
    grad_fgain = jnp.zeros_like(ffn_gain)
    outputs = []
    input_grads = []
    for micro_idx in range(MB):
        in_full, out_full, router_full, up_full, down_full = kept_full
        x_rows = tokens[micro_idx].astype(jnp.float32)
        position = lax.axis_index("seq") * row_count + jnp.arange(row_count)
        valid_rows = (position < lengths[micro_idx]).astype(jnp.float32)[:, None]
        normed, norm_pull = jax.vjp(rms_norm, x_rows, norm_gain)
        normed_low = normed.astype(jnp.bfloat16)
        projected = jnp.dot(normed_low, in_full, preferred_element_type=jnp.float32).astype(
            jnp.bfloat16
        )
        previous = from_behind(projected[row_count - (KCONV - 1) :, INNER : INNER + CONV], "seq", 1)
        front_out, front_pull = jax.vjp(
            partial(mixer_front, valid_rows),
            projected.astype(jnp.float32),
            previous.astype(jnp.float32),
            conv_weight,
            conv_bias,
            dt_bias,
            a_log,
        )
        gate_z, head_in, c_rows, cumulative, local_out, local_state, decay_total = front_out
        identity = (jnp.ones_like(decay_total), jnp.zeros_like(local_state))
        _, state_in = prefix((decay_total, local_state), "seq", link_states, identity)
        normed_mix, tail_pull = jax.vjp(
            mixer_tail, gate_z, head_in, c_rows, cumulative, local_out, state_in, d_skip, mix_gain
        )
        mix_low = normed_mix.astype(jnp.bfloat16)
        mixer_out = jnp.dot(mix_low, out_full, preferred_element_type=jnp.float32)
        hidden = x_rows + mixer_out * valid_rows
        normed_ffn, ffn_pull = jax.vjp(rms_norm, hidden, ffn_gain)
        ffn_low = normed_ffn.astype(jnp.bfloat16)
        logits = jnp.dot(ffn_low, router_full, preferred_element_type=jnp.float32)
        route_row = routes[micro_idx]
        picked = jnp.take_along_axis(logits, route_row, axis=1)
        gate_probs = jax.nn.softmax(picked, axis=-1)
        shared_gu = jnp.dot(ffn_low, up_full, preferred_element_type=jnp.float32)
        shared_act, shared_pull = jax.vjp(partial(swiglu, half_width=SFF), shared_gu)
        shared_h = shared_act.astype(jnp.bfloat16)
        shared_y = jnp.dot(shared_h, down_full, preferred_element_type=jnp.float32)
        flat_route = route_row.reshape(-1)
        member = (flat_route[:, None] == jnp.arange(experts)[None, :]).astype(jnp.int32)
        slot_pos = jnp.sum((jnp.cumsum(member, axis=0) - member) * member, axis=1)
        target = flat_route * capacity + slot_pos
        source = (
            jnp.zeros((experts * capacity,), jnp.int32)
            .at[target]
            .set(jnp.arange(row_count * top_count, dtype=jnp.int32))
        )
        filled = jnp.zeros((experts * capacity, 1), jnp.bfloat16).at[target].set(jnp.bfloat16(1))
        outgoing = (jnp.take(ffn_low, source // top_count, axis=0) * filled).reshape(
            groups, resident_experts, capacity, MODEL_WIDTH
        )
        received_rows = lax.all_to_all(outgoing, "dp", split_axis=0, concat_axis=2, tiled=True)[0]
        expert_gu = jnp.einsum(
            "erd,edf->erf", received_rows, expert_up, preferred_element_type=jnp.float32
        )
        expert_act, expert_pull = jax.vjp(partial(swiglu, half_width=EXPERT_HIDDEN), expert_gu)
        expert_h = expert_act.astype(jnp.bfloat16)
        expert_y = jnp.einsum(
            "erf,efd->erd", expert_h, expert_down, preferred_element_type=jnp.float32
        ).astype(jnp.bfloat16)
        returned = lax.all_to_all(expert_y[None], "dp", split_axis=2, concat_axis=0, tiled=True)
        per_choice = (
            jnp.take(returned.reshape(experts * capacity, MODEL_WIDTH), target, axis=0)
            .reshape(row_count, top_count, MODEL_WIDTH)
            .astype(jnp.float32)
        )
        routed = jnp.einsum("lk,lkd->ld", gate_probs, per_choice, precision=PRECISE)
        outputs.append((hidden + valid_rows * (shared_y + routed)).astype(jnp.bfloat16))
        in_back, out_back, router_back, up_back, down_back = kept_full
        grad_out = cotangent[micro_idx].astype(jnp.float32)
        branch = valid_rows * grad_out
        shared_g = branch.astype(jnp.bfloat16)
        grad_sdown = grad_sdown + contract_rows(shared_h, shared_g)
        grad_sgu = shared_pull(contract_cols(shared_g, down_back))[0].astype(jnp.bfloat16)
        grad_sup = grad_sup + contract_rows(ffn_low, grad_sgu)
        grad_ffn = contract_cols(grad_sgu, up_back)
        grad_choice = (gate_probs[:, :, None] * branch[:, None, :]).astype(jnp.bfloat16)
        grad_gate = jnp.sum(branch[:, None, :] * per_choice, axis=-1)
        grad_pick = gate_probs * (
            grad_gate - jnp.sum(gate_probs * grad_gate, axis=-1, keepdims=True)
        )
        onehot = (route_row[:, :, None] == jnp.arange(experts)[None, None, :]).astype(jnp.float32)
        grad_logit = jnp.einsum("lk,lke->le", grad_pick, onehot, precision=PRECISE).astype(
            jnp.bfloat16
        )
        grad_router = grad_router + contract_rows(ffn_low, grad_logit)
        grad_ffn = grad_ffn + contract_cols(grad_logit, router_back)
        back_out = (
            jnp.take(grad_choice.reshape(row_count * top_count, MODEL_WIDTH), source, axis=0)
            * filled
        ).reshape(groups, resident_experts, capacity, MODEL_WIDTH)
        grad_arrived = lax.all_to_all(back_out, "dp", split_axis=0, concat_axis=2, tiled=True)[0]
        step_edown = jnp.einsum(
            "erf,erd->efd", expert_h, grad_arrived, preferred_element_type=jnp.float32
        )
        grad_eh = jnp.einsum(
            "erd,efd->erf", grad_arrived, expert_down, preferred_element_type=jnp.float32
        )
        expert_gate_up_grad = expert_pull(grad_eh)[0].astype(jnp.bfloat16)
        expert_upward_step = jnp.einsum(
            "tbw,tbj->twj", received_rows, expert_gate_up_grad, preferred_element_type=jnp.float32
        )
        grad_ein = jnp.einsum(
            "erf,edf->erd", expert_gate_up_grad, expert_up, preferred_element_type=jnp.float32
        ).astype(jnp.bfloat16)
        expert_upward_grad = expert_upward_grad + expert_upward_step
        grad_edown = grad_edown + step_edown
        came_back = lax.all_to_all(grad_ein[None], "dp", split_axis=2, concat_axis=0, tiled=True)
        grad_ffn = grad_ffn + jnp.sum(
            jnp.take(came_back.reshape(experts * capacity, MODEL_WIDTH), target, axis=0)
            .reshape(row_count, top_count, MODEL_WIDTH)
            .astype(jnp.float32),
            axis=1,
        )
        grad_hidden, step_fgain = ffn_pull(grad_ffn)
        grad_fgain = grad_fgain + step_fgain
        grad_hidden = grad_hidden + grad_out
        grad_mix_out = (grad_hidden * valid_rows).astype(jnp.bfloat16)
        grad_outw = grad_outw + contract_rows(mix_low, grad_mix_out)
        grad_mix = contract_cols(grad_mix_out, out_back)
        grad_z, grad_head, grad_c, grad_cum, grad_local, grad_state, step_skip, step_mgain = (
            tail_pull(grad_mix)
        )
        grad_skip = grad_skip + step_skip
        grad_mgain = grad_mgain + step_mgain
        _, grad_carry = prefix_2((decay_total, grad_state), "seq", link_states, identity)
        grad_decay = jnp.sum(grad_carry * state_in, axis=(1, 2))
        grad_proj, grad_prev, step_cw, step_cb, step_db, step_al = front_pull(
            (grad_z, grad_head, grad_c, grad_cum, grad_local, grad_carry, grad_decay)
        )
        grad_cw = grad_cw + step_cw
        grad_cb = grad_cb + step_cb
        grad_db = grad_db + step_db
        grad_al = grad_al + step_al
        from_next = from_behind(grad_prev.astype(jnp.bfloat16), "seq", -1).astype(grad_prev.dtype)
        grad_proj = (
            grad_proj.at[row_count - (KCONV - 1) :, INNER : INNER + CONV]
            .add(from_next)
            .astype(jnp.bfloat16)
        )
        grad_inw = grad_inw + contract_rows(normed_low, grad_proj)
        grad_normed = contract_cols(grad_proj, in_back)
        grad_x, step_ngain = norm_pull(grad_normed)
        grad_ngain = grad_ngain + step_ngain
        input_grads.append((grad_x + grad_hidden).astype(jnp.bfloat16))
    weight_grads = (
        lax.psum_scatter(grad_inw, ("dp", "seq"), scatter_dimension=0, tiled=True),
        lax.psum_scatter(grad_outw, ("dp", "seq"), scatter_dimension=0, tiled=True),
        lax.psum_scatter(grad_router, ("dp", "seq"), scatter_dimension=0, tiled=True),
        lax.psum_scatter(grad_sup, ("dp", "seq"), scatter_dimension=0, tiled=True),
        lax.psum_scatter(grad_sdown, ("dp", "seq"), scatter_dimension=0, tiled=True),
    )
    small_sums = lax.psum(
        (grad_ngain, grad_cw, grad_cb, grad_db, grad_al, grad_skip, grad_mgain, grad_fgain),
        ("dp", "seq"),
    )
    expert_sums = (
        lax.psum_scatter(
            expert_upward_grad.astype(jnp.bfloat16), "seq", scatter_dimension=1, tiled=True
        ).astype(jnp.float32),
        lax.psum_scatter(
            grad_edown.astype(jnp.bfloat16), "seq", scatter_dimension=1, tiled=True
        ).astype(jnp.float32),
    )
    return (
        jnp.stack(outputs),
        jnp.stack(input_grads),
        small_sums[0],
        weight_grads[0],
        small_sums[1],
        small_sums[2],
        small_sums[3],
        small_sums[4],
        small_sums[5],
        small_sums[6],
        weight_grads[1],
        small_sums[7],
        weight_grads[2],
        weight_grads[3],
        weight_grads[4],
        expert_sums[0],
        expert_sums[1],
    )


def at_neighbours():
    d = lax.axis_index("dp")
    core, x, y = d % 2, (d // 2) % 2, d // 4
    return d, core, x, y, d + 1 - 2 * core, d + 2 - 4 * x, d + 4 - 8 * y


def meet(devices):
    barrier = pltpu.get_barrier_semaphore()
    for there in devices:
        pl.semaphore_signal(barrier, inc=1, device_id=there, device_id_type=MESH)
    pl.semaphore_wait(barrier, len(devices))


def send(source, target, send_sem, recv_sem, there):
    copy = pltpu.make_async_remote_copy(
        src_ref=source, dst_ref=target, send_sem=send_sem, recv_sem=recv_sem,
        device_id=there, device_id_type=MESH,
    )
    copy.start()
    return copy


def add_into(target, source, high):
    step = 16
    for s in (64, 48, 32):
        if high % s == 0:
            step = s
            break

    @pl.loop(0, high // step)
    def _(i):
        rows = pl.ds(pl.multiple_of(i * step, step), step)
        target[rows, :] = target[rows, :] + source[rows, :]


def swap_start(swaps, landed, line, lines, local_sem, send_sem, recv_sem):
    copies = []
    for n, (a, b) in enumerate(zip(swaps, landed)):
        keep = pltpu.make_async_copy(a.at[line], b.at[line], local_sem.at[n])
        keep.start()
        away = [
            send(a.at[o], b.at[line], send_sem.at[n, k], recv_sem.at[n, k], {"seq": o})
            for k, o in enumerate(lax.rem(line + k, lines) for k in range(1, lines))
        ]
        copies.append((keep, away))
    return copies


def swap_end(copies):
    for keep, away in copies:
        for copy in away:
            copy.wait_recv()
    for keep, away in copies:
        for copy in away:
            copy.wait_send()
        keep.wait()


def swap_sems(count, lines):
    dma = pltpu.SemaphoreType.DMA
    return [dma((count,)), dma((count, lines - 1)), dma((count, lines - 1))]


def sum_body(items, arrays, lines, tiny, moved, relative, *refs):
    count = len(items)
    grads, refs = refs[:arrays], refs[arrays:]
    swaps, refs = refs[:moved], refs[moved:]
    if tiny:
        small_in, refs = refs[0], refs[1:]
    outs, refs = refs[:arrays], refs[arrays:]
    landed, refs = refs[:moved], refs[moved:]
    if tiny:
        small_out, refs = refs[0], refs[1:]
    own, refs = refs[:count], refs[count:]
    got, refs = refs[:count], refs[count:]
    from_x, refs = refs[:count], refs[count:]
    from_y, refs = refs[:count], refs[count:]
    last_x, refs = refs[:count], refs[count:]
    last_y, refs = refs[:count], refs[count:]
    if lines > 1:
        from_z, refs = refs[:count], refs[count:]
    (load_sem, send_sem, recv_sem), refs = refs[:3], refs[3:]
    if moved:
        swap_sem, refs = refs[:3], refs[3:]
    if tiny:
        half, t_core, t_x, t_y, t_z, t_back, t_send, t_recv = refs
    d, core, x, y, at_core, at_x, at_y = at_neighbours()
    if relative:
        core = x = y = 0
    line = lax.axis_index("seq")
    others = [lax.rem(line + k, lines) for k in range(1, lines)]
    meet([{"dp": at_core}, {"dp": at_x}, {"dp": at_y}] + [{"seq": o} for o in others])
    sent = [[] for _ in items]
    stage = [None] * count
    cross = [None] * count
    close = [None] * count
    along = [None] * count
    loads = [None] * count

    def begin(t):
        a, c0, wide, high = items[t]
        cols = pl.ds(c0, wide)
        loads[t] = pltpu.make_async_copy(grads[a].at[:, :, core, :, cols], own[t], load_sem.at[t])
        loads[t].start()
        stage[t] = send(
            grads[a].at[:, :, 1 - core, :, cols], got[t], send_sem.at[t, 0], recv_sem.at[t, 0], {"dp": at_core}
        )

    def fold(t):
        a, c0, wide, high = items[t]
        loads[t].wait()
        stage[t].wait_recv()
        for i in range(2):
            for j in range(2):
                add_into(got[t].at[i, j], own[t].at[i, j], high)
        top, low = pl.ds(0, high // 2), pl.ds(high // 2, high // 2)
        cross[t] = (
            send(got[t].at[:, 1 - x, top, :], from_x[t], send_sem.at[t, 1], recv_sem.at[t, 1], {"dp": at_x}),
            send(got[t].at[1 - y, :, low, :], from_y[t], send_sem.at[t, 2], recv_sem.at[t, 2], {"dp": at_y}),
        )

    def turn(t):
        a, c0, wide, high = items[t]
        top, low = pl.ds(0, high // 2), pl.ds(high // 2, high // 2)
        cross[t][0].wait_recv()
        for i in range(2):
            add_into(got[t].at[i, x, top, :], from_x[t].at[i], high // 2)
        close_y = send(got[t].at[1 - y, x, top, :], last_y[t], send_sem.at[t, 3], recv_sem.at[t, 3], {"dp": at_y})
        cross[t][1].wait_recv()
        for j in range(2):
            add_into(got[t].at[y, j, low, :], from_y[t].at[j], high // 2)
        close_x = send(got[t].at[y, 1 - x, low, :], last_x[t], send_sem.at[t, 4], recv_sem.at[t, 4], {"dp": at_x})
        close[t] = (close_y, close_x)

    def settle(t):
        a, c0, wide, high = items[t]
        top, low = pl.ds(0, high // 2), pl.ds(high // 2, high // 2)
        cols = pl.ds(c0, wide)
        close[t][0].wait_recv()
        add_into(got[t].at[y, x, top, :], last_y[t], high // 2)
        close[t][1].wait_recv()
        add_into(got[t].at[y, x, low, :], last_x[t], high // 2)
        if lines == 1:
            outs[a][:, cols] = got[t][y, x].astype(outs[a].dtype)
            return
        each = high // lines
        along[t] = [
            send(
                got[t].at[y, x, pl.ds(pl.multiple_of(o * each, 16), each), :], from_z[t].at[k],
                send_sem.at[t, 5 + k], recv_sem.at[t, 5 + k], {"seq": o},
            )
            for k, o in enumerate(others)
        ]

    def finish(t):
        a, c0, wide, high = items[t]
        each = high // lines
        total = got[t][y, x, pl.ds(pl.multiple_of(line * each, 16), each), :].astype(jnp.float32)
        for k in range(lines - 1):
            along[t][k].wait_recv()
            total = total + from_z[t][k].astype(jnp.float32)
        outs[a][:, pl.ds(c0, wide)] = total

    little = []

    def tiny_step(n):
        rows = half.shape[1]
        if n == 0:
            there = pl.ds(pl.multiple_of((1 - core) * rows, 8), rows)
            little.append(send(small_in.at[there, :], t_core, t_send.at[0], t_recv.at[0], {"dp": at_core}))
        elif n == 1:
            little[0].wait_recv()
            here = pl.ds(pl.multiple_of(core * rows, 8), rows)
            half[0] = small_in[here, :] + t_core[...]
            little.append(send(half.at[0], t_x, t_send.at[1], t_recv.at[1], {"dp": at_x}))
        elif n == 2:
            little[1].wait_recv()
            half[1] = half[0] + t_x[...]
            little.append(send(half.at[1], t_y, t_send.at[2], t_recv.at[2], {"dp": at_y}))
        elif n == 3:
            little[2].wait_recv()
            half[2] = half[1] + t_y[...]
            t_z[line] = half[2]
            for k, o in enumerate(others):
                little.append(send(half.at[2], t_z.at[line], t_send.at[3 + k], t_recv.at[3 + k], {"seq": o}))
        elif n == 4:
            for k in range(lines - 1):
                little[3 + k].wait_recv()
            total = t_z[0]
            for k in range(1, lines):
                total = total + t_z[k]
            half[3] = total
            small_out[pl.ds(pl.multiple_of(core * rows, 8), rows), :] = total
            little.append(send(half.at[3], t_back, t_send.at[7], t_recv.at[7], {"dp": at_core}))
        elif n == 5:
            little[-1].wait_recv()
            small_out[pl.ds(pl.multiple_of((1 - core) * rows, 8), rows), :] = t_back[...]
            for copy in little:
                copy.wait_send()

    begin(0)
    if tiny:
        tiny_step(0)
    moves = swap_start(swaps, landed, line, lines, *swap_sem) if moved else ()
    for t in range(max(count + 3, 5 if tiny else 0)):
        if t + 1 < count:
            begin(t + 1)
        if t < count:
            fold(t)
        if 0 <= t - 1 < count:
            turn(t - 1)
        if 0 <= t - 2 < count:
            settle(t - 2)
        if lines > 1 and 0 <= t - 3 < count:
            finish(t - 3)
        if tiny and t < 5:
            tiny_step(t + 1)
    swap_end(moves)
    for t in range(count):
        stage[t].wait_send()
        for copy in cross[t] + close[t] + tuple(along[t] or ()):
            copy.wait_send()


def sum_to_owners(grads, widths, lines, kinds, small, swaps, relative, identity):
    items, views = [], []
    for a, (g, wide) in enumerate(zip(grads, widths)):
        high, cols = g.shape[0] // 8, g.shape[1]
        views.append(g.reshape(2, 2, 2, high, cols))
        start = 0
        while start < cols:
            w = min(wide, cols - start)
            items.append((a, start, w, high))
            start += w
    tiny = small is not None
    bf = jnp.bfloat16
    scratch = [pltpu.VMEM((2, 2, h, w), bf) for _, _, w, h in items]
    scratch += [pltpu.VMEM((2, 2, h, w), bf) for _, _, w, h in items]
    scratch += [pltpu.VMEM((2, h // 2, w), bf) for _, _, w, h in items] * 2
    scratch += [pltpu.VMEM((h // 2, w), bf) for _, _, w, h in items] * 2
    if lines > 1:
        scratch += [pltpu.VMEM((lines - 1, h // lines, w), bf) for _, _, w, h in items]
    ways = 4 + lines
    scratch += [
        pltpu.SemaphoreType.DMA((len(items),)),
        pltpu.SemaphoreType.DMA((len(items), ways)),
        pltpu.SemaphoreType.DMA((len(items), ways)),
    ]
    out_shape = [
        jax.ShapeDtypeStruct((g.shape[0] // 8 // lines, g.shape[1]), kind) for g, kind in zip(grads, kinds)
    ]
    ins = list(views)
    in_specs = [pl.BlockSpec(memory_space=pl.ANY)] * len(views)
    out_specs = [pl.BlockSpec(memory_space=pltpu.VMEM)] * len(views)
    if swaps:
        scratch += swap_sems(len(swaps), lines)
        ins += swaps
        in_specs += [pl.BlockSpec(memory_space=pl.ANY)] * len(swaps)
        out_specs += [pl.BlockSpec(memory_space=pl.ANY)] * len(swaps)
        out_shape += [jax.ShapeDtypeStruct(a.shape, a.dtype) for a in swaps]
    if tiny:
        rows = small.shape[0] // 2
        part = lambda *lead: pltpu.VMEM(lead + (rows, 128), jnp.float32)
        scratch += [part(4), part(), part(), part(), part(lines), part()]
        scratch += [pltpu.SemaphoreType.DMA((8,)), pltpu.SemaphoreType.DMA((8,))]
        out_shape.append(jax.ShapeDtypeStruct(small.shape, jnp.float32))
        ins.append(small)
        in_specs.append(pl.BlockSpec(memory_space=pltpu.VMEM))
        out_specs.append(pl.BlockSpec(memory_space=pltpu.VMEM))
    return pl.pallas_call(
        partial(sum_body, items, len(views), lines, tiny, len(swaps), relative),
        out_shape=out_shape,
        in_specs=in_specs,
        out_specs=out_specs,
        scratch_shapes=scratch,
        name="sum_to_owners_%d" % identity,
        compiler_params=pltpu.CompilerParams(
            collective_id=identity, has_side_effects=True, vmem_limit_bytes=60 << 20
        ),
    )(*ins)


def gather_body(pieces, arrays, lines, ahead, moved, relative, *refs):
    mine, refs = refs[:arrays], refs[arrays:]
    swaps, refs = refs[:moved], refs[moved:]
    full, refs = refs[:arrays], refs[arrays:]
    landed, refs = refs[:moved], refs[moved:]
    keep_sem, send_sem, recv_sem, z_send, z_recv = refs[:5]
    swap_sem = refs[5:]
    d, core, x, y, at_core, at_x, at_y = at_neighbours()
    at_far = at_x + at_y - d
    line = lax.rem(lax.axis_index("seq"), lines)
    hops = [line]
    if lines > 1:
        upper = line // 2
        hops += [line + 1 - 2 * (line % 2), 2 - upper, 3 - 3 * upper]
    meet([{"dp": at_core}, {"dp": at_x}, {"dp": at_y}] + [{"seq": o} for o in hops[1:]])
    keep = []
    for a in range(arrays):
        keep.append(pltpu.make_async_copy(mine[a], full[a].at[0 if relative else d, line], keep_sem.at[a]))
        keep[a].start()
    order = [(j, p) for j in range(lines) for p in range(len(pieces))]
    total = len(order)
    out = [[None] * 7 for _ in order]
    z_copies = []
    blocks = dict(own=d, core=at_core, x=at_x, y=at_y, far=at_far)
    if relative:
        blocks = dict(own=0, core=1, x=2, y=4, far=6)
        lands = dict(x=2, y=4, core=1, x_y=6, x_core=3, y_x=6, y_core=5, far_core=7)
    else:
        lands = dict(x=d, y=d, core=d, x_y=at_x, x_core=at_x, y_x=at_y, y_core=at_y, far_core=at_far)

    def place(j, p, block):
        a, r0, high = pieces[p]
        return full[a].at[block, hops[j], pl.ds(r0, high), :]

    def z_copy(j, p, slot):
        a, r0, high = pieces[p]
        return pltpu.make_async_remote_copy(
            src_ref=mine[a].at[pl.ds(r0, high), :],
            dst_ref=full[a].at[blocks["own"], line, pl.ds(r0, high), :],
            send_sem=z_send.at[p, j - 1], recv_sem=z_recv.at[p, slot],
            device_id={"seq": hops[j]}, device_id_type=MESH,
        )

    def z_round(j):
        for p in range(len(pieces)):
            z_copies.append(z_copy(j, p, line))
            z_copies[-1].start()

    def pass_on(i, n, block, lands_at, there):
        j, p = order[i]
        a, r0, high = pieces[p]
        if block is None:
            source = mine[a].at[pl.ds(r0, high), :]
        else:
            source = place(j, p, block)
        out[i][n] = send(
            source, place(j, p, lands[lands_at]), send_sem.at[i, n], recv_sem.at[i, n], {"dp": there}
        )

    def first(i):
        j, p = order[i]
        block = None
        if j > 0:
            z_copy(j, p, hops[j]).wait_recv()
            block = blocks["own"]
        pass_on(i, 0, block, "x", at_x)
        pass_on(i, 1, block, "y", at_y)
        pass_on(i, 2, block, "core", at_core)

    def second(i):
        out[i][0].wait_recv()
        if i % 2 == 0:
            pass_on(i, 5, blocks["x"], "x_y", at_y)
        pass_on(i, 3, blocks["x"], "x_core", at_core)
        out[i][1].wait_recv()
        if i % 2 == 1:
            pass_on(i, 5, blocks["y"], "y_x", at_x)
        pass_on(i, 4, blocks["y"], "y_core", at_core)

    def third(i):
        out[i][5].wait_recv()
        pass_on(i, 6, blocks["far"], "far_core", at_core)

    moves = swap_start(swaps, landed, line, lines, *swap_sem) if moved else ()
    if lines > 1:
        z_round(1)
    for i in range(min(ahead, total)):
        first(i)
    if lines > 1:
        z_round(2)
    for i in range(total):
        if i + ahead < total:
            first(i + ahead)
            if lines > 1 and order[i + ahead] == (2, 0):
                z_round(3)
        second(i)
        if i:
            third(i - 1)
    third(total - 1)
    for i in range(total):
        for n in (2, 3, 4, 6):
            out[i][n].wait_recv()
        for copy in out[i]:
            copy.wait_send()
    swap_end(moves)
    for copy in z_copies:
        copy.wait_send()
    for copy in keep:
        copy.wait()


def gather_rows(arrays, chunks, lines, ahead, swaps, relative, identity):
    pieces = []
    for a, (w, chunk) in enumerate(zip(arrays, chunks)):
        for r0 in range(0, w.shape[0], chunk):
            pieces.append((a, r0, chunk))
    total = lines * len(pieces)
    anywhere = pl.BlockSpec(memory_space=pl.ANY)
    return pl.pallas_call(
        partial(gather_body, pieces, len(arrays), lines, ahead, len(swaps), relative),
        out_shape=[jax.ShapeDtypeStruct((8, lines) + w.shape, w.dtype) for w in arrays]
        + [jax.ShapeDtypeStruct(a.shape, a.dtype) for a in swaps],
        in_specs=[anywhere] * (len(arrays) + len(swaps)),
        out_specs=[anywhere] * (len(arrays) + len(swaps)),
        scratch_shapes=[
            pltpu.SemaphoreType.DMA((len(arrays),)),
            pltpu.SemaphoreType.DMA((total, 7)),
            pltpu.SemaphoreType.DMA((total, 7)),
            pltpu.SemaphoreType.DMA((len(pieces), max(1, lines - 1))),
            pltpu.SemaphoreType.DMA((len(pieces), lines)),
        ]
        + (swap_sems(len(swaps), lines) if swaps else []),
        name="gather_rows_%d" % identity,
        compiler_params=pltpu.CompilerParams(collective_id=identity, has_side_effects=True),
    )(*arrays, *swaps)


def sigmoid(v):
    return 1.0 / (1.0 + jnp.exp(-v))


def shifted(v, by):
    if by == 0:
        return v
    rows = v.shape[0]
    at = lax.broadcasted_iota(jnp.int32, v.shape, 0)
    keep = at >= by if by > 0 else at < rows + by
    return jnp.where(keep, pltpu.roll(v, by % rows, 0), 0.0)


def conv_sums(v, taps, bias):
    total = bias
    for k in range(KCONV):
        total = total + taps[k : k + 1, :] * shifted(v, KCONV - 1 - k)
    return total


def conv_back(v, taps, bias, valid, grad):
    conv_sum = conv_sums(v, taps, bias)
    s = sigmoid(conv_sum)
    grad = grad * valid * (s * (1.0 + conv_sum * (1.0 - s)))
    total = taps[KCONV - 1 : KCONV, :] * grad
    for k in range(KCONV - 1):
        total = total + taps[k : k + 1, :] * shifted(grad, k - (KCONV - 1))
    sums = [jnp.sum(grad, axis=0, keepdims=True)]
    for k in range(KCONV):
        sums.append(jnp.sum(grad * shifted(v, KCONV - 1 - k), axis=0, keepdims=True))
    return total, sums


def lower_left(rows):
    return lax.broadcasted_iota(jnp.int32, (rows, rows), 0) >= lax.broadcasted_iota(
        jnp.int32, (rows, rows), 1
    )


def product(a, b, over_a=1, over_b=0):
    return lax.dot_general(
        a, b, (((over_a,), (over_b,)), ((), ())), preferred_element_type=jnp.float32
    )


def bc_scores(bc_ref, bc_taps, bc_bias, valid, scores, bc_keep):
    conv_sum = conv_sums(bc_ref[...].astype(jnp.float32), bc_taps[...], bc_bias[...])
    bc = conv_sum * sigmoid(conv_sum) * valid[:, :1]
    bc_keep[...] = bc.astype(jnp.bfloat16)
    rows = scores.shape[0]
    g = product(bc_keep[:, STATE:], bc_keep[:, :STATE], 1, 1)
    scores[...] = jnp.where(lower_left(rows), g, 0.0)


def front_body(
    z_ref, x_ref, bc_ref, taps, bias, bc_taps, bc_bias, valid, step, cum, cum_rows, skip,
    mixed_ref, gated_ref, squares, scores, bc_keep,
):
    f32, bf = jnp.float32, jnp.bfloat16

    @pl.when(pl.program_id(0) == 0)
    def _():
        bc_scores(bc_ref, bc_taps, bc_bias, valid, scores, bc_keep)
        squares[...] = jnp.zeros_like(squares)

    rows = x_ref.shape[0]
    half = rows // 2
    conv_sum = conv_sums(x_ref[...].astype(f32), taps[...], bias[...])
    x = conv_sum * sigmoid(conv_sum) * valid[...]
    xs = (x * step[...]).astype(bf)
    lane = lax.broadcasted_iota(jnp.int32, (half, 128), 1)
    for r in range(2):
        at, wide = pl.ds(r * half, half), (r + 1) * half
        parts = []
        for h in range(2):
            gap = cum[at, h * HDIM : h * HDIM + 1] - cum_rows[0, h : h + 1, :wide]
            m = (jnp.exp(jnp.minimum(gap, 0.0)) * scores[at, :wide]).astype(bf)
            parts.append(product(m, xs[:wide, :]))
        mixed = jnp.where(lane < HDIM, parts[0], parts[1]) + skip[...] * x[r * half : (r + 1) * half, :]
        z = z_ref[at, :].astype(f32)
        gated = mixed * (z * sigmoid(z))
        mixed_ref[at, :] = mixed
        gated_ref[at, :] = gated
        squares[at, :] += gated * gated


def back_body(
    z_ref, x_ref, bc_ref, taps, bias, bc_taps, bc_bias, valid, step, cum, cum_rows, skip,
    mixed_ref, grad_ref, gain, scale, mean_dot,
    grad_z, grad_x, stats, grad_bc, bc_stats, row_sums, col_sums, step_sums,
    scores, bc_keep, grad_scores, grad_xs,
):
    f32, bf = jnp.float32, jnp.bfloat16
    pair = pl.program_id(0)

    @pl.when(pair == 0)
    def _():
        bc_scores(bc_ref, bc_taps, bc_bias, valid, scores, bc_keep)
        grad_scores[...] = jnp.zeros_like(grad_scores)
        row_sums[...] = jnp.zeros_like(row_sums)
        col_sums[...] = jnp.zeros_like(col_sums)
        step_sums[...] = jnp.zeros_like(step_sums)

    rows = x_ref.shape[0]
    half = rows // 2
    v = x_ref[...].astype(f32)
    conv_sum = conv_sums(v, taps[...], bias[...])
    x = conv_sum * sigmoid(conv_sum) * valid[...]
    xs = (x * step[...]).astype(bf)
    z = z_ref[...].astype(f32)
    s = sigmoid(z)
    silu = z * s
    mixed = mixed_ref[...]
    normal = mixed * silu * scale[...]
    grad = grad_ref[...]
    grad_gated = scale[...] * (grad * gain[...] - normal * mean_dot[...])
    grad_mixed = grad_gated * silu
    grad_z[...] = (grad_gated * mixed * (s * (1.0 + z * (1.0 - s)))).astype(bf)
    lane = lax.broadcasted_iota(jnp.int32, (rows, 128), 1)
    dy = [
        jnp.where(lane < HDIM, grad_mixed, 0.0).astype(bf),
        jnp.where(lane < HDIM, 0.0, grad_mixed).astype(bf),
    ]
    for r in range(2):
        at, wide = pl.ds(r * half, half), (r + 1) * half
        total = None
        for h in range(2):
            head = 2 * pair + h
            g = scores[at, :wide]
            gap = cum[at, h * HDIM : h * HDIM + 1] - cum_rows[0, h : h + 1, :wide]
            e = jnp.exp(jnp.minimum(gap, 0.0))
            m = (e * g).astype(bf)
            dy_rows = dy[h][r * half : (r + 1) * half, :]
            slope = product(dy_rows, xs[:wide, :], 1, 1) * e
            grad_scores[at, :wide] += slope
            both = (slope * g).astype(bf)
            back = product(m, dy_rows, 0, 0)
            total = back if total is None else total + back
            to_lane = (lax.broadcasted_iota(jnp.int32, (wide, 128), 1) == head).astype(bf)
            row_sums[at, :] += product(both, to_lane)
            to_row = (lax.broadcasted_iota(jnp.int32, (64, half), 0) == head).astype(bf)
            col_sums[:, :wide] += product(to_row, both)
        if r == 0:
            grad_xs[:half, :] = total
        else:
            grad_xs[:half, :] += total[:half, :]
            grad_xs[half:, :] = total[half:, :]
    gxs = grad_xs[...]
    fold = (
        lax.broadcasted_iota(jnp.int32, (128, 128), 1)
        == 2 * pair + lax.broadcasted_iota(jnp.int32, (128, 128), 0) // HDIM
    ).astype(bf)
    step_sums[...] += product((gxs * x).astype(bf), fold)
    gx, sums = conv_back(v, taps[...], bias[...], valid[...], gxs * step[...] + skip[...] * grad_mixed)
    grad_x[...] = gx.astype(bf)
    stats[0:1, :] = jnp.sum(grad * normal, axis=0, keepdims=True)
    stats[1:2, :] = jnp.sum(grad_mixed * x, axis=0, keepdims=True)
    for k, total in enumerate(sums):
        stats[2 + k : 3 + k, :] = total
    stats[7:8, :] = jnp.zeros((1, 128), f32)

    @pl.when(pair == pl.num_programs(0) - 1)
    def _():
        gs = jnp.where(lower_left(rows), grad_scores[...], 0.0).astype(bf)
        grad_c = product(gs, bc_keep[:, :STATE])
        grad_b = product(gs, bc_keep[:, STATE:], 0, 0)
        ends = ((grad_b, 0), (grad_c, STATE))
        for g, at in ends:
            cols = pl.ds(at, STATE)
            gi, sums = conv_back(
                bc_ref[:, cols].astype(f32), bc_taps[:, cols], bc_bias[:, cols], valid[...], g
            )
            grad_bc[:, cols] = gi.astype(bf)
            for k, total in enumerate(sums):
                bc_stats[k : k + 1, cols] = total
            bc_stats[5:8, cols] = jnp.zeros((3, STATE), f32)


def mixer_specs(rows):
    tile = lambda at: pl.BlockSpec((rows, 128), at)
    whole = lambda shape: pl.BlockSpec(shape, lambda p: (0,) * len(shape))
    pairs = INNER // 128
    return tile, whole, [
        tile(lambda p: (0, p)),
        tile(lambda p: (0, pairs + p)),
        pl.BlockSpec((rows, 2 * STATE), lambda p: (0, 2 * INNER // (2 * STATE))),
        pl.BlockSpec((KCONV, 128), lambda p: (0, p)),
        pl.BlockSpec((1, 128), lambda p: (0, p)),
        pl.BlockSpec((KCONV, 2 * STATE), lambda p: (0, INNER // (2 * STATE))),
        pl.BlockSpec((1, 2 * STATE), lambda p: (0, INNER // (2 * STATE))),
        whole((rows, 128)),
        tile(lambda p: (0, p)),
        tile(lambda p: (0, p)),
        pl.BlockSpec((1, 2, rows), lambda p: (p, 0, 0)),
        pl.BlockSpec((1, 128), lambda p: (0, p)),
    ]


def mixer_front_call(inputs, rows):
    f32 = jnp.float32
    tile, whole, specs = mixer_specs(rows)
    return pl.pallas_call(
        front_body,
        grid=(INNER // 128,),
        in_specs=specs,
        out_specs=[tile(lambda p: (0, p)), tile(lambda p: (0, p)), whole((rows, 128))],
        out_shape=[
            jax.ShapeDtypeStruct((rows, INNER), f32),
            jax.ShapeDtypeStruct((rows, INNER), f32),
            jax.ShapeDtypeStruct((rows, 128), f32),
        ],
        scratch_shapes=[pltpu.VMEM((rows, rows), f32), pltpu.VMEM((rows, 2 * STATE), jnp.bfloat16)],
        name="mixer_front",
        cost_estimate=pl.CostEstimate(flops=10**10, bytes_accessed=2 * 10**7, transcendentals=5 * 10**6),
    )(*inputs)


def mixer_back_call(inputs, extra, rows):
    f32, bf = jnp.float32, jnp.bfloat16
    tile, whole, specs = mixer_specs(rows)
    by_pair = tile(lambda p: (0, p))
    return pl.pallas_call(
        back_body,
        grid=(INNER // 128,),
        in_specs=specs
        + [by_pair, by_pair, pl.BlockSpec((1, 128), lambda p: (0, p)), whole((rows, 128)), whole((rows, 128))],
        out_specs=[
            by_pair, by_pair, pl.BlockSpec((8, 128), lambda p: (0, p)), whole((rows, 2 * STATE)),
            whole((8, 2 * STATE)), whole((rows, 128)), whole((64, rows)), whole((rows, 128)),
        ],
        out_shape=[
            jax.ShapeDtypeStruct((rows, INNER), bf),
            jax.ShapeDtypeStruct((rows, INNER), bf),
            jax.ShapeDtypeStruct((8, INNER), f32),
            jax.ShapeDtypeStruct((rows, 2 * STATE), bf),
            jax.ShapeDtypeStruct((8, 2 * STATE), f32),
            jax.ShapeDtypeStruct((rows, 128), f32),
            jax.ShapeDtypeStruct((64, rows), f32),
            jax.ShapeDtypeStruct((rows, 128), f32),
        ],
        scratch_shapes=[
            pltpu.VMEM((rows, rows), f32), pltpu.VMEM((rows, 2 * STATE), bf),
            pltpu.VMEM((rows, rows), f32), pltpu.VMEM((rows, 128), f32),
        ],
        name="mixer_back",
        cost_estimate=pl.CostEstimate(flops=3 * 10**10, bytes_accessed=3 * 10**7, transcendentals=5 * 10**6),
    )(*inputs, *extra)


def local_fast(
    tokens, lengths, routes, cotangent, norm_gain, in_weight, conv_weight, conv_bias, dt_bias,
    a_log, d_skip, mix_gain, out_weight, ffn_gain, router_weight, shared_up, shared_down,
    expert_up, expert_down,
):
    bf, f32 = jnp.bfloat16, jnp.float32
    block = tokens.shape[1]
    parts = tokens.shape[0]
    rows = block * parts
    groups = lax.axis_size("dp")
    lines = lax.axis_size("seq")

    def to(a, bit):
        return lax.ppermute(a, "dp", [(i, i ^ bit) for i in range(groups)])

    def to_home(a):
        a = a[0::2] + to(a[1::2], 1)
        cut = a.shape[2] // 2
        left, right = a[:, :, :cut], a[:, :, cut:]
        left = left[0::2] + to(left[1::2], 2)
        right = right[:2] + to(right[2:], 4)
        left = left[0] + to(left[1], 4)
        right = right[0] + to(right[1], 2)
        return jnp.concatenate([left, right], axis=1)

    def around(a):
        by_x, by_y = to(a, 2), to(a, 4)
        near = [a, by_x, by_y, to(by_x, 4)]
        far = [to(b, 1) for b in near]
        return jnp.stack([b for pair in zip(near, far) for b in pair])

    held = expert_up.shape[0]
    experts = held * groups
    top = routes.shape[2]
    slots = block * top * 5 // (4 * experts) * parts
    slots = -(-slots // 128) * 128
    place = lax.axis_index("seq")
    group = lax.axis_index("dp")

    in_blocks, x_low, route = gather_rows(
        [in_weight], [in_weight.shape[0] // 3], lines, 2, [tokens, routes], False, 1
    )
    in_full = in_blocks.reshape(MODEL_WIDTH, -1)
    in_full, late_out, late_cot = lax.optimization_barrier((in_full, out_weight, cotangent))
    cot_low = lax.all_to_all(late_cot, "seq", split_axis=0, concat_axis=0, tiled=True)
    out_full = lax.all_gather(late_out, ("dp", "seq"), axis=0, tiled=True)
    router_full = lax.all_gather(router_weight, ("dp", "seq"), axis=0, tiled=True)
    width = SFF // groups
    up_cols = shared_up.reshape(-1, 2, groups, width).transpose(2, 0, 1, 3).reshape(groups, -1, 2 * width)
    up_cols = lax.all_to_all(up_cols, "dp", split_axis=0, concat_axis=0, tiled=True)
    up_part = lax.all_gather(up_cols, "seq", axis=1).reshape(MODEL_WIDTH, 2 * width)
    down_part = lax.all_gather(shared_down, "seq", axis=0, tiled=True)

    length = lax.dynamic_index_in_dim(lengths, place, 0, False)
    x_low = x_low.reshape(rows, MODEL_WIDTH)
    cot_low = cot_low.reshape(rows, MODEL_WIDTH)
    route = route.reshape(rows, top)
    used = jnp.arange(rows) < length
    valid = used.astype(f32)[:, None]
    all_cot = around(jnp.where(used[:, None], cot_low, 0))
    all_route = around(jnp.where(used[:, None], route, -1))
    x_rows = x_low.astype(f32)
    normed, norm_pull = jax.vjp(rms_norm, x_rows, norm_gain)
    normed_low = normed.astype(bf)
    projected = jnp.dot(normed_low, in_full, preferred_element_type=f32).astype(bf)
    before_step = projected[:, INNER + CONV :].astype(f32) + dt_bias
    steps = jax.nn.softplus(before_step)
    rates = -steps * jnp.exp(a_log)
    lower = (jnp.arange(rows)[:, None] >= jnp.arange(rows)[None, :]).astype(f32)
    cumulative = jnp.dot(lower, rates, precision=PRECISE)
    wide = lambda a: jnp.broadcast_to(a[:, :, None], a.shape + (HDIM,)).reshape(a.shape[0], -1)
    lanes = lambda a: jnp.broadcast_to(a, (rows, 128))
    mixer_in = (
        projected, projected, projected, conv_weight, conv_bias[None], conv_weight, conv_bias[None],
        lanes(valid), wide(steps), wide(cumulative), cumulative.T.reshape(HEADS // 2, 2, rows),
        wide(d_skip[None]),
    )
    mixed, gated, squares = mixer_front_call(mixer_in, rows)
    scale = lax.rsqrt(jnp.sum(squares, axis=1, keepdims=True) / INNER + EPSILON)
    mix_low = (gated * scale * mix_gain).astype(bf)
    mixer_out = jnp.dot(mix_low, out_full, preferred_element_type=f32)
    hidden = x_rows + mixer_out * valid
    normed_ffn, ffn_pull = jax.vjp(rms_norm, hidden, ffn_gain)
    ffn_low = normed_ffn.astype(bf)
    logits = jnp.dot(ffn_low, router_full, preferred_element_type=f32)
    onehot = (route[:, :, None] == jnp.arange(experts)[None, None, :]).astype(f32)
    chosen = jnp.sum(onehot, axis=1)
    peak = jnp.max(jnp.where(chosen > 0, logits, -jnp.inf), axis=1, keepdims=True)
    raised = jnp.exp(jnp.where(chosen > 0, logits - peak, -jnp.inf))
    probs = raised / jnp.sum(raised, axis=1, keepdims=True)

    all_rows, all_probs = gather_rows(
        [ffn_low, jnp.pad(probs, ((0, 0), (0, 128 - experts)))], [64, rows], 1, 2, [], True, 2
    )
    all_rows, all_probs = all_rows[:, 0], all_probs[:, 0]
    mine = group * held + jnp.arange(held)
    member = jnp.any(all_route[:, :, :, None] == mine, axis=2).astype(f32)
    before = jnp.cumsum(member, axis=1) - member
    pick = (
        (before.transpose(2, 0, 1)[:, :, None, :] == jnp.arange(slots)[None, None, :, None].astype(f32))
        & (member.transpose(2, 0, 1)[:, :, None, :] > 0)
    ).astype(bf)
    gate = lax.dynamic_slice_in_dim(all_probs, group * held, held, 2)
    ein = partial(jnp.einsum, preferred_element_type=f32)
    slot_rows = ein("egst,gtd->egsd", pick, all_rows).astype(bf).reshape(held, groups * slots, MODEL_WIDTH)
    slot_cot = ein("egst,gtd->egsd", pick, all_cot).reshape(held, groups * slots, MODEL_WIDTH)
    slot_gate = jnp.einsum("egst,gte->egs", pick.astype(f32), gate, precision=PRECISE).reshape(held, groups * slots, 1)
    expert_gu = ein("erd,edf->erf", slot_rows, expert_up)
    expert_act, expert_pull = jax.vjp(partial(swiglu, half_width=EXPERT_HIDDEN), expert_gu)
    expert_h = expert_act.astype(bf)
    expert_y = ein("erf,efd->erd", expert_h, expert_down).astype(bf).astype(f32)
    slot_dot = jnp.sum(expert_y * slot_cot, axis=-1)
    grad_ey = (slot_gate * slot_cot).astype(bf)
    grad_edown = ein("erf,erd->efd", expert_h, grad_ey)
    grad_eu = expert_pull(ein("erd,efd->erf", grad_ey, expert_down))[0].astype(bf)
    grad_eup = ein("erd,erf->edf", slot_rows, grad_eu)
    grad_ein = ein("erf,edf->erd", grad_eu, expert_up).astype(bf)
    spread = lambda a: ein("egst,egsd->gtd", pick, a.reshape(held, groups, slots, MODEL_WIDTH))
    flat_rows = all_rows.reshape(-1, MODEL_WIDTH)
    flat_cot = all_cot.reshape(-1, MODEL_WIDTH)
    shared_gu = jnp.dot(flat_rows, up_part, preferred_element_type=f32)
    shared_act, shared_pull = jax.vjp(partial(swiglu, half_width=width), shared_gu)
    shared_h = shared_act.astype(bf)
    grad_sdown = contract_rows(shared_h, flat_cot)
    grad_sgu = shared_pull(contract_cols(flat_cot, down_part))[0].astype(bf)
    grad_sup = contract_rows(flat_rows, grad_sgu)
    y_part = spread((slot_gate * expert_y).astype(bf)) + jnp.dot(
        shared_h, down_part, preferred_element_type=f32
    ).reshape(groups, rows, MODEL_WIDTH)
    g_part = spread(grad_ein) + contract_cols(grad_sgu, up_part).reshape(groups, rows, MODEL_WIDTH)
    dots = jnp.einsum("egst,egs->gte", pick.astype(f32), slot_dot.reshape(held, groups, slots), precision=PRECISE)
    at_own = jnp.arange(128) == mine[:, None]
    dots = jnp.einsum("gte,ef->gtf", dots, at_own.astype(f32), precision=PRECISE)
    dots_hi = dots.astype(bf)
    dots_lo = jnp.roll((dots - dots_hi.astype(f32)).astype(bf), experts, axis=-1)
    g_sum, dots = sum_to_owners(
        [g_part.astype(bf).reshape(-1, MODEL_WIDTH), (dots_hi + dots_lo).reshape(-1, 128)],
        [384, 128], 1, [f32, f32], None, [], True, 3,
    )
    dots = dots[:, :experts] + dots[:, experts : 2 * experts]
    y_sum = to_home(y_part.astype(bf)).astype(f32)
    output = (hidden + valid * y_sum).astype(bf)

    grad_out = cot_low.astype(f32)
    grad_logit = (probs * (dots - jnp.sum(probs * dots, axis=1, keepdims=True))).astype(bf)
    grad_router = contract_rows(ffn_low, grad_logit)
    grad_ffn = g_sum + contract_cols(grad_logit, router_full)
    grad_hidden, grad_fgain = ffn_pull(grad_ffn)
    grad_hidden = grad_hidden + grad_out
    grad_mo = (grad_hidden * valid).astype(bf)
    grad_outw = contract_rows(mix_low, grad_mo)
    grad_mix = contract_cols(grad_mo, out_full)
    mean_dot = jnp.sum(grad_mo.astype(f32) * mixer_out, axis=1, keepdims=True) / INNER
    grad_z, grad_in, stats, grad_bc, bc_stats, row_sums, col_sums, step_sums = mixer_back_call(
        mixer_in, (mixed, grad_mix, mix_gain[None], lanes(scale), lanes(mean_dot)), rows
    )
    grad_rates = jnp.dot(lower.T, row_sums[:, :HEADS] - col_sums[:HEADS].T, precision=PRECISE)
    grad_raw = (step_sums[:, :HEADS] - grad_rates * jnp.exp(a_log)) * jax.nn.sigmoid(before_step)
    grad_al = jnp.sum(grad_rates * rates, axis=0)
    grad_db = jnp.sum(grad_raw, axis=0)
    grad_mgain = stats[0]
    grad_skip = jnp.sum(stats[1].reshape(HEADS, HDIM), axis=1)
    grad_cb = jnp.concatenate([stats[2], bc_stats[0]])
    grad_cw = jnp.concatenate([stats[3 : 3 + KCONV], bc_stats[1 : 1 + KCONV]], axis=1)
    grad_proj = jnp.concatenate([grad_z, grad_in, grad_bc, grad_raw.astype(bf)], axis=1)
    spare = -PROJ % 128
    grad_inw = contract_rows(normed_low, jnp.pad(grad_proj, ((0, 0), (0, spare)))).astype(bf)
    grad_x, grad_ngain = norm_pull(contract_cols(grad_proj, in_full))
    input_grad = (grad_x + grad_hidden).astype(bf)
    grad_router = contract_rows(ffn_low, jnp.pad(grad_logit, ((0, 0), (0, 128 - experts)))).astype(bf)

    pieces = (grad_ngain, grad_cw, grad_cb, grad_db, grad_al, grad_skip, grad_mgain, grad_fgain)
    flat = jnp.concatenate([p.reshape(-1) for p in pieces])
    flat = jnp.pad(flat, (0, -flat.shape[0] % 2048)).reshape(-1, 128)
    own_out, own_in, own_router, output, input_grad, flat = sum_to_owners(
        [grad_outw.astype(bf), grad_inw, grad_router], [512, 768, 128], lines, [f32] * 3, flat,
        [a.reshape(tokens.shape) for a in (output, input_grad)], False, 4,
    )
    flat = flat.reshape(-1)
    small = []
    start = 0
    for p in pieces:
        small.append(flat[start : start + p.size].reshape(p.shape))
        start += p.size
    along = lambda g, d: lax.psum_scatter(g.astype(bf), "seq", scatter_dimension=d, tiled=True)
    sup = grad_sup.astype(bf).reshape(groups, lines, -1, 2 * width).transpose(1, 0, 2, 3)
    sup = along(sup.reshape(MODEL_WIDTH, 2 * width), 0).reshape(groups, -1, 2 * width)
    sup = lax.all_to_all(sup, "dp", split_axis=0, concat_axis=0, tiled=True).astype(f32)
    sup = sup.reshape(groups, -1, 2, width).transpose(1, 2, 0, 3).reshape(-1, 2 * SFF)
    sdown = along(grad_sdown, 0).astype(f32)
    return (
        output, input_grad, small[0], own_in[:, :PROJ], small[1], small[2],
        small[3], small[4], small[5], small[6], own_out, small[7], own_router[:, :experts], sup, sdown,
        along(grad_eup, 1).astype(f32), along(grad_edown, 1).astype(f32),
    )


def solution(mesh):
    def program(*arrays):
        each = arrays[0].shape[0] == lax.axis_size("seq") == 4 and lax.axis_size("dp") == 8
        return (local_fast if each else local)(*arrays)

    return jax.shard_map(
        program,
        mesh=mesh,
        in_specs=(
            P("dp", "seq", None),
            P("dp"),
            P("dp", "seq", None),
            P("dp", "seq", None),
            P(),
            P(("dp", "seq"), None),
            P(),
            P(),
            P(),
            P(),
            P(),
            P(),
            P(("dp", "seq"), None),
            P(),
            P(("dp", "seq"), None),
            P(("dp", "seq"), None),
            P(("dp", "seq"), None),
            P("dp", None, None),
            P("dp", None, None),
        ),
        out_specs=(
            P("dp", "seq", None),
            P("dp", "seq", None),
            P(),
            P(("dp", "seq"), None),
            P(),
            P(),
            P(),
            P(),
            P(),
            P(),
            P(("dp", "seq"), None),
            P(),
            P(("dp", "seq"), None),
            P(("dp", "seq"), None),
            P(("dp", "seq"), None),
            P("dp", "seq", None),
            P("dp", "seq", None),
        ),
        check_vma=False,
    )
```

```python
from functools import partial

import jax
import jax.numpy as jnp
from jax import lax
from jax.experimental import pallas as pl
from jax.experimental.pallas import tpu as pltpu
from jax.sharding import PartitionSpec as P

MODEL_WIDTH = 1536
INNER = 3072
HEADS = 48
HDIM = 64
STATE = 128
KCONV = 4
EXPERT_HIDDEN = 512
SFF = 1024
MB = 4
CONV = 3328
PROJ = 6448


EPSILON = 1e-05
PRECISE = lax.Precision.HIGHEST
MESH = pl.DeviceIdType.MESH


def from_behind(x, axis, by):
    size = lax.axis_size(axis)
    pairs = [(i, i + by) for i in range(size) if 0 <= i + by < size]
    return lax.ppermute(x, axis, pairs)


def prefix(x, axis, join, neutral):
    place = lax.axis_index(axis)
    gathered = jax.tree.map(
        lambda a, kind: lax.all_gather(a.astype(kind), axis), x, (jnp.bfloat16, jnp.bfloat16)
    )
    state = jax.tree.map(lambda a, e: jnp.zeros_like(a) + jnp.asarray(e, a.dtype), x, neutral)

    def one(step, state):
        return join(
            state,
            jax.tree.map(
                lambda a, own: lax.dynamic_index_in_dim(a, step, 0, False).astype(own.dtype),
                gathered,
                x,
            ),
        )

    return lax.fori_loop(0, place, one, state)


def prefix_2(x, axis, join, neutral):
    count = lax.axis_size(axis)
    place = lax.axis_index(axis)
    ahead = count - 1 - place
    gathered = jax.tree.map(
        lambda a, kind: lax.all_gather(a.astype(kind), axis),
        x,
        jax.tree.map(lambda a: jnp.bfloat16 if a.dtype == jnp.float32 else a.dtype, x),
    )
    state = jax.tree.map(lambda a, e: jnp.zeros_like(a) + jnp.asarray(e, a.dtype), x, neutral)

    def one(step, state):
        source = count - 1 - step
        return join(
            state,
            jax.tree.map(
                lambda a, own: lax.dynamic_index_in_dim(a, source, 0, False).astype(own.dtype),
                gathered,
                x,
            ),
        )

    return lax.fori_loop(0, ahead, one, state)


def rms_norm(values, gain_vec):
    return (
        values * lax.rsqrt(jnp.mean(values * values, axis=-1, keepdims=True) + EPSILON) * gain_vec
    )


def swiglu(values, half_width):
    return jax.nn.silu(values[..., :half_width]) * values[..., half_width:]


def contract_rows(left_mat, right_mat):
    return lax.dot_general(
        left_mat, right_mat, (((0,), (0,)), ((), ())), preferred_element_type=jnp.float32
    )


def contract_cols(left_mat, right_mat):
    return lax.dot_general(
        left_mat, right_mat, (((1,), (1,)), ((), ())), preferred_element_type=jnp.float32
    )


def block_terms(head_in, b_rows, c_rows, step_sizes, a_log):
    log_rates = -step_sizes * jnp.exp(a_log)
    cumulative = jnp.cumsum(log_rates, axis=0)
    block_len = head_in.shape[0]
    lower_tri = jnp.arange(block_len)[:, None] >= jnp.arange(block_len)[None, :]
    spread = jnp.where(
        lower_tri[:, :, None], cumulative[:, None, :] - cumulative[None, :, :], -jnp.inf
    )
    scores = jnp.dot(c_rows, b_rows.T, precision=PRECISE)
    weights = jnp.exp(spread) * scores[:, :, None] * step_sizes[None, :, :]
    local_out = jnp.einsum("tih,ihp->thp", weights, head_in, precision=PRECISE)
    tail_weight = jnp.exp(cumulative[-1][None, :] - cumulative) * step_sizes
    local_state = jnp.einsum("ih,ihp,in->hpn", tail_weight, head_in, b_rows, precision=PRECISE)
    return (cumulative, local_out, local_state, jnp.exp(cumulative[-1]))


def carried_out(c_rows, cumulative, state_in):
    return (
        jnp.einsum("tn,hpn->thp", c_rows, state_in, precision=PRECISE)
        * jnp.exp(cumulative)[:, :, None]
    )


def mixer_front(valid_rows, projected, previous, conv_weight, conv_bias, dt_bias, a_log):
    row_count = projected.shape[0]
    conv_in = projected[:, INNER : INNER + CONV]
    padded = jnp.concatenate([previous, conv_in], axis=0)
    conv_sum = conv_bias + conv_weight[0] * padded[0:row_count]
    for tap_idx in range(1, KCONV):
        conv_sum = conv_sum + conv_weight[tap_idx] * padded[tap_idx : tap_idx + row_count]
    activated = jax.nn.silu(conv_sum) * valid_rows
    head_in = activated[:, :INNER].reshape(row_count, HEADS, HDIM)
    b_rows = activated[:, INNER : INNER + STATE]
    c_rows = activated[:, INNER + STATE :]
    step_sizes = jax.nn.softplus(projected[:, INNER + CONV :] + dt_bias)
    cumulative, local_out, local_state, decay_total = block_terms(
        head_in, b_rows, c_rows, step_sizes, a_log
    )
    return (projected[:, :INNER], head_in, c_rows, cumulative, local_out, local_state, decay_total)


def mixer_tail(gate_z, head_in, c_rows, cumulative, local_out, state_in, d_skip, mix_gain):
    mixed_out = local_out + carried_out(c_rows, cumulative, state_in) + d_skip[:, None] * head_in
    gated_out = mixed_out.reshape(head_in.shape[0], INNER) * jax.nn.silu(gate_z)
    return rms_norm(gated_out, mix_gain)


def link_states(earlier, latter):
    return (earlier[0] * latter[0], latter[1] + latter[0][:, None, None] * earlier[1])


def local(
    tokens,
    lengths,
    routes,
    cotangent,
    norm_gain,
    in_weight,
    conv_weight,
    conv_bias,
    dt_bias,
    a_log,
    d_skip,
    mix_gain,
    out_weight,
    ffn_gain,
    router_weight,
    shared_up,
    shared_down,
    expert_up,
    expert_down,
):
    row_count = tokens.shape[1]
    resident_experts = expert_up.shape[0]
    groups = lax.axis_size("dp")
    experts = resident_experts * groups
    top_count = routes.shape[2]
    capacity = row_count * top_count * 5 // (4 * experts)
    shards = (in_weight, out_weight, router_weight, shared_up, shared_down)
    kept_full = (
        lax.all_gather(shards[0], ("dp", "seq"), axis=0, tiled=True),
        lax.all_gather(shards[1], ("dp", "seq"), axis=0, tiled=True),
        lax.all_gather(shards[2], ("dp", "seq"), axis=0, tiled=True),
        lax.all_gather(shards[3], ("dp", "seq"), axis=0, tiled=True),
        lax.all_gather(shards[4], ("dp", "seq"), axis=0, tiled=True),
    )
    grad_inw = jnp.zeros((MODEL_WIDTH, PROJ), jnp.float32)
    grad_outw = jnp.zeros((INNER, MODEL_WIDTH), jnp.float32)
    grad_router = jnp.zeros((MODEL_WIDTH, experts), jnp.float32)
    grad_sup = jnp.zeros((MODEL_WIDTH, 2 * SFF), jnp.float32)
    grad_sdown = jnp.zeros((SFF, MODEL_WIDTH), jnp.float32)
    expert_upward_grad = jnp.zeros((resident_experts, MODEL_WIDTH, 2 * EXPERT_HIDDEN), jnp.float32)
    grad_edown = jnp.zeros((resident_experts, EXPERT_HIDDEN, MODEL_WIDTH), jnp.float32)
    grad_ngain = jnp.zeros_like(norm_gain)
    grad_cw = jnp.zeros_like(conv_weight)
    grad_cb = jnp.zeros_like(conv_bias)
    grad_db = jnp.zeros_like(dt_bias)
    grad_al = jnp.zeros_like(a_log)
    grad_skip = jnp.zeros_like(d_skip)
    grad_mgain = jnp.zeros_like(mix_gain)
    grad_fgain = jnp.zeros_like(ffn_gain)
    outputs = []
    input_grads = []
    for micro_idx in range(MB):
        in_full, out_full, router_full, up_full, down_full = kept_full
        x_rows = tokens[micro_idx].astype(jnp.float32)
        position = lax.axis_index("seq") * row_count + jnp.arange(row_count)
        valid_rows = (position < lengths[micro_idx]).astype(jnp.float32)[:, None]
        normed, norm_pull = jax.vjp(rms_norm, x_rows, norm_gain)
        normed_low = normed.astype(jnp.bfloat16)
        projected = jnp.dot(normed_low, in_full, preferred_element_type=jnp.float32).astype(
            jnp.bfloat16
        )
        previous = from_behind(projected[row_count - (KCONV - 1) :, INNER : INNER + CONV], "seq", 1)
        front_out, front_pull = jax.vjp(
            partial(mixer_front, valid_rows),
            projected.astype(jnp.float32),
            previous.astype(jnp.float32),
            conv_weight,
            conv_bias,
            dt_bias,
            a_log,
        )
        gate_z, head_in, c_rows, cumulative, local_out, local_state, decay_total = front_out
        identity = (jnp.ones_like(decay_total), jnp.zeros_like(local_state))
        _, state_in = prefix((decay_total, local_state), "seq", link_states, identity)
        normed_mix, tail_pull = jax.vjp(
            mixer_tail, gate_z, head_in, c_rows, cumulative, local_out, state_in, d_skip, mix_gain
        )
        mix_low = normed_mix.astype(jnp.bfloat16)
        mixer_out = jnp.dot(mix_low, out_full, preferred_element_type=jnp.float32)
        hidden = x_rows + mixer_out * valid_rows
        normed_ffn, ffn_pull = jax.vjp(rms_norm, hidden, ffn_gain)
        ffn_low = normed_ffn.astype(jnp.bfloat16)
        logits = jnp.dot(ffn_low, router_full, preferred_element_type=jnp.float32)
        route_row = routes[micro_idx]
        picked = jnp.take_along_axis(logits, route_row, axis=1)
        gate_probs = jax.nn.softmax(picked, axis=-1)
        shared_gu = jnp.dot(ffn_low, up_full, preferred_element_type=jnp.float32)
        shared_act, shared_pull = jax.vjp(partial(swiglu, half_width=SFF), shared_gu)
        shared_h = shared_act.astype(jnp.bfloat16)
        shared_y = jnp.dot(shared_h, down_full, preferred_element_type=jnp.float32)
        flat_route = route_row.reshape(-1)
        member = (flat_route[:, None] == jnp.arange(experts)[None, :]).astype(jnp.int32)
        slot_pos = jnp.sum((jnp.cumsum(member, axis=0) - member) * member, axis=1)
        target = flat_route * capacity + slot_pos
        source = (
            jnp.zeros((experts * capacity,), jnp.int32)
            .at[target]
            .set(jnp.arange(row_count * top_count, dtype=jnp.int32))
        )
        filled = jnp.zeros((experts * capacity, 1), jnp.bfloat16).at[target].set(jnp.bfloat16(1))
        outgoing = (jnp.take(ffn_low, source // top_count, axis=0) * filled).reshape(
            groups, resident_experts, capacity, MODEL_WIDTH
        )
        received_rows = lax.all_to_all(outgoing, "dp", split_axis=0, concat_axis=2, tiled=True)[0]
        expert_gu = jnp.einsum(
            "erd,edf->erf", received_rows, expert_up, preferred_element_type=jnp.float32
        )
        expert_act, expert_pull = jax.vjp(partial(swiglu, half_width=EXPERT_HIDDEN), expert_gu)
        expert_h = expert_act.astype(jnp.bfloat16)
        expert_y = jnp.einsum(
            "erf,efd->erd", expert_h, expert_down, preferred_element_type=jnp.float32
        ).astype(jnp.bfloat16)
        returned = lax.all_to_all(expert_y[None], "dp", split_axis=2, concat_axis=0, tiled=True)
        per_choice = (
            jnp.take(returned.reshape(experts * capacity, MODEL_WIDTH), target, axis=0)
            .reshape(row_count, top_count, MODEL_WIDTH)
            .astype(jnp.float32)
        )
        routed = jnp.einsum("lk,lkd->ld", gate_probs, per_choice, precision=PRECISE)
        outputs.append((hidden + valid_rows * (shared_y + routed)).astype(jnp.bfloat16))
        in_back, out_back, router_back, up_back, down_back = kept_full
        grad_out = cotangent[micro_idx].astype(jnp.float32)
        branch = valid_rows * grad_out
        shared_g = branch.astype(jnp.bfloat16)
        grad_sdown = grad_sdown + contract_rows(shared_h, shared_g)
        grad_sgu = shared_pull(contract_cols(shared_g, down_back))[0].astype(jnp.bfloat16)
        grad_sup = grad_sup + contract_rows(ffn_low, grad_sgu)
        grad_ffn = contract_cols(grad_sgu, up_back)
        grad_choice = (gate_probs[:, :, None] * branch[:, None, :]).astype(jnp.bfloat16)
        grad_gate = jnp.sum(branch[:, None, :] * per_choice, axis=-1)
        grad_pick = gate_probs * (
            grad_gate - jnp.sum(gate_probs * grad_gate, axis=-1, keepdims=True)
        )
        onehot = (route_row[:, :, None] == jnp.arange(experts)[None, None, :]).astype(jnp.float32)
        grad_logit = jnp.einsum("lk,lke->le", grad_pick, onehot, precision=PRECISE).astype(
            jnp.bfloat16
        )
        grad_router = grad_router + contract_rows(ffn_low, grad_logit)
        grad_ffn = grad_ffn + contract_cols(grad_logit, router_back)
        back_out = (
            jnp.take(grad_choice.reshape(row_count * top_count, MODEL_WIDTH), source, axis=0)
            * filled
        ).reshape(groups, resident_experts, capacity, MODEL_WIDTH)
        grad_arrived = lax.all_to_all(back_out, "dp", split_axis=0, concat_axis=2, tiled=True)[0]
        step_edown = jnp.einsum(
            "erf,erd->efd", expert_h, grad_arrived, preferred_element_type=jnp.float32
        )
        grad_eh = jnp.einsum(
            "erd,efd->erf", grad_arrived, expert_down, preferred_element_type=jnp.float32
        )
        expert_gate_up_grad = expert_pull(grad_eh)[0].astype(jnp.bfloat16)
        expert_upward_step = jnp.einsum(
            "tbw,tbj->twj", received_rows, expert_gate_up_grad, preferred_element_type=jnp.float32
        )
        grad_ein = jnp.einsum(
            "erf,edf->erd", expert_gate_up_grad, expert_up, preferred_element_type=jnp.float32
        ).astype(jnp.bfloat16)
        expert_upward_grad = expert_upward_grad + expert_upward_step
        grad_edown = grad_edown + step_edown
        came_back = lax.all_to_all(grad_ein[None], "dp", split_axis=2, concat_axis=0, tiled=True)
        grad_ffn = grad_ffn + jnp.sum(
            jnp.take(came_back.reshape(experts * capacity, MODEL_WIDTH), target, axis=0)
            .reshape(row_count, top_count, MODEL_WIDTH)
            .astype(jnp.float32),
            axis=1,
        )
        grad_hidden, step_fgain = ffn_pull(grad_ffn)
        grad_fgain = grad_fgain + step_fgain
        grad_hidden = grad_hidden + grad_out
        grad_mix_out = (grad_hidden * valid_rows).astype(jnp.bfloat16)
        grad_outw = grad_outw + contract_rows(mix_low, grad_mix_out)
        grad_mix = contract_cols(grad_mix_out, out_back)
        grad_z, grad_head, grad_c, grad_cum, grad_local, grad_state, step_skip, step_mgain = (
            tail_pull(grad_mix)
        )
        grad_skip = grad_skip + step_skip
        grad_mgain = grad_mgain + step_mgain
        _, grad_carry = prefix_2((decay_total, grad_state), "seq", link_states, identity)
        grad_decay = jnp.sum(grad_carry * state_in, axis=(1, 2))
        grad_proj, grad_prev, step_cw, step_cb, step_db, step_al = front_pull(
            (grad_z, grad_head, grad_c, grad_cum, grad_local, grad_carry, grad_decay)
        )
        grad_cw = grad_cw + step_cw
        grad_cb = grad_cb + step_cb
        grad_db = grad_db + step_db
        grad_al = grad_al + step_al
        from_next = from_behind(grad_prev.astype(jnp.bfloat16), "seq", -1).astype(grad_prev.dtype)
        grad_proj = (
            grad_proj.at[row_count - (KCONV - 1) :, INNER : INNER + CONV]
            .add(from_next)
            .astype(jnp.bfloat16)
        )
        grad_inw = grad_inw + contract_rows(normed_low, grad_proj)
        grad_normed = contract_cols(grad_proj, in_back)
        grad_x, step_ngain = norm_pull(grad_normed)
        grad_ngain = grad_ngain + step_ngain
        input_grads.append((grad_x + grad_hidden).astype(jnp.bfloat16))
    weight_grads = (
        lax.psum_scatter(grad_inw, ("dp", "seq"), scatter_dimension=0, tiled=True),
        lax.psum_scatter(grad_outw, ("dp", "seq"), scatter_dimension=0, tiled=True),
        lax.psum_scatter(grad_router, ("dp", "seq"), scatter_dimension=0, tiled=True),
        lax.psum_scatter(grad_sup, ("dp", "seq"), scatter_dimension=0, tiled=True),
        lax.psum_scatter(grad_sdown, ("dp", "seq"), scatter_dimension=0, tiled=True),
    )
    small_sums = lax.psum(
        (grad_ngain, grad_cw, grad_cb, grad_db, grad_al, grad_skip, grad_mgain, grad_fgain),
        ("dp", "seq"),
    )
    expert_sums = (
        lax.psum_scatter(
            expert_upward_grad.astype(jnp.bfloat16), "seq", scatter_dimension=1, tiled=True
        ).astype(jnp.float32),
        lax.psum_scatter(
            grad_edown.astype(jnp.bfloat16), "seq", scatter_dimension=1, tiled=True
        ).astype(jnp.float32),
    )
    return (
        jnp.stack(outputs),
        jnp.stack(input_grads),
        small_sums[0],
        weight_grads[0],
        small_sums[1],
        small_sums[2],
        small_sums[3],
        small_sums[4],
        small_sums[5],
        small_sums[6],
        weight_grads[1],
        small_sums[7],
        weight_grads[2],
        weight_grads[3],
        weight_grads[4],
        expert_sums[0],
        expert_sums[1],
    )


def at_neighbours():
    d = lax.axis_index("dp")
    core, x, y = d % 2, (d // 2) % 2, d // 4
    return d, core, x, y, d + 1 - 2 * core, d + 2 - 4 * x, d + 4 - 8 * y


def meet(devices):
    barrier = pltpu.get_barrier_semaphore()
    for there in devices:
        pl.semaphore_signal(barrier, inc=1, device_id=there, device_id_type=MESH)
    pl.semaphore_wait(barrier, len(devices))


def send(source, target, send_sem, recv_sem, there):
    copy = pltpu.make_async_remote_copy(
        src_ref=source, dst_ref=target, send_sem=send_sem, recv_sem=recv_sem,
        device_id=there, device_id_type=MESH,
    )
    copy.start()
    return copy


def add_into(target, source, high):
    step = 16
    for s in (64, 48, 32):
        if high % s == 0:
            step = s
            break

    @pl.loop(0, high // step)
    def _(i):
        rows = pl.ds(pl.multiple_of(i * step, step), step)
        target[rows, :] = target[rows, :] + source[rows, :]


def swap_start(swaps, landed, line, lines, local_sem, send_sem, recv_sem):
    copies = []
    for n, (a, b) in enumerate(zip(swaps, landed)):
        keep = pltpu.make_async_copy(a.at[line], b.at[line], local_sem.at[n])
        keep.start()
        away = [
            send(a.at[o], b.at[line], send_sem.at[n, k], recv_sem.at[n, k], {"seq": o})
            for k, o in enumerate(lax.rem(line + k, lines) for k in range(1, lines))
        ]
        copies.append((keep, away))
    return copies


def swap_end(copies):
    for keep, away in copies:
        for copy in away:
            copy.wait_recv()
    for keep, away in copies:
        for copy in away:
            copy.wait_send()
        keep.wait()


def swap_sems(count, lines):
    dma = pltpu.SemaphoreType.DMA
    return [dma((count,)), dma((count, lines - 1)), dma((count, lines - 1))]


def sum_body(items, arrays, lines, tiny, moved, relative, *refs):
    count = len(items)
    grads, refs = refs[:arrays], refs[arrays:]
    swaps, refs = refs[:moved], refs[moved:]
    if tiny:
        small_in, refs = refs[0], refs[1:]
    outs, refs = refs[:arrays], refs[arrays:]
    landed, refs = refs[:moved], refs[moved:]
    if tiny:
        small_out, refs = refs[0], refs[1:]
    own, refs = refs[:count], refs[count:]
    got, refs = refs[:count], refs[count:]
    from_x, refs = refs[:count], refs[count:]
    from_y, refs = refs[:count], refs[count:]
    last_x, refs = refs[:count], refs[count:]
    last_y, refs = refs[:count], refs[count:]
    if lines > 1:
        from_z, refs = refs[:count], refs[count:]
    (load_sem, send_sem, recv_sem), refs = refs[:3], refs[3:]
    if moved:
        swap_sem, refs = refs[:3], refs[3:]
    if tiny:
        half, t_core, t_x, t_y, t_z, t_back, t_send, t_recv = refs
    d, core, x, y, at_core, at_x, at_y = at_neighbours()
    bits = [(0, 0, 0) if own else (core, x, y) for own in relative]
    own_core = core
    line = lax.axis_index("seq")
    others = [lax.rem(line + k, lines) for k in range(1, lines)]
    meet([{"dp": at_core}, {"dp": at_x}, {"dp": at_y}] + [{"seq": o} for o in others])
    sent = [[] for _ in items]
    stage = [None] * count
    cross = [None] * count
    close = [None] * count
    along = [None] * count
    loads = [None] * count

    def begin(t):
        a, c0, wide, high = items[t]
        core, x, y = bits[a]
        cols = pl.ds(c0, wide)
        loads[t] = pltpu.make_async_copy(grads[a].at[:, :, core, :, cols], own[t], load_sem.at[t])
        loads[t].start()
        stage[t] = send(
            grads[a].at[:, :, 1 - core, :, cols], got[t], send_sem.at[t, 0], recv_sem.at[t, 0], {"dp": at_core}
        )

    def fold(t):
        a, c0, wide, high = items[t]
        core, x, y = bits[a]
        loads[t].wait()
        stage[t].wait_recv()
        for i in range(2):
            for j in range(2):
                add_into(got[t].at[i, j], own[t].at[i, j], high)
        top, low = pl.ds(0, high // 2), pl.ds(high // 2, high // 2)
        cross[t] = (
            send(got[t].at[:, 1 - x, top, :], from_x[t], send_sem.at[t, 1], recv_sem.at[t, 1], {"dp": at_x}),
            send(got[t].at[1 - y, :, low, :], from_y[t], send_sem.at[t, 2], recv_sem.at[t, 2], {"dp": at_y}),
        )

    def turn(t):
        a, c0, wide, high = items[t]
        core, x, y = bits[a]
        top, low = pl.ds(0, high // 2), pl.ds(high // 2, high // 2)
        cross[t][0].wait_recv()
        for i in range(2):
            add_into(got[t].at[i, x, top, :], from_x[t].at[i], high // 2)
        close_y = send(got[t].at[1 - y, x, top, :], last_y[t], send_sem.at[t, 3], recv_sem.at[t, 3], {"dp": at_y})
        cross[t][1].wait_recv()
        for j in range(2):
            add_into(got[t].at[y, j, low, :], from_y[t].at[j], high // 2)
        close_x = send(got[t].at[y, 1 - x, low, :], last_x[t], send_sem.at[t, 4], recv_sem.at[t, 4], {"dp": at_x})
        close[t] = (close_y, close_x)

    def settle(t):
        a, c0, wide, high = items[t]
        core, x, y = bits[a]
        top, low = pl.ds(0, high // 2), pl.ds(high // 2, high // 2)
        cols = pl.ds(c0, wide)
        close[t][0].wait_recv()
        add_into(got[t].at[y, x, top, :], last_y[t], high // 2)
        close[t][1].wait_recv()
        add_into(got[t].at[y, x, low, :], last_x[t], high // 2)
        if lines == 1:
            outs[a][:, cols] = got[t][y, x].astype(outs[a].dtype)
            return
        each = high // lines
        along[t] = [
            send(
                got[t].at[y, x, pl.ds(pl.multiple_of(o * each, 16), each), :], from_z[t].at[k],
                send_sem.at[t, 5 + k], recv_sem.at[t, 5 + k], {"seq": o},
            )
            for k, o in enumerate(others)
        ]

    def finish(t):
        a, c0, wide, high = items[t]
        core, x, y = bits[a]
        each = high // lines
        total = got[t][y, x, pl.ds(pl.multiple_of(line * each, 16), each), :].astype(jnp.float32)
        for k in range(lines - 1):
            along[t][k].wait_recv()
            total = total + from_z[t][k].astype(jnp.float32)
        outs[a][:, pl.ds(c0, wide)] = total

    little = []

    def tiny_step(n):
        rows = half.shape[1]
        if n == 0:
            there = pl.ds(pl.multiple_of((1 - own_core) * rows, 8), rows)
            little.append(send(small_in.at[there, :], t_core, t_send.at[0], t_recv.at[0], {"dp": at_core}))
        elif n == 1:
            little[0].wait_recv()
            here = pl.ds(pl.multiple_of(own_core * rows, 8), rows)
            half[0] = small_in[here, :] + t_core[...]
            little.append(send(half.at[0], t_x, t_send.at[1], t_recv.at[1], {"dp": at_x}))
        elif n == 2:
            little[1].wait_recv()
            half[1] = half[0] + t_x[...]
            little.append(send(half.at[1], t_y, t_send.at[2], t_recv.at[2], {"dp": at_y}))
        elif n == 3:
            little[2].wait_recv()
            half[2] = half[1] + t_y[...]
            t_z[line] = half[2]
            for k, o in enumerate(others):
                little.append(send(half.at[2], t_z.at[line], t_send.at[3 + k], t_recv.at[3 + k], {"seq": o}))
        elif n == 4:
            for k in range(lines - 1):
                little[3 + k].wait_recv()
            total = t_z[0]
            for k in range(1, lines):
                total = total + t_z[k]
            half[3] = total
            small_out[pl.ds(pl.multiple_of(own_core * rows, 8), rows), :] = total
            little.append(send(half.at[3], t_back, t_send.at[7], t_recv.at[7], {"dp": at_core}))
        elif n == 5:
            little[-1].wait_recv()
            small_out[pl.ds(pl.multiple_of((1 - own_core) * rows, 8), rows), :] = t_back[...]
            for copy in little:
                copy.wait_send()

    begin(0)
    if tiny:
        tiny_step(0)
    moves = swap_start(swaps, landed, line, lines, *swap_sem) if moved else ()
    for t in range(max(count + 3, 5 if tiny else 0)):
        if t + 1 < count:
            begin(t + 1)
        if t < count:
            fold(t)
        if 0 <= t - 1 < count:
            turn(t - 1)
        if 0 <= t - 2 < count:
            settle(t - 2)
        if lines > 1 and 0 <= t - 3 < count:
            finish(t - 3)
        if tiny and t < 5:
            tiny_step(t + 1)
    swap_end(moves)
    for t in range(count):
        stage[t].wait_send()
        for copy in cross[t] + close[t] + tuple(along[t] or ()):
            copy.wait_send()


def sum_to_owners(grads, widths, lines, kinds, small, swaps, relative, identity):
    items, views = [], []
    for a, (g, wide) in enumerate(zip(grads, widths)):
        high, cols = g.shape[0] // 8, g.shape[1]
        views.append(g.reshape(2, 2, 2, high, cols))
        start = 0
        while start < cols:
            w = min(wide, cols - start)
            items.append((a, start, w, high))
            start += w
    tiny = small is not None
    bf = jnp.bfloat16
    scratch = [pltpu.VMEM((2, 2, h, w), bf) for _, _, w, h in items]
    scratch += [pltpu.VMEM((2, 2, h, w), bf) for _, _, w, h in items]
    scratch += [pltpu.VMEM((2, h // 2, w), bf) for _, _, w, h in items] * 2
    scratch += [pltpu.VMEM((h // 2, w), bf) for _, _, w, h in items] * 2
    if lines > 1:
        scratch += [pltpu.VMEM((lines - 1, h // lines, w), bf) for _, _, w, h in items]
    ways = 4 + lines
    scratch += [
        pltpu.SemaphoreType.DMA((len(items),)),
        pltpu.SemaphoreType.DMA((len(items), ways)),
        pltpu.SemaphoreType.DMA((len(items), ways)),
    ]
    out_shape = [
        jax.ShapeDtypeStruct((g.shape[0] // 8 // lines, g.shape[1]), kind) for g, kind in zip(grads, kinds)
    ]
    ins = list(views)
    in_specs = [pl.BlockSpec(memory_space=pl.ANY)] * len(views)
    out_specs = [pl.BlockSpec(memory_space=pltpu.VMEM)] * len(views)
    if swaps:
        scratch += swap_sems(len(swaps), lines)
        ins += swaps
        in_specs += [pl.BlockSpec(memory_space=pl.ANY)] * len(swaps)
        out_specs += [pl.BlockSpec(memory_space=pl.ANY)] * len(swaps)
        out_shape += [jax.ShapeDtypeStruct(a.shape, a.dtype) for a in swaps]
    if tiny:
        rows = small.shape[0] // 2
        part = lambda *lead: pltpu.VMEM(lead + (rows, 128), jnp.float32)
        scratch += [part(4), part(), part(), part(), part(lines), part()]
        scratch += [pltpu.SemaphoreType.DMA((8,)), pltpu.SemaphoreType.DMA((8,))]
        out_shape.append(jax.ShapeDtypeStruct(small.shape, jnp.float32))
        ins.append(small)
        in_specs.append(pl.BlockSpec(memory_space=pltpu.VMEM))
        out_specs.append(pl.BlockSpec(memory_space=pltpu.VMEM))
    return pl.pallas_call(
        partial(sum_body, items, len(views), lines, tiny, len(swaps), relative),
        out_shape=out_shape,
        in_specs=in_specs,
        out_specs=out_specs,
        scratch_shapes=scratch,
        name="sum_to_owners_%d" % identity,
        compiler_params=pltpu.CompilerParams(
            collective_id=identity, has_side_effects=True, vmem_limit_bytes=60 << 20
        ),
    )(*ins)


def gather_body(pieces, arrays, flat, lines, ahead, moved, relative, *refs):
    mine, refs = refs[:arrays], refs[arrays:]
    swaps, refs = refs[:moved], refs[moved:]
    full, refs = refs[:arrays], refs[arrays:]
    landed, refs = refs[:moved], refs[moved:]
    keep_sem, send_sem, recv_sem, z_send, z_recv = refs[:5]
    swap_sem = refs[5:]
    d, core, x, y, at_core, at_x, at_y = at_neighbours()
    at_far = at_x + at_y - d
    line = lax.rem(lax.axis_index("seq"), lines)
    hops = [line]
    if lines > 1:
        upper = line // 2
        hops += [line + 1 - 2 * (line % 2), 2 - upper, 3 - 3 * upper]
    meet([{"dp": at_core}, {"dp": at_x}, {"dp": at_y}] + [{"seq": o} for o in hops[1:]])
    blocks = dict(own=d, x=at_x, y=at_y, far=at_far)
    lands = dict(x=d, y=d, core=d, x_y=at_x, x_core=at_x, y_x=at_y, y_core=at_y, far_core=at_far)
    if relative:
        blocks = dict(own=0, x=2, y=4, far=6)
        lands = dict(x=2, y=4, core=1, x_y=6, x_core=3, y_x=6, y_core=5, far_core=7)
    mains = [q for q, piece in enumerate(pieces) if piece[0] < arrays - flat]
    sides = [q for q, piece in enumerate(pieces) if piece[0] >= arrays - flat]
    home = lambda a: blocks["own"] if a < arrays - flat else 0
    keep = []
    for a in range(arrays):
        keep.append(pltpu.make_async_copy(mine[a], full[a].at[home(a), line], keep_sem.at[a]))
        keep[a].start()
    order = [(j, q) for j in range(lines) for q in mains]
    total = len(order)
    out = [[None] * 7 for _ in order]

    def place(j, q, block):
        a, r0, high = pieces[q]
        return full[a].at[block, hops[j], pl.ds(r0, high), :]

    def own_piece(q):
        a, r0, high = pieces[q]
        return mine[a].at[pl.ds(r0, high), :]

    def hop(j, q, sem, to):
        a = pieces[q][0]
        return pltpu.make_async_remote_copy(
            src_ref=own_piece(q) if j == 0 else place(j, q, home(a)),
            dst_ref=place(j, q, home(a)),
            send_sem=z_send.at[q, sem], recv_sem=z_recv.at[q, hops[j]],
            device_id={"seq": to}, device_id_type=MESH,
        )

    def onward(j, q, act):
        o = hops[j]

        @pl.when((o <= line) & (line < lines - 1))
        def _():
            act(hop(j, q, 2 * j, jnp.minimum(line + 1, lines - 1)))

        @pl.when((o >= line) & (line > 0))
        def _():
            act(hop(j, q, 2 * j + 1, jnp.maximum(line - 1, 0)))

    def relay(j, q):
        hop(j, q, 2 * j, line).wait_recv()
        onward(j, q, lambda copy: copy.start())

    def pass_on(i, n, block, lands_at, there):
        j, q = order[i]
        source = own_piece(q) if block is None else place(j, q, block)
        out[i][n] = send(
            source, place(j, q, lands[lands_at]), send_sem.at[i, n], recv_sem.at[i, n], {"dp": there}
        )

    def first(i):
        block = None if order[i][0] == 0 else blocks["own"]
        pass_on(i, 0, block, "x", at_x)
        pass_on(i, 1, block, "y", at_y)
        pass_on(i, 2, block, "core", at_core)

    def second(i):
        out[i][0].wait_recv()
        if i % 2 == 0:
            pass_on(i, 5, blocks["x"], "x_y", at_y)
        pass_on(i, 3, blocks["x"], "x_core", at_core)
        out[i][1].wait_recv()
        if i % 2 == 1:
            pass_on(i, 5, blocks["y"], "y_x", at_x)
        pass_on(i, 4, blocks["y"], "y_core", at_core)

    def third(i):
        out[i][5].wait_recv()
        pass_on(i, 6, blocks["far"], "far_core", at_core)

    lead = ahead + 2
    if lines > 1:
        for q in mains:
            onward(0, q, lambda copy: copy.start())
    for i in range(min(ahead, total)):
        first(i)
    moves = swap_start(swaps, landed, line, lines, *swap_sem) if moved else ()
    for i in range(total):
        if i + lead < total and order[i + lead][0] > 0:
            relay(*order[i + lead])
        if i % len(mains) == 1:
            j = i // len(mains)
            for q in sides:
                if j == 0:
                    onward(0, q, lambda copy: copy.start())
                else:
                    relay(j, q)
        if i + ahead < total:
            first(i + ahead)
        second(i)
        if i:
            third(i - 1)
    third(total - 1)
    for i in range(total):
        for n in (2, 3, 4, 6):
            out[i][n].wait_recv()
        for copy in out[i]:
            copy.wait_send()
    swap_end(moves)
    if lines > 1:
        for q in range(len(pieces)):
            for j in range(lines):
                onward(j, q, lambda copy: copy.wait_send())
    for copy in keep:
        copy.wait()


def gather_rows(arrays, chunks, flat, lines, ahead, swaps, relative, identity):
    pieces = []
    count = len(arrays) + len(flat)
    for a, (w, chunk) in enumerate(zip(list(arrays) + list(flat), chunks)):
        for r0 in range(0, w.shape[0], chunk):
            pieces.append((a, r0, chunk))
    total = lines * len([p for p in pieces if p[0] < len(arrays)])
    anywhere = pl.BlockSpec(memory_space=pl.ANY)
    return pl.pallas_call(
        partial(gather_body, pieces, count, len(flat), lines, ahead, len(swaps), relative),
        out_shape=[jax.ShapeDtypeStruct((8, lines) + w.shape, w.dtype) for w in arrays]
        + [jax.ShapeDtypeStruct((1, lines) + w.shape, w.dtype) for w in flat]
        + [jax.ShapeDtypeStruct(a.shape, a.dtype) for a in swaps],
        in_specs=[anywhere] * (count + len(swaps)),
        out_specs=[anywhere] * (count + len(swaps)),
        scratch_shapes=[
            pltpu.SemaphoreType.DMA((count,)),
            pltpu.SemaphoreType.DMA((total, 7)),
            pltpu.SemaphoreType.DMA((total, 7)),
            pltpu.SemaphoreType.DMA((len(pieces), 2 * lines)),
            pltpu.SemaphoreType.DMA((len(pieces), lines)),
        ]
        + (swap_sems(len(swaps), lines) if swaps else []),
        name="gather_rows_%d" % identity,
        compiler_params=pltpu.CompilerParams(collective_id=identity, has_side_effects=True),
    )(*arrays, *flat, *swaps)


def sigmoid(v):
    return 1.0 / (1.0 + jnp.exp(-v))


def shifted(v, by):
    if by == 0:
        return v
    rows = v.shape[0]
    at = lax.broadcasted_iota(jnp.int32, v.shape, 0)
    keep = at >= by if by > 0 else at < rows + by
    return jnp.where(keep, pltpu.roll(v, by % rows, 0), 0.0)


def conv_sums(v, taps, bias):
    total = bias
    for k in range(KCONV):
        total = total + taps[k : k + 1, :] * shifted(v, KCONV - 1 - k)
    return total


def conv_back(v, taps, bias, valid, grad):
    conv_sum = conv_sums(v, taps, bias)
    s = sigmoid(conv_sum)
    grad = grad * valid * (s * (1.0 + conv_sum * (1.0 - s)))
    total = taps[KCONV - 1 : KCONV, :] * grad
    for k in range(KCONV - 1):
        total = total + taps[k : k + 1, :] * shifted(grad, k - (KCONV - 1))
    sums = [jnp.sum(grad, axis=0, keepdims=True)]
    for k in range(KCONV):
        sums.append(jnp.sum(grad * shifted(v, KCONV - 1 - k), axis=0, keepdims=True))
    return total, sums


def lower_left(rows):
    return lax.broadcasted_iota(jnp.int32, (rows, rows), 0) >= lax.broadcasted_iota(
        jnp.int32, (rows, rows), 1
    )


def product(a, b, over_a=1, over_b=0):
    return lax.dot_general(
        a, b, (((over_a,), (over_b,)), ((), ())), preferred_element_type=jnp.float32
    )


def bc_scores(bc_ref, bc_taps, bc_bias, valid, scores, bc_keep):
    conv_sum = conv_sums(bc_ref[...].astype(jnp.float32), bc_taps[...], bc_bias[...])
    bc = conv_sum * sigmoid(conv_sum) * valid[:, :1]
    bc_keep[...] = bc.astype(jnp.bfloat16)
    rows = scores.shape[0]
    g = product(bc_keep[:, STATE:], bc_keep[:, :STATE], 1, 1)
    scores[...] = jnp.where(lower_left(rows), g, 0.0)


def front_body(
    where, z_ref, x_ref, bc_ref, taps, bias, bc_taps, bc_bias, valid, step, cum, cum_rows, skip,
    mixed_ref, gated_ref, squares, scores, bc_keep,
):
    f32, bf = jnp.float32, jnp.bfloat16

    @pl.when(pl.program_id(0) == 0)
    def _():
        bc_scores(bc_ref, bc_taps, bc_bias, valid, scores, bc_keep)
        squares[...] = jnp.zeros_like(squares)

    rows = x_ref.shape[0]
    half = rows // 2
    conv_sum = conv_sums(x_ref[...].astype(f32), taps[...], bias[...])
    x = conv_sum * sigmoid(conv_sum) * valid[...]
    xs = (x * step[...]).astype(bf)
    lane = lax.broadcasted_iota(jnp.int32, (half, 128), 1)
    for r in range(2):
        at, wide = pl.ds(r * half, half), (r + 1) * half
        parts = []
        for h in range(2):
            gap = cum[at, h * HDIM : h * HDIM + 1] - cum_rows[0, h : h + 1, :wide]
            m = (jnp.exp(jnp.minimum(gap, 0.0)) * scores[at, :wide]).astype(bf)
            parts.append(product(m, xs[:wide, :]))
        mixed = jnp.where(lane < HDIM, parts[0], parts[1]) + skip[...] * x[r * half : (r + 1) * half, :]
        z = z_ref[at, :].astype(f32)
        gated = mixed * (z * sigmoid(z))
        mixed_ref[at, :] = mixed
        gated_ref[at, :] = gated
        squares[at, :] += gated * gated


def back_body(
    where, z_ref, x_ref, bc_ref, taps, bias, bc_taps, bc_bias, valid, step, cum, cum_rows, skip,
    mixed_ref, grad_ref, gain, scale, mean_dot,
    grad_z, grad_x, stats, grad_bc, bc_stats, row_sums, col_sums, step_sums,
    scores, bc_keep, grad_scores, grad_xs,
):
    f32, bf = jnp.float32, jnp.bfloat16
    pair = pl.program_id(0)

    @pl.when(pair == 0)
    def _():
        bc_scores(bc_ref, bc_taps, bc_bias, valid, scores, bc_keep)
        grad_scores[...] = jnp.zeros_like(grad_scores)
        row_sums[...] = jnp.zeros_like(row_sums)
        col_sums[...] = jnp.zeros_like(col_sums)
        step_sums[...] = jnp.zeros_like(step_sums)

    rows = x_ref.shape[0]
    half = rows // 2
    v = x_ref[...].astype(f32)
    conv_sum = conv_sums(v, taps[...], bias[...])
    x = conv_sum * sigmoid(conv_sum) * valid[...]
    xs = (x * step[...]).astype(bf)
    z = z_ref[...].astype(f32)
    s = sigmoid(z)
    silu = z * s
    mixed = mixed_ref[...]
    normal = mixed * silu * scale[...]
    grad = grad_ref[...]
    grad_gated = scale[...] * (grad * gain[...] - normal * mean_dot[...])
    grad_mixed = grad_gated * silu
    grad_z[...] = (grad_gated * mixed * (s * (1.0 + z * (1.0 - s)))).astype(bf)
    lane = lax.broadcasted_iota(jnp.int32, (rows, 128), 1)
    dy = [
        jnp.where(lane < HDIM, grad_mixed, 0.0).astype(bf),
        jnp.where(lane < HDIM, 0.0, grad_mixed).astype(bf),
    ]
    for r in range(2):
        at, wide = pl.ds(r * half, half), (r + 1) * half
        total = None
        for h in range(2):
            head = 2 * pair + h
            g = scores[at, :wide]
            gap = cum[at, h * HDIM : h * HDIM + 1] - cum_rows[0, h : h + 1, :wide]
            e = jnp.exp(jnp.minimum(gap, 0.0))
            m = (e * g).astype(bf)
            dy_rows = dy[h][r * half : (r + 1) * half, :]
            slope = product(dy_rows, xs[:wide, :], 1, 1) * e
            grad_scores[at, :wide] += slope
            both = (slope * g).astype(bf)
            back = product(m, dy_rows, 0, 0)
            total = back if total is None else total + back
            to_lane = (lax.broadcasted_iota(jnp.int32, (wide, 128), 1) == head).astype(bf)
            row_sums[at, :] += product(both, to_lane)
            to_row = (lax.broadcasted_iota(jnp.int32, (64, half), 0) == head).astype(bf)
            col_sums[:, :wide] += product(to_row, both)
        if r == 0:
            grad_xs[:half, :] = total
        else:
            grad_xs[:half, :] += total[:half, :]
            grad_xs[half:, :] = total[half:, :]
    gxs = grad_xs[...]
    fold = (
        lax.broadcasted_iota(jnp.int32, (128, 128), 1)
        == 2 * pair + lax.broadcasted_iota(jnp.int32, (128, 128), 0) // HDIM
    ).astype(bf)
    step_sums[...] += product((gxs * x).astype(bf), fold)
    gx, sums = conv_back(v, taps[...], bias[...], valid[...], gxs * step[...] + skip[...] * grad_mixed)
    grad_x[...] = gx.astype(bf)
    stats[0:1, :] = jnp.sum(grad * normal, axis=0, keepdims=True)
    stats[1:2, :] = jnp.sum(grad_mixed * x, axis=0, keepdims=True)
    for k, total in enumerate(sums):
        stats[2 + k : 3 + k, :] = total
    stats[7:8, :] = jnp.zeros((1, 128), f32)

    @pl.when(pair == pl.num_programs(0) - 1)
    def _():
        gs = jnp.where(lower_left(rows), grad_scores[...], 0.0).astype(bf)
        grad_c = product(gs, bc_keep[:, :STATE])
        grad_b = product(gs, bc_keep[:, STATE:], 0, 0)
        ends = ((grad_b, 0), (grad_c, STATE))
        for g, at in ends:
            cols = pl.ds(at, STATE)
            gi, sums = conv_back(
                bc_ref[:, cols].astype(f32), bc_taps[:, cols], bc_bias[:, cols], valid[...], g
            )
            grad_bc[:, cols] = gi.astype(bf)
            for k, total in enumerate(sums):
                bc_stats[k : k + 1, cols] = total
            bc_stats[5:8, cols] = jnp.zeros((3, STATE), f32)


def mixer_specs(rows):
    tile = lambda at: pl.BlockSpec((rows, 128), at)
    whole = lambda shape: pl.BlockSpec(shape, lambda p, w: (0,) * len(shape))
    pairs = INNER // 128
    each = pairs // 8
    relative = lambda p, w: (0, (p // each ^ w[0]) * each + p % each)
    by_pair = lambda shape: pl.BlockSpec(shape, lambda p, w: (0, p))
    return tile(relative), whole, by_pair, [
        by_pair((rows, 128)),
        tile(lambda p, w: (0, pairs + p)),
        pl.BlockSpec((rows, 2 * STATE), lambda p, w: (0, 2 * INNER // (2 * STATE))),
        by_pair((KCONV, 128)),
        by_pair((1, 128)),
        pl.BlockSpec((KCONV, 2 * STATE), lambda p, w: (0, INNER // (2 * STATE))),
        pl.BlockSpec((1, 2 * STATE), lambda p, w: (0, INNER // (2 * STATE))),
        whole((rows, 128)),
        by_pair((rows, 128)),
        by_pair((rows, 128)),
        pl.BlockSpec((1, 2, rows), lambda p, w: (p, 0, 0)),
        by_pair((1, 128)),
    ]


def mixer_front_call(where, inputs, rows):
    f32 = jnp.float32
    mixed_up, whole, by_pair, specs = mixer_specs(rows)
    return pl.pallas_call(
        front_body,
        grid_spec=pltpu.PrefetchScalarGridSpec(
            num_scalar_prefetch=1,
            grid=(INNER // 128,),
            in_specs=specs,
            out_specs=[by_pair((rows, 128)), mixed_up, whole((rows, 128))],
            scratch_shapes=[pltpu.VMEM((rows, rows), f32), pltpu.VMEM((rows, 2 * STATE), jnp.bfloat16)],
        ),
        out_shape=[
            jax.ShapeDtypeStruct((rows, INNER), f32),
            jax.ShapeDtypeStruct((rows, INNER), f32),
            jax.ShapeDtypeStruct((rows, 128), f32),
        ],
        name="mixer_front",
        cost_estimate=pl.CostEstimate(flops=10**10, bytes_accessed=2 * 10**7, transcendentals=5 * 10**6),
    )(where, *inputs)


def mixer_back_call(where, inputs, extra, rows):
    f32, bf = jnp.float32, jnp.bfloat16
    mixed_up, whole, by_pair, specs = mixer_specs(rows)
    tile = by_pair((rows, 128))
    return pl.pallas_call(
        back_body,
        grid_spec=pltpu.PrefetchScalarGridSpec(
            num_scalar_prefetch=1,
            grid=(INNER // 128,),
            in_specs=specs + [tile, mixed_up, by_pair((1, 128)), whole((rows, 128)), whole((rows, 128))],
            out_specs=[
                tile, tile, by_pair((8, 128)), whole((rows, 2 * STATE)),
                whole((8, 2 * STATE)), whole((rows, 128)), whole((64, rows)), whole((rows, 128)),
            ],
            scratch_shapes=[
                pltpu.VMEM((rows, rows), f32), pltpu.VMEM((rows, 2 * STATE), bf),
                pltpu.VMEM((rows, rows), f32), pltpu.VMEM((rows, 128), f32),
            ],
        ),
        out_shape=[
            jax.ShapeDtypeStruct((rows, INNER), bf),
            jax.ShapeDtypeStruct((rows, INNER), bf),
            jax.ShapeDtypeStruct((8, INNER), f32),
            jax.ShapeDtypeStruct((rows, 2 * STATE), bf),
            jax.ShapeDtypeStruct((8, 2 * STATE), f32),
            jax.ShapeDtypeStruct((rows, 128), f32),
            jax.ShapeDtypeStruct((64, rows), f32),
            jax.ShapeDtypeStruct((rows, 128), f32),
        ],
        name="mixer_back",
        cost_estimate=pl.CostEstimate(flops=3 * 10**10, bytes_accessed=3 * 10**7, transcendentals=5 * 10**6),
    )(where, *inputs, *extra)


def picks(slot_row, slots):
    rows = slot_row.shape[1]
    at = lax.broadcasted_iota(jnp.int32, (slots, rows), 0).astype(jnp.float32)
    return at == slot_row


def experts_body(
    x_ref, cot_ref, up, down, slot_rows, gates,
    y_out, gin_out, up_grad, down_grad, dots,
    xe, gy, gu_grad, hid, gate_cols,
):
    f32, bf = jnp.float32, jnp.bfloat16
    chunks, rows, width = x_ref.shape
    slots = xe.shape[0] // chunks
    hidden = down.shape[1]

    @pl.loop(0, chunks)
    def _(g):
        p = picks(slot_rows[0, pl.ds(g, 1), :], slots)
        one = p.astype(bf)
        at = pl.ds(pl.multiple_of(g * slots, slots), slots)
        xe[at, :] = product(one, x_ref[g]).astype(bf)
        gate = jnp.sum(jnp.where(p, gates[0, pl.ds(g, 1), :], 0.0), axis=1, keepdims=True)
        gate_cols[at, :] = jnp.broadcast_to(gate, (slots, 128))
        gy[at, :] = (gate * product(one, cot_ref[g])).astype(bf)

    tile = 2 * slots

    @pl.loop(0, xe.shape[0] // tile)
    def _(t):
        at = pl.ds(pl.multiple_of(t * tile, tile), tile)
        gu = product(xe[at, :], up[0])
        a, b = gu[:, :hidden], gu[:, hidden:]
        s = sigmoid(a)
        silu = a * s
        h = (silu * b).astype(bf)
        hid[at, :] = h
        gh = product(gy[at, :], down[0], 1, 1)
        gu_grad[at, :hidden] = (gh * b * (s * (1.0 + a * (1.0 - s)))).astype(bf)
        gu_grad[at, hidden:] = (gh * silu).astype(bf)
        y = product(h, down[0]).astype(bf).astype(f32)
        dot = jnp.sum(y * gy[at, :].astype(f32), axis=1, keepdims=True)
        y_out[0, at, :] = (gate_cols[at, :1] * y).astype(bf)
        for i in range(2):
            p = picks(slot_rows[0, pl.ds(2 * t + i, 1), :], slots)
            dots[0, pl.ds(2 * t + i, 1), :] = jnp.sum(
                jnp.where(p, dot[i * slots : (i + 1) * slots, :], 0.0), axis=0, keepdims=True
            )
        gin_out[0, at, :] = product(gu_grad[at, :], up[0], 1, 1).astype(bf)

    for r in range(0, width, 256):
        up_grad[0, r : r + 256, :] = product(xe[:, r : r + 256], gu_grad[...], 0, 0).astype(bf)
    for r in range(0, hidden, 256):
        down_grad[0, r : r + 256, :] = product(hid[:, r : r + 256], gy[...], 0, 0).astype(bf)


def experts_call(x, cot, up, down, slot_rows, gates, slots):
    f32, bf = jnp.float32, jnp.bfloat16
    chunks, rows, width = x.shape
    held, _, double = up.shape
    total = chunks * slots
    once = pl.Buffered(1)
    each = lambda *shape: pl.BlockSpec((1,) + shape, lambda e: (e, 0, 0))
    keep = lambda *shape: pl.BlockSpec((1,) + shape, lambda e: (e, 0, 0), pipeline_mode=once)
    whole = pl.BlockSpec((chunks, rows, width), lambda e: (0, 0, 0), pipeline_mode=once)
    shape = lambda *s: jax.ShapeDtypeStruct((held,) + s, bf)
    return pl.pallas_call(
        experts_body,
        grid=(held,),
        in_specs=[
            whole, whole, keep(width, double), keep(double // 2, width), each(chunks, rows), each(chunks, rows),
        ],
        out_specs=[
            each(total, width), each(total, width), each(width, double), each(double // 2, width), each(chunks, rows),
        ],
        out_shape=[
            shape(total, width), shape(total, width), shape(width, double), shape(double // 2, width),
            jax.ShapeDtypeStruct((held, chunks, rows), f32),
        ],
        scratch_shapes=[
            pltpu.VMEM((total, width), bf), pltpu.VMEM((total, width), bf), pltpu.VMEM((total, double), bf),
            pltpu.VMEM((total, double // 2), bf), pltpu.VMEM((total, 128), f32),
        ],
        name="experts",
        compiler_params=pltpu.CompilerParams(vmem_limit_bytes=62 << 20),
        cost_estimate=pl.CostEstimate(flops=4 * 10**10, bytes_accessed=5 * 10**7, transcendentals=10**6),
    )(x, cot, up, down, slot_rows, gates)


def join_body(
    x_ref, cot_ref, y_ref, gin_ref, slot_rows, up, down,
    y_part, g_part, up_grad, down_grad, up_acc, down_acc,
):
    f32, bf = jnp.float32, jnp.bfloat16
    g = pl.program_id(0)

    @pl.when(g == 0)
    def _():
        up_acc[...] = jnp.zeros_like(up_acc)
        down_acc[...] = jnp.zeros_like(down_acc)

    x, cot = x_ref[0], cot_ref[0]
    half = down.shape[0]
    gu = product(x, up[...])
    a, b = gu[:, :half], gu[:, half:]
    s = sigmoid(a)
    silu = a * s
    h = (silu * b).astype(bf)
    gh = product(cot, down[...], 1, 1)
    gu_grad = jnp.concatenate(
        [gh * b * (s * (1.0 + a * (1.0 - s))), gh * silu], axis=1
    ).astype(bf)
    up_acc[...] += product(x, gu_grad, 0, 0)
    down_acc[...] += product(h, cot, 0, 0)
    y = product(h, down[...])
    gx = product(gu_grad, up[...], 1, 1)
    for e in range(y_ref.shape[0]):
        one = picks(slot_rows[e, pl.ds(g, 1), :], y_ref.shape[1]).astype(bf)
        y = y + product(one, y_ref[e], 0, 0)
        gx = gx + product(one, gin_ref[e], 0, 0)
    y_part[0] = y.astype(bf)
    g_part[0] = gx.astype(bf)

    @pl.when(g == pl.num_programs(0) - 1)
    def _():
        up_grad[...] = up_acc[...].astype(bf)
        down_grad[...] = down_acc[...].astype(bf)


def join_call(x, cot, y, gin, slot_rows, up, down, slots):
    f32, bf = jnp.float32, jnp.bfloat16
    chunks, rows, width = x.shape
    held = y.shape[0]
    chunk = pl.BlockSpec((1, rows, width), lambda g: (g, 0, 0))
    rows_of = pl.BlockSpec((held, slots, width), lambda g: (0, g, 0))
    whole = lambda a: pl.BlockSpec(a.shape, lambda g: (0,) * a.ndim)
    return pl.pallas_call(
        join_body,
        grid=(chunks,),
        in_specs=[chunk, chunk, rows_of, rows_of, whole(slot_rows), whole(up), whole(down)],
        out_specs=[chunk, chunk, whole(up), whole(down)],
        out_shape=[
            jax.ShapeDtypeStruct(x.shape, bf), jax.ShapeDtypeStruct(x.shape, bf),
            jax.ShapeDtypeStruct(up.shape, bf), jax.ShapeDtypeStruct(down.shape, bf),
        ],
        scratch_shapes=[pltpu.VMEM(up.shape, f32), pltpu.VMEM(down.shape, f32)],
        name="join",
        compiler_params=pltpu.CompilerParams(vmem_limit_bytes=48 << 20),
        cost_estimate=pl.CostEstimate(flops=10**10, bytes_accessed=4 * 10**7, transcendentals=10**6),
    )(x, cot, y, gin, slot_rows, up, down)


def local_fast(
    tokens, lengths, routes, cotangent, norm_gain, in_weight, conv_weight, conv_bias, dt_bias,
    a_log, d_skip, mix_gain, out_weight, ffn_gain, router_weight, shared_up, shared_down,
    expert_up, expert_down,
):
    bf, f32 = jnp.bfloat16, jnp.float32
    block = tokens.shape[1]
    parts = tokens.shape[0]
    rows = block * parts
    groups = lax.axis_size("dp")
    lines = lax.axis_size("seq")
    held = expert_up.shape[0]
    experts = held * groups
    top = routes.shape[2]
    slots = block * top * 5 // (4 * experts) * parts
    slots = -(-slots // 128) * 128
    place = lax.axis_index("seq")
    group = lax.axis_index("dp")

    def to(a, bit):
        return lax.ppermute(a, "dp", [(i, i ^ bit) for i in range(groups)])

    def fold(a):
        a = a[0::2] + to(a[1::2], 1)
        cut = a.shape[2] // 2
        left, right = a[:, :, :cut], a[:, :, cut:]
        left = left[0::2] + to(left[1::2], 2)
        right = right[:2] + to(right[2:], 4)
        left = left[0] + to(left[1], 4)
        right = right[0] + to(right[1], 2)
        return jnp.concatenate([left, right], axis=1)

    def around(a):
        cut = a.shape[0] // 2
        by_x, by_y = to(a, 2), to(a, 4)
        near = [a, by_x, by_y, to(by_x[:cut], 4), to(by_y[cut:], 2)]
        far = [to(b, 1) for b in near]
        halves = [b for pair in zip(near[:3], far[:3]) for b in pair] + [near[3], near[4], far[3], far[4]]
        return jnp.concatenate(halves, axis=0)

    def spread(a):
        return lax.all_to_all(
            jnp.broadcast_to(a[None], (lines,) + a.shape), "seq", split_axis=0, concat_axis=0, tiled=True
        )

    pad = lambda a, n: jnp.pad(a, ((0, 0), (0, n - a.shape[1])))
    in_blocks, router_blocks, out_line, down_line, x_low, route = gather_rows(
        [in_weight, pad(router_weight, 128)],
        [in_weight.shape[0] // 3, router_weight.shape[0], out_weight.shape[0], shared_down.shape[0]],
        [out_weight, shared_down], lines, 2, [tokens, routes], False, 1,
    )
    in_full = in_blocks.reshape(MODEL_WIDTH, -1)
    router_full = router_blocks.reshape(MODEL_WIDTH, -1)[:, :experts]
    down_part = down_line.reshape(-1, MODEL_WIDTH)
    in_full, late_up, late_cot = lax.optimization_barrier((in_full, shared_up, cotangent))
    out_full = around(out_line.reshape(-1, MODEL_WIDTH))
    cot_low = lax.all_to_all(late_cot, "seq", split_axis=0, concat_axis=0, tiled=True)
    width = SFF // groups
    up_cols = late_up.reshape(-1, 2, groups, width).transpose(2, 0, 1, 3).reshape(groups, -1, 2 * width)
    up_cols = lax.all_to_all(up_cols, "dp", split_axis=0, concat_axis=0, tiled=True)
    up_part = spread(up_cols).transpose(1, 0, 2, 3).reshape(MODEL_WIDTH, 2 * width)

    length = lax.dynamic_index_in_dim(lengths, place, 0, False)
    x_low = x_low.reshape(rows, MODEL_WIDTH)
    cot_low = cot_low.reshape(rows, MODEL_WIDTH)
    route = route.reshape(rows, top)
    used = jnp.arange(rows) < length
    valid = used.astype(f32)[:, None]
    all_cot = around(jnp.where(used[:, None], cot_low, 0)).reshape(groups, rows, MODEL_WIDTH)
    all_route = around(jnp.where(used[:, None], route, -1)).reshape(groups, rows, top)
    mine = group * held + jnp.arange(held)
    member = jnp.any(all_route[None] == mine[:, None, None, None], axis=3)
    earlier = (jnp.arange(rows)[:, None] < jnp.arange(rows)[None, :]).astype(bf)
    before = jnp.einsum("egt,ts->egs", member.astype(bf), earlier, preferred_element_type=f32)
    slot_rows = jnp.where(member, before, -1.0)
    x_rows = x_low.astype(f32)
    normed, norm_pull = jax.vjp(rms_norm, x_rows, norm_gain)
    normed_low = normed.astype(bf)
    projected = jnp.dot(normed_low, in_full, preferred_element_type=f32).astype(bf)
    before_step = projected[:, INNER + CONV :].astype(f32) + dt_bias
    steps = jax.nn.softplus(before_step)
    rates = -steps * jnp.exp(a_log)
    lower = (jnp.arange(rows)[:, None] >= jnp.arange(rows)[None, :]).astype(f32)
    cumulative = jnp.dot(lower, rates, precision=PRECISE)
    wide = lambda a: jnp.broadcast_to(a[:, :, None], a.shape + (HDIM,)).reshape(a.shape[0], -1)
    lanes = lambda a: jnp.broadcast_to(a, (rows, 128))
    mixer_in = (
        projected, projected, projected, conv_weight, conv_bias[None], conv_weight, conv_bias[None],
        lanes(valid), wide(steps), wide(cumulative), cumulative.T.reshape(HEADS // 2, 2, rows),
        wide(d_skip[None]),
    )
    where = group.reshape(1)
    mixed, gated, squares = mixer_front_call(where, mixer_in, rows)
    scale = lax.rsqrt(jnp.sum(squares, axis=1, keepdims=True) / INNER + EPSILON)
    gain_blocks = mix_gain.reshape(groups, -1)[jnp.arange(groups) ^ group].reshape(-1)
    mix_low = (gated * scale * gain_blocks).astype(bf)
    mixer_out = jnp.dot(mix_low, out_full, preferred_element_type=f32)
    hidden = x_rows + mixer_out * valid
    normed_ffn, ffn_pull = jax.vjp(rms_norm, hidden, ffn_gain)
    ffn_low = normed_ffn.astype(bf)
    logits = jnp.dot(ffn_low, router_full, preferred_element_type=f32)
    onehot = (route[:, :, None] == jnp.arange(experts)[None, None, :]).astype(f32)
    chosen = jnp.sum(onehot, axis=1)
    peak = jnp.max(jnp.where(chosen > 0, logits, -jnp.inf), axis=1, keepdims=True)
    raised = jnp.exp(jnp.where(chosen > 0, logits - peak, -jnp.inf))
    probs = raised / jnp.sum(raised, axis=1, keepdims=True)

    all_rows, all_probs = gather_rows(
        [ffn_low, pad(probs, 128)], [64, rows], [], 1, 2, [], True, 2
    )
    all_rows = all_rows[:, 0]
    gates = lax.dynamic_slice_in_dim(all_probs[:, 0], group * held, held, 2).transpose(2, 0, 1)
    y_slots, gin_slots, grad_eup, grad_edown, dots = experts_call(
        all_rows, all_cot, expert_up, expert_down, slot_rows, gates, slots
    )
    y_part, g_part, grad_sup, grad_sdown = join_call(
        all_rows, all_cot, y_slots, gin_slots, slot_rows, up_part, down_part, slots
    )
    at_own = (jnp.arange(experts)[None, :] == mine[:, None]).astype(f32)
    dots = jnp.einsum("egt,ef->gtf", dots, at_own, precision=PRECISE).reshape(-1, experts)
    dots_hi = dots.astype(bf)
    dots_lo = (dots - dots_hi.astype(f32)).astype(bf)
    g_sum, dots = sum_to_owners(
        [g_part.reshape(-1, MODEL_WIDTH), pad(jnp.concatenate([dots_hi, dots_lo], axis=1), 128)],
        [384, 128], 1, [f32, f32], None, [], (True, True), 3,
    )
    dots = dots[:, :experts] + dots[:, experts : 2 * experts]
    y_sum = fold(y_part).astype(f32)
    output = (hidden + valid * y_sum).astype(bf)

    grad_out = cot_low.astype(f32)
    grad_logit = (dots - probs * jnp.sum(dots, axis=1, keepdims=True)).astype(bf)
    grad_router = contract_rows(ffn_low, grad_logit)
    grad_ffn = g_sum + contract_cols(grad_logit, router_full)
    grad_hidden, grad_fgain = ffn_pull(grad_ffn)
    grad_hidden = grad_hidden + grad_out
    grad_mo = (grad_hidden * valid).astype(bf)
    grad_outw = contract_rows(mix_low, grad_mo).astype(bf).reshape(groups, -1, MODEL_WIDTH)
    own_out = fold(grad_outw).reshape(lines, -1, MODEL_WIDTH)
    own_out = lax.all_to_all(own_out, "seq", split_axis=0, concat_axis=0, tiled=True)
    own_out = jnp.sum(own_out.astype(f32), axis=0)
    grad_mix = contract_cols(grad_mo, out_full)
    mean_dot = jnp.sum(grad_mo.astype(f32) * mixer_out, axis=1, keepdims=True) / INNER
    grad_z, grad_in, stats, grad_bc, bc_stats, row_sums, col_sums, step_sums = mixer_back_call(
        where, mixer_in, (mixed, grad_mix, mix_gain[None], lanes(scale), lanes(mean_dot)), rows
    )
    grad_rates = jnp.dot(lower.T, row_sums[:, :HEADS] - col_sums[:HEADS].T, precision=PRECISE)
    grad_raw = (step_sums[:, :HEADS] - grad_rates * jnp.exp(a_log)) * jax.nn.sigmoid(before_step)
    grad_al = jnp.sum(grad_rates * rates, axis=0)
    grad_db = jnp.sum(grad_raw, axis=0)
    grad_mgain = stats[0]
    grad_skip = jnp.sum(stats[1].reshape(HEADS, HDIM), axis=1)
    grad_cb = jnp.concatenate([stats[2], bc_stats[0]])
    grad_cw = jnp.concatenate([stats[3 : 3 + KCONV], bc_stats[1 : 1 + KCONV]], axis=1)
    grad_proj = jnp.concatenate([grad_z, grad_in, grad_bc, grad_raw.astype(bf)], axis=1)
    spare = -PROJ % 128
    grad_inw = contract_rows(normed_low, pad(grad_proj, PROJ + spare)).astype(bf)
    grad_x, grad_ngain = norm_pull(contract_cols(grad_proj, in_full))
    input_grad = (grad_x + grad_hidden).astype(bf)
    grad_router = contract_rows(ffn_low, pad(grad_logit, 128)).astype(bf)

    pieces = (grad_ngain, grad_cw, grad_cb, grad_db, grad_al, grad_skip, grad_mgain, grad_fgain)
    flat = jnp.concatenate([p.reshape(-1) for p in pieces])
    flat = jnp.pad(flat, (0, -flat.shape[0] % 2048)).reshape(-1, 128)
    own_in, own_router, output, input_grad, flat = sum_to_owners(
        [grad_inw, grad_router], [768, 128], lines, [f32] * 2, flat,
        [a.reshape(tokens.shape) for a in (output, input_grad)], (False, False), 4,
    )
    flat = flat.reshape(-1)
    small = []
    start = 0
    for p in pieces:
        small.append(flat[start : start + p.size].reshape(p.shape))
        start += p.size
    along = lambda g, d: lax.psum_scatter(g.astype(bf), "seq", scatter_dimension=d, tiled=True)
    sup = grad_sup.astype(bf).reshape(groups, lines, -1, 2 * width).transpose(1, 0, 2, 3)
    sup = along(sup.reshape(MODEL_WIDTH, 2 * width), 0).reshape(groups, -1, 2 * width)
    sup = lax.all_to_all(sup, "dp", split_axis=0, concat_axis=0, tiled=True).astype(f32)
    sup = sup.reshape(groups, -1, 2, width).transpose(1, 2, 0, 3).reshape(-1, 2 * SFF)
    sdown = along(grad_sdown, 0).astype(f32)
    return (
        output, input_grad, small[0], own_in[:, :PROJ], small[1], small[2],
        small[3], small[4], small[5], small[6], own_out, small[7], own_router[:, :experts], sup, sdown,
        along(grad_eup, 1).astype(f32), along(grad_edown, 1).astype(f32),
    )


def solution(mesh):
    def program(*arrays):
        each = arrays[0].shape[0] == lax.axis_size("seq") == 4 and lax.axis_size("dp") == 8
        return (local_fast if each else local)(*arrays)

    return jax.shard_map(
        program,
        mesh=mesh,
        in_specs=(
            P("dp", "seq", None),
            P("dp"),
            P("dp", "seq", None),
            P("dp", "seq", None),
            P(),
            P(("dp", "seq"), None),
            P(),
            P(),
            P(),
            P(),
            P(),
            P(),
            P(("dp", "seq"), None),
            P(),
            P(("dp", "seq"), None),
            P(("dp", "seq"), None),
            P(("dp", "seq"), None),
            P("dp", None, None),
            P("dp", None, None),
        ),
        out_specs=(
            P("dp", "seq", None),
            P("dp", "seq", None),
            P(),
            P(("dp", "seq"), None),
            P(),
            P(),
            P(),
            P(),
            P(),
            P(),
            P(("dp", "seq"), None),
            P(),
            P(("dp", "seq"), None),
            P(("dp", "seq"), None),
            P(("dp", "seq"), None),
            P("dp", "seq", None),
            P("dp", "seq", None),
        ),
        check_vma=False,
    )
```

```python
from functools import partial

import jax
import jax.numpy as jnp
from jax import lax
from jax.experimental import pallas as pl
from jax.experimental.pallas import tpu as pltpu
from jax.sharding import PartitionSpec as P

MODEL_WIDTH = 1536
INNER = 3072
HEADS = 48
HDIM = 64
STATE = 128
KCONV = 4
EXPERT_HIDDEN = 512
SFF = 1024
MB = 4
CONV = 3328
PROJ = 6448


EPSILON = 1e-05
PRECISE = lax.Precision.HIGHEST
MESH = pl.DeviceIdType.MESH


def from_behind(x, axis, by):
    size = lax.axis_size(axis)
    pairs = [(i, i + by) for i in range(size) if 0 <= i + by < size]
    return lax.ppermute(x, axis, pairs)


def prefix(x, axis, join, neutral):
    place = lax.axis_index(axis)
    gathered = jax.tree.map(
        lambda a, kind: lax.all_gather(a.astype(kind), axis), x, (jnp.bfloat16, jnp.bfloat16)
    )
    state = jax.tree.map(lambda a, e: jnp.zeros_like(a) + jnp.asarray(e, a.dtype), x, neutral)

    def one(step, state):
        return join(
            state,
            jax.tree.map(
                lambda a, own: lax.dynamic_index_in_dim(a, step, 0, False).astype(own.dtype),
                gathered,
                x,
            ),
        )

    return lax.fori_loop(0, place, one, state)


def prefix_2(x, axis, join, neutral):
    count = lax.axis_size(axis)
    place = lax.axis_index(axis)
    ahead = count - 1 - place
    gathered = jax.tree.map(
        lambda a, kind: lax.all_gather(a.astype(kind), axis),
        x,
        jax.tree.map(lambda a: jnp.bfloat16 if a.dtype == jnp.float32 else a.dtype, x),
    )
    state = jax.tree.map(lambda a, e: jnp.zeros_like(a) + jnp.asarray(e, a.dtype), x, neutral)

    def one(step, state):
        source = count - 1 - step
        return join(
            state,
            jax.tree.map(
                lambda a, own: lax.dynamic_index_in_dim(a, source, 0, False).astype(own.dtype),
                gathered,
                x,
            ),
        )

    return lax.fori_loop(0, ahead, one, state)


def rms_norm(values, gain_vec):
    return (
        values * lax.rsqrt(jnp.mean(values * values, axis=-1, keepdims=True) + EPSILON) * gain_vec
    )


def swiglu(values, half_width):
    return jax.nn.silu(values[..., :half_width]) * values[..., half_width:]


def contract_rows(left_mat, right_mat):
    return lax.dot_general(
        left_mat, right_mat, (((0,), (0,)), ((), ())), preferred_element_type=jnp.float32
    )


def contract_cols(left_mat, right_mat):
    return lax.dot_general(
        left_mat, right_mat, (((1,), (1,)), ((), ())), preferred_element_type=jnp.float32
    )


def block_terms(head_in, b_rows, c_rows, step_sizes, a_log):
    log_rates = -step_sizes * jnp.exp(a_log)
    cumulative = jnp.cumsum(log_rates, axis=0)
    block_len = head_in.shape[0]
    lower_tri = jnp.arange(block_len)[:, None] >= jnp.arange(block_len)[None, :]
    spread = jnp.where(
        lower_tri[:, :, None], cumulative[:, None, :] - cumulative[None, :, :], -jnp.inf
    )
    scores = jnp.dot(c_rows, b_rows.T, precision=PRECISE)
    weights = jnp.exp(spread) * scores[:, :, None] * step_sizes[None, :, :]
    local_out = jnp.einsum("tih,ihp->thp", weights, head_in, precision=PRECISE)
    tail_weight = jnp.exp(cumulative[-1][None, :] - cumulative) * step_sizes
    local_state = jnp.einsum("ih,ihp,in->hpn", tail_weight, head_in, b_rows, precision=PRECISE)
    return (cumulative, local_out, local_state, jnp.exp(cumulative[-1]))


def carried_out(c_rows, cumulative, state_in):
    return (
        jnp.einsum("tn,hpn->thp", c_rows, state_in, precision=PRECISE)
        * jnp.exp(cumulative)[:, :, None]
    )


def mixer_front(valid_rows, projected, previous, conv_weight, conv_bias, dt_bias, a_log):
    row_count = projected.shape[0]
    conv_in = projected[:, INNER : INNER + CONV]
    padded = jnp.concatenate([previous, conv_in], axis=0)
    conv_sum = conv_bias + conv_weight[0] * padded[0:row_count]
    for tap_idx in range(1, KCONV):
        conv_sum = conv_sum + conv_weight[tap_idx] * padded[tap_idx : tap_idx + row_count]
    activated = jax.nn.silu(conv_sum) * valid_rows
    head_in = activated[:, :INNER].reshape(row_count, HEADS, HDIM)
    b_rows = activated[:, INNER : INNER + STATE]
    c_rows = activated[:, INNER + STATE :]
    step_sizes = jax.nn.softplus(projected[:, INNER + CONV :] + dt_bias)
    cumulative, local_out, local_state, decay_total = block_terms(
        head_in, b_rows, c_rows, step_sizes, a_log
    )
    return (projected[:, :INNER], head_in, c_rows, cumulative, local_out, local_state, decay_total)


def mixer_tail(gate_z, head_in, c_rows, cumulative, local_out, state_in, d_skip, mix_gain):
    mixed_out = local_out + carried_out(c_rows, cumulative, state_in) + d_skip[:, None] * head_in
    gated_out = mixed_out.reshape(head_in.shape[0], INNER) * jax.nn.silu(gate_z)
    return rms_norm(gated_out, mix_gain)


def link_states(earlier, latter):
    return (earlier[0] * latter[0], latter[1] + latter[0][:, None, None] * earlier[1])


def local(
    tokens,
    lengths,
    routes,
    cotangent,
    norm_gain,
    in_weight,
    conv_weight,
    conv_bias,
    dt_bias,
    a_log,
    d_skip,
    mix_gain,
    out_weight,
    ffn_gain,
    router_weight,
    shared_up,
    shared_down,
    expert_up,
    expert_down,
):
    row_count = tokens.shape[1]
    resident_experts = expert_up.shape[0]
    groups = lax.axis_size("dp")
    experts = resident_experts * groups
    top_count = routes.shape[2]
    capacity = row_count * top_count * 5 // (4 * experts)
    shards = (in_weight, out_weight, router_weight, shared_up, shared_down)
    kept_full = (
        lax.all_gather(shards[0], ("dp", "seq"), axis=0, tiled=True),
        lax.all_gather(shards[1], ("dp", "seq"), axis=0, tiled=True),
        lax.all_gather(shards[2], ("dp", "seq"), axis=0, tiled=True),
        lax.all_gather(shards[3], ("dp", "seq"), axis=0, tiled=True),
        lax.all_gather(shards[4], ("dp", "seq"), axis=0, tiled=True),
    )
    grad_inw = jnp.zeros((MODEL_WIDTH, PROJ), jnp.float32)
    grad_outw = jnp.zeros((INNER, MODEL_WIDTH), jnp.float32)
    grad_router = jnp.zeros((MODEL_WIDTH, experts), jnp.float32)
    grad_sup = jnp.zeros((MODEL_WIDTH, 2 * SFF), jnp.float32)
    grad_sdown = jnp.zeros((SFF, MODEL_WIDTH), jnp.float32)
    expert_upward_grad = jnp.zeros((resident_experts, MODEL_WIDTH, 2 * EXPERT_HIDDEN), jnp.float32)
    grad_edown = jnp.zeros((resident_experts, EXPERT_HIDDEN, MODEL_WIDTH), jnp.float32)
    grad_ngain = jnp.zeros_like(norm_gain)
    grad_cw = jnp.zeros_like(conv_weight)
    grad_cb = jnp.zeros_like(conv_bias)
    grad_db = jnp.zeros_like(dt_bias)
    grad_al = jnp.zeros_like(a_log)
    grad_skip = jnp.zeros_like(d_skip)
    grad_mgain = jnp.zeros_like(mix_gain)
    grad_fgain = jnp.zeros_like(ffn_gain)
    outputs = []
    input_grads = []
    for micro_idx in range(MB):
        in_full, out_full, router_full, up_full, down_full = kept_full
        x_rows = tokens[micro_idx].astype(jnp.float32)
        position = lax.axis_index("seq") * row_count + jnp.arange(row_count)
        valid_rows = (position < lengths[micro_idx]).astype(jnp.float32)[:, None]
        normed, norm_pull = jax.vjp(rms_norm, x_rows, norm_gain)
        normed_low = normed.astype(jnp.bfloat16)
        projected = jnp.dot(normed_low, in_full, preferred_element_type=jnp.float32).astype(
            jnp.bfloat16
        )
        previous = from_behind(projected[row_count - (KCONV - 1) :, INNER : INNER + CONV], "seq", 1)
        front_out, front_pull = jax.vjp(
            partial(mixer_front, valid_rows),
            projected.astype(jnp.float32),
            previous.astype(jnp.float32),
            conv_weight,
            conv_bias,
            dt_bias,
            a_log,
        )
        gate_z, head_in, c_rows, cumulative, local_out, local_state, decay_total = front_out
        identity = (jnp.ones_like(decay_total), jnp.zeros_like(local_state))
        _, state_in = prefix((decay_total, local_state), "seq", link_states, identity)
        normed_mix, tail_pull = jax.vjp(
            mixer_tail, gate_z, head_in, c_rows, cumulative, local_out, state_in, d_skip, mix_gain
        )
        mix_low = normed_mix.astype(jnp.bfloat16)
        mixer_out = jnp.dot(mix_low, out_full, preferred_element_type=jnp.float32)
        hidden = x_rows + mixer_out * valid_rows
        normed_ffn, ffn_pull = jax.vjp(rms_norm, hidden, ffn_gain)
        ffn_low = normed_ffn.astype(jnp.bfloat16)
        logits = jnp.dot(ffn_low, router_full, preferred_element_type=jnp.float32)
        route_row = routes[micro_idx]
        picked = jnp.take_along_axis(logits, route_row, axis=1)
        gate_probs = jax.nn.softmax(picked, axis=-1)
        shared_gu = jnp.dot(ffn_low, up_full, preferred_element_type=jnp.float32)
        shared_act, shared_pull = jax.vjp(partial(swiglu, half_width=SFF), shared_gu)
        shared_h = shared_act.astype(jnp.bfloat16)
        shared_y = jnp.dot(shared_h, down_full, preferred_element_type=jnp.float32)
        flat_route = route_row.reshape(-1)
        member = (flat_route[:, None] == jnp.arange(experts)[None, :]).astype(jnp.int32)
        slot_pos = jnp.sum((jnp.cumsum(member, axis=0) - member) * member, axis=1)
        target = flat_route * capacity + slot_pos
        source = (
            jnp.zeros((experts * capacity,), jnp.int32)
            .at[target]
            .set(jnp.arange(row_count * top_count, dtype=jnp.int32))
        )
        filled = jnp.zeros((experts * capacity, 1), jnp.bfloat16).at[target].set(jnp.bfloat16(1))
        outgoing = (jnp.take(ffn_low, source // top_count, axis=0) * filled).reshape(
            groups, resident_experts, capacity, MODEL_WIDTH
        )
        received_rows = lax.all_to_all(outgoing, "dp", split_axis=0, concat_axis=2, tiled=True)[0]
        expert_gu = jnp.einsum(
            "erd,edf->erf", received_rows, expert_up, preferred_element_type=jnp.float32
        )
        expert_act, expert_pull = jax.vjp(partial(swiglu, half_width=EXPERT_HIDDEN), expert_gu)
        expert_h = expert_act.astype(jnp.bfloat16)
        expert_y = jnp.einsum(
            "erf,efd->erd", expert_h, expert_down, preferred_element_type=jnp.float32
        ).astype(jnp.bfloat16)
        returned = lax.all_to_all(expert_y[None], "dp", split_axis=2, concat_axis=0, tiled=True)
        per_choice = (
            jnp.take(returned.reshape(experts * capacity, MODEL_WIDTH), target, axis=0)
            .reshape(row_count, top_count, MODEL_WIDTH)
            .astype(jnp.float32)
        )
        routed = jnp.einsum("lk,lkd->ld", gate_probs, per_choice, precision=PRECISE)
        outputs.append((hidden + valid_rows * (shared_y + routed)).astype(jnp.bfloat16))
        in_back, out_back, router_back, up_back, down_back = kept_full
        grad_out = cotangent[micro_idx].astype(jnp.float32)
        branch = valid_rows * grad_out
        shared_g = branch.astype(jnp.bfloat16)
        grad_sdown = grad_sdown + contract_rows(shared_h, shared_g)
        grad_sgu = shared_pull(contract_cols(shared_g, down_back))[0].astype(jnp.bfloat16)
        grad_sup = grad_sup + contract_rows(ffn_low, grad_sgu)
        grad_ffn = contract_cols(grad_sgu, up_back)
        grad_choice = (gate_probs[:, :, None] * branch[:, None, :]).astype(jnp.bfloat16)
        grad_gate = jnp.sum(branch[:, None, :] * per_choice, axis=-1)
        grad_pick = gate_probs * (
            grad_gate - jnp.sum(gate_probs * grad_gate, axis=-1, keepdims=True)
        )
        onehot = (route_row[:, :, None] == jnp.arange(experts)[None, None, :]).astype(jnp.float32)
        grad_logit = jnp.einsum("lk,lke->le", grad_pick, onehot, precision=PRECISE).astype(
            jnp.bfloat16
        )
        grad_router = grad_router + contract_rows(ffn_low, grad_logit)
        grad_ffn = grad_ffn + contract_cols(grad_logit, router_back)
        back_out = (
            jnp.take(grad_choice.reshape(row_count * top_count, MODEL_WIDTH), source, axis=0)
            * filled
        ).reshape(groups, resident_experts, capacity, MODEL_WIDTH)
        grad_arrived = lax.all_to_all(back_out, "dp", split_axis=0, concat_axis=2, tiled=True)[0]
        step_edown = jnp.einsum(
            "erf,erd->efd", expert_h, grad_arrived, preferred_element_type=jnp.float32
        )
        grad_eh = jnp.einsum(
            "erd,efd->erf", grad_arrived, expert_down, preferred_element_type=jnp.float32
        )
        expert_gate_up_grad = expert_pull(grad_eh)[0].astype(jnp.bfloat16)
        expert_upward_step = jnp.einsum(
            "tbw,tbj->twj", received_rows, expert_gate_up_grad, preferred_element_type=jnp.float32
        )
        grad_ein = jnp.einsum(
            "erf,edf->erd", expert_gate_up_grad, expert_up, preferred_element_type=jnp.float32
        ).astype(jnp.bfloat16)
        expert_upward_grad = expert_upward_grad + expert_upward_step
        grad_edown = grad_edown + step_edown
        came_back = lax.all_to_all(grad_ein[None], "dp", split_axis=2, concat_axis=0, tiled=True)
        grad_ffn = grad_ffn + jnp.sum(
            jnp.take(came_back.reshape(experts * capacity, MODEL_WIDTH), target, axis=0)
            .reshape(row_count, top_count, MODEL_WIDTH)
            .astype(jnp.float32),
            axis=1,
        )
        grad_hidden, step_fgain = ffn_pull(grad_ffn)
        grad_fgain = grad_fgain + step_fgain
        grad_hidden = grad_hidden + grad_out
        grad_mix_out = (grad_hidden * valid_rows).astype(jnp.bfloat16)
        grad_outw = grad_outw + contract_rows(mix_low, grad_mix_out)
        grad_mix = contract_cols(grad_mix_out, out_back)
        grad_z, grad_head, grad_c, grad_cum, grad_local, grad_state, step_skip, step_mgain = (
            tail_pull(grad_mix)
        )
        grad_skip = grad_skip + step_skip
        grad_mgain = grad_mgain + step_mgain
        _, grad_carry = prefix_2((decay_total, grad_state), "seq", link_states, identity)
        grad_decay = jnp.sum(grad_carry * state_in, axis=(1, 2))
        grad_proj, grad_prev, step_cw, step_cb, step_db, step_al = front_pull(
            (grad_z, grad_head, grad_c, grad_cum, grad_local, grad_carry, grad_decay)
        )
        grad_cw = grad_cw + step_cw
        grad_cb = grad_cb + step_cb
        grad_db = grad_db + step_db
        grad_al = grad_al + step_al
        from_next = from_behind(grad_prev.astype(jnp.bfloat16), "seq", -1).astype(grad_prev.dtype)
        grad_proj = (
            grad_proj.at[row_count - (KCONV - 1) :, INNER : INNER + CONV]
            .add(from_next)
            .astype(jnp.bfloat16)
        )
        grad_inw = grad_inw + contract_rows(normed_low, grad_proj)
        grad_normed = contract_cols(grad_proj, in_back)
        grad_x, step_ngain = norm_pull(grad_normed)
        grad_ngain = grad_ngain + step_ngain
        input_grads.append((grad_x + grad_hidden).astype(jnp.bfloat16))
    weight_grads = (
        lax.psum_scatter(grad_inw, ("dp", "seq"), scatter_dimension=0, tiled=True),
        lax.psum_scatter(grad_outw, ("dp", "seq"), scatter_dimension=0, tiled=True),
        lax.psum_scatter(grad_router, ("dp", "seq"), scatter_dimension=0, tiled=True),
        lax.psum_scatter(grad_sup, ("dp", "seq"), scatter_dimension=0, tiled=True),
        lax.psum_scatter(grad_sdown, ("dp", "seq"), scatter_dimension=0, tiled=True),
    )
    small_sums = lax.psum(
        (grad_ngain, grad_cw, grad_cb, grad_db, grad_al, grad_skip, grad_mgain, grad_fgain),
        ("dp", "seq"),
    )
    expert_sums = (
        lax.psum_scatter(
            expert_upward_grad.astype(jnp.bfloat16), "seq", scatter_dimension=1, tiled=True
        ).astype(jnp.float32),
        lax.psum_scatter(
            grad_edown.astype(jnp.bfloat16), "seq", scatter_dimension=1, tiled=True
        ).astype(jnp.float32),
    )
    return (
        jnp.stack(outputs),
        jnp.stack(input_grads),
        small_sums[0],
        weight_grads[0],
        small_sums[1],
        small_sums[2],
        small_sums[3],
        small_sums[4],
        small_sums[5],
        small_sums[6],
        weight_grads[1],
        small_sums[7],
        weight_grads[2],
        weight_grads[3],
        weight_grads[4],
        expert_sums[0],
        expert_sums[1],
    )


def at_neighbours():
    d = lax.axis_index("dp")
    core, x, y = d % 2, (d // 2) % 2, d // 4
    return d, core, x, y, d + 1 - 2 * core, d + 2 - 4 * x, d + 4 - 8 * y


def meet(devices):
    barrier = pltpu.get_barrier_semaphore()
    for there in devices:
        pl.semaphore_signal(barrier, inc=1, device_id=there, device_id_type=MESH)
    pl.semaphore_wait(barrier, len(devices))


def send(source, target, send_sem, recv_sem, there):
    copy = pltpu.make_async_remote_copy(
        src_ref=source, dst_ref=target, send_sem=send_sem, recv_sem=recv_sem,
        device_id=there, device_id_type=MESH,
    )
    copy.start()
    return copy


def add_into(target, source, high):
    step = 16
    for s in (64, 48, 32):
        if high % s == 0:
            step = s
            break

    @pl.loop(0, high // step)
    def _(i):
        rows = pl.ds(pl.multiple_of(i * step, step), step)
        target[rows, :] = target[rows, :] + source[rows, :]


def swap_start(swaps, landed, line, lines, local_sem, send_sem, recv_sem):
    copies = []
    for n, (a, b) in enumerate(zip(swaps, landed)):
        keep = pltpu.make_async_copy(a.at[line], b.at[line], local_sem.at[n])
        keep.start()
        away = [
            send(a.at[o], b.at[line], send_sem.at[n, k], recv_sem.at[n, k], {"seq": o})
            for k, o in enumerate(lax.rem(line + k, lines) for k in range(1, lines))
        ]
        copies.append((keep, away))
    return copies


def swap_end(copies):
    for keep, away in copies:
        for copy in away:
            copy.wait_recv()
    for keep, away in copies:
        for copy in away:
            copy.wait_send()
        keep.wait()


def swap_sems(count, lines):
    dma = pltpu.SemaphoreType.DMA
    return [dma((count,)), dma((count, lines - 1)), dma((count, lines - 1))]


def sum_body(items, arrays, lines, tiny, moved, relative, *refs):
    count = len(items)
    grads, refs = refs[:arrays], refs[arrays:]
    swaps, refs = refs[:moved], refs[moved:]
    if tiny:
        small_in, refs = refs[0], refs[1:]
    outs, refs = refs[:arrays], refs[arrays:]
    landed, refs = refs[:moved], refs[moved:]
    if tiny:
        small_out, refs = refs[0], refs[1:]
    own, refs = refs[:count], refs[count:]
    got, refs = refs[:count], refs[count:]
    from_x, refs = refs[:count], refs[count:]
    from_y, refs = refs[:count], refs[count:]
    last_x, refs = refs[:count], refs[count:]
    last_y, refs = refs[:count], refs[count:]
    if lines > 1:
        from_z, refs = refs[:count], refs[count:]
    (load_sem, send_sem, recv_sem), refs = refs[:3], refs[3:]
    if moved:
        swap_sem, refs = refs[:3], refs[3:]
    if tiny:
        half, t_core, t_x, t_y, t_z, t_back, t_send, t_recv = refs
    d, core, x, y, at_core, at_x, at_y = at_neighbours()
    bits = [(0, 0, 0) if own else (core, x, y) for own in relative]
    own_core = core
    line = lax.axis_index("seq")
    others = [lax.rem(line + k, lines) for k in range(1, lines)]
    meet([{"dp": at_core}, {"dp": at_x}, {"dp": at_y}] + [{"seq": o} for o in others])
    sent = [[] for _ in items]
    stage = [None] * count
    cross = [None] * count
    close = [None] * count
    along = [None] * count
    loads = [None] * count

    def begin(t):
        a, c0, wide, high = items[t]
        core, x, y = bits[a]
        cols = pl.ds(c0, wide)
        loads[t] = pltpu.make_async_copy(grads[a].at[:, :, core, :, cols], own[t], load_sem.at[t])
        loads[t].start()
        stage[t] = send(
            grads[a].at[:, :, 1 - core, :, cols], got[t], send_sem.at[t, 0], recv_sem.at[t, 0], {"dp": at_core}
        )

    def fold(t):
        a, c0, wide, high = items[t]
        core, x, y = bits[a]
        loads[t].wait()
        stage[t].wait_recv()
        for i in range(2):
            for j in range(2):
                add_into(got[t].at[i, j], own[t].at[i, j], high)
        top, low = pl.ds(0, high // 2), pl.ds(high // 2, high // 2)
        cross[t] = (
            send(got[t].at[:, 1 - x, top, :], from_x[t], send_sem.at[t, 1], recv_sem.at[t, 1], {"dp": at_x}),
            send(got[t].at[1 - y, :, low, :], from_y[t], send_sem.at[t, 2], recv_sem.at[t, 2], {"dp": at_y}),
        )

    def turn(t):
        a, c0, wide, high = items[t]
        core, x, y = bits[a]
        top, low = pl.ds(0, high // 2), pl.ds(high // 2, high // 2)
        cross[t][0].wait_recv()
        for i in range(2):
            add_into(got[t].at[i, x, top, :], from_x[t].at[i], high // 2)
        close_y = send(got[t].at[1 - y, x, top, :], last_y[t], send_sem.at[t, 3], recv_sem.at[t, 3], {"dp": at_y})
        cross[t][1].wait_recv()
        for j in range(2):
            add_into(got[t].at[y, j, low, :], from_y[t].at[j], high // 2)
        close_x = send(got[t].at[y, 1 - x, low, :], last_x[t], send_sem.at[t, 4], recv_sem.at[t, 4], {"dp": at_x})
        close[t] = (close_y, close_x)

    def settle(t):
        a, c0, wide, high = items[t]
        core, x, y = bits[a]
        top, low = pl.ds(0, high // 2), pl.ds(high // 2, high // 2)
        cols = pl.ds(c0, wide)
        close[t][0].wait_recv()
        add_into(got[t].at[y, x, top, :], last_y[t], high // 2)
        close[t][1].wait_recv()
        add_into(got[t].at[y, x, low, :], last_x[t], high // 2)
        if lines == 1:
            outs[a][:, cols] = got[t][y, x].astype(outs[a].dtype)
            return
        each = high // lines
        along[t] = [
            send(
                got[t].at[y, x, pl.ds(pl.multiple_of(o * each, 16), each), :], from_z[t].at[k],
                send_sem.at[t, 5 + k], recv_sem.at[t, 5 + k], {"seq": o},
            )
            for k, o in enumerate(others)
        ]

    def finish(t):
        a, c0, wide, high = items[t]
        core, x, y = bits[a]
        each = high // lines
        total = got[t][y, x, pl.ds(pl.multiple_of(line * each, 16), each), :].astype(jnp.float32)
        for k in range(lines - 1):
            along[t][k].wait_recv()
            total = total + from_z[t][k].astype(jnp.float32)
        outs[a][:, pl.ds(c0, wide)] = total

    little = []

    def tiny_step(n):
        rows = half.shape[1]
        if n == 0:
            there = pl.ds(pl.multiple_of((1 - own_core) * rows, 8), rows)
            little.append(send(small_in.at[there, :], t_core, t_send.at[0], t_recv.at[0], {"dp": at_core}))
        elif n == 1:
            little[0].wait_recv()
            here = pl.ds(pl.multiple_of(own_core * rows, 8), rows)
            half[0] = small_in[here, :] + t_core[...]
            little.append(send(half.at[0], t_x, t_send.at[1], t_recv.at[1], {"dp": at_x}))
        elif n == 2:
            little[1].wait_recv()
            half[1] = half[0] + t_x[...]
            little.append(send(half.at[1], t_y, t_send.at[2], t_recv.at[2], {"dp": at_y}))
        elif n == 3:
            little[2].wait_recv()
            half[2] = half[1] + t_y[...]
            t_z[line] = half[2]
            for k, o in enumerate(others):
                little.append(send(half.at[2], t_z.at[line], t_send.at[3 + k], t_recv.at[3 + k], {"seq": o}))
        elif n == 4:
            for k in range(lines - 1):
                little[3 + k].wait_recv()
            total = t_z[0]
            for k in range(1, lines):
                total = total + t_z[k]
            half[3] = total
            small_out[pl.ds(pl.multiple_of(own_core * rows, 8), rows), :] = total
            little.append(send(half.at[3], t_back, t_send.at[7], t_recv.at[7], {"dp": at_core}))
        elif n == 5:
            little[-1].wait_recv()
            small_out[pl.ds(pl.multiple_of((1 - own_core) * rows, 8), rows), :] = t_back[...]
            for copy in little:
                copy.wait_send()

    begin(0)
    if tiny:
        tiny_step(0)
    moves = swap_start(swaps, landed, line, lines, *swap_sem) if moved else ()
    for t in range(max(count + 3, 5 if tiny else 0)):
        if t + 1 < count:
            begin(t + 1)
        if t < count:
            fold(t)
        if 0 <= t - 1 < count:
            turn(t - 1)
        if 0 <= t - 2 < count:
            settle(t - 2)
        if lines > 1 and 0 <= t - 3 < count:
            finish(t - 3)
        if tiny and t < 5:
            tiny_step(t + 1)
    swap_end(moves)
    for t in range(count):
        stage[t].wait_send()
        for copy in cross[t] + close[t] + tuple(along[t] or ()):
            copy.wait_send()


def sum_to_owners(grads, widths, lines, kinds, small, swaps, relative, identity):
    items, views = [], []
    for a, (g, wide) in enumerate(zip(grads, widths)):
        high, cols = g.shape[0] // 8, g.shape[1]
        views.append(g.reshape(2, 2, 2, high, cols))
        start = 0
        while start < cols:
            w = min(wide, cols - start)
            items.append((a, start, w, high))
            start += w
    tiny = small is not None
    bf = jnp.bfloat16
    scratch = [pltpu.VMEM((2, 2, h, w), bf) for _, _, w, h in items]
    scratch += [pltpu.VMEM((2, 2, h, w), bf) for _, _, w, h in items]
    scratch += [pltpu.VMEM((2, h // 2, w), bf) for _, _, w, h in items] * 2
    scratch += [pltpu.VMEM((h // 2, w), bf) for _, _, w, h in items] * 2
    if lines > 1:
        scratch += [pltpu.VMEM((lines - 1, h // lines, w), bf) for _, _, w, h in items]
    ways = 4 + lines
    scratch += [
        pltpu.SemaphoreType.DMA((len(items),)),
        pltpu.SemaphoreType.DMA((len(items), ways)),
        pltpu.SemaphoreType.DMA((len(items), ways)),
    ]
    out_shape = [
        jax.ShapeDtypeStruct((g.shape[0] // 8 // lines, g.shape[1]), kind) for g, kind in zip(grads, kinds)
    ]
    ins = list(views)
    in_specs = [pl.BlockSpec(memory_space=pl.ANY)] * len(views)
    out_specs = [pl.BlockSpec(memory_space=pltpu.VMEM)] * len(views)
    if swaps:
        scratch += swap_sems(len(swaps), lines)
        ins += swaps
        in_specs += [pl.BlockSpec(memory_space=pl.ANY)] * len(swaps)
        out_specs += [pl.BlockSpec(memory_space=pl.ANY)] * len(swaps)
        out_shape += [jax.ShapeDtypeStruct(a.shape, a.dtype) for a in swaps]
    if tiny:
        rows = small.shape[0] // 2
        part = lambda *lead: pltpu.VMEM(lead + (rows, 128), jnp.float32)
        scratch += [part(4), part(), part(), part(), part(lines), part()]
        scratch += [pltpu.SemaphoreType.DMA((8,)), pltpu.SemaphoreType.DMA((8,))]
        out_shape.append(jax.ShapeDtypeStruct(small.shape, jnp.float32))
        ins.append(small)
        in_specs.append(pl.BlockSpec(memory_space=pltpu.VMEM))
        out_specs.append(pl.BlockSpec(memory_space=pltpu.VMEM))
    return pl.pallas_call(
        partial(sum_body, items, len(views), lines, tiny, len(swaps), relative),
        out_shape=out_shape,
        in_specs=in_specs,
        out_specs=out_specs,
        scratch_shapes=scratch,
        name="sum_to_owners_%d" % identity,
        compiler_params=pltpu.CompilerParams(
            collective_id=identity, has_side_effects=True, vmem_limit_bytes=60 << 20
        ),
    )(*ins)


def gather_body(pieces, arrays, flat, lines, ahead, moved, relative, *refs):
    mine, refs = refs[:arrays], refs[arrays:]
    swaps, refs = refs[:moved], refs[moved:]
    full, refs = refs[:arrays], refs[arrays:]
    landed, refs = refs[:moved], refs[moved:]
    keep_sem, send_sem, recv_sem, z_send, z_recv = refs[:5]
    swap_sem = refs[5:]
    d, core, x, y, at_core, at_x, at_y = at_neighbours()
    at_far = at_x + at_y - d
    line = lax.rem(lax.axis_index("seq"), lines)
    hops = [line]
    if lines > 1:
        upper = line // 2
        hops += [line + 1 - 2 * (line % 2), 2 - upper, 3 - 3 * upper]
    meet([{"dp": at_core}, {"dp": at_x}, {"dp": at_y}] + [{"seq": o} for o in hops[1:]])
    blocks = dict(own=d, x=at_x, y=at_y, far=at_far)
    lands = dict(x=d, y=d, core=d, x_y=at_x, x_core=at_x, y_x=at_y, y_core=at_y, far_core=at_far)
    if relative:
        blocks = dict(own=0, x=2, y=4, far=6)
        lands = dict(x=2, y=4, core=1, x_y=6, x_core=3, y_x=6, y_core=5, far_core=7)
    mains = [q for q, piece in enumerate(pieces) if piece[0] < arrays - flat]
    sides = [q for q, piece in enumerate(pieces) if piece[0] >= arrays - flat]
    home = lambda a: blocks["own"] if a < arrays - flat else 0
    keep = []
    for a in range(arrays):
        keep.append(pltpu.make_async_copy(mine[a], full[a].at[home(a), line], keep_sem.at[a]))
        keep[a].start()
    order = [(j, q) for j in range(lines) for q in mains]
    total = len(order)
    out = [[None] * 7 for _ in order]

    def place(j, q, block):
        a, r0, high = pieces[q]
        return full[a].at[block, hops[j], pl.ds(r0, high), :]

    def own_piece(q):
        a, r0, high = pieces[q]
        return mine[a].at[pl.ds(r0, high), :]

    def hop(j, q, sem, to):
        a = pieces[q][0]
        return pltpu.make_async_remote_copy(
            src_ref=own_piece(q) if j == 0 else place(j, q, home(a)),
            dst_ref=place(j, q, home(a)),
            send_sem=z_send.at[q, sem], recv_sem=z_recv.at[q, hops[j]],
            device_id={"seq": to}, device_id_type=MESH,
        )

    def onward(j, q, act):
        o = hops[j]

        @pl.when((o <= line) & (line < lines - 1))
        def _():
            act(hop(j, q, 2 * j, jnp.minimum(line + 1, lines - 1)))

        @pl.when((o >= line) & (line > 0))
        def _():
            act(hop(j, q, 2 * j + 1, jnp.maximum(line - 1, 0)))

    def relay(j, q):
        hop(j, q, 2 * j, line).wait_recv()
        onward(j, q, lambda copy: copy.start())

    def pass_on(i, n, block, lands_at, there):
        j, q = order[i]
        source = own_piece(q) if block is None else place(j, q, block)
        out[i][n] = send(
            source, place(j, q, lands[lands_at]), send_sem.at[i, n], recv_sem.at[i, n], {"dp": there}
        )

    def first(i):
        block = None if order[i][0] == 0 else blocks["own"]
        pass_on(i, 0, block, "x", at_x)
        pass_on(i, 1, block, "y", at_y)
        pass_on(i, 2, block, "core", at_core)

    def second(i):
        out[i][0].wait_recv()
        if i % 2 == 0:
            pass_on(i, 5, blocks["x"], "x_y", at_y)
        pass_on(i, 3, blocks["x"], "x_core", at_core)
        out[i][1].wait_recv()
        if i % 2 == 1:
            pass_on(i, 5, blocks["y"], "y_x", at_x)
        pass_on(i, 4, blocks["y"], "y_core", at_core)

    def third(i):
        out[i][5].wait_recv()
        pass_on(i, 6, blocks["far"], "far_core", at_core)

    lead = ahead + 2
    if lines > 1:
        for q in mains:
            onward(0, q, lambda copy: copy.start())
    for i in range(min(ahead, total)):
        first(i)
    moves = swap_start(swaps, landed, line, lines, *swap_sem) if moved else ()
    for i in range(total):
        if i + lead < total and order[i + lead][0] > 0:
            relay(*order[i + lead])
        if i % len(mains) == 1:
            j = i // len(mains)
            for q in sides:
                if j == 0:
                    onward(0, q, lambda copy: copy.start())
                else:
                    relay(j, q)
        if i + ahead < total:
            first(i + ahead)
        second(i)
        if i:
            third(i - 1)
    third(total - 1)
    for i in range(total):
        for n in (2, 3, 4, 6):
            out[i][n].wait_recv()
        for copy in out[i]:
            copy.wait_send()
    swap_end(moves)
    if lines > 1:
        for q in range(len(pieces)):
            for j in range(lines):
                onward(j, q, lambda copy: copy.wait_send())
    for copy in keep:
        copy.wait()


def gather_rows(arrays, chunks, flat, lines, ahead, swaps, relative, identity):
    pieces = []
    count = len(arrays) + len(flat)
    for a, (w, chunk) in enumerate(zip(list(arrays) + list(flat), chunks)):
        for r0 in range(0, w.shape[0], chunk):
            pieces.append((a, r0, chunk))
    total = lines * len([p for p in pieces if p[0] < len(arrays)])
    anywhere = pl.BlockSpec(memory_space=pl.ANY)
    return pl.pallas_call(
        partial(gather_body, pieces, count, len(flat), lines, ahead, len(swaps), relative),
        out_shape=[jax.ShapeDtypeStruct((8, lines) + w.shape, w.dtype) for w in arrays]
        + [jax.ShapeDtypeStruct((1, lines) + w.shape, w.dtype) for w in flat]
        + [jax.ShapeDtypeStruct(a.shape, a.dtype) for a in swaps],
        in_specs=[anywhere] * (count + len(swaps)),
        out_specs=[anywhere] * (count + len(swaps)),
        scratch_shapes=[
            pltpu.SemaphoreType.DMA((count,)),
            pltpu.SemaphoreType.DMA((total, 7)),
            pltpu.SemaphoreType.DMA((total, 7)),
            pltpu.SemaphoreType.DMA((len(pieces), 2 * lines)),
            pltpu.SemaphoreType.DMA((len(pieces), lines)),
        ]
        + (swap_sems(len(swaps), lines) if swaps else []),
        name="gather_rows_%d" % identity,
        compiler_params=pltpu.CompilerParams(collective_id=identity, has_side_effects=True),
    )(*arrays, *flat, *swaps)


def sigmoid(v):
    return 1.0 / (1.0 + jnp.exp(-v))


def shifted(v, by):
    if by == 0:
        return v
    rows = v.shape[0]
    at = lax.broadcasted_iota(jnp.int32, v.shape, 0)
    keep = at >= by if by > 0 else at < rows + by
    return jnp.where(keep, pltpu.roll(v, by % rows, 0), 0.0)


def conv_sums(v, taps, bias):
    total = bias
    for k in range(KCONV):
        total = total + taps[k : k + 1, :] * shifted(v, KCONV - 1 - k)
    return total


def conv_back(v, taps, bias, valid, grad):
    conv_sum = conv_sums(v, taps, bias)
    s = sigmoid(conv_sum)
    grad = grad * valid * (s * (1.0 + conv_sum * (1.0 - s)))
    total = taps[KCONV - 1 : KCONV, :] * grad
    for k in range(KCONV - 1):
        total = total + taps[k : k + 1, :] * shifted(grad, k - (KCONV - 1))
    sums = [jnp.sum(grad, axis=0, keepdims=True)]
    for k in range(KCONV):
        sums.append(jnp.sum(grad * shifted(v, KCONV - 1 - k), axis=0, keepdims=True))
    return total, sums


def head_columns(ref, pair):
    v = pltpu.roll(ref[...], lax.rem(128 - 2 * pair, 128), 1)
    return v[:, 0:1], v[:, 1:2]


def over_lanes(columns):
    rows = columns[0].shape[0]
    lane = lax.broadcasted_iota(jnp.int32, (rows, 128), 1)
    return jnp.where(lane < HDIM, columns[0], columns[1])


def lower_left(rows):
    return lax.broadcasted_iota(jnp.int32, (rows, rows), 0) >= lax.broadcasted_iota(
        jnp.int32, (rows, rows), 1
    )


def product(a, b, over_a=1, over_b=0):
    return lax.dot_general(
        a, b, (((over_a,), (over_b,)), ((), ())), preferred_element_type=jnp.float32
    )


def bc_scores(bc_ref, bc_taps, bc_bias, valid, scores, bc_keep):
    conv_sum = conv_sums(bc_ref[...].astype(jnp.float32), bc_taps[...], bc_bias[...])
    bc = conv_sum * sigmoid(conv_sum) * valid[:, :1]
    bc_keep[...] = bc.astype(jnp.bfloat16)
    rows = scores.shape[0]
    g = product(bc_keep[:, STATE:], bc_keep[:, :STATE], 1, 1)
    scores[...] = jnp.where(lower_left(rows), g, 0.0)


def front_body(
    z_ref, x_ref, bc_ref, taps, bias, bc_taps, bc_bias, valid, step, cum, cum_rows, skip,
    mixed_ref, gated_ref, squares, scores, bc_keep,
):
    f32, bf = jnp.float32, jnp.bfloat16

    @pl.when(pl.program_id(0) == 0)
    def _():
        bc_scores(bc_ref, bc_taps, bc_bias, valid, scores, bc_keep)
        squares[...] = jnp.zeros_like(squares)

    rows = x_ref.shape[0]
    half = rows // 2
    conv_sum = conv_sums(x_ref[...].astype(f32), taps[...], bias[...])
    x = conv_sum * sigmoid(conv_sum) * valid[...]
    xs = (x * over_lanes(head_columns(step, pl.program_id(0)))).astype(bf)
    sums = head_columns(cum, pl.program_id(0))
    lane = lax.broadcasted_iota(jnp.int32, (half, 128), 1)
    for r in range(2):
        at, wide = pl.ds(r * half, half), (r + 1) * half
        parts = []
        for h in range(2):
            gap = sums[h][r * half : (r + 1) * half, :] - cum_rows[0, h : h + 1, :wide]
            m = (jnp.exp(jnp.minimum(gap, 0.0)) * scores[at, :wide]).astype(bf)
            parts.append(product(m, xs[:wide, :]))
        mixed = jnp.where(lane < HDIM, parts[0], parts[1]) + skip[...] * x[r * half : (r + 1) * half, :]
        z = z_ref[at, :].astype(f32)
        gated = mixed * (z * sigmoid(z))
        mixed_ref[at, :] = mixed
        gated_ref[at, :] = gated
        squares[at, :] += gated * gated


def back_body(
    z_ref, x_ref, bc_ref, taps, bias, bc_taps, bc_bias, valid, step, cum, cum_rows, skip,
    mixed_ref, grad_ref, gain, scale, mean_dot,
    grad_z, grad_x, stats, grad_bc, bc_stats, row_sums, col_sums, step_sums,
    scores, bc_keep, grad_scores, grad_xs,
):
    f32, bf = jnp.float32, jnp.bfloat16
    pair = pl.program_id(0)

    @pl.when(pair == 0)
    def _():
        bc_scores(bc_ref, bc_taps, bc_bias, valid, scores, bc_keep)
        grad_scores[...] = jnp.zeros_like(grad_scores)
        row_sums[...] = jnp.zeros_like(row_sums)
        col_sums[...] = jnp.zeros_like(col_sums)
        step_sums[...] = jnp.zeros_like(step_sums)

    rows = x_ref.shape[0]
    half = rows // 2
    v = x_ref[...].astype(f32)
    conv_sum = conv_sums(v, taps[...], bias[...])
    x = conv_sum * sigmoid(conv_sum) * valid[...]
    steps = over_lanes(head_columns(step, pair))
    sums = head_columns(cum, pair)
    xs = (x * steps).astype(bf)
    z = z_ref[...].astype(f32)
    s = sigmoid(z)
    silu = z * s
    mixed = mixed_ref[...]
    normal = mixed * silu * scale[...]
    grad = grad_ref[...]
    grad_gated = scale[...] * (grad * gain[...] - normal * mean_dot[...])
    grad_mixed = grad_gated * silu
    grad_z[...] = (grad_gated * mixed * (s * (1.0 + z * (1.0 - s)))).astype(bf)
    lane = lax.broadcasted_iota(jnp.int32, (rows, 128), 1)
    dy = [
        jnp.where(lane < HDIM, grad_mixed, 0.0).astype(bf),
        jnp.where(lane < HDIM, 0.0, grad_mixed).astype(bf),
    ]
    for r in range(2):
        at, wide = pl.ds(r * half, half), (r + 1) * half
        total = None
        for h in range(2):
            head = 2 * pair + h
            g = scores[at, :wide]
            gap = sums[h][r * half : (r + 1) * half, :] - cum_rows[0, h : h + 1, :wide]
            e = jnp.exp(jnp.minimum(gap, 0.0))
            m = (e * g).astype(bf)
            dy_rows = dy[h][r * half : (r + 1) * half, :]
            slope = product(dy_rows, xs[:wide, :], 1, 1) * e
            grad_scores[at, :wide] += slope
            both = (slope * g).astype(bf)
            back = product(m, dy_rows, 0, 0)
            total = back if total is None else total + back
            to_lane = (lax.broadcasted_iota(jnp.int32, (wide, 128), 1) == head).astype(bf)
            row_sums[at, :] += product(both, to_lane)
            to_row = (lax.broadcasted_iota(jnp.int32, (64, half), 0) == head).astype(bf)
            col_sums[:, :wide] += product(to_row, both)
        if r == 0:
            grad_xs[:half, :] = total
        else:
            grad_xs[:half, :] += total[:half, :]
            grad_xs[half:, :] = total[half:, :]
    gxs = grad_xs[...]
    fold = (
        lax.broadcasted_iota(jnp.int32, (128, 128), 1)
        == 2 * pair + lax.broadcasted_iota(jnp.int32, (128, 128), 0) // HDIM
    ).astype(bf)
    step_sums[...] += product((gxs * x).astype(bf), fold)
    gx, parts = conv_back(v, taps[...], bias[...], valid[...], gxs * steps + skip[...] * grad_mixed)
    grad_x[...] = gx.astype(bf)
    stats[0:1, :] = jnp.sum(grad * normal, axis=0, keepdims=True)
    stats[1:2, :] = jnp.sum(grad_mixed * x, axis=0, keepdims=True)
    for k, total in enumerate(parts):
        stats[2 + k : 3 + k, :] = total
    stats[7:8, :] = jnp.zeros((1, 128), f32)

    @pl.when(pair == pl.num_programs(0) - 1)
    def _():
        gs = jnp.where(lower_left(rows), grad_scores[...], 0.0).astype(bf)
        grad_c = product(gs, bc_keep[:, :STATE])
        grad_b = product(gs, bc_keep[:, STATE:], 0, 0)
        ends = ((grad_b, 0), (grad_c, STATE))
        for g, at in ends:
            cols = pl.ds(at, STATE)
            gi, sums = conv_back(
                bc_ref[:, cols].astype(f32), bc_taps[:, cols], bc_bias[:, cols], valid[...], g
            )
            grad_bc[:, cols] = gi.astype(bf)
            for k, total in enumerate(sums):
                bc_stats[k : k + 1, cols] = total
            bc_stats[5:8, cols] = jnp.zeros((3, STATE), f32)


def mixer_specs(rows):
    tile = lambda at: pl.BlockSpec((rows, 128), at)
    whole = lambda shape: pl.BlockSpec(shape, lambda p: (0,) * len(shape))
    pairs = INNER // 128
    return tile, whole, [
        tile(lambda p: (0, p)),
        tile(lambda p: (0, pairs + p)),
        pl.BlockSpec((rows, 2 * STATE), lambda p: (0, 2 * INNER // (2 * STATE))),
        pl.BlockSpec((KCONV, 128), lambda p: (0, p)),
        pl.BlockSpec((1, 128), lambda p: (0, p)),
        pl.BlockSpec((KCONV, 2 * STATE), lambda p: (0, INNER // (2 * STATE))),
        pl.BlockSpec((1, 2 * STATE), lambda p: (0, INNER // (2 * STATE))),
        whole((rows, 128)),
        whole((rows, 128)),
        whole((rows, 128)),
        pl.BlockSpec((1, 2, rows), lambda p: (p, 0, 0)),
        pl.BlockSpec((1, 128), lambda p: (0, p)),
    ]


def mixer_front_call(inputs, rows):
    f32 = jnp.float32
    tile, whole, specs = mixer_specs(rows)
    return pl.pallas_call(
        front_body,
        grid=(INNER // 128,),
        in_specs=specs,
        out_specs=[tile(lambda p: (0, p)), tile(lambda p: (0, p)), whole((rows, 128))],
        out_shape=[
            jax.ShapeDtypeStruct((rows, INNER), f32),
            jax.ShapeDtypeStruct((rows, INNER), f32),
            jax.ShapeDtypeStruct((rows, 128), f32),
        ],
        scratch_shapes=[pltpu.VMEM((rows, rows), f32), pltpu.VMEM((rows, 2 * STATE), jnp.bfloat16)],
        name="mixer_front",
        cost_estimate=pl.CostEstimate(flops=10**10, bytes_accessed=2 * 10**7, transcendentals=5 * 10**6),
    )(*inputs)


def mixer_back_call(inputs, extra, rows):
    f32, bf = jnp.float32, jnp.bfloat16
    tile, whole, specs = mixer_specs(rows)
    by_pair = tile(lambda p: (0, p))
    return pl.pallas_call(
        back_body,
        grid=(INNER // 128,),
        in_specs=specs
        + [by_pair, by_pair, pl.BlockSpec((1, 128), lambda p: (0, p)), whole((rows, 128)), whole((rows, 128))],
        out_specs=[
            by_pair, by_pair, pl.BlockSpec((8, 128), lambda p: (0, p)), whole((rows, 2 * STATE)),
            whole((8, 2 * STATE)), whole((rows, 128)), whole((64, rows)), whole((rows, 128)),
        ],
        out_shape=[
            jax.ShapeDtypeStruct((rows, INNER), bf),
            jax.ShapeDtypeStruct((rows, INNER), bf),
            jax.ShapeDtypeStruct((8, INNER), f32),
            jax.ShapeDtypeStruct((rows, 2 * STATE), bf),
            jax.ShapeDtypeStruct((8, 2 * STATE), f32),
            jax.ShapeDtypeStruct((rows, 128), f32),
            jax.ShapeDtypeStruct((64, rows), f32),
            jax.ShapeDtypeStruct((rows, 128), f32),
        ],
        scratch_shapes=[
            pltpu.VMEM((rows, rows), f32), pltpu.VMEM((rows, 2 * STATE), bf),
            pltpu.VMEM((rows, rows), f32), pltpu.VMEM((rows, 128), f32),
        ],
        name="mixer_back",
        cost_estimate=pl.CostEstimate(flops=3 * 10**10, bytes_accessed=3 * 10**7, transcendentals=5 * 10**6),
    )(*inputs, *extra)


def picks(slot_row, slots):
    rows = slot_row.shape[1]
    at = lax.broadcasted_iota(jnp.int32, (slots, rows), 0).astype(jnp.float32)
    return at == slot_row


def experts_body(
    x_ref, cot_ref, up, down, slot_rows, gates,
    y_out, gin_out, up_grad, down_grad, dots,
    xe, gy, gu_grad, hid, gate_cols,
):
    f32, bf = jnp.float32, jnp.bfloat16
    chunks, rows, width = x_ref.shape
    slots = xe.shape[0] // chunks
    hidden = down.shape[1]

    @pl.loop(0, chunks)
    def _(g):
        p = picks(slot_rows[0, pl.ds(g, 1), :], slots)
        one = p.astype(bf)
        at = pl.ds(pl.multiple_of(g * slots, slots), slots)
        xe[at, :] = product(one, x_ref[g]).astype(bf)
        gate = jnp.sum(jnp.where(p, gates[0, pl.ds(g, 1), :], 0.0), axis=1, keepdims=True)
        gate_cols[at, :] = jnp.broadcast_to(gate, (slots, 128))
        gy[at, :] = (gate * product(one, cot_ref[g])).astype(bf)

    tile = 2 * slots

    @pl.loop(0, xe.shape[0] // tile)
    def _(t):
        at = pl.ds(pl.multiple_of(t * tile, tile), tile)
        gu = product(xe[at, :], up[0])
        a, b = gu[:, :hidden], gu[:, hidden:]
        s = sigmoid(a)
        silu = a * s
        h = (silu * b).astype(bf)
        hid[at, :] = h
        gh = product(gy[at, :], down[0], 1, 1)
        gu_grad[at, :hidden] = (gh * b * (s * (1.0 + a * (1.0 - s)))).astype(bf)
        gu_grad[at, hidden:] = (gh * silu).astype(bf)
        y = product(h, down[0]).astype(bf).astype(f32)
        dot = jnp.sum(y * gy[at, :].astype(f32), axis=1, keepdims=True)
        y_out[0, at, :] = (gate_cols[at, :1] * y).astype(bf)
        for i in range(2):
            p = picks(slot_rows[0, pl.ds(2 * t + i, 1), :], slots)
            dots[0, pl.ds(2 * t + i, 1), :] = jnp.sum(
                jnp.where(p, dot[i * slots : (i + 1) * slots, :], 0.0), axis=0, keepdims=True
            )
        gin_out[0, at, :] = product(gu_grad[at, :], up[0], 1, 1).astype(bf)

    for r in range(0, width, 256):
        up_grad[0, r : r + 256, :] = product(xe[:, r : r + 256], gu_grad[...], 0, 0).astype(bf)
    for r in range(0, hidden, 256):
        down_grad[0, r : r + 256, :] = product(hid[:, r : r + 256], gy[...], 0, 0).astype(bf)


def experts_call(x, cot, up, down, slot_rows, gates, slots):
    f32, bf = jnp.float32, jnp.bfloat16
    chunks, rows, width = x.shape
    held, _, double = up.shape
    total = chunks * slots
    once = pl.Buffered(1)
    each = lambda *shape: pl.BlockSpec((1,) + shape, lambda e: (e, 0, 0))
    keep = lambda *shape: pl.BlockSpec((1,) + shape, lambda e: (e, 0, 0), pipeline_mode=once)
    whole = pl.BlockSpec((chunks, rows, width), lambda e: (0, 0, 0), pipeline_mode=once)
    shape = lambda *s: jax.ShapeDtypeStruct((held,) + s, bf)
    return pl.pallas_call(
        experts_body,
        grid=(held,),
        in_specs=[
            whole, whole, keep(width, double), keep(double // 2, width), each(chunks, rows), each(chunks, rows),
        ],
        out_specs=[
            each(total, width), each(total, width), each(width, double), each(double // 2, width), each(chunks, rows),
        ],
        out_shape=[
            shape(total, width), shape(total, width), shape(width, double), shape(double // 2, width),
            jax.ShapeDtypeStruct((held, chunks, rows), f32),
        ],
        scratch_shapes=[
            pltpu.VMEM((total, width), bf), pltpu.VMEM((total, width), bf), pltpu.VMEM((total, double), bf),
            pltpu.VMEM((total, double // 2), bf), pltpu.VMEM((total, 128), f32),
        ],
        name="experts",
        compiler_params=pltpu.CompilerParams(vmem_limit_bytes=62 << 20),
        cost_estimate=pl.CostEstimate(flops=4 * 10**10, bytes_accessed=5 * 10**7, transcendentals=10**6),
    )(x, cot, up, down, slot_rows, gates)


def join_body(
    where, x_ref, cot_ref, y_ref, gin_ref, slot_rows, up, down,
    y_part, g_part, up_grad, down_grad, up_acc, down_acc,
):
    f32, bf = jnp.float32, jnp.bfloat16
    g = pl.program_id(0)

    @pl.when(g == 0)
    def _():
        up_acc[...] = jnp.zeros_like(up_acc)
        down_acc[...] = jnp.zeros_like(down_acc)

    x, cot = x_ref[0], cot_ref[0]
    half = down.shape[0]
    gu = product(x, up[...])
    a, b = gu[:, :half], gu[:, half:]
    s = sigmoid(a)
    silu = a * s
    h = (silu * b).astype(bf)
    gh = product(cot, down[...], 1, 1)
    gu_grad = jnp.concatenate(
        [gh * b * (s * (1.0 + a * (1.0 - s))), gh * silu], axis=1
    ).astype(bf)
    up_acc[...] += product(x, gu_grad, 0, 0)
    down_acc[...] += product(h, cot, 0, 0)
    y = product(h, down[...])
    gx = product(gu_grad, up[...], 1, 1)
    for e in range(y_ref.shape[0]):
        one = picks(slot_rows[e, pl.ds(g, 1), :], y_ref.shape[1]).astype(bf)
        y = y + product(one, y_ref[e], 0, 0)
        gx = gx + product(one, gin_ref[e], 0, 0)
    y_part[0] = y.astype(bf)
    g_part[0] = gx.astype(bf)

    @pl.when(g == pl.num_programs(0) - 1)
    def _():
        up_grad[...] = up_acc[...].astype(bf)
        down_grad[...] = down_acc[...].astype(bf)


def join_call(where, x, cot, y, gin, slot_rows, up, down, slots):
    f32, bf = jnp.float32, jnp.bfloat16
    chunks, rows, width = x.shape
    held = y.shape[0]
    chunk = pl.BlockSpec((1, rows, width), lambda g, w: (g, 0, 0))
    placed = pl.BlockSpec((1, rows, width), lambda g, w: (g ^ w[0], 0, 0))
    rows_of = pl.BlockSpec((held, slots, width), lambda g, w: (0, g, 0))
    whole = lambda a: pl.BlockSpec(a.shape, lambda g, w: (0,) * a.ndim)
    return pl.pallas_call(
        join_body,
        grid_spec=pltpu.PrefetchScalarGridSpec(
            num_scalar_prefetch=1,
            grid=(chunks,),
            in_specs=[chunk, chunk, rows_of, rows_of, whole(slot_rows), whole(up), whole(down)],
            out_specs=[placed, chunk, whole(up), whole(down)],
            scratch_shapes=[pltpu.VMEM(up.shape, f32), pltpu.VMEM(down.shape, f32)],
        ),
        out_shape=[
            jax.ShapeDtypeStruct(x.shape, bf), jax.ShapeDtypeStruct(x.shape, bf),
            jax.ShapeDtypeStruct(up.shape, bf), jax.ShapeDtypeStruct(down.shape, bf),
        ],
        name="join",
        compiler_params=pltpu.CompilerParams(vmem_limit_bytes=48 << 20),
        cost_estimate=pl.CostEstimate(flops=10**10, bytes_accessed=4 * 10**7, transcendentals=10**6),
    )(where, x, cot, y, gin, slot_rows, up, down)


def pile_body(spots, *refs):
    count = len(spots)
    parts, whole, sems = refs[:count], refs[count], refs[count + 1]
    copies = []
    for n, (part, (block, row)) in enumerate(zip(parts, spots)):
        to = whole.at[block, pl.ds(row, part.shape[0]), :]
        copies.append(pltpu.make_async_copy(part, to, sems.at[n]))
        copies[n].start()
    for copy in copies:
        copy.wait()


def pile(parts, spots, blocks):
    if parts[0].shape[1] % 128:
        by_block = [[p for p, spot in zip(parts, spots) if spot[0] == m] for m in range(blocks)]
        return jnp.stack([jnp.concatenate(b, axis=0) for b in by_block])
    anywhere = pl.BlockSpec(memory_space=pl.ANY)
    return pl.pallas_call(
        partial(pile_body, spots),
        out_shape=jax.ShapeDtypeStruct((blocks,) + parts[0].shape, parts[0].dtype),
        in_specs=[anywhere] * len(parts),
        out_specs=anywhere,
        scratch_shapes=[pltpu.SemaphoreType.DMA((len(parts),))],
        name="pile",
        cost_estimate=pl.CostEstimate(flops=0, bytes_accessed=13 * 10**6, transcendentals=0),
    )(*parts)


def local_fast(
    tokens, lengths, routes, cotangent, norm_gain, in_weight, conv_weight, conv_bias, dt_bias,
    a_log, d_skip, mix_gain, out_weight, ffn_gain, router_weight, shared_up, shared_down,
    expert_up, expert_down,
):
    bf, f32 = jnp.bfloat16, jnp.float32
    block = tokens.shape[1]
    parts = tokens.shape[0]
    rows = block * parts
    groups = lax.axis_size("dp")
    lines = lax.axis_size("seq")
    held = expert_up.shape[0]
    experts = held * groups
    top = routes.shape[2]
    slots = block * top * 5 // (4 * experts) * parts
    slots = -(-slots // 128) * 128
    place = lax.axis_index("seq")
    group = lax.axis_index("dp")

    def to(a, bit):
        return lax.ppermute(a, "dp", [(i, i ^ bit) for i in range(groups)])

    def around(a):
        cut = a.shape[0] // 2
        by_x, by_y = to(a, 2), to(a, 4)
        near = [a, by_x, by_y, to(by_x[:cut], 4), to(by_y[cut:], 2)]
        far = [to(b, 1) for b in near]
        spots = [(m, 0) for m in range(6)] + [(6, 0), (6, cut), (7, 0), (7, cut)]
        near_far = [b for pair in zip(near[:3], far[:3]) for b in pair]
        return pile(near_far + [near[3], near[4], far[3], far[4]], spots, groups)

    def spread(a):
        return lax.all_to_all(
            jnp.broadcast_to(a[None], (lines,) + a.shape), "seq", split_axis=0, concat_axis=0, tiled=True
        )

    pad = lambda a, n: jnp.pad(a, ((0, 0), (0, n - a.shape[1])))
    in_blocks, router_blocks, out_blocks, down_line, x_low, route = gather_rows(
        [in_weight, pad(router_weight, 128), out_weight],
        [in_weight.shape[0] // 3, router_weight.shape[0], out_weight.shape[0] // 2, shared_down.shape[0]],
        [shared_down], lines, 2, [tokens, routes], False, 1,
    )
    out_full = out_blocks.reshape(-1, MODEL_WIDTH)
    in_full = in_blocks.reshape(MODEL_WIDTH, -1)
    router_full = router_blocks.reshape(MODEL_WIDTH, -1)[:, :experts]
    down_part = down_line.reshape(-1, MODEL_WIDTH)
    in_full, late_up, late_cot = lax.optimization_barrier((in_full, shared_up, cotangent))
    cot_low = lax.all_to_all(late_cot, "seq", split_axis=0, concat_axis=0, tiled=True)
    width = SFF // groups
    up_cols = late_up.reshape(-1, 2, groups, width).transpose(2, 0, 1, 3).reshape(groups, -1, 2 * width)
    up_cols = lax.all_to_all(up_cols, "dp", split_axis=0, concat_axis=0, tiled=True)
    up_part = spread(up_cols).transpose(1, 0, 2, 3).reshape(MODEL_WIDTH, 2 * width)

    length = lax.dynamic_index_in_dim(lengths, place, 0, False)
    x_low = x_low.reshape(rows, MODEL_WIDTH)
    cot_low = cot_low.reshape(rows, MODEL_WIDTH)
    route = route.reshape(rows, top)
    used = jnp.arange(rows) < length
    valid = used.astype(f32)[:, None]
    all_cot = around(jnp.where(used[:, None], cot_low, 0))
    all_route = around(jnp.where(used[:, None], route, -1))
    mine = group * held + jnp.arange(held)
    member = jnp.any(all_route[None] == mine[:, None, None, None], axis=3)
    earlier = (jnp.arange(rows)[:, None] < jnp.arange(rows)[None, :]).astype(bf)
    before = jnp.einsum("egt,ts->egs", member.astype(bf), earlier, preferred_element_type=f32)
    slot_rows = jnp.where(member, before, -1.0)
    x_rows = x_low.astype(f32)
    normed, norm_pull = jax.vjp(rms_norm, x_rows, norm_gain)
    normed_low = normed.astype(bf)
    projected = jnp.dot(normed_low, in_full, preferred_element_type=f32).astype(bf)
    before_step = projected[:, INNER + CONV :].astype(f32) + dt_bias
    steps = jax.nn.softplus(before_step)
    rates = -steps * jnp.exp(a_log)
    lower = (jnp.arange(rows)[:, None] >= jnp.arange(rows)[None, :]).astype(f32)
    cumulative = jnp.dot(lower, rates, precision=PRECISE)
    wide = lambda a: jnp.broadcast_to(a[:, :, None], a.shape + (HDIM,)).reshape(a.shape[0], -1)
    lanes = lambda a: jnp.broadcast_to(a, (rows, 128))
    mixer_in = (
        projected, projected, projected, conv_weight, conv_bias[None], conv_weight, conv_bias[None],
        lanes(valid), pad(steps, 128), pad(cumulative, 128), cumulative.T.reshape(HEADS // 2, 2, rows),
        wide(d_skip[None]),
    )
    mixed, gated, squares = mixer_front_call(mixer_in, rows)
    scale = lax.rsqrt(jnp.sum(squares, axis=1, keepdims=True) / INNER + EPSILON)
    mix_low = (gated * scale * mix_gain).astype(bf)
    mixer_out = jnp.dot(mix_low, out_full, preferred_element_type=f32)
    hidden = x_rows + mixer_out * valid
    normed_ffn, ffn_pull = jax.vjp(rms_norm, hidden, ffn_gain)
    ffn_low = normed_ffn.astype(bf)
    logits = jnp.dot(ffn_low, router_full, preferred_element_type=f32)
    onehot = (route[:, :, None] == jnp.arange(experts)[None, None, :]).astype(f32)
    chosen = jnp.sum(onehot, axis=1)
    peak = jnp.max(jnp.where(chosen > 0, logits, -jnp.inf), axis=1, keepdims=True)
    raised = jnp.exp(jnp.where(chosen > 0, logits - peak, -jnp.inf))
    probs = raised / jnp.sum(raised, axis=1, keepdims=True)

    all_rows, all_probs = gather_rows(
        [ffn_low, pad(probs, 128)], [64, rows], [], 1, 2, [], True, 2
    )
    all_rows = all_rows[:, 0]
    gates = lax.dynamic_slice_in_dim(all_probs[:, 0], group * held, held, 2).transpose(2, 0, 1)
    y_slots, gin_slots, grad_eup, grad_edown, dots = experts_call(
        all_rows, all_cot, expert_up, expert_down, slot_rows, gates, slots
    )
    y_part, g_part, grad_sup, grad_sdown = join_call(
        group.reshape(1), all_rows, all_cot, y_slots, gin_slots, slot_rows, up_part, down_part, slots
    )
    at_own = (jnp.arange(experts)[None, :] == mine[:, None]).astype(f32)
    dots = jnp.einsum("egt,ef->gtf", dots, at_own, precision=PRECISE).reshape(-1, experts)
    dots_hi = dots.astype(bf)
    dots_lo = (dots - dots_hi.astype(f32)).astype(bf)
    g_sum, dots = sum_to_owners(
        [g_part.reshape(-1, MODEL_WIDTH), pad(jnp.concatenate([dots_hi, dots_lo], axis=1), 128)],
        [384, 128], 1, [f32, f32], None, [], (True, True), 3,
    )
    dots = dots[:, :experts] + dots[:, experts : 2 * experts]
    y_sum = lax.psum_scatter(y_part, "dp", scatter_dimension=0, tiled=False).astype(f32)
    output = (hidden + valid * y_sum).astype(bf).reshape(tokens.shape)
    output = lax.all_to_all(output, "seq", split_axis=0, concat_axis=0, tiled=True)

    grad_out = cot_low.astype(f32)
    grad_logit = (dots - probs * jnp.sum(dots, axis=1, keepdims=True)).astype(bf)
    grad_router = contract_rows(ffn_low, grad_logit)
    grad_ffn = g_sum + contract_cols(grad_logit, router_full)
    grad_hidden, grad_fgain = ffn_pull(grad_ffn)
    grad_hidden = grad_hidden + grad_out
    grad_mo = (grad_hidden * valid).astype(bf)
    grad_outw = contract_rows(mix_low, grad_mo).astype(bf)
    grad_mix = contract_cols(grad_mo, out_full)
    mean_dot = jnp.sum(grad_mo.astype(f32) * mixer_out, axis=1, keepdims=True) / INNER
    grad_z, grad_in, stats, grad_bc, bc_stats, row_sums, col_sums, step_sums = mixer_back_call(
        mixer_in, (mixed, grad_mix, mix_gain[None], lanes(scale), lanes(mean_dot)), rows
    )
    grad_rates = jnp.dot(lower.T, row_sums[:, :HEADS] - col_sums[:HEADS].T, precision=PRECISE)
    grad_raw = (step_sums[:, :HEADS] - grad_rates * jnp.exp(a_log)) * jax.nn.sigmoid(before_step)
    grad_al = jnp.sum(grad_rates * rates, axis=0)
    grad_db = jnp.sum(grad_raw, axis=0)
    grad_mgain = stats[0]
    grad_skip = jnp.sum(stats[1].reshape(HEADS, HDIM), axis=1)
    grad_cb = jnp.concatenate([stats[2], bc_stats[0]])
    grad_cw = jnp.concatenate([stats[3 : 3 + KCONV], bc_stats[1 : 1 + KCONV]], axis=1)
    grad_proj = jnp.concatenate([grad_z, grad_in, grad_bc, grad_raw.astype(bf)], axis=1)
    spare = -PROJ % 128
    grad_inw = contract_rows(normed_low, pad(grad_proj, PROJ + spare)).astype(bf)
    grad_x, grad_ngain = norm_pull(contract_cols(grad_proj, in_full))
    input_grad = (grad_x + grad_hidden).astype(bf)
    grad_router = contract_rows(ffn_low, pad(grad_logit, 128)).astype(bf)

    pieces = (grad_ngain, grad_cw, grad_cb, grad_db, grad_al, grad_skip, grad_mgain, grad_fgain)
    flat = jnp.concatenate([p.reshape(-1) for p in pieces])
    flat = jnp.pad(flat, (0, -flat.shape[0] % 2048)).reshape(-1, 128)
    own_out, own_in, own_router, input_grad, flat = sum_to_owners(
        [grad_outw, grad_inw, grad_router], [512, 768, 128], lines, [f32] * 3, flat,
        [input_grad.reshape(tokens.shape)], (False, False, False), 4,
    )
    flat = flat.reshape(-1)
    small = []
    start = 0
    for p in pieces:
        small.append(flat[start : start + p.size].reshape(p.shape))
        start += p.size
    along = lambda g, d: lax.psum_scatter(g.astype(bf), "seq", scatter_dimension=d, tiled=True)
    sup = grad_sup.astype(bf).reshape(groups, lines, -1, 2 * width).transpose(1, 0, 2, 3)
    sup = along(sup.reshape(MODEL_WIDTH, 2 * width), 0).reshape(groups, -1, 2 * width)
    sup = lax.all_to_all(sup, "dp", split_axis=0, concat_axis=0, tiled=True).astype(f32)
    sup = sup.reshape(groups, -1, 2, width).transpose(1, 2, 0, 3).reshape(-1, 2 * SFF)
    sdown = along(grad_sdown, 0).astype(f32)
    return (
        output, input_grad, small[0], own_in[:, :PROJ], small[1], small[2],
        small[3], small[4], small[5], small[6], own_out, small[7], own_router[:, :experts], sup, sdown,
        along(grad_eup, 1).astype(f32), along(grad_edown, 1).astype(f32),
    )


def solution(mesh):
    def program(*arrays):
        each = arrays[0].shape[0] == lax.axis_size("seq") == 4 and lax.axis_size("dp") == 8
        return (local_fast if each else local)(*arrays)

    return jax.shard_map(
        program,
        mesh=mesh,
        in_specs=(
            P("dp", "seq", None),
            P("dp"),
            P("dp", "seq", None),
            P("dp", "seq", None),
            P(),
            P(("dp", "seq"), None),
            P(),
            P(),
            P(),
            P(),
            P(),
            P(),
            P(("dp", "seq"), None),
            P(),
            P(("dp", "seq"), None),
            P(("dp", "seq"), None),
            P(("dp", "seq"), None),
            P("dp", None, None),
            P("dp", None, None),
        ),
        out_specs=(
            P("dp", "seq", None),
            P("dp", "seq", None),
            P(),
            P(("dp", "seq"), None),
            P(),
            P(),
            P(),
            P(),
            P(),
            P(),
            P(("dp", "seq"), None),
            P(),
            P(("dp", "seq"), None),
            P(("dp", "seq"), None),
            P(("dp", "seq"), None),
            P("dp", "seq", None),
            P("dp", "seq", None),
        ),
        check_vma=False,
    )
```

```python
from functools import partial

import jax
import jax.numpy as jnp
from jax import lax
from jax.experimental import pallas as pl
from jax.experimental.pallas import tpu as pltpu
from jax.sharding import PartitionSpec as P

MODEL_WIDTH = 1536
INNER = 3072
HEADS = 48
HDIM = 64
STATE = 128
KCONV = 4
EXPERT_HIDDEN = 512
SFF = 1024
MB = 4
CONV = 3328
PROJ = 6448


EPSILON = 1e-05
PRECISE = lax.Precision.HIGHEST
MESH = pl.DeviceIdType.MESH


def from_behind(x, axis, by):
    size = lax.axis_size(axis)
    pairs = [(i, i + by) for i in range(size) if 0 <= i + by < size]
    return lax.ppermute(x, axis, pairs)


def prefix(x, axis, join, neutral):
    place = lax.axis_index(axis)
    gathered = jax.tree.map(
        lambda a, kind: lax.all_gather(a.astype(kind), axis), x, (jnp.bfloat16, jnp.bfloat16)
    )
    state = jax.tree.map(lambda a, e: jnp.zeros_like(a) + jnp.asarray(e, a.dtype), x, neutral)

    def one(step, state):
        return join(
            state,
            jax.tree.map(
                lambda a, own: lax.dynamic_index_in_dim(a, step, 0, False).astype(own.dtype),
                gathered,
                x,
            ),
        )

    return lax.fori_loop(0, place, one, state)


def prefix_2(x, axis, join, neutral):
    count = lax.axis_size(axis)
    place = lax.axis_index(axis)
    ahead = count - 1 - place
    gathered = jax.tree.map(
        lambda a, kind: lax.all_gather(a.astype(kind), axis),
        x,
        jax.tree.map(lambda a: jnp.bfloat16 if a.dtype == jnp.float32 else a.dtype, x),
    )
    state = jax.tree.map(lambda a, e: jnp.zeros_like(a) + jnp.asarray(e, a.dtype), x, neutral)

    def one(step, state):
        source = count - 1 - step
        return join(
            state,
            jax.tree.map(
                lambda a, own: lax.dynamic_index_in_dim(a, source, 0, False).astype(own.dtype),
                gathered,
                x,
            ),
        )

    return lax.fori_loop(0, ahead, one, state)


def rms_norm(values, gain_vec):
    return (
        values * lax.rsqrt(jnp.mean(values * values, axis=-1, keepdims=True) + EPSILON) * gain_vec
    )


def swiglu(values, half_width):
    return jax.nn.silu(values[..., :half_width]) * values[..., half_width:]


def contract_rows(left_mat, right_mat):
    return lax.dot_general(
        left_mat, right_mat, (((0,), (0,)), ((), ())), preferred_element_type=jnp.float32
    )


def contract_cols(left_mat, right_mat):
    return lax.dot_general(
        left_mat, right_mat, (((1,), (1,)), ((), ())), preferred_element_type=jnp.float32
    )


def block_terms(head_in, b_rows, c_rows, step_sizes, a_log):
    log_rates = -step_sizes * jnp.exp(a_log)
    cumulative = jnp.cumsum(log_rates, axis=0)
    block_len = head_in.shape[0]
    lower_tri = jnp.arange(block_len)[:, None] >= jnp.arange(block_len)[None, :]
    spread = jnp.where(
        lower_tri[:, :, None], cumulative[:, None, :] - cumulative[None, :, :], -jnp.inf
    )
    scores = jnp.dot(c_rows, b_rows.T, precision=PRECISE)
    weights = jnp.exp(spread) * scores[:, :, None] * step_sizes[None, :, :]
    local_out = jnp.einsum("tih,ihp->thp", weights, head_in, precision=PRECISE)
    tail_weight = jnp.exp(cumulative[-1][None, :] - cumulative) * step_sizes
    local_state = jnp.einsum("ih,ihp,in->hpn", tail_weight, head_in, b_rows, precision=PRECISE)
    return (cumulative, local_out, local_state, jnp.exp(cumulative[-1]))


def carried_out(c_rows, cumulative, state_in):
    return (
        jnp.einsum("tn,hpn->thp", c_rows, state_in, precision=PRECISE)
        * jnp.exp(cumulative)[:, :, None]
    )


def mixer_front(valid_rows, projected, previous, conv_weight, conv_bias, dt_bias, a_log):
    row_count = projected.shape[0]
    conv_in = projected[:, INNER : INNER + CONV]
    padded = jnp.concatenate([previous, conv_in], axis=0)
    conv_sum = conv_bias + conv_weight[0] * padded[0:row_count]
    for tap_idx in range(1, KCONV):
        conv_sum = conv_sum + conv_weight[tap_idx] * padded[tap_idx : tap_idx + row_count]
    activated = jax.nn.silu(conv_sum) * valid_rows
    head_in = activated[:, :INNER].reshape(row_count, HEADS, HDIM)
    b_rows = activated[:, INNER : INNER + STATE]
    c_rows = activated[:, INNER + STATE :]
    step_sizes = jax.nn.softplus(projected[:, INNER + CONV :] + dt_bias)
    cumulative, local_out, local_state, decay_total = block_terms(
        head_in, b_rows, c_rows, step_sizes, a_log
    )
    return (projected[:, :INNER], head_in, c_rows, cumulative, local_out, local_state, decay_total)


def mixer_tail(gate_z, head_in, c_rows, cumulative, local_out, state_in, d_skip, mix_gain):
    mixed_out = local_out + carried_out(c_rows, cumulative, state_in) + d_skip[:, None] * head_in
    gated_out = mixed_out.reshape(head_in.shape[0], INNER) * jax.nn.silu(gate_z)
    return rms_norm(gated_out, mix_gain)


def link_states(earlier, latter):
    return (earlier[0] * latter[0], latter[1] + latter[0][:, None, None] * earlier[1])


def local(
    tokens,
    lengths,
    routes,
    cotangent,
    norm_gain,
    in_weight,
    conv_weight,
    conv_bias,
    dt_bias,
    a_log,
    d_skip,
    mix_gain,
    out_weight,
    ffn_gain,
    router_weight,
    shared_up,
    shared_down,
    expert_up,
    expert_down,
):
    row_count = tokens.shape[1]
    resident_experts = expert_up.shape[0]
    groups = lax.axis_size("dp")
    experts = resident_experts * groups
    top_count = routes.shape[2]
    capacity = row_count * top_count * 5 // (4 * experts)
    shards = (in_weight, out_weight, router_weight, shared_up, shared_down)
    kept_full = (
        lax.all_gather(shards[0], ("dp", "seq"), axis=0, tiled=True),
        lax.all_gather(shards[1], ("dp", "seq"), axis=0, tiled=True),
        lax.all_gather(shards[2], ("dp", "seq"), axis=0, tiled=True),
        lax.all_gather(shards[3], ("dp", "seq"), axis=0, tiled=True),
        lax.all_gather(shards[4], ("dp", "seq"), axis=0, tiled=True),
    )
    grad_inw = jnp.zeros((MODEL_WIDTH, PROJ), jnp.float32)
    grad_outw = jnp.zeros((INNER, MODEL_WIDTH), jnp.float32)
    grad_router = jnp.zeros((MODEL_WIDTH, experts), jnp.float32)
    grad_sup = jnp.zeros((MODEL_WIDTH, 2 * SFF), jnp.float32)
    grad_sdown = jnp.zeros((SFF, MODEL_WIDTH), jnp.float32)
    expert_upward_grad = jnp.zeros((resident_experts, MODEL_WIDTH, 2 * EXPERT_HIDDEN), jnp.float32)
    grad_edown = jnp.zeros((resident_experts, EXPERT_HIDDEN, MODEL_WIDTH), jnp.float32)
    grad_ngain = jnp.zeros_like(norm_gain)
    grad_cw = jnp.zeros_like(conv_weight)
    grad_cb = jnp.zeros_like(conv_bias)
    grad_db = jnp.zeros_like(dt_bias)
    grad_al = jnp.zeros_like(a_log)
    grad_skip = jnp.zeros_like(d_skip)
    grad_mgain = jnp.zeros_like(mix_gain)
    grad_fgain = jnp.zeros_like(ffn_gain)
    outputs = []
    input_grads = []
    for micro_idx in range(MB):
        in_full, out_full, router_full, up_full, down_full = kept_full
        x_rows = tokens[micro_idx].astype(jnp.float32)
        position = lax.axis_index("seq") * row_count + jnp.arange(row_count)
        valid_rows = (position < lengths[micro_idx]).astype(jnp.float32)[:, None]
        normed, norm_pull = jax.vjp(rms_norm, x_rows, norm_gain)
        normed_low = normed.astype(jnp.bfloat16)
        projected = jnp.dot(normed_low, in_full, preferred_element_type=jnp.float32).astype(
            jnp.bfloat16
        )
        previous = from_behind(projected[row_count - (KCONV - 1) :, INNER : INNER + CONV], "seq", 1)
        front_out, front_pull = jax.vjp(
            partial(mixer_front, valid_rows),
            projected.astype(jnp.float32),
            previous.astype(jnp.float32),
            conv_weight,
            conv_bias,
            dt_bias,
            a_log,
        )
        gate_z, head_in, c_rows, cumulative, local_out, local_state, decay_total = front_out
        identity = (jnp.ones_like(decay_total), jnp.zeros_like(local_state))
        _, state_in = prefix((decay_total, local_state), "seq", link_states, identity)
        normed_mix, tail_pull = jax.vjp(
            mixer_tail, gate_z, head_in, c_rows, cumulative, local_out, state_in, d_skip, mix_gain
        )
        mix_low = normed_mix.astype(jnp.bfloat16)
        mixer_out = jnp.dot(mix_low, out_full, preferred_element_type=jnp.float32)
        hidden = x_rows + mixer_out * valid_rows
        normed_ffn, ffn_pull = jax.vjp(rms_norm, hidden, ffn_gain)
        ffn_low = normed_ffn.astype(jnp.bfloat16)
        logits = jnp.dot(ffn_low, router_full, preferred_element_type=jnp.float32)
        route_row = routes[micro_idx]
        picked = jnp.take_along_axis(logits, route_row, axis=1)
        gate_probs = jax.nn.softmax(picked, axis=-1)
        shared_gu = jnp.dot(ffn_low, up_full, preferred_element_type=jnp.float32)
        shared_act, shared_pull = jax.vjp(partial(swiglu, half_width=SFF), shared_gu)
        shared_h = shared_act.astype(jnp.bfloat16)
        shared_y = jnp.dot(shared_h, down_full, preferred_element_type=jnp.float32)
        flat_route = route_row.reshape(-1)
        member = (flat_route[:, None] == jnp.arange(experts)[None, :]).astype(jnp.int32)
        slot_pos = jnp.sum((jnp.cumsum(member, axis=0) - member) * member, axis=1)
        target = flat_route * capacity + slot_pos
        source = (
            jnp.zeros((experts * capacity,), jnp.int32)
            .at[target]
            .set(jnp.arange(row_count * top_count, dtype=jnp.int32))
        )
        filled = jnp.zeros((experts * capacity, 1), jnp.bfloat16).at[target].set(jnp.bfloat16(1))
        outgoing = (jnp.take(ffn_low, source // top_count, axis=0) * filled).reshape(
            groups, resident_experts, capacity, MODEL_WIDTH
        )
        received_rows = lax.all_to_all(outgoing, "dp", split_axis=0, concat_axis=2, tiled=True)[0]
        expert_gu = jnp.einsum(
            "erd,edf->erf", received_rows, expert_up, preferred_element_type=jnp.float32
        )
        expert_act, expert_pull = jax.vjp(partial(swiglu, half_width=EXPERT_HIDDEN), expert_gu)
        expert_h = expert_act.astype(jnp.bfloat16)
        expert_y = jnp.einsum(
            "erf,efd->erd", expert_h, expert_down, preferred_element_type=jnp.float32
        ).astype(jnp.bfloat16)
        returned = lax.all_to_all(expert_y[None], "dp", split_axis=2, concat_axis=0, tiled=True)
        per_choice = (
            jnp.take(returned.reshape(experts * capacity, MODEL_WIDTH), target, axis=0)
            .reshape(row_count, top_count, MODEL_WIDTH)
            .astype(jnp.float32)
        )
        routed = jnp.einsum("lk,lkd->ld", gate_probs, per_choice, precision=PRECISE)
        outputs.append((hidden + valid_rows * (shared_y + routed)).astype(jnp.bfloat16))
        in_back, out_back, router_back, up_back, down_back = kept_full
        grad_out = cotangent[micro_idx].astype(jnp.float32)
        branch = valid_rows * grad_out
        shared_g = branch.astype(jnp.bfloat16)
        grad_sdown = grad_sdown + contract_rows(shared_h, shared_g)
        grad_sgu = shared_pull(contract_cols(shared_g, down_back))[0].astype(jnp.bfloat16)
        grad_sup = grad_sup + contract_rows(ffn_low, grad_sgu)
        grad_ffn = contract_cols(grad_sgu, up_back)
        grad_choice = (gate_probs[:, :, None] * branch[:, None, :]).astype(jnp.bfloat16)
        grad_gate = jnp.sum(branch[:, None, :] * per_choice, axis=-1)
        grad_pick = gate_probs * (
            grad_gate - jnp.sum(gate_probs * grad_gate, axis=-1, keepdims=True)
        )
        onehot = (route_row[:, :, None] == jnp.arange(experts)[None, None, :]).astype(jnp.float32)
        grad_logit = jnp.einsum("lk,lke->le", grad_pick, onehot, precision=PRECISE).astype(
            jnp.bfloat16
        )
        grad_router = grad_router + contract_rows(ffn_low, grad_logit)
        grad_ffn = grad_ffn + contract_cols(grad_logit, router_back)
        back_out = (
            jnp.take(grad_choice.reshape(row_count * top_count, MODEL_WIDTH), source, axis=0)
            * filled
        ).reshape(groups, resident_experts, capacity, MODEL_WIDTH)
        grad_arrived = lax.all_to_all(back_out, "dp", split_axis=0, concat_axis=2, tiled=True)[0]
        step_edown = jnp.einsum(
            "erf,erd->efd", expert_h, grad_arrived, preferred_element_type=jnp.float32
        )
        grad_eh = jnp.einsum(
            "erd,efd->erf", grad_arrived, expert_down, preferred_element_type=jnp.float32
        )
        expert_gate_up_grad = expert_pull(grad_eh)[0].astype(jnp.bfloat16)
        expert_upward_step = jnp.einsum(
            "tbw,tbj->twj", received_rows, expert_gate_up_grad, preferred_element_type=jnp.float32
        )
        grad_ein = jnp.einsum(
            "erf,edf->erd", expert_gate_up_grad, expert_up, preferred_element_type=jnp.float32
        ).astype(jnp.bfloat16)
        expert_upward_grad = expert_upward_grad + expert_upward_step
        grad_edown = grad_edown + step_edown
        came_back = lax.all_to_all(grad_ein[None], "dp", split_axis=2, concat_axis=0, tiled=True)
        grad_ffn = grad_ffn + jnp.sum(
            jnp.take(came_back.reshape(experts * capacity, MODEL_WIDTH), target, axis=0)
            .reshape(row_count, top_count, MODEL_WIDTH)
            .astype(jnp.float32),
            axis=1,
        )
        grad_hidden, step_fgain = ffn_pull(grad_ffn)
        grad_fgain = grad_fgain + step_fgain
        grad_hidden = grad_hidden + grad_out
        grad_mix_out = (grad_hidden * valid_rows).astype(jnp.bfloat16)
        grad_outw = grad_outw + contract_rows(mix_low, grad_mix_out)
        grad_mix = contract_cols(grad_mix_out, out_back)
        grad_z, grad_head, grad_c, grad_cum, grad_local, grad_state, step_skip, step_mgain = (
            tail_pull(grad_mix)
        )
        grad_skip = grad_skip + step_skip
        grad_mgain = grad_mgain + step_mgain
        _, grad_carry = prefix_2((decay_total, grad_state), "seq", link_states, identity)
        grad_decay = jnp.sum(grad_carry * state_in, axis=(1, 2))
        grad_proj, grad_prev, step_cw, step_cb, step_db, step_al = front_pull(
            (grad_z, grad_head, grad_c, grad_cum, grad_local, grad_carry, grad_decay)
        )
        grad_cw = grad_cw + step_cw
        grad_cb = grad_cb + step_cb
        grad_db = grad_db + step_db
        grad_al = grad_al + step_al
        from_next = from_behind(grad_prev.astype(jnp.bfloat16), "seq", -1).astype(grad_prev.dtype)
        grad_proj = (
            grad_proj.at[row_count - (KCONV - 1) :, INNER : INNER + CONV]
            .add(from_next)
            .astype(jnp.bfloat16)
        )
        grad_inw = grad_inw + contract_rows(normed_low, grad_proj)
        grad_normed = contract_cols(grad_proj, in_back)
        grad_x, step_ngain = norm_pull(grad_normed)
        grad_ngain = grad_ngain + step_ngain
        input_grads.append((grad_x + grad_hidden).astype(jnp.bfloat16))
    weight_grads = (
        lax.psum_scatter(grad_inw, ("dp", "seq"), scatter_dimension=0, tiled=True),
        lax.psum_scatter(grad_outw, ("dp", "seq"), scatter_dimension=0, tiled=True),
        lax.psum_scatter(grad_router, ("dp", "seq"), scatter_dimension=0, tiled=True),
        lax.psum_scatter(grad_sup, ("dp", "seq"), scatter_dimension=0, tiled=True),
        lax.psum_scatter(grad_sdown, ("dp", "seq"), scatter_dimension=0, tiled=True),
    )
    small_sums = lax.psum(
        (grad_ngain, grad_cw, grad_cb, grad_db, grad_al, grad_skip, grad_mgain, grad_fgain),
        ("dp", "seq"),
    )
    expert_sums = (
        lax.psum_scatter(
            expert_upward_grad.astype(jnp.bfloat16), "seq", scatter_dimension=1, tiled=True
        ).astype(jnp.float32),
        lax.psum_scatter(
            grad_edown.astype(jnp.bfloat16), "seq", scatter_dimension=1, tiled=True
        ).astype(jnp.float32),
    )
    return (
        jnp.stack(outputs),
        jnp.stack(input_grads),
        small_sums[0],
        weight_grads[0],
        small_sums[1],
        small_sums[2],
        small_sums[3],
        small_sums[4],
        small_sums[5],
        small_sums[6],
        weight_grads[1],
        small_sums[7],
        weight_grads[2],
        weight_grads[3],
        weight_grads[4],
        expert_sums[0],
        expert_sums[1],
    )


def at_neighbours():
    d = lax.axis_index("dp")
    core, x, y = d % 2, (d // 2) % 2, d // 4
    return d, core, x, y, d + 1 - 2 * core, d + 2 - 4 * x, d + 4 - 8 * y


def meet(devices):
    barrier = pltpu.get_barrier_semaphore()
    for there in devices:
        pl.semaphore_signal(barrier, inc=1, device_id=there, device_id_type=MESH)
    pl.semaphore_wait(barrier, len(devices))


def send(source, target, send_sem, recv_sem, there):
    copy = pltpu.make_async_remote_copy(
        src_ref=source, dst_ref=target, send_sem=send_sem, recv_sem=recv_sem,
        device_id=there, device_id_type=MESH,
    )
    copy.start()
    return copy


def add_into(target, source, high):
    step = 16
    for s in (64, 48, 32):
        if high % s == 0:
            step = s
            break

    @pl.loop(0, high // step)
    def _(i):
        rows = pl.ds(pl.multiple_of(i * step, step), step)
        target[rows, :] = target[rows, :] + source[rows, :]


def swap_start(swaps, landed, line, lines, local_sem, send_sem, recv_sem):
    copies = []
    for n, (a, b) in enumerate(zip(swaps, landed)):
        keep = pltpu.make_async_copy(a.at[line], b.at[line], local_sem.at[n])
        keep.start()
        away = [
            send(a.at[o], b.at[line], send_sem.at[n, k], recv_sem.at[n, k], {"seq": o})
            for k, o in enumerate(lax.rem(line + k, lines) for k in range(1, lines))
        ]
        copies.append((keep, away))
    return copies


def swap_end(copies):
    for keep, away in copies:
        for copy in away:
            copy.wait_recv()
    for keep, away in copies:
        for copy in away:
            copy.wait_send()
        keep.wait()


def swap_sems(count, lines):
    dma = pltpu.SemaphoreType.DMA
    return [dma((count,)), dma((count, lines - 1)), dma((count, lines - 1))]


def sum_body(items, arrays, lines, tiny, moved, relative, *refs):
    count = len(items)
    grads, refs = refs[:arrays], refs[arrays:]
    swaps, refs = refs[:moved], refs[moved:]
    if tiny:
        small_in, refs = refs[:4], refs[4:]
    outs, refs = refs[:arrays], refs[arrays:]
    landed, refs = refs[:moved], refs[moved:]
    if tiny:
        small_out, refs = refs[:6], refs[6:]
    own, refs = refs[:count], refs[count:]
    got, refs = refs[:count], refs[count:]
    from_x, refs = refs[:count], refs[count:]
    from_y, refs = refs[:count], refs[count:]
    last_x, refs = refs[:count], refs[count:]
    last_y, refs = refs[:count], refs[count:]
    if lines > 1:
        from_z, refs = refs[:count], refs[count:]
    (load_sem, send_sem, recv_sem), refs = refs[:3], refs[3:]
    if moved:
        swap_sem, refs = refs[:3], refs[3:]
    if tiny:
        packed, half, t_core, t_x, t_y, t_z, t_back, t_send, t_recv = refs
    d, core, x, y, at_core, at_x, at_y = at_neighbours()
    bits = [(0, 0, 0) if own else (core, x, y) for own in relative]
    own_core = core
    line = lax.axis_index("seq")
    others = [lax.rem(line + k, lines) for k in range(1, lines)]
    meet([{"dp": at_core}, {"dp": at_x}, {"dp": at_y}] + [{"seq": o} for o in others])
    sent = [[] for _ in items]
    stage = [None] * count
    cross = [None] * count
    close = [None] * count
    along = [None] * count
    loads = [None] * count

    def begin(t):
        a, c0, wide, high = items[t]
        core, x, y = bits[a]
        cols = pl.ds(c0, wide)
        loads[t] = pltpu.make_async_copy(grads[a].at[:, :, core, :, cols], own[t], load_sem.at[t])
        loads[t].start()
        stage[t] = send(
            grads[a].at[:, :, 1 - core, :, cols], got[t], send_sem.at[t, 0], recv_sem.at[t, 0], {"dp": at_core}
        )

    def fold(t):
        a, c0, wide, high = items[t]
        core, x, y = bits[a]
        loads[t].wait()
        stage[t].wait_recv()
        for i in range(2):
            for j in range(2):
                add_into(got[t].at[i, j], own[t].at[i, j], high)
        top, low = pl.ds(0, high // 2), pl.ds(high // 2, high // 2)
        cross[t] = (
            send(got[t].at[:, 1 - x, top, :], from_x[t], send_sem.at[t, 1], recv_sem.at[t, 1], {"dp": at_x}),
            send(got[t].at[1 - y, :, low, :], from_y[t], send_sem.at[t, 2], recv_sem.at[t, 2], {"dp": at_y}),
        )

    def turn(t):
        a, c0, wide, high = items[t]
        core, x, y = bits[a]
        top, low = pl.ds(0, high // 2), pl.ds(high // 2, high // 2)
        cross[t][0].wait_recv()
        for i in range(2):
            add_into(got[t].at[i, x, top, :], from_x[t].at[i], high // 2)
        close_y = send(got[t].at[1 - y, x, top, :], last_y[t], send_sem.at[t, 3], recv_sem.at[t, 3], {"dp": at_y})
        cross[t][1].wait_recv()
        for j in range(2):
            add_into(got[t].at[y, j, low, :], from_y[t].at[j], high // 2)
        close_x = send(got[t].at[y, 1 - x, low, :], last_x[t], send_sem.at[t, 4], recv_sem.at[t, 4], {"dp": at_x})
        close[t] = (close_y, close_x)

    def settle(t):
        a, c0, wide, high = items[t]
        core, x, y = bits[a]
        top, low = pl.ds(0, high // 2), pl.ds(high // 2, high // 2)
        cols = pl.ds(c0, wide)
        close[t][0].wait_recv()
        add_into(got[t].at[y, x, top, :], last_y[t], high // 2)
        close[t][1].wait_recv()
        add_into(got[t].at[y, x, low, :], last_x[t], high // 2)
        if lines == 1:
            show = min(wide, outs[a].shape[1] - c0)
            outs[a][:, c0 : c0 + show] = got[t][y, x, :, :show].astype(jnp.float32)
            return
        each = high // lines
        along[t] = [
            send(
                got[t].at[y, x, pl.ds(pl.multiple_of(o * each, 16), each), :], from_z[t].at[k],
                send_sem.at[t, 5 + k], recv_sem.at[t, 5 + k], {"seq": o},
            )
            for k, o in enumerate(others)
        ]

    def finish(t):
        a, c0, wide, high = items[t]
        core, x, y = bits[a]
        each = high // lines
        total = got[t][y, x, pl.ds(pl.multiple_of(line * each, 16), each), :].astype(jnp.float32)
        for k in range(lines - 1):
            along[t][k].wait_recv()
            total = total + from_z[t][k].astype(jnp.float32)
        show = min(wide, outs[a].shape[1] - c0)
        outs[a][:, c0 : c0 + show] = total[:, :show]

    little = []

    def tiny_step(n):
        if n == 0:
            at = 0
            for part in small_in:
                size = part.shape[1] // 2
                for k in range(2):
                    packed[k, :, at : at + size] = part[:, k * size : (k + 1) * size]
                at += size
            little.append(send(packed.at[1 - own_core], t_core, t_send.at[0], t_recv.at[0], {"dp": at_core}))
        elif n == 1:
            little[0].wait_recv()
            half[0] = packed[own_core] + t_core[...]
            little.append(send(half.at[0], t_x, t_send.at[1], t_recv.at[1], {"dp": at_x}))
        elif n == 2:
            little[1].wait_recv()
            half[1] = half[0] + t_x[...]
            little.append(send(half.at[1], t_y, t_send.at[2], t_recv.at[2], {"dp": at_y}))
        elif n == 3:
            little[2].wait_recv()
            half[2] = half[1] + t_y[...]
            t_z[line] = half[2]
            for k, o in enumerate(others):
                little.append(send(half.at[2], t_z.at[line], t_send.at[3 + k], t_recv.at[3 + k], {"seq": o}))
        elif n == 4:
            for k in range(lines - 1):
                little[3 + k].wait_recv()
            total = t_z[0]
            for k in range(1, lines):
                total = total + t_z[k]
            t_back[own_core] = total
            little.append(
                send(t_back.at[own_core], t_back.at[own_core], t_send.at[7], t_recv.at[7], {"dp": at_core})
            )
        elif n == 5:
            little[-1].wait_recv()
            for copy in little:
                copy.wait_send()
            conv_w, conv_b, mix_g, norm_g, ffn_g, heads = small_out
            at = 0
            spans = []
            for part in small_in:
                size = part.shape[1] // 2
                spans.append((at, size))
                at += size
            for k in range(2):
                at, size = spans[0]
                mix_g[:, k * size : (k + 1) * size] = t_back[k, 0:1, at : at + size]
                conv_b[:, k * size : (k + 1) * size] = t_back[k, 2:3, at : at + size]
                conv_w[:, k * size : (k + 1) * size] = t_back[k, 3:7, at : at + size]
                at, size = spans[1]
                here = INNER + k * size
                conv_b[:, here : here + size] = t_back[k, 0:1, at : at + size]
                conv_w[:, here : here + size] = t_back[k, 1:5, at : at + size]
                at, size = spans[2]
                norm_g[:, k * size : (k + 1) * size] = t_back[k, 0:1, at : at + size]
                ffn_g[:, k * size : (k + 1) * size] = t_back[k, 1:2, at : at + size]
                at, size = spans[3]
                heads[:, k * size : (k + 1) * size] = t_back[k, :, at : at + size]

    begin(0)
    if tiny:
        tiny_step(0)
    moves = swap_start(swaps, landed, line, lines, *swap_sem) if moved else ()
    for t in range(max(count + 3, 5 if tiny else 0)):
        if t + 1 < count:
            begin(t + 1)
        if t < count:
            fold(t)
        if 0 <= t - 1 < count:
            turn(t - 1)
        if 0 <= t - 2 < count:
            settle(t - 2)
        if lines > 1 and 0 <= t - 3 < count:
            finish(t - 3)
        if tiny and t < 5:
            tiny_step(t + 1)
    swap_end(moves)
    for t in range(count):
        stage[t].wait_send()
        for copy in cross[t] + close[t] + tuple(along[t] or ()):
            copy.wait_send()


def sum_to_owners(grads, widths, lines, shown, small, swaps, relative, identity):
    items, views = [], []
    for a, (g, wide) in enumerate(zip(grads, widths)):
        high, cols = g.shape[0] // 8, g.shape[1]
        views.append(g.reshape(2, 2, 2, high, cols))
        start = 0
        while start < cols:
            w = min(wide, cols - start)
            items.append((a, start, w, high))
            start += w
    tiny = small is not None
    bf = jnp.bfloat16
    scratch = [pltpu.VMEM((2, 2, h, w), bf) for _, _, w, h in items]
    scratch += [pltpu.VMEM((2, 2, h, w), bf) for _, _, w, h in items]
    scratch += [pltpu.VMEM((2, h // 2, w), bf) for _, _, w, h in items] * 2
    scratch += [pltpu.VMEM((h // 2, w), bf) for _, _, w, h in items] * 2
    if lines > 1:
        scratch += [pltpu.VMEM((lines - 1, h // lines, w), bf) for _, _, w, h in items]
    ways = 4 + lines
    scratch += [
        pltpu.SemaphoreType.DMA((len(items),)),
        pltpu.SemaphoreType.DMA((len(items), ways)),
        pltpu.SemaphoreType.DMA((len(items), ways)),
    ]
    out_shape = [
        jax.ShapeDtypeStruct((g.shape[0] // 8 // lines, cols), jnp.float32) for g, cols in zip(grads, shown)
    ]
    ins = list(views)
    in_specs = [pl.BlockSpec(memory_space=pl.ANY)] * len(views)
    out_specs = [pl.BlockSpec(memory_space=pltpu.VMEM)] * len(views)
    if swaps:
        scratch += swap_sems(len(swaps), lines)
        ins += swaps
        in_specs += [pl.BlockSpec(memory_space=pl.ANY)] * len(swaps)
        out_specs += [pl.BlockSpec(memory_space=pl.ANY)] * len(swaps)
        out_shape += [jax.ShapeDtypeStruct(a.shape, a.dtype) for a in swaps]
    if tiny:
        cols = sum(part.shape[1] for part in small) // 2
        part = lambda *lead: pltpu.VMEM(lead + (8, cols), jnp.float32)
        scratch += [part(2), part(3), part(), part(), part(), part(lines), part(2)]
        scratch += [pltpu.SemaphoreType.DMA((8,)), pltpu.SemaphoreType.DMA((8,))]
        ins += small
        in_specs += [pl.BlockSpec(memory_space=pltpu.VMEM)] * 4
        for shape in ((KCONV, CONV), (1, CONV), (1, INNER), (1, MODEL_WIDTH), (1, MODEL_WIDTH), (8, 256)):
            out_shape.append(jax.ShapeDtypeStruct(shape, jnp.float32))
            out_specs.append(pl.BlockSpec(memory_space=pltpu.VMEM))
    return pl.pallas_call(
        partial(sum_body, items, len(views), lines, tiny, len(swaps), relative),
        out_shape=out_shape,
        in_specs=in_specs,
        out_specs=out_specs,
        scratch_shapes=scratch,
        name="sum_to_owners_%d" % identity,
        compiler_params=pltpu.CompilerParams(
            collective_id=identity, has_side_effects=True, vmem_limit_bytes=60 << 20
        ),
    )(*ins)


def gather_body(pieces, arrays, flat, lines, ahead, moved, relative, *refs):
    mine, refs = refs[:arrays], refs[arrays:]
    swaps, refs = refs[:moved], refs[moved:]
    full, refs = refs[:arrays], refs[arrays:]
    landed, refs = refs[:moved], refs[moved:]
    keep_sem, send_sem, recv_sem, z_send, z_recv = refs[:5]
    swap_sem = refs[5:]
    d, core, x, y, at_core, at_x, at_y = at_neighbours()
    at_far = at_x + at_y - d
    line = lax.rem(lax.axis_index("seq"), lines)
    hops = [line]
    if lines > 1:
        upper = line // 2
        hops += [line + 1 - 2 * (line % 2), 2 - upper, 3 - 3 * upper]
    meet([{"dp": at_core}, {"dp": at_x}, {"dp": at_y}] + [{"seq": o} for o in hops[1:]])
    blocks = dict(own=d, x=at_x, y=at_y, far=at_far)
    lands = dict(x=d, y=d, core=d, x_y=at_x, x_core=at_x, y_x=at_y, y_core=at_y, far_core=at_far)
    if relative:
        blocks = dict(own=0, x=2, y=4, far=6)
        lands = dict(x=2, y=4, core=1, x_y=6, x_core=3, y_x=6, y_core=5, far_core=7)
    mains = [q for q, piece in enumerate(pieces) if piece[0] < arrays - flat]
    sides = [q for q, piece in enumerate(pieces) if piece[0] >= arrays - flat]
    home = lambda a: blocks["own"] if a < arrays - flat else 0
    keep = []
    for a in range(arrays):
        keep.append(pltpu.make_async_copy(mine[a], full[a].at[home(a), line], keep_sem.at[a]))
        keep[a].start()
    order = [(j, q) for j in range(lines) for q in mains]
    total = len(order)
    out = [[None] * 7 for _ in order]

    def place(j, q, block):
        a, r0, high = pieces[q]
        return full[a].at[block, hops[j], pl.ds(r0, high), :]

    def own_piece(q):
        a, r0, high = pieces[q]
        return mine[a].at[pl.ds(r0, high), :]

    def hop(j, q, sem, to):
        a = pieces[q][0]
        return pltpu.make_async_remote_copy(
            src_ref=own_piece(q) if j == 0 else place(j, q, home(a)),
            dst_ref=place(j, q, home(a)),
            send_sem=z_send.at[q, sem], recv_sem=z_recv.at[q, hops[j]],
            device_id={"seq": to}, device_id_type=MESH,
        )

    def onward(j, q, act):
        o = hops[j]

        @pl.when((o <= line) & (line < lines - 1))
        def _():
            act(hop(j, q, 2 * j, jnp.minimum(line + 1, lines - 1)))

        @pl.when((o >= line) & (line > 0))
        def _():
            act(hop(j, q, 2 * j + 1, jnp.maximum(line - 1, 0)))

    def relay(j, q):
        hop(j, q, 2 * j, line).wait_recv()
        onward(j, q, lambda copy: copy.start())

    def pass_on(i, n, block, lands_at, there):
        j, q = order[i]
        source = own_piece(q) if block is None else place(j, q, block)
        out[i][n] = send(
            source, place(j, q, lands[lands_at]), send_sem.at[i, n], recv_sem.at[i, n], {"dp": there}
        )

    def first(i):
        block = None if order[i][0] == 0 else blocks["own"]
        pass_on(i, 0, block, "x", at_x)
        pass_on(i, 1, block, "y", at_y)
        pass_on(i, 2, block, "core", at_core)

    def second(i):
        out[i][0].wait_recv()
        if i % 2 == 0:
            pass_on(i, 5, blocks["x"], "x_y", at_y)
        pass_on(i, 3, blocks["x"], "x_core", at_core)
        out[i][1].wait_recv()
        if i % 2 == 1:
            pass_on(i, 5, blocks["y"], "y_x", at_x)
        pass_on(i, 4, blocks["y"], "y_core", at_core)

    def third(i):
        out[i][5].wait_recv()
        pass_on(i, 6, blocks["far"], "far_core", at_core)

    lead = ahead + 2
    if lines > 1:
        for q in mains:
            onward(0, q, lambda copy: copy.start())
    for i in range(min(ahead, total)):
        first(i)
    moves = swap_start(swaps, landed, line, lines, *swap_sem) if moved else ()
    for i in range(total):
        if i + lead < total and order[i + lead][0] > 0:
            relay(*order[i + lead])
        if i % len(mains) == 1:
            j = i // len(mains)
            for q in sides:
                if j == 0:
                    onward(0, q, lambda copy: copy.start())
                else:
                    relay(j, q)
        if i + ahead < total:
            first(i + ahead)
        second(i)
        if i:
            third(i - 1)
    third(total - 1)
    for i in range(total):
        for n in (2, 3, 4, 6):
            out[i][n].wait_recv()
        for copy in out[i]:
            copy.wait_send()
    swap_end(moves)
    if lines > 1:
        for q in range(len(pieces)):
            for j in range(lines):
                onward(j, q, lambda copy: copy.wait_send())
    for copy in keep:
        copy.wait()


def gather_rows(arrays, chunks, flat, lines, ahead, swaps, relative, identity):
    pieces = []
    count = len(arrays) + len(flat)
    for a, (w, chunk) in enumerate(zip(list(arrays) + list(flat), chunks)):
        for r0 in range(0, w.shape[0], chunk):
            pieces.append((a, r0, chunk))
    total = lines * len([p for p in pieces if p[0] < len(arrays)])
    anywhere = pl.BlockSpec(memory_space=pl.ANY)
    return pl.pallas_call(
        partial(gather_body, pieces, count, len(flat), lines, ahead, len(swaps), relative),
        out_shape=[jax.ShapeDtypeStruct((8, lines) + w.shape, w.dtype) for w in arrays]
        + [jax.ShapeDtypeStruct((1, lines) + w.shape, w.dtype) for w in flat]
        + [jax.ShapeDtypeStruct(a.shape, a.dtype) for a in swaps],
        in_specs=[anywhere] * (count + len(swaps)),
        out_specs=[anywhere] * (count + len(swaps)),
        scratch_shapes=[
            pltpu.SemaphoreType.DMA((count,)),
            pltpu.SemaphoreType.DMA((total, 7)),
            pltpu.SemaphoreType.DMA((total, 7)),
            pltpu.SemaphoreType.DMA((len(pieces), 2 * lines)),
            pltpu.SemaphoreType.DMA((len(pieces), lines)),
        ]
        + (swap_sems(len(swaps), lines) if swaps else []),
        name="gather_rows_%d" % identity,
        compiler_params=pltpu.CompilerParams(collective_id=identity, has_side_effects=True),
    )(*arrays, *flat, *swaps)


def sigmoid(v):
    return 1.0 / (1.0 + jnp.exp(-v))


def shifted(v, by):
    if by == 0:
        return v
    rows = v.shape[0]
    at = lax.broadcasted_iota(jnp.int32, v.shape, 0)
    keep = at >= by if by > 0 else at < rows + by
    return jnp.where(keep, pltpu.roll(v, by % rows, 0), 0.0)


def conv_sums(v, taps, bias):
    total = bias
    for k in range(KCONV):
        total = total + taps[k : k + 1, :] * shifted(v, KCONV - 1 - k)
    return total


def conv_back(v, taps, bias, valid, grad):
    conv_sum = conv_sums(v, taps, bias)
    s = sigmoid(conv_sum)
    grad = grad * valid * (s * (1.0 + conv_sum * (1.0 - s)))
    total = taps[KCONV - 1 : KCONV, :] * grad
    for k in range(KCONV - 1):
        total = total + taps[k : k + 1, :] * shifted(grad, k - (KCONV - 1))
    sums = [jnp.sum(grad, axis=0, keepdims=True)]
    for k in range(KCONV):
        sums.append(jnp.sum(grad * shifted(v, KCONV - 1 - k), axis=0, keepdims=True))
    return total, sums


def head_columns(ref, pair):
    v = pltpu.roll(ref[...], lax.rem(128 - 2 * pair, 128), 1)
    return v[:, 0:1], v[:, 1:2]


def over_lanes(columns):
    rows = columns[0].shape[0]
    lane = lax.broadcasted_iota(jnp.int32, (rows, 128), 1)
    return jnp.where(lane < HDIM, columns[0], columns[1])


def lower_left(rows):
    return lax.broadcasted_iota(jnp.int32, (rows, rows), 0) >= lax.broadcasted_iota(
        jnp.int32, (rows, rows), 1
    )


def product(a, b, over_a=1, over_b=0):
    return lax.dot_general(
        a, b, (((over_a,), (over_b,)), ((), ())), preferred_element_type=jnp.float32
    )


def bc_scores(bc_ref, bc_taps, bc_bias, valid, scores, bc_keep):
    conv_sum = conv_sums(bc_ref[...].astype(jnp.float32), bc_taps[...], bc_bias[...])
    bc = conv_sum * sigmoid(conv_sum) * valid[:, :1]
    bc_keep[...] = bc.astype(jnp.bfloat16)
    rows = scores.shape[0]
    g = product(bc_keep[:, STATE:], bc_keep[:, :STATE], 1, 1)
    scores[...] = jnp.where(lower_left(rows), g, 0.0)


def front_body(
    z_ref, x_ref, bc_ref, taps, bias, bc_taps, bc_bias, valid, step, cum, cum_rows, skip,
    mixed_ref, gated_ref, squares, scores, bc_keep,
):
    f32, bf = jnp.float32, jnp.bfloat16

    @pl.when(pl.program_id(0) == 0)
    def _():
        bc_scores(bc_ref, bc_taps, bc_bias, valid, scores, bc_keep)
        squares[...] = jnp.zeros_like(squares)

    rows = x_ref.shape[0]
    half = rows // 2
    conv_sum = conv_sums(x_ref[...].astype(f32), taps[...], bias[...])
    x = conv_sum * sigmoid(conv_sum) * valid[...]
    xs = (x * over_lanes(head_columns(step, pl.program_id(0)))).astype(bf)
    sums = head_columns(cum, pl.program_id(0))
    lane = lax.broadcasted_iota(jnp.int32, (half, 128), 1)
    for r in range(2):
        at, wide = pl.ds(r * half, half), (r + 1) * half
        parts = []
        for h in range(2):
            gap = sums[h][r * half : (r + 1) * half, :] - cum_rows[0, h : h + 1, :wide]
            m = (jnp.exp(jnp.minimum(gap, 0.0)) * scores[at, :wide]).astype(bf)
            parts.append(product(m, xs[:wide, :]))
        mixed = jnp.where(lane < HDIM, parts[0], parts[1]) + skip[...] * x[r * half : (r + 1) * half, :]
        z = z_ref[at, :].astype(f32)
        gated = mixed * (z * sigmoid(z))
        mixed_ref[at, :] = mixed
        gated_ref[at, :] = gated
        squares[at, :] += gated * gated


def back_body(
    z_ref, x_ref, bc_ref, taps, bias, bc_taps, bc_bias, valid, step, cum, cum_rows, skip,
    mixed_ref, grad_ref, gain, scale, mean_dot,
    grad_z, grad_x, stats, grad_bc, bc_stats, row_sums, col_sums, step_sums,
    scores, bc_keep, grad_scores, grad_xs,
):
    f32, bf = jnp.float32, jnp.bfloat16
    pair = pl.program_id(0)

    @pl.when(pair == 0)
    def _():
        bc_scores(bc_ref, bc_taps, bc_bias, valid, scores, bc_keep)
        grad_scores[...] = jnp.zeros_like(grad_scores)
        row_sums[...] = jnp.zeros_like(row_sums)
        col_sums[...] = jnp.zeros_like(col_sums)
        step_sums[...] = jnp.zeros_like(step_sums)

    rows = x_ref.shape[0]
    half = rows // 2
    v = x_ref[...].astype(f32)
    conv_sum = conv_sums(v, taps[...], bias[...])
    x = conv_sum * sigmoid(conv_sum) * valid[...]
    steps = over_lanes(head_columns(step, pair))
    sums = head_columns(cum, pair)
    xs = (x * steps).astype(bf)
    z = z_ref[...].astype(f32)
    s = sigmoid(z)
    silu = z * s
    mixed = mixed_ref[...]
    normal = mixed * silu * scale[...]
    grad = grad_ref[...]
    grad_gated = scale[...] * (grad * gain[...] - normal * mean_dot[...])
    grad_mixed = grad_gated * silu
    grad_z[...] = (grad_gated * mixed * (s * (1.0 + z * (1.0 - s)))).astype(bf)
    lane = lax.broadcasted_iota(jnp.int32, (rows, 128), 1)
    dy = [
        jnp.where(lane < HDIM, grad_mixed, 0.0).astype(bf),
        jnp.where(lane < HDIM, 0.0, grad_mixed).astype(bf),
    ]
    for r in range(2):
        at, wide = pl.ds(r * half, half), (r + 1) * half
        total = None
        for h in range(2):
            head = 2 * pair + h
            g = scores[at, :wide]
            gap = sums[h][r * half : (r + 1) * half, :] - cum_rows[0, h : h + 1, :wide]
            e = jnp.exp(jnp.minimum(gap, 0.0))
            m = (e * g).astype(bf)
            dy_rows = dy[h][r * half : (r + 1) * half, :]
            slope = product(dy_rows, xs[:wide, :], 1, 1) * e
            grad_scores[at, :wide] += slope
            both = (slope * g).astype(bf)
            back = product(m, dy_rows, 0, 0)
            total = back if total is None else total + back
            to_lane = (lax.broadcasted_iota(jnp.int32, (wide, 128), 1) == head).astype(bf)
            row_sums[at, :] += product(both, to_lane)
            to_row = (lax.broadcasted_iota(jnp.int32, (64, half), 0) == head).astype(bf)
            col_sums[:, :wide] += product(to_row, both)
        if r == 0:
            grad_xs[:half, :] = total
        else:
            grad_xs[:half, :] += total[:half, :]
            grad_xs[half:, :] = total[half:, :]
    gxs = grad_xs[...]
    fold = (
        lax.broadcasted_iota(jnp.int32, (128, 128), 1)
        == 2 * pair + lax.broadcasted_iota(jnp.int32, (128, 128), 0) // HDIM
    ).astype(bf)
    step_sums[...] += product((gxs * x).astype(bf), fold)
    gx, parts = conv_back(v, taps[...], bias[...], valid[...], gxs * steps + skip[...] * grad_mixed)
    grad_x[...] = gx.astype(bf)
    stats[0:1, :] = jnp.sum(grad * normal, axis=0, keepdims=True)
    stats[1:2, :] = jnp.sum(grad_mixed * x, axis=0, keepdims=True)
    for k, total in enumerate(parts):
        stats[2 + k : 3 + k, :] = total
    stats[7:8, :] = jnp.zeros((1, 128), f32)

    @pl.when(pair == pl.num_programs(0) - 1)
    def _():
        gs = jnp.where(lower_left(rows), grad_scores[...], 0.0).astype(bf)
        grad_c = product(gs, bc_keep[:, :STATE])
        grad_b = product(gs, bc_keep[:, STATE:], 0, 0)
        ends = ((grad_b, 0), (grad_c, STATE))
        for g, at in ends:
            cols = pl.ds(at, STATE)
            gi, sums = conv_back(
                bc_ref[:, cols].astype(f32), bc_taps[:, cols], bc_bias[:, cols], valid[...], g
            )
            grad_bc[:, cols] = gi.astype(bf)
            for k, total in enumerate(sums):
                bc_stats[k : k + 1, cols] = total
            bc_stats[5:8, cols] = jnp.zeros((3, STATE), f32)


def mixer_specs(rows):
    tile = lambda at: pl.BlockSpec((rows, 128), at)
    whole = lambda shape: pl.BlockSpec(shape, lambda p: (0,) * len(shape))
    pairs = INNER // 128
    return tile, whole, [
        tile(lambda p: (0, p)),
        tile(lambda p: (0, pairs + p)),
        pl.BlockSpec((rows, 2 * STATE), lambda p: (0, 2 * INNER // (2 * STATE))),
        pl.BlockSpec((KCONV, 128), lambda p: (0, p)),
        pl.BlockSpec((1, 128), lambda p: (0, p)),
        pl.BlockSpec((KCONV, 2 * STATE), lambda p: (0, INNER // (2 * STATE))),
        pl.BlockSpec((1, 2 * STATE), lambda p: (0, INNER // (2 * STATE))),
        whole((rows, 128)),
        whole((rows, 128)),
        whole((rows, 128)),
        pl.BlockSpec((1, 2, rows), lambda p: (p, 0, 0)),
        pl.BlockSpec((1, 128), lambda p: (0, p)),
    ]


def mixer_front_call(inputs, rows):
    f32 = jnp.float32
    tile, whole, specs = mixer_specs(rows)
    return pl.pallas_call(
        front_body,
        grid=(INNER // 128,),
        in_specs=specs,
        out_specs=[tile(lambda p: (0, p)), tile(lambda p: (0, p)), whole((rows, 128))],
        out_shape=[
            jax.ShapeDtypeStruct((rows, INNER), f32),
            jax.ShapeDtypeStruct((rows, INNER), f32),
            jax.ShapeDtypeStruct((rows, 128), f32),
        ],
        scratch_shapes=[pltpu.VMEM((rows, rows), f32), pltpu.VMEM((rows, 2 * STATE), jnp.bfloat16)],
        name="mixer_front",
        cost_estimate=pl.CostEstimate(flops=10**10, bytes_accessed=2 * 10**7, transcendentals=5 * 10**6),
    )(*inputs)


def mixer_back_call(inputs, extra, rows):
    f32, bf = jnp.float32, jnp.bfloat16
    tile, whole, specs = mixer_specs(rows)
    by_pair = tile(lambda p: (0, p))
    return pl.pallas_call(
        back_body,
        grid=(INNER // 128,),
        in_specs=specs
        + [by_pair, by_pair, pl.BlockSpec((1, 128), lambda p: (0, p)), whole((rows, 128)), whole((rows, 128))],
        out_specs=[
            by_pair, by_pair, pl.BlockSpec((8, 128), lambda p: (0, p)), whole((rows, 2 * STATE)),
            whole((8, 2 * STATE)), whole((rows, 128)), whole((64, rows)), whole((rows, 128)),
        ],
        out_shape=[
            jax.ShapeDtypeStruct((rows, INNER), bf),
            jax.ShapeDtypeStruct((rows, INNER), bf),
            jax.ShapeDtypeStruct((8, INNER), f32),
            jax.ShapeDtypeStruct((rows, 2 * STATE), bf),
            jax.ShapeDtypeStruct((8, 2 * STATE), f32),
            jax.ShapeDtypeStruct((rows, 128), f32),
            jax.ShapeDtypeStruct((64, rows), f32),
            jax.ShapeDtypeStruct((rows, 128), f32),
        ],
        scratch_shapes=[
            pltpu.VMEM((rows, rows), f32), pltpu.VMEM((rows, 2 * STATE), bf),
            pltpu.VMEM((rows, rows), f32), pltpu.VMEM((rows, 128), f32),
        ],
        name="mixer_back",
        cost_estimate=pl.CostEstimate(flops=3 * 10**10, bytes_accessed=3 * 10**7, transcendentals=5 * 10**6),
    )(*inputs, *extra)


def picks(slot_row, slots):
    rows = slot_row.shape[1]
    at = lax.broadcasted_iota(jnp.int32, (slots, rows), 0).astype(jnp.float32)
    return at == slot_row


def cot_chunk(cots, g):
    if g < 6:
        return cots[g][...]
    return jnp.concatenate([cots[2 * g - 6][...], cots[2 * g - 5][...]], axis=0)


def experts_body(x_ref, *refs):
    cots, refs = refs[:10], refs[10:]
    experts_step(x_ref, cots, *refs)


def experts_step(
    x_ref, cots, up, down, slot_rows, gates,
    y_out, gin_out, up_grad, down_grad, dots,
    xe, gy, gu_grad, hid, gate_cols,
):
    f32, bf = jnp.float32, jnp.bfloat16
    chunks, rows, width = x_ref.shape
    slots = xe.shape[0] // chunks
    hidden = down.shape[1]

    for g in range(chunks):
        p = picks(slot_rows[0, g : g + 1, :], slots)
        one = p.astype(bf)
        at = pl.ds(g * slots, slots)
        xe[at, :] = product(one, x_ref[g]).astype(bf)
        gate = jnp.sum(jnp.where(p, gates[0, g : g + 1, :], 0.0), axis=1, keepdims=True)
        gate_cols[at, :] = jnp.broadcast_to(gate, (slots, 128))
        gy[at, :] = (gate * product(one, cot_chunk(cots, g))).astype(bf)

    tile = 2 * slots

    @pl.loop(0, xe.shape[0] // tile)
    def _(t):
        at = pl.ds(pl.multiple_of(t * tile, tile), tile)
        gu = product(xe[at, :], up[0])
        a, b = gu[:, :hidden], gu[:, hidden:]
        s = sigmoid(a)
        silu = a * s
        h = (silu * b).astype(bf)
        hid[at, :] = h
        gh = product(gy[at, :], down[0], 1, 1)
        gu_grad[at, :hidden] = (gh * b * (s * (1.0 + a * (1.0 - s)))).astype(bf)
        gu_grad[at, hidden:] = (gh * silu).astype(bf)
        y = product(h, down[0]).astype(bf).astype(f32)
        dot = jnp.sum(y * gy[at, :].astype(f32), axis=1, keepdims=True)
        y_out[0, at, :] = (gate_cols[at, :1] * y).astype(bf)
        for i in range(2):
            p = picks(slot_rows[0, pl.ds(2 * t + i, 1), :], slots)
            dots[0, pl.ds(2 * t + i, 1), :] = jnp.sum(
                jnp.where(p, dot[i * slots : (i + 1) * slots, :], 0.0), axis=0, keepdims=True
            )
        gin_out[0, at, :] = product(gu_grad[at, :], up[0], 1, 1).astype(bf)

    for r in range(0, width, 256):
        up_grad[0, r : r + 256, :] = product(xe[:, r : r + 256], gu_grad[...], 0, 0).astype(bf)
    for r in range(0, hidden, 256):
        down_grad[0, r : r + 256, :] = product(hid[:, r : r + 256], gy[...], 0, 0).astype(bf)


def experts_call(x, cots, up, down, slot_rows, gates, slots):
    f32, bf = jnp.float32, jnp.bfloat16
    chunks, rows, width = x.shape
    held, _, double = up.shape
    total = chunks * slots
    once = pl.Buffered(1)
    each = lambda *shape: pl.BlockSpec((1,) + shape, lambda e: (e, 0, 0))
    keep = lambda *shape: pl.BlockSpec((1,) + shape, lambda e: (e, 0, 0), pipeline_mode=once)
    whole = pl.BlockSpec((chunks, rows, width), lambda e: (0, 0, 0), pipeline_mode=once)
    shape = lambda *s: jax.ShapeDtypeStruct((held,) + s, bf)
    return pl.pallas_call(
        experts_body,
        grid=(held,),
        in_specs=[
            whole, *[pl.BlockSpec(c.shape, lambda e: (0, 0), pipeline_mode=once) for c in cots], keep(width, double), keep(double // 2, width), each(chunks, rows), each(chunks, rows),
        ],
        out_specs=[
            each(total, width), each(total, width), each(width, double), each(double // 2, width), each(chunks, rows),
        ],
        out_shape=[
            shape(total, width), shape(total, width), shape(width, double), shape(double // 2, width),
            jax.ShapeDtypeStruct((held, chunks, rows), f32),
        ],
        scratch_shapes=[
            pltpu.VMEM((total, width), bf), pltpu.VMEM((total, width), bf), pltpu.VMEM((total, double), bf),
            pltpu.VMEM((total, double // 2), bf), pltpu.VMEM((total, 128), f32),
        ],
        name="experts",
        compiler_params=pltpu.CompilerParams(vmem_limit_bytes=62 << 20),
        cost_estimate=pl.CostEstimate(flops=4 * 10**10, bytes_accessed=5 * 10**7, transcendentals=10**6),
    )(x, *cots, up, down, slot_rows, gates)


def join_body(where, x_ref, *refs):
    cots, refs = refs[:10], refs[10:]
    join_step(x_ref, cots, *refs)


def join_step(
    x_ref, cots, y_ref, gin_ref, slot_rows, up, down,
    y_part, g_part, up_grad, down_grad, up_acc, down_acc, cot_ref,
):
    f32, bf = jnp.float32, jnp.bfloat16
    g = pl.program_id(0)

    @pl.when(g == 0)
    def _():
        up_acc[...] = jnp.zeros_like(up_acc)
        down_acc[...] = jnp.zeros_like(down_acc)

    for k in range(8):

        @pl.when(g == k)
        def _(k=k):
            cot_ref[...] = cot_chunk(cots, k)

    x, cot = x_ref[0], cot_ref[...]
    half = down.shape[0]
    gu = product(x, up[...])
    a, b = gu[:, :half], gu[:, half:]
    s = sigmoid(a)
    silu = a * s
    h = (silu * b).astype(bf)
    gh = product(cot, down[...], 1, 1)
    gu_grad = jnp.concatenate(
        [gh * b * (s * (1.0 + a * (1.0 - s))), gh * silu], axis=1
    ).astype(bf)
    up_acc[...] += product(x, gu_grad, 0, 0)
    down_acc[...] += product(h, cot, 0, 0)
    y = product(h, down[...])
    gx = product(gu_grad, up[...], 1, 1)
    for e in range(y_ref.shape[0]):
        one = picks(slot_rows[e, pl.ds(g, 1), :], y_ref.shape[1]).astype(bf)
        y = y + product(one, y_ref[e], 0, 0)
        gx = gx + product(one, gin_ref[e], 0, 0)
    y_part[0] = y.astype(bf)
    g_part[0] = gx.astype(bf)

    @pl.when(g == pl.num_programs(0) - 1)
    def _():
        up_grad[...] = up_acc[...].astype(bf)
        down_grad[...] = down_acc[...].astype(bf)


def join_call(where, x, cots, y, gin, slot_rows, up, down, slots):
    f32, bf = jnp.float32, jnp.bfloat16
    chunks, rows, width = x.shape
    held = y.shape[0]
    chunk = pl.BlockSpec((1, rows, width), lambda g, w: (g, 0, 0))
    placed = pl.BlockSpec((1, rows, width), lambda g, w: (g ^ w[0], 0, 0))
    rows_of = pl.BlockSpec((held, slots, width), lambda g, w: (0, g, 0))
    whole = lambda a: pl.BlockSpec(a.shape, lambda g, w: (0,) * a.ndim)
    return pl.pallas_call(
        join_body,
        grid_spec=pltpu.PrefetchScalarGridSpec(
            num_scalar_prefetch=1,
            grid=(chunks,),
            in_specs=[chunk, *[whole(c) for c in cots], rows_of, rows_of, whole(slot_rows), whole(up), whole(down)],
            out_specs=[placed, chunk, whole(up), whole(down)],
            scratch_shapes=[
                pltpu.VMEM(up.shape, f32), pltpu.VMEM(down.shape, f32), pltpu.VMEM((rows, width), bf),
            ],
        ),
        out_shape=[
            jax.ShapeDtypeStruct(x.shape, bf), jax.ShapeDtypeStruct(x.shape, bf),
            jax.ShapeDtypeStruct(up.shape, bf), jax.ShapeDtypeStruct(down.shape, bf),
        ],
        name="join",
        compiler_params=pltpu.CompilerParams(vmem_limit_bytes=48 << 20),
        cost_estimate=pl.CostEstimate(flops=10**10, bytes_accessed=4 * 10**7, transcendentals=10**6),
    )(where, x, *cots, y, gin, slot_rows, up, down)


def local_fast(
    tokens, lengths, routes, cotangent, norm_gain, in_weight, conv_weight, conv_bias, dt_bias,
    a_log, d_skip, mix_gain, out_weight, ffn_gain, router_weight, shared_up, shared_down,
    expert_up, expert_down,
):
    bf, f32 = jnp.bfloat16, jnp.float32
    block = tokens.shape[1]
    parts = tokens.shape[0]
    rows = block * parts
    groups = lax.axis_size("dp")
    lines = lax.axis_size("seq")
    held = expert_up.shape[0]
    experts = held * groups
    top = routes.shape[2]
    slots = block * top * 5 // (4 * experts) * parts
    slots = -(-slots // 128) * 128
    place = lax.axis_index("seq")
    group = lax.axis_index("dp")

    def to(a, bit):
        return lax.ppermute(a, "dp", [(i, i ^ bit) for i in range(groups)])

    pad = lambda a, n: jnp.pad(a, ((0, 0), (0, n - a.shape[1])))
    in_blocks, router_blocks, out_blocks, down_line, up_line, x_low, route = gather_rows(
        [in_weight, pad(router_weight, 128), out_weight],
        [in_weight.shape[0] // 3, router_weight.shape[0], out_weight.shape[0] // 2, shared_down.shape[0],
         shared_up.shape[0]],
        [shared_down, shared_up], lines, 2, [tokens, routes], False, 1,
    )
    out_full = out_blocks.reshape(-1, MODEL_WIDTH)
    in_full = in_blocks.reshape(MODEL_WIDTH, -1)
    router_full = router_blocks.reshape(MODEL_WIDTH, -1)[:, :experts]
    down_part = down_line.reshape(-1, MODEL_WIDTH)
    in_full, late_cot = lax.optimization_barrier((in_full, cotangent))
    cot_low = lax.all_to_all(late_cot, "seq", split_axis=0, concat_axis=0, tiled=True)
    width = SFF // groups
    up_cols = up_line.reshape(-1, 2, groups, width).transpose(2, 0, 1, 3).reshape(groups, -1, 2 * width)

    length = lax.dynamic_index_in_dim(lengths, place, 0, False)
    x_low = x_low.reshape(rows, MODEL_WIDTH)
    cot_low = cot_low.reshape(rows, MODEL_WIDTH)
    cotangent_rows = cot_low
    route = route.reshape(rows, top)
    used = jnp.arange(rows) < length
    valid = used.astype(f32)[:, None]
    x_rows = x_low.astype(f32)
    normed, norm_pull = jax.vjp(rms_norm, x_rows, norm_gain)
    normed_low = normed.astype(bf)
    projected = jnp.dot(normed_low, in_full, preferred_element_type=f32).astype(bf)
    before_step = projected[:, INNER + CONV :].astype(f32) + dt_bias
    steps = jax.nn.softplus(before_step)
    rates = -steps * jnp.exp(a_log)
    lower = (jnp.arange(rows)[:, None] >= jnp.arange(rows)[None, :]).astype(f32)
    cumulative = jnp.dot(lower, rates, precision=PRECISE)
    wide = lambda a: jnp.broadcast_to(a[:, :, None], a.shape + (HDIM,)).reshape(a.shape[0], -1)
    lanes = lambda a: jnp.broadcast_to(a, (rows, 128))
    mixer_in = (
        projected, projected, projected, conv_weight, conv_bias[None], conv_weight, conv_bias[None],
        lanes(valid), pad(steps, 128), pad(cumulative, 128), cumulative.T.reshape(HEADS // 2, 2, rows),
        wide(d_skip[None]),
    )
    cot_low = jnp.where(used[:, None], cot_low, 0)
    first_in, cot_own = lax.optimization_barrier((mixer_in[0], cot_low))
    cut = rows // 2
    cot_x, cot_y = to(cot_own, 2), to(cot_own, 4)
    mixed, gated, squares = mixer_front_call((first_in,) + mixer_in[1:], rows)
    gated, cot_x, cot_y, up_cols = lax.optimization_barrier((gated, cot_x, cot_y, up_cols))
    up_part = lax.all_to_all(up_cols, "dp", split_axis=0, concat_axis=0, tiled=True)
    up_part = up_part.reshape(MODEL_WIDTH, 2 * width)
    cot_far = (to(cot_x[:cut], 4), to(cot_y[cut:], 2))
    cot_core = [to(a, 1) for a in (cot_own, cot_x, cot_y)]
    scale = lax.rsqrt(jnp.sum(squares, axis=1, keepdims=True) / INNER + EPSILON)
    mix_low = (gated * scale * mix_gain).astype(bf)
    mixer_out = jnp.dot(mix_low, out_full, preferred_element_type=f32)
    hidden = x_rows + mixer_out * valid
    normed_ffn, ffn_pull = jax.vjp(rms_norm, hidden, ffn_gain)
    ffn_low = normed_ffn.astype(bf)
    logits = jnp.dot(ffn_low, router_full, preferred_element_type=f32)
    onehot = (route[:, :, None] == jnp.arange(experts)[None, None, :]).astype(f32)
    chosen = jnp.sum(onehot, axis=1)
    peak = jnp.max(jnp.where(chosen > 0, logits, -jnp.inf), axis=1, keepdims=True)
    raised = jnp.exp(jnp.where(chosen > 0, logits - peak, -jnp.inf))
    probs = raised / jnp.sum(raised, axis=1, keepdims=True)

    ffn_low, cot_far, cot_core = lax.optimization_barrier((ffn_low, cot_far, cot_core))
    cot_far_core = tuple(to(a, 1) for a in cot_far)
    all_rows, all_probs = gather_rows(
        [ffn_low, pad(probs * valid, 128)], [64, rows], [], 1, 2, [], True, 2
    )
    all_rows = all_rows[:, 0]
    all_cot = [cot_own, cot_core[0], cot_x, cot_core[1], cot_y, cot_core[2], *cot_far, *cot_far_core]
    mine = group * held + jnp.arange(held)
    gates = lax.dynamic_slice_in_dim(all_probs[:, 0], group * held, held, 2).transpose(2, 0, 1)
    member = gates > 0
    earlier = (jnp.arange(rows)[:, None] < jnp.arange(rows)[None, :]).astype(bf)
    before = jnp.einsum("egt,ts->egs", member.astype(bf), earlier, preferred_element_type=f32)
    slot_rows = jnp.where(member, before, -1.0)
    y_slots, gin_slots, grad_eup, grad_edown, dots = experts_call(
        all_rows, all_cot, expert_up, expert_down, slot_rows, gates, slots
    )
    y_part, g_part, grad_sup, grad_sdown = join_call(
        group.reshape(1), all_rows, all_cot, y_slots, gin_slots, slot_rows, up_part, down_part, slots
    )
    at_own = (jnp.arange(experts)[None, :] == mine[:, None]).astype(f32)
    dots = jnp.einsum("egt,ef->gtf", dots, at_own, precision=PRECISE).reshape(-1, experts)
    dots_hi = dots.astype(bf)
    dots_lo = (dots - dots_hi.astype(f32)).astype(bf)
    g_sum, dots = sum_to_owners(
        [g_part.reshape(-1, MODEL_WIDTH), pad(jnp.concatenate([dots_hi, dots_lo], axis=1), 128)],
        [384, 128], 1, [MODEL_WIDTH, 128], None, [], (True, True), 3,
    )
    dots = dots[:, :experts] + dots[:, experts : 2 * experts]
    g_sum, y_part = lax.optimization_barrier((g_sum, y_part))
    y_part = lax.all_to_all(y_part, "dp", split_axis=0, concat_axis=0, tiled=True)
    grad_out = cotangent_rows.astype(f32)
    grad_logit = (dots - probs * jnp.sum(dots, axis=1, keepdims=True)).astype(bf)
    grad_router = contract_rows(ffn_low, grad_logit)
    grad_ffn = g_sum + contract_cols(grad_logit, router_full)
    grad_hidden, grad_fgain = ffn_pull(grad_ffn)
    grad_hidden = grad_hidden + grad_out
    grad_mo = (grad_hidden * valid).astype(bf)
    grad_outw = contract_rows(mix_low, grad_mo).astype(bf)
    grad_mix = contract_cols(grad_mo, out_full)
    mean_dot = jnp.sum(grad_mo.astype(f32) * mixer_out, axis=1, keepdims=True) / INNER
    grad_z, grad_in, stats, grad_bc, bc_stats, row_sums, col_sums, step_sums = mixer_back_call(
        mixer_in, (mixed, grad_mix, mix_gain[None], lanes(scale), lanes(mean_dot)), rows
    )
    grad_z, y_part, grad_sup, grad_sdown = lax.optimization_barrier((grad_z, y_part, grad_sup, grad_sdown))
    y_sum = jnp.sum(y_part.astype(f32), axis=0)
    output = (hidden + valid * y_sum).astype(bf).reshape(tokens.shape)

    grad_rates = jnp.dot(lower.T, row_sums[:, :HEADS] - col_sums[:HEADS].T, precision=PRECISE)
    grad_raw = (step_sums[:, :HEADS] - grad_rates * jnp.exp(a_log)) * jax.nn.sigmoid(before_step)
    grad_al = jnp.sum(grad_rates * rates, axis=0)
    grad_db = jnp.sum(grad_raw, axis=0)
    grad_skip = jnp.sum(stats[1].reshape(HEADS, HDIM), axis=1)
    grad_proj = jnp.concatenate([grad_z, grad_in, grad_bc, grad_raw.astype(bf)], axis=1)
    spare = -PROJ % 128
    grad_inw = contract_rows(normed_low, pad(grad_proj, PROJ + spare)).astype(bf)
    grad_x, grad_ngain = norm_pull(contract_cols(grad_proj, in_full))
    input_grad = (grad_x + grad_hidden).astype(bf)
    grad_router = contract_rows(ffn_low, pad(grad_logit, 128)).astype(bf)

    heads = jnp.pad(jnp.stack([grad_db, grad_al, grad_skip]), ((0, 5), (0, 256 - HEADS)))
    gains = jnp.pad(jnp.stack([grad_ngain, grad_fgain]), ((0, 6), (0, 0)))
    own_out, own_in, own_router, output, input_grad, sdown, conv_w, conv_b, mix_g, norm_g, ffn_g, heads = sum_to_owners(
        [grad_outw, grad_inw, grad_router], [512, 768, 128], lines, [MODEL_WIDTH, PROJ, experts],
        [stats, bc_stats, gains, heads], [output, input_grad.reshape(tokens.shape), grad_sdown.reshape(lines, -1, MODEL_WIDTH)],
        (False, False, False), 4,
    )
    along = lambda g, d: lax.psum_scatter(g.astype(bf), "seq", scatter_dimension=d, tiled=True)
    sup = lax.all_to_all(
        grad_sup.reshape(groups * lines, -1, 2 * width), ("dp", "seq"), split_axis=0, concat_axis=0, tiled=True
    ).astype(f32)
    sup = jnp.sum(sup.reshape(groups, lines, -1, 2 * width), axis=1)
    sup = sup.reshape(groups, -1, 2, width).transpose(1, 2, 0, 3).reshape(-1, 2 * SFF)
    sdown = jnp.sum(sdown.astype(f32), axis=0)
    return (
        output, input_grad, norm_g[0], own_in, conv_w, conv_b[0], heads[0, :HEADS], heads[1, :HEADS],
        heads[2, :HEADS], mix_g[0], own_out, ffn_g[0], own_router, sup, sdown,
        along(grad_eup, 1).astype(f32), along(grad_edown, 1).astype(f32),
    )


def solution(mesh):
    def program(*arrays):
        each = arrays[0].shape[0] == lax.axis_size("seq") == 4 and lax.axis_size("dp") == 8
        return (local_fast if each else local)(*arrays)

    return jax.shard_map(
        program,
        mesh=mesh,
        in_specs=(
            P("dp", "seq", None),
            P("dp"),
            P("dp", "seq", None),
            P("dp", "seq", None),
            P(),
            P(("dp", "seq"), None),
            P(),
            P(),
            P(),
            P(),
            P(),
            P(),
            P(("dp", "seq"), None),
            P(),
            P(("dp", "seq"), None),
            P(("dp", "seq"), None),
            P(("dp", "seq"), None),
            P("dp", None, None),
            P("dp", None, None),
        ),
        out_specs=(
            P("dp", "seq", None),
            P("dp", "seq", None),
            P(),
            P(("dp", "seq"), None),
            P(),
            P(),
            P(),
            P(),
            P(),
            P(),
            P(("dp", "seq"), None),
            P(),
            P(("dp", "seq"), None),
            P(("dp", "seq"), None),
            P(("dp", "seq"), None),
            P("dp", "seq", None),
            P("dp", "seq", None),
        ),
        check_vma=False,
    )
```

```python
from functools import partial

import jax
import jax.numpy as jnp
from jax import lax
from jax.experimental import pallas as pl
from jax.experimental.pallas import tpu as pltpu
from jax.sharding import PartitionSpec as P

MODEL_WIDTH = 1536
INNER = 3072
HEADS = 48
HDIM = 64
STATE = 128
KCONV = 4
EXPERT_HIDDEN = 512
SFF = 1024
MB = 4
CONV = 3328
PROJ = 6448


EPSILON = 1e-05
PRECISE = lax.Precision.HIGHEST
MESH = pl.DeviceIdType.MESH


def from_behind(x, axis, by):
    size = lax.axis_size(axis)
    pairs = [(i, i + by) for i in range(size) if 0 <= i + by < size]
    return lax.ppermute(x, axis, pairs)


def prefix(x, axis, join, neutral):
    place = lax.axis_index(axis)
    gathered = jax.tree.map(
        lambda a, kind: lax.all_gather(a.astype(kind), axis), x, (jnp.bfloat16, jnp.bfloat16)
    )
    state = jax.tree.map(lambda a, e: jnp.zeros_like(a) + jnp.asarray(e, a.dtype), x, neutral)

    def one(step, state):
        return join(
            state,
            jax.tree.map(
                lambda a, own: lax.dynamic_index_in_dim(a, step, 0, False).astype(own.dtype),
                gathered,
                x,
            ),
        )

    return lax.fori_loop(0, place, one, state)


def prefix_2(x, axis, join, neutral):
    count = lax.axis_size(axis)
    place = lax.axis_index(axis)
    ahead = count - 1 - place
    gathered = jax.tree.map(
        lambda a, kind: lax.all_gather(a.astype(kind), axis),
        x,
        jax.tree.map(lambda a: jnp.bfloat16 if a.dtype == jnp.float32 else a.dtype, x),
    )
    state = jax.tree.map(lambda a, e: jnp.zeros_like(a) + jnp.asarray(e, a.dtype), x, neutral)

    def one(step, state):
        source = count - 1 - step
        return join(
            state,
            jax.tree.map(
                lambda a, own: lax.dynamic_index_in_dim(a, source, 0, False).astype(own.dtype),
                gathered,
                x,
            ),
        )

    return lax.fori_loop(0, ahead, one, state)


def rms_norm(values, gain_vec):
    return (
        values * lax.rsqrt(jnp.mean(values * values, axis=-1, keepdims=True) + EPSILON) * gain_vec
    )


def swiglu(values, half_width):
    return jax.nn.silu(values[..., :half_width]) * values[..., half_width:]


def contract_rows(left_mat, right_mat):
    return lax.dot_general(
        left_mat, right_mat, (((0,), (0,)), ((), ())), preferred_element_type=jnp.float32
    )


def contract_cols(left_mat, right_mat):
    return lax.dot_general(
        left_mat, right_mat, (((1,), (1,)), ((), ())), preferred_element_type=jnp.float32
    )


def block_terms(head_in, b_rows, c_rows, step_sizes, a_log):
    log_rates = -step_sizes * jnp.exp(a_log)
    cumulative = jnp.cumsum(log_rates, axis=0)
    block_len = head_in.shape[0]
    lower_tri = jnp.arange(block_len)[:, None] >= jnp.arange(block_len)[None, :]
    spread = jnp.where(
        lower_tri[:, :, None], cumulative[:, None, :] - cumulative[None, :, :], -jnp.inf
    )
    scores = jnp.dot(c_rows, b_rows.T, precision=PRECISE)
    weights = jnp.exp(spread) * scores[:, :, None] * step_sizes[None, :, :]
    local_out = jnp.einsum("tih,ihp->thp", weights, head_in, precision=PRECISE)
    tail_weight = jnp.exp(cumulative[-1][None, :] - cumulative) * step_sizes
    local_state = jnp.einsum("ih,ihp,in->hpn", tail_weight, head_in, b_rows, precision=PRECISE)
    return (cumulative, local_out, local_state, jnp.exp(cumulative[-1]))


def carried_out(c_rows, cumulative, state_in):
    return (
        jnp.einsum("tn,hpn->thp", c_rows, state_in, precision=PRECISE)
        * jnp.exp(cumulative)[:, :, None]
    )


def mixer_front(valid_rows, projected, previous, conv_weight, conv_bias, dt_bias, a_log):
    row_count = projected.shape[0]
    conv_in = projected[:, INNER : INNER + CONV]
    padded = jnp.concatenate([previous, conv_in], axis=0)
    conv_sum = conv_bias + conv_weight[0] * padded[0:row_count]
    for tap_idx in range(1, KCONV):
        conv_sum = conv_sum + conv_weight[tap_idx] * padded[tap_idx : tap_idx + row_count]
    activated = jax.nn.silu(conv_sum) * valid_rows
    head_in = activated[:, :INNER].reshape(row_count, HEADS, HDIM)
    b_rows = activated[:, INNER : INNER + STATE]
    c_rows = activated[:, INNER + STATE :]
    step_sizes = jax.nn.softplus(projected[:, INNER + CONV :] + dt_bias)
    cumulative, local_out, local_state, decay_total = block_terms(
        head_in, b_rows, c_rows, step_sizes, a_log
    )
    return (projected[:, :INNER], head_in, c_rows, cumulative, local_out, local_state, decay_total)


def mixer_tail(gate_z, head_in, c_rows, cumulative, local_out, state_in, d_skip, mix_gain):
    mixed_out = local_out + carried_out(c_rows, cumulative, state_in) + d_skip[:, None] * head_in
    gated_out = mixed_out.reshape(head_in.shape[0], INNER) * jax.nn.silu(gate_z)
    return rms_norm(gated_out, mix_gain)


def link_states(earlier, latter):
    return (earlier[0] * latter[0], latter[1] + latter[0][:, None, None] * earlier[1])


def local(
    tokens,
    lengths,
    routes,
    cotangent,
    norm_gain,
    in_weight,
    conv_weight,
    conv_bias,
    dt_bias,
    a_log,
    d_skip,
    mix_gain,
    out_weight,
    ffn_gain,
    router_weight,
    shared_up,
    shared_down,
    expert_up,
    expert_down,
):
    row_count = tokens.shape[1]
    resident_experts = expert_up.shape[0]
    groups = lax.axis_size("dp")
    experts = resident_experts * groups
    top_count = routes.shape[2]
    capacity = row_count * top_count * 5 // (4 * experts)
    shards = (in_weight, out_weight, router_weight, shared_up, shared_down)
    kept_full = (
        lax.all_gather(shards[0], ("dp", "seq"), axis=0, tiled=True),
        lax.all_gather(shards[1], ("dp", "seq"), axis=0, tiled=True),
        lax.all_gather(shards[2], ("dp", "seq"), axis=0, tiled=True),
        lax.all_gather(shards[3], ("dp", "seq"), axis=0, tiled=True),
        lax.all_gather(shards[4], ("dp", "seq"), axis=0, tiled=True),
    )
    grad_inw = jnp.zeros((MODEL_WIDTH, PROJ), jnp.float32)
    grad_outw = jnp.zeros((INNER, MODEL_WIDTH), jnp.float32)
    grad_router = jnp.zeros((MODEL_WIDTH, experts), jnp.float32)
    grad_sup = jnp.zeros((MODEL_WIDTH, 2 * SFF), jnp.float32)
    grad_sdown = jnp.zeros((SFF, MODEL_WIDTH), jnp.float32)
    expert_upward_grad = jnp.zeros((resident_experts, MODEL_WIDTH, 2 * EXPERT_HIDDEN), jnp.float32)
    grad_edown = jnp.zeros((resident_experts, EXPERT_HIDDEN, MODEL_WIDTH), jnp.float32)
    grad_ngain = jnp.zeros_like(norm_gain)
    grad_cw = jnp.zeros_like(conv_weight)
    grad_cb = jnp.zeros_like(conv_bias)
    grad_db = jnp.zeros_like(dt_bias)
    grad_al = jnp.zeros_like(a_log)
    grad_skip = jnp.zeros_like(d_skip)
    grad_mgain = jnp.zeros_like(mix_gain)
    grad_fgain = jnp.zeros_like(ffn_gain)
    outputs = []
    input_grads = []
    for micro_idx in range(MB):
        in_full, out_full, router_full, up_full, down_full = kept_full
        x_rows = tokens[micro_idx].astype(jnp.float32)
        position = lax.axis_index("seq") * row_count + jnp.arange(row_count)
        valid_rows = (position < lengths[micro_idx]).astype(jnp.float32)[:, None]
        normed, norm_pull = jax.vjp(rms_norm, x_rows, norm_gain)
        normed_low = normed.astype(jnp.bfloat16)
        projected = jnp.dot(normed_low, in_full, preferred_element_type=jnp.float32).astype(
            jnp.bfloat16
        )
        previous = from_behind(projected[row_count - (KCONV - 1) :, INNER : INNER + CONV], "seq", 1)
        front_out, front_pull = jax.vjp(
            partial(mixer_front, valid_rows),
            projected.astype(jnp.float32),
            previous.astype(jnp.float32),
            conv_weight,
            conv_bias,
            dt_bias,
            a_log,
        )
        gate_z, head_in, c_rows, cumulative, local_out, local_state, decay_total = front_out
        identity = (jnp.ones_like(decay_total), jnp.zeros_like(local_state))
        _, state_in = prefix((decay_total, local_state), "seq", link_states, identity)
        normed_mix, tail_pull = jax.vjp(
            mixer_tail, gate_z, head_in, c_rows, cumulative, local_out, state_in, d_skip, mix_gain
        )
        mix_low = normed_mix.astype(jnp.bfloat16)
        mixer_out = jnp.dot(mix_low, out_full, preferred_element_type=jnp.float32)
        hidden = x_rows + mixer_out * valid_rows
        normed_ffn, ffn_pull = jax.vjp(rms_norm, hidden, ffn_gain)
        ffn_low = normed_ffn.astype(jnp.bfloat16)
        logits = jnp.dot(ffn_low, router_full, preferred_element_type=jnp.float32)
        route_row = routes[micro_idx]
        picked = jnp.take_along_axis(logits, route_row, axis=1)
        gate_probs = jax.nn.softmax(picked, axis=-1)
        shared_gu = jnp.dot(ffn_low, up_full, preferred_element_type=jnp.float32)
        shared_act, shared_pull = jax.vjp(partial(swiglu, half_width=SFF), shared_gu)
        shared_h = shared_act.astype(jnp.bfloat16)
        shared_y = jnp.dot(shared_h, down_full, preferred_element_type=jnp.float32)
        flat_route = route_row.reshape(-1)
        member = (flat_route[:, None] == jnp.arange(experts)[None, :]).astype(jnp.int32)
        slot_pos = jnp.sum((jnp.cumsum(member, axis=0) - member) * member, axis=1)
        target = flat_route * capacity + slot_pos
        source = (
            jnp.zeros((experts * capacity,), jnp.int32)
            .at[target]
            .set(jnp.arange(row_count * top_count, dtype=jnp.int32))
        )
        filled = jnp.zeros((experts * capacity, 1), jnp.bfloat16).at[target].set(jnp.bfloat16(1))
        outgoing = (jnp.take(ffn_low, source // top_count, axis=0) * filled).reshape(
            groups, resident_experts, capacity, MODEL_WIDTH
        )
        received_rows = lax.all_to_all(outgoing, "dp", split_axis=0, concat_axis=2, tiled=True)[0]
        expert_gu = jnp.einsum(
            "erd,edf->erf", received_rows, expert_up, preferred_element_type=jnp.float32
        )
        expert_act, expert_pull = jax.vjp(partial(swiglu, half_width=EXPERT_HIDDEN), expert_gu)
        expert_h = expert_act.astype(jnp.bfloat16)
        expert_y = jnp.einsum(
            "erf,efd->erd", expert_h, expert_down, preferred_element_type=jnp.float32
        ).astype(jnp.bfloat16)
        returned = lax.all_to_all(expert_y[None], "dp", split_axis=2, concat_axis=0, tiled=True)
        per_choice = (
            jnp.take(returned.reshape(experts * capacity, MODEL_WIDTH), target, axis=0)
            .reshape(row_count, top_count, MODEL_WIDTH)
            .astype(jnp.float32)
        )
        routed = jnp.einsum("lk,lkd->ld", gate_probs, per_choice, precision=PRECISE)
        outputs.append((hidden + valid_rows * (shared_y + routed)).astype(jnp.bfloat16))
        in_back, out_back, router_back, up_back, down_back = kept_full
        grad_out = cotangent[micro_idx].astype(jnp.float32)
        branch = valid_rows * grad_out
        shared_g = branch.astype(jnp.bfloat16)
        grad_sdown = grad_sdown + contract_rows(shared_h, shared_g)
        grad_sgu = shared_pull(contract_cols(shared_g, down_back))[0].astype(jnp.bfloat16)
        grad_sup = grad_sup + contract_rows(ffn_low, grad_sgu)
        grad_ffn = contract_cols(grad_sgu, up_back)
        grad_choice = (gate_probs[:, :, None] * branch[:, None, :]).astype(jnp.bfloat16)
        grad_gate = jnp.sum(branch[:, None, :] * per_choice, axis=-1)
        grad_pick = gate_probs * (
            grad_gate - jnp.sum(gate_probs * grad_gate, axis=-1, keepdims=True)
        )
        onehot = (route_row[:, :, None] == jnp.arange(experts)[None, None, :]).astype(jnp.float32)
        grad_logit = jnp.einsum("lk,lke->le", grad_pick, onehot, precision=PRECISE).astype(
            jnp.bfloat16
        )
        grad_router = grad_router + contract_rows(ffn_low, grad_logit)
        grad_ffn = grad_ffn + contract_cols(grad_logit, router_back)
        back_out = (
            jnp.take(grad_choice.reshape(row_count * top_count, MODEL_WIDTH), source, axis=0)
            * filled
        ).reshape(groups, resident_experts, capacity, MODEL_WIDTH)
        grad_arrived = lax.all_to_all(back_out, "dp", split_axis=0, concat_axis=2, tiled=True)[0]
        step_edown = jnp.einsum(
            "erf,erd->efd", expert_h, grad_arrived, preferred_element_type=jnp.float32
        )
        grad_eh = jnp.einsum(
            "erd,efd->erf", grad_arrived, expert_down, preferred_element_type=jnp.float32
        )
        expert_gate_up_grad = expert_pull(grad_eh)[0].astype(jnp.bfloat16)
        expert_upward_step = jnp.einsum(
            "tbw,tbj->twj", received_rows, expert_gate_up_grad, preferred_element_type=jnp.float32
        )
        grad_ein = jnp.einsum(
            "erf,edf->erd", expert_gate_up_grad, expert_up, preferred_element_type=jnp.float32
        ).astype(jnp.bfloat16)
        expert_upward_grad = expert_upward_grad + expert_upward_step
        grad_edown = grad_edown + step_edown
        came_back = lax.all_to_all(grad_ein[None], "dp", split_axis=2, concat_axis=0, tiled=True)
        grad_ffn = grad_ffn + jnp.sum(
            jnp.take(came_back.reshape(experts * capacity, MODEL_WIDTH), target, axis=0)
            .reshape(row_count, top_count, MODEL_WIDTH)
            .astype(jnp.float32),
            axis=1,
        )
        grad_hidden, step_fgain = ffn_pull(grad_ffn)
        grad_fgain = grad_fgain + step_fgain
        grad_hidden = grad_hidden + grad_out
        grad_mix_out = (grad_hidden * valid_rows).astype(jnp.bfloat16)
        grad_outw = grad_outw + contract_rows(mix_low, grad_mix_out)
        grad_mix = contract_cols(grad_mix_out, out_back)
        grad_z, grad_head, grad_c, grad_cum, grad_local, grad_state, step_skip, step_mgain = (
            tail_pull(grad_mix)
        )
        grad_skip = grad_skip + step_skip
        grad_mgain = grad_mgain + step_mgain
        _, grad_carry = prefix_2((decay_total, grad_state), "seq", link_states, identity)
        grad_decay = jnp.sum(grad_carry * state_in, axis=(1, 2))
        grad_proj, grad_prev, step_cw, step_cb, step_db, step_al = front_pull(
            (grad_z, grad_head, grad_c, grad_cum, grad_local, grad_carry, grad_decay)
        )
        grad_cw = grad_cw + step_cw
        grad_cb = grad_cb + step_cb
        grad_db = grad_db + step_db
        grad_al = grad_al + step_al
        from_next = from_behind(grad_prev.astype(jnp.bfloat16), "seq", -1).astype(grad_prev.dtype)
        grad_proj = (
            grad_proj.at[row_count - (KCONV - 1) :, INNER : INNER + CONV]
            .add(from_next)
            .astype(jnp.bfloat16)
        )
        grad_inw = grad_inw + contract_rows(normed_low, grad_proj)
        grad_normed = contract_cols(grad_proj, in_back)
        grad_x, step_ngain = norm_pull(grad_normed)
        grad_ngain = grad_ngain + step_ngain
        input_grads.append((grad_x + grad_hidden).astype(jnp.bfloat16))
    weight_grads = (
        lax.psum_scatter(grad_inw, ("dp", "seq"), scatter_dimension=0, tiled=True),
        lax.psum_scatter(grad_outw, ("dp", "seq"), scatter_dimension=0, tiled=True),
        lax.psum_scatter(grad_router, ("dp", "seq"), scatter_dimension=0, tiled=True),
        lax.psum_scatter(grad_sup, ("dp", "seq"), scatter_dimension=0, tiled=True),
        lax.psum_scatter(grad_sdown, ("dp", "seq"), scatter_dimension=0, tiled=True),
    )
    small_sums = lax.psum(
        (grad_ngain, grad_cw, grad_cb, grad_db, grad_al, grad_skip, grad_mgain, grad_fgain),
        ("dp", "seq"),
    )
    expert_sums = (
        lax.psum_scatter(
            expert_upward_grad.astype(jnp.bfloat16), "seq", scatter_dimension=1, tiled=True
        ).astype(jnp.float32),
        lax.psum_scatter(
            grad_edown.astype(jnp.bfloat16), "seq", scatter_dimension=1, tiled=True
        ).astype(jnp.float32),
    )
    return (
        jnp.stack(outputs),
        jnp.stack(input_grads),
        small_sums[0],
        weight_grads[0],
        small_sums[1],
        small_sums[2],
        small_sums[3],
        small_sums[4],
        small_sums[5],
        small_sums[6],
        weight_grads[1],
        small_sums[7],
        weight_grads[2],
        weight_grads[3],
        weight_grads[4],
        expert_sums[0],
        expert_sums[1],
    )


def at_neighbours():
    d = lax.axis_index("dp")
    core, x, y = d % 2, (d // 2) % 2, d // 4
    return d, core, x, y, d + 1 - 2 * core, d + 2 - 4 * x, d + 4 - 8 * y


def meet(devices):
    barrier = pltpu.get_barrier_semaphore()
    for there in devices:
        pl.semaphore_signal(barrier, inc=1, device_id=there, device_id_type=MESH)
    pl.semaphore_wait(barrier, len(devices))


def send(source, target, send_sem, recv_sem, there):
    copy = pltpu.make_async_remote_copy(
        src_ref=source, dst_ref=target, send_sem=send_sem, recv_sem=recv_sem,
        device_id=there, device_id_type=MESH,
    )
    copy.start()
    return copy


def add_into(target, source, high):
    step = 16
    for s in (64, 48, 32):
        if high % s == 0:
            step = s
            break

    @pl.loop(0, high // step)
    def _(i):
        rows = pl.ds(pl.multiple_of(i * step, step), step)
        target[rows, :] = target[rows, :] + source[rows, :]


def swap_start(swaps, landed, line, lines, local_sem, send_sem, recv_sem):
    copies = []
    for n, (a, b) in enumerate(zip(swaps, landed)):
        keep = pltpu.make_async_copy(a.at[line], b.at[line], local_sem.at[n])
        keep.start()
        away = [
            send(a.at[o], b.at[line], send_sem.at[n, k], recv_sem.at[n, k], {"seq": o})
            for k, o in enumerate(lax.rem(line + k, lines) for k in range(1, lines))
        ]
        copies.append((keep, away))
    return copies


def swap_end(copies):
    for keep, away in copies:
        for copy in away:
            copy.wait_recv()
    for keep, away in copies:
        for copy in away:
            copy.wait_send()
        keep.wait()


def swap_sems(count, lines):
    dma = pltpu.SemaphoreType.DMA
    return [dma((count,)), dma((count, lines - 1)), dma((count, lines - 1))]


def sum_body(items, arrays, lines, tiny, moved, relative, *refs):
    count = len(items)
    grads, refs = refs[:arrays], refs[arrays:]
    swaps, refs = refs[:moved], refs[moved:]
    if tiny:
        small_in, refs = refs[:4], refs[4:]
    outs, refs = refs[:arrays], refs[arrays:]
    landed, refs = refs[:moved], refs[moved:]
    if tiny:
        small_out, refs = refs[:6], refs[6:]
    own, refs = refs[:count], refs[count:]
    got, refs = refs[:count], refs[count:]
    from_x, refs = refs[:count], refs[count:]
    from_y, refs = refs[:count], refs[count:]
    last_x, refs = refs[:count], refs[count:]
    last_y, refs = refs[:count], refs[count:]
    if lines > 1:
        from_z, refs = refs[:count], refs[count:]
    (load_sem, send_sem, recv_sem), refs = refs[:3], refs[3:]
    if moved:
        swap_sem, refs = refs[:3], refs[3:]
    if tiny:
        packed, half, t_core, t_x, t_y, t_z, t_back, t_send, t_recv = refs
    d, core, x, y, at_core, at_x, at_y = at_neighbours()
    bits = [(0, 0, 0) if own else (core, x, y) for own in relative]
    own_core = core
    line = lax.axis_index("seq")
    others = [lax.rem(line + k, lines) for k in range(1, lines)]
    beside, across = line + 1 - 2 * (line % 2), lax.rem(line + 2, 4)
    meet([{"dp": at_core}, {"dp": at_x}, {"dp": at_y}] + [{"seq": o} for o in others])
    sent = [[] for _ in items]
    stage = [None] * count
    cross = [None] * count
    close = [None] * count
    along = [None] * count
    loads = [None] * count

    def begin(t):
        a, c0, wide, high = items[t]
        core, x, y = bits[a]
        cols = pl.ds(c0, wide)
        loads[t] = pltpu.make_async_copy(grads[a].at[:, :, core, :, cols], own[t], load_sem.at[t])
        loads[t].start()
        stage[t] = send(
            grads[a].at[:, :, 1 - core, :, cols], got[t], send_sem.at[t, 0], recv_sem.at[t, 0], {"dp": at_core}
        )

    def fold(t):
        a, c0, wide, high = items[t]
        core, x, y = bits[a]
        loads[t].wait()
        stage[t].wait_recv()
        for i in range(2):
            for j in range(2):
                add_into(got[t].at[i, j], own[t].at[i, j], high)
        top, low = pl.ds(0, high // 2), pl.ds(high // 2, high // 2)
        cross[t] = (
            send(got[t].at[:, 1 - x, top, :], from_x[t], send_sem.at[t, 1], recv_sem.at[t, 1], {"dp": at_x}),
            send(got[t].at[1 - y, :, low, :], from_y[t], send_sem.at[t, 2], recv_sem.at[t, 2], {"dp": at_y}),
        )

    def turn(t):
        a, c0, wide, high = items[t]
        core, x, y = bits[a]
        top, low = pl.ds(0, high // 2), pl.ds(high // 2, high // 2)
        cross[t][0].wait_recv()
        for i in range(2):
            add_into(got[t].at[i, x, top, :], from_x[t].at[i], high // 2)
        close_y = send(got[t].at[1 - y, x, top, :], last_y[t], send_sem.at[t, 3], recv_sem.at[t, 3], {"dp": at_y})
        cross[t][1].wait_recv()
        for j in range(2):
            add_into(got[t].at[y, j, low, :], from_y[t].at[j], high // 2)
        close_x = send(got[t].at[y, 1 - x, low, :], last_x[t], send_sem.at[t, 4], recv_sem.at[t, 4], {"dp": at_x})
        close[t] = (close_y, close_x)

    def settle(t):
        a, c0, wide, high = items[t]
        core, x, y = bits[a]
        top, low = pl.ds(0, high // 2), pl.ds(high // 2, high // 2)
        cols = pl.ds(c0, wide)
        close[t][0].wait_recv()
        add_into(got[t].at[y, x, top, :], last_y[t], high // 2)
        close[t][1].wait_recv()
        add_into(got[t].at[y, x, low, :], last_x[t], high // 2)
        if lines == 1:
            show = min(wide, outs[a].shape[1] - c0)
            outs[a][:, c0 : c0 + show] = got[t][y, x, :, :show].astype(jnp.float32)
            return
        each = high // lines
        along[t] = tuple(
            send(
                unit(t, 1 - line % 2 + 2 * k, each), from_z[t].at[k],
                send_sem.at[t, 5 + k], recv_sem.at[t, 5 + k], {"seq": beside},
            )
            for k in range(2)
        )

    def unit(t, u, each):
        core, x, y = bits[items[t][0]]
        return got[t].at[y, x, pl.ds(pl.multiple_of(u * each, 16), each), :]

    def halve(t):
        each = items[t][3] // lines
        for k in range(2):
            along[t][k].wait_recv()
            add_into(unit(t, line % 2 + 2 * k, each), from_z[t].at[k], each)
        along[t] += (
            send(unit(t, across, each), from_z[t].at[2], send_sem.at[t, 7], recv_sem.at[t, 7], {"seq": across}),
        )

    def finish(t):
        a, c0, wide, high = items[t]
        along[t][2].wait_recv()
        total = unit(t, line, high // lines)[...].astype(jnp.float32) + from_z[t][2].astype(jnp.float32)
        show = min(wide, outs[a].shape[1] - c0)
        outs[a][:, c0 : c0 + show] = total[:, :show]

    little = []

    def tiny_step(n):
        if n == 0:
            at = 0
            for part in small_in:
                size = part.shape[1] // 2
                for k in range(2):
                    packed[k, :, at : at + size] = part[:, k * size : (k + 1) * size]
                at += size
            little.append(send(packed.at[1 - own_core], t_core, t_send.at[0], t_recv.at[0], {"dp": at_core}))
        elif n == 1:
            little[0].wait_recv()
            half[0] = packed[own_core] + t_core[...]
            little.append(send(half.at[0], t_x, t_send.at[1], t_recv.at[1], {"dp": at_x}))
        elif n == 2:
            little[1].wait_recv()
            half[1] = half[0] + t_x[...]
            little.append(send(half.at[1], t_y, t_send.at[2], t_recv.at[2], {"dp": at_y}))
        elif n == 3:
            little[2].wait_recv()
            half[2] = half[1] + t_y[...]
            t_z[line] = half[2]
            for k, o in enumerate(others):
                little.append(send(half.at[2], t_z.at[line], t_send.at[3 + k], t_recv.at[3 + k], {"seq": o}))
        elif n == 4:
            for k in range(lines - 1):
                little[3 + k].wait_recv()
            total = t_z[0]
            for k in range(1, lines):
                total = total + t_z[k]
            t_back[own_core] = total
            little.append(
                send(t_back.at[own_core], t_back.at[own_core], t_send.at[7], t_recv.at[7], {"dp": at_core})
            )
        elif n == 5:
            little[-1].wait_recv()
            for copy in little:
                copy.wait_send()
            conv_w, conv_b, mix_g, norm_g, ffn_g, heads = small_out
            at = 0
            spans = []
            for part in small_in:
                size = part.shape[1] // 2
                spans.append((at, size))
                at += size
            for k in range(2):
                at, size = spans[0]
                mix_g[:, k * size : (k + 1) * size] = t_back[k, 0:1, at : at + size]
                conv_b[:, k * size : (k + 1) * size] = t_back[k, 2:3, at : at + size]
                conv_w[:, k * size : (k + 1) * size] = t_back[k, 3:7, at : at + size]
                at, size = spans[1]
                here = INNER + k * size
                conv_b[:, here : here + size] = t_back[k, 0:1, at : at + size]
                conv_w[:, here : here + size] = t_back[k, 1:5, at : at + size]
                at, size = spans[2]
                norm_g[:, k * size : (k + 1) * size] = t_back[k, 0:1, at : at + size]
                ffn_g[:, k * size : (k + 1) * size] = t_back[k, 1:2, at : at + size]
                at, size = spans[3]
                heads[:, k * size : (k + 1) * size] = t_back[k, :, at : at + size]

    begin(0)
    if tiny:
        tiny_step(0)
    moves = swap_start(swaps, landed, line, lines, *swap_sem) if moved else ()
    for t in range(max(count + 4, 5 if tiny else 0)):
        if t + 1 < count:
            begin(t + 1)
        if t < count:
            fold(t)
        if 0 <= t - 1 < count:
            turn(t - 1)
        if 0 <= t - 2 < count:
            settle(t - 2)
        if lines > 1 and 0 <= t - 3 < count:
            halve(t - 3)
        if lines > 1 and 0 <= t - 4 < count:
            finish(t - 4)
        if tiny and t < 5:
            tiny_step(t + 1)
    swap_end(moves)
    for t in range(count):
        stage[t].wait_send()
        for copy in cross[t] + close[t] + tuple(along[t] or ()):
            copy.wait_send()


def sum_to_owners(grads, widths, lines, shown, small, swaps, relative, identity):
    items, views = [], []
    for a, (g, wide) in enumerate(zip(grads, widths)):
        high, cols = g.shape[0] // 8, g.shape[1]
        views.append(g.reshape(2, 2, 2, high, cols))
        start = 0
        while start < cols:
            w = min(wide, cols - start)
            items.append((a, start, w, high))
            start += w
    tiny = small is not None
    bf = jnp.bfloat16
    scratch = [pltpu.VMEM((2, 2, h, w), bf) for _, _, w, h in items]
    scratch += [pltpu.VMEM((2, 2, h, w), bf) for _, _, w, h in items]
    scratch += [pltpu.VMEM((2, h // 2, w), bf) for _, _, w, h in items] * 2
    scratch += [pltpu.VMEM((h // 2, w), bf) for _, _, w, h in items] * 2
    if lines > 1:
        scratch += [pltpu.VMEM((lines - 1, h // lines, w), bf) for _, _, w, h in items]
    ways = 4 + lines
    scratch += [
        pltpu.SemaphoreType.DMA((len(items),)),
        pltpu.SemaphoreType.DMA((len(items), ways)),
        pltpu.SemaphoreType.DMA((len(items), ways)),
    ]
    out_shape = [
        jax.ShapeDtypeStruct((g.shape[0] // 8 // lines, cols), jnp.float32) for g, cols in zip(grads, shown)
    ]
    ins = list(views)
    in_specs = [pl.BlockSpec(memory_space=pl.ANY)] * len(views)
    out_specs = [pl.BlockSpec(memory_space=pltpu.VMEM)] * len(views)
    if swaps:
        scratch += swap_sems(len(swaps), lines)
        ins += swaps
        in_specs += [pl.BlockSpec(memory_space=pl.ANY)] * len(swaps)
        out_specs += [pl.BlockSpec(memory_space=pl.ANY)] * len(swaps)
        out_shape += [jax.ShapeDtypeStruct(a.shape, a.dtype) for a in swaps]
    if tiny:
        cols = sum(part.shape[1] for part in small) // 2
        part = lambda *lead: pltpu.VMEM(lead + (8, cols), jnp.float32)
        scratch += [part(2), part(3), part(), part(), part(), part(lines), part(2)]
        scratch += [pltpu.SemaphoreType.DMA((8,)), pltpu.SemaphoreType.DMA((8,))]
        ins += small
        in_specs += [pl.BlockSpec(memory_space=pltpu.VMEM)] * 4
        for shape in ((KCONV, CONV), (1, CONV), (1, INNER), (1, MODEL_WIDTH), (1, MODEL_WIDTH), (8, 256)):
            out_shape.append(jax.ShapeDtypeStruct(shape, jnp.float32))
            out_specs.append(pl.BlockSpec(memory_space=pltpu.VMEM))
    return pl.pallas_call(
        partial(sum_body, items, len(views), lines, tiny, len(swaps), relative),
        out_shape=out_shape,
        in_specs=in_specs,
        out_specs=out_specs,
        scratch_shapes=scratch,
        name="sum_to_owners_%d" % identity,
        compiler_params=pltpu.CompilerParams(
            collective_id=identity, has_side_effects=True, vmem_limit_bytes=60 << 20
        ),
    )(*ins)


def gather_body(pieces, arrays, flat, lines, ahead, moved, relative, *refs):
    mine, refs = refs[:arrays], refs[arrays:]
    swaps, refs = refs[:moved], refs[moved:]
    full, refs = refs[:arrays], refs[arrays:]
    landed, refs = refs[:moved], refs[moved:]
    keep_sem, send_sem, recv_sem, z_send, z_recv = refs[:5]
    swap_sem = refs[5:]
    d, core, x, y, at_core, at_x, at_y = at_neighbours()
    at_far = at_x + at_y - d
    line = lax.rem(lax.axis_index("seq"), lines)
    hops = [line]
    if lines > 1:
        upper = line // 2
        hops += [line + 1 - 2 * (line % 2), 2 - upper, 3 - 3 * upper]
    meet([{"dp": at_core}, {"dp": at_x}, {"dp": at_y}] + [{"seq": o} for o in hops[1:]])
    blocks = dict(own=d, x=at_x, y=at_y, far=at_far)
    lands = dict(x=d, y=d, core=d, x_y=at_x, x_core=at_x, y_x=at_y, y_core=at_y, far_core=at_far)
    if relative:
        blocks = dict(own=0, x=2, y=4, far=6)
        lands = dict(x=2, y=4, core=1, x_y=6, x_core=3, y_x=6, y_core=5, far_core=7)
    mains = [q for q, piece in enumerate(pieces) if piece[0] < arrays - flat]
    sides = [q for q, piece in enumerate(pieces) if piece[0] >= arrays - flat]
    home = lambda a: blocks["own"] if a < arrays - flat else 0
    keep = []
    for a in range(arrays):
        keep.append(pltpu.make_async_copy(mine[a], full[a].at[home(a), line], keep_sem.at[a]))
        keep[a].start()
    order = [(j, q) for j in range(lines) for q in mains]
    total = len(order)
    out = [[None] * 7 for _ in order]

    def place(j, q, block):
        a, r0, high = pieces[q]
        return full[a].at[block, hops[j], pl.ds(r0, high), :]

    def own_piece(q):
        a, r0, high = pieces[q]
        return mine[a].at[pl.ds(r0, high), :]

    def hop(j, q, sem, to):
        a = pieces[q][0]
        return pltpu.make_async_remote_copy(
            src_ref=own_piece(q) if j == 0 else place(j, q, home(a)),
            dst_ref=place(j, q, home(a)),
            send_sem=z_send.at[q, sem], recv_sem=z_recv.at[q, hops[j]],
            device_id={"seq": to}, device_id_type=MESH,
        )

    def onward(j, q, act):
        o = hops[j]

        @pl.when((o <= line) & (line < lines - 1))
        def _():
            act(hop(j, q, 2 * j, jnp.minimum(line + 1, lines - 1)))

        @pl.when((o >= line) & (line > 0))
        def _():
            act(hop(j, q, 2 * j + 1, jnp.maximum(line - 1, 0)))

    def relay(j, q):
        hop(j, q, 2 * j, line).wait_recv()
        onward(j, q, lambda copy: copy.start())

    def pass_on(i, n, block, lands_at, there):
        j, q = order[i]
        source = own_piece(q) if block is None else place(j, q, block)
        out[i][n] = send(
            source, place(j, q, lands[lands_at]), send_sem.at[i, n], recv_sem.at[i, n], {"dp": there}
        )

    def first(i):
        block = None if order[i][0] == 0 else blocks["own"]
        pass_on(i, 0, block, "x", at_x)
        pass_on(i, 1, block, "y", at_y)
        pass_on(i, 2, block, "core", at_core)

    def second(i):
        out[i][0].wait_recv()
        if sum((i,) + order[i][:1]) % 2 == 0:
            pass_on(i, 5, blocks["x"], "x_y", at_y)
        pass_on(i, 3, blocks["x"], "x_core", at_core)
        out[i][1].wait_recv()
        if sum((i,) + order[i][:1]) % 2 == 1:
            pass_on(i, 5, blocks["y"], "y_x", at_x)
        pass_on(i, 4, blocks["y"], "y_core", at_core)

    def third(i):
        out[i][5].wait_recv()
        pass_on(i, 6, blocks["far"], "far_core", at_core)

    lead = ahead + 2
    if lines > 1:
        for q in mains:
            onward(0, q, lambda copy: copy.start())
    for i in range(min(ahead, total)):
        first(i)
    moves = swap_start(swaps, landed, line, lines, *swap_sem) if moved else ()
    for i in range(total):
        if i + lead < total and order[i + lead][0] > 0:
            relay(*order[i + lead])
        if i % len(mains) == 1:
            j = i // len(mains)
            for q in sides:
                if j == 0:
                    onward(0, q, lambda copy: copy.start())
                else:
                    relay(j, q)
        if i + ahead < total:
            first(i + ahead)
        second(i)
        if i:
            third(i - 1)
    third(total - 1)
    for i in range(total):
        for n in (2, 3, 4, 6):
            out[i][n].wait_recv()
        for copy in out[i]:
            copy.wait_send()
    swap_end(moves)
    if lines > 1:
        for q in range(len(pieces)):
            for j in range(lines):
                onward(j, q, lambda copy: copy.wait_send())
    for copy in keep:
        copy.wait()


def gather_rows(arrays, chunks, flat, lines, ahead, swaps, relative, identity):
    pieces = []
    count = len(arrays) + len(flat)
    for a, (w, chunk) in enumerate(zip(list(arrays) + list(flat), chunks)):
        for r0 in range(0, w.shape[0], chunk):
            pieces.append((a, r0, chunk))
    total = lines * len([p for p in pieces if p[0] < len(arrays)])
    anywhere = pl.BlockSpec(memory_space=pl.ANY)
    return pl.pallas_call(
        partial(gather_body, pieces, count, len(flat), lines, ahead, len(swaps), relative),
        out_shape=[jax.ShapeDtypeStruct((8, lines) + w.shape, w.dtype) for w in arrays]
        + [jax.ShapeDtypeStruct((1, lines) + w.shape, w.dtype) for w in flat]
        + [jax.ShapeDtypeStruct(a.shape, a.dtype) for a in swaps],
        in_specs=[anywhere] * (count + len(swaps)),
        out_specs=[anywhere] * (count + len(swaps)),
        scratch_shapes=[
            pltpu.SemaphoreType.DMA((count,)),
            pltpu.SemaphoreType.DMA((total, 7)),
            pltpu.SemaphoreType.DMA((total, 7)),
            pltpu.SemaphoreType.DMA((len(pieces), 2 * lines)),
            pltpu.SemaphoreType.DMA((len(pieces), lines)),
        ]
        + (swap_sems(len(swaps), lines) if swaps else []),
        name="gather_rows_%d" % identity,
        compiler_params=pltpu.CompilerParams(collective_id=identity, has_side_effects=True),
    )(*arrays, *flat, *swaps)


def sigmoid(v):
    return 1.0 / (1.0 + jnp.exp(-v))


def shifted(v, by):
    if by == 0:
        return v
    rows = v.shape[0]
    at = lax.broadcasted_iota(jnp.int32, v.shape, 0)
    keep = at >= by if by > 0 else at < rows + by
    return jnp.where(keep, pltpu.roll(v, by % rows, 0), 0.0)


def conv_sums(v, taps, bias):
    total = bias
    for k in range(KCONV):
        total = total + taps[k : k + 1, :] * shifted(v, KCONV - 1 - k)
    return total


def conv_back(v, taps, bias, valid, grad):
    conv_sum = conv_sums(v, taps, bias)
    s = sigmoid(conv_sum)
    grad = grad * valid * (s * (1.0 + conv_sum * (1.0 - s)))
    total = taps[KCONV - 1 : KCONV, :] * grad
    for k in range(KCONV - 1):
        total = total + taps[k : k + 1, :] * shifted(grad, k - (KCONV - 1))
    sums = [jnp.sum(grad, axis=0, keepdims=True)]
    for k in range(KCONV):
        sums.append(jnp.sum(grad * shifted(v, KCONV - 1 - k), axis=0, keepdims=True))
    return total, sums


def head_columns(ref, pair):
    v = pltpu.roll(ref[...], lax.rem(128 - 2 * pair, 128), 1)
    return v[:, 0:1], v[:, 1:2]


def over_lanes(columns):
    rows = columns[0].shape[0]
    lane = lax.broadcasted_iota(jnp.int32, (rows, 128), 1)
    return jnp.where(lane < HDIM, columns[0], columns[1])


def lower_left(rows):
    return lax.broadcasted_iota(jnp.int32, (rows, rows), 0) >= lax.broadcasted_iota(
        jnp.int32, (rows, rows), 1
    )


def product(a, b, over_a=1, over_b=0):
    return lax.dot_general(
        a, b, (((over_a,), (over_b,)), ((), ())), preferred_element_type=jnp.float32
    )


def bc_scores(bc_ref, bc_taps, bc_bias, valid, scores, bc_keep):
    conv_sum = conv_sums(bc_ref[...].astype(jnp.float32), bc_taps[...], bc_bias[...])
    bc = conv_sum * sigmoid(conv_sum) * valid[:, :1]
    bc_keep[...] = bc.astype(jnp.bfloat16)
    rows = scores.shape[0]
    g = product(bc_keep[:, STATE:], bc_keep[:, :STATE], 1, 1)
    scores[...] = jnp.where(lower_left(rows), g, 0.0)


def front_body(
    z_ref, x_ref, bc_ref, taps, bias, bc_taps, bc_bias, valid, step, cum, cum_rows, skip,
    mixed_ref, gated_ref, squares, scores, bc_keep,
):
    f32, bf = jnp.float32, jnp.bfloat16

    @pl.when(pl.program_id(0) == 0)
    def _():
        bc_scores(bc_ref, bc_taps, bc_bias, valid, scores, bc_keep)
        squares[...] = jnp.zeros_like(squares)

    rows = x_ref.shape[0]
    half = rows // 2
    conv_sum = conv_sums(x_ref[...].astype(f32), taps[...], bias[...])
    x = conv_sum * sigmoid(conv_sum) * valid[...]
    xs = (x * over_lanes(head_columns(step, pl.program_id(0)))).astype(bf)
    sums = head_columns(cum, pl.program_id(0))
    lane = lax.broadcasted_iota(jnp.int32, (half, 128), 1)
    for r in range(2):
        at, wide = pl.ds(r * half, half), (r + 1) * half
        parts = []
        for h in range(2):
            gap = sums[h][r * half : (r + 1) * half, :] - cum_rows[0, h : h + 1, :wide]
            m = (jnp.exp(jnp.minimum(gap, 0.0)) * scores[at, :wide]).astype(bf)
            parts.append(product(m, xs[:wide, :]))
        mixed = jnp.where(lane < HDIM, parts[0], parts[1]) + skip[...] * x[r * half : (r + 1) * half, :]
        z = z_ref[at, :].astype(f32)
        gated = mixed * (z * sigmoid(z))
        mixed_ref[at, :] = mixed
        gated_ref[at, :] = gated
        squares[at, :] += gated * gated


def back_body(
    z_ref, x_ref, bc_ref, taps, bias, bc_taps, bc_bias, valid, step, cum, cum_rows, skip,
    mixed_ref, grad_ref, gain, scale, mean_dot,
    grad_z, grad_x, stats, grad_bc, bc_stats, row_sums, col_sums, step_sums,
    scores, bc_keep, grad_scores, grad_xs,
):
    f32, bf = jnp.float32, jnp.bfloat16
    pair = pl.program_id(0)

    @pl.when(pair == 0)
    def _():
        bc_scores(bc_ref, bc_taps, bc_bias, valid, scores, bc_keep)
        grad_scores[...] = jnp.zeros_like(grad_scores)
        row_sums[...] = jnp.zeros_like(row_sums)
        col_sums[...] = jnp.zeros_like(col_sums)
        step_sums[...] = jnp.zeros_like(step_sums)

    rows = x_ref.shape[0]
    half = rows // 2
    v = x_ref[...].astype(f32)
    conv_sum = conv_sums(v, taps[...], bias[...])
    x = conv_sum * sigmoid(conv_sum) * valid[...]
    steps = over_lanes(head_columns(step, pair))
    sums = head_columns(cum, pair)
    xs = (x * steps).astype(bf)
    z = z_ref[...].astype(f32)
    s = sigmoid(z)
    silu = z * s
    mixed = mixed_ref[...]
    normal = mixed * silu * scale[...]
    grad = grad_ref[...]
    grad_gated = scale[...] * (grad * gain[...] - normal * mean_dot[...])
    grad_mixed = grad_gated * silu
    grad_z[...] = (grad_gated * mixed * (s * (1.0 + z * (1.0 - s)))).astype(bf)
    lane = lax.broadcasted_iota(jnp.int32, (rows, 128), 1)
    dy = [
        jnp.where(lane < HDIM, grad_mixed, 0.0).astype(bf),
        jnp.where(lane < HDIM, 0.0, grad_mixed).astype(bf),
    ]
    for r in range(2):
        at, wide = pl.ds(r * half, half), (r + 1) * half
        total = None
        for h in range(2):
            head = 2 * pair + h
            g = scores[at, :wide]
            gap = sums[h][r * half : (r + 1) * half, :] - cum_rows[0, h : h + 1, :wide]
            e = jnp.exp(jnp.minimum(gap, 0.0))
            m = (e * g).astype(bf)
            dy_rows = dy[h][r * half : (r + 1) * half, :]
            slope = product(dy_rows, xs[:wide, :], 1, 1) * e
            grad_scores[at, :wide] += slope
            both = (slope * g).astype(bf)
            back = product(m, dy_rows, 0, 0)
            total = back if total is None else total + back
            to_lane = (lax.broadcasted_iota(jnp.int32, (wide, 128), 1) == head).astype(bf)
            row_sums[at, :] += product(both, to_lane)
            to_row = (lax.broadcasted_iota(jnp.int32, (64, half), 0) == head).astype(bf)
            col_sums[:, :wide] += product(to_row, both)
        if r == 0:
            grad_xs[:half, :] = total
        else:
            grad_xs[:half, :] += total[:half, :]
            grad_xs[half:, :] = total[half:, :]
    gxs = grad_xs[...]
    fold = (
        lax.broadcasted_iota(jnp.int32, (128, 128), 1)
        == 2 * pair + lax.broadcasted_iota(jnp.int32, (128, 128), 0) // HDIM
    ).astype(bf)
    step_sums[...] += product((gxs * x).astype(bf), fold)
    gx, parts = conv_back(v, taps[...], bias[...], valid[...], gxs * steps + skip[...] * grad_mixed)
    grad_x[...] = gx.astype(bf)
    stats[0:1, :] = jnp.sum(grad * normal, axis=0, keepdims=True)
    stats[1:2, :] = jnp.sum(grad_mixed * x, axis=0, keepdims=True)
    for k, total in enumerate(parts):
        stats[2 + k : 3 + k, :] = total
    stats[7:8, :] = jnp.zeros((1, 128), f32)

    @pl.when(pair == pl.num_programs(0) - 1)
    def _():
        gs = jnp.where(lower_left(rows), grad_scores[...], 0.0).astype(bf)
        grad_c = product(gs, bc_keep[:, :STATE])
        grad_b = product(gs, bc_keep[:, STATE:], 0, 0)
        ends = ((grad_b, 0), (grad_c, STATE))
        for g, at in ends:
            cols = pl.ds(at, STATE)
            gi, sums = conv_back(
                bc_ref[:, cols].astype(f32), bc_taps[:, cols], bc_bias[:, cols], valid[...], g
            )
            grad_bc[:, cols] = gi.astype(bf)
            for k, total in enumerate(sums):
                bc_stats[k : k + 1, cols] = total
            bc_stats[5:8, cols] = jnp.zeros((3, STATE), f32)


def mixer_specs(rows):
    tile = lambda at: pl.BlockSpec((rows, 128), at)
    whole = lambda shape: pl.BlockSpec(shape, lambda p: (0,) * len(shape))
    pairs = INNER // 128
    return tile, whole, [
        tile(lambda p: (0, p)),
        tile(lambda p: (0, pairs + p)),
        pl.BlockSpec((rows, 2 * STATE), lambda p: (0, 2 * INNER // (2 * STATE))),
        pl.BlockSpec((KCONV, 128), lambda p: (0, p)),
        pl.BlockSpec((1, 128), lambda p: (0, p)),
        pl.BlockSpec((KCONV, 2 * STATE), lambda p: (0, INNER // (2 * STATE))),
        pl.BlockSpec((1, 2 * STATE), lambda p: (0, INNER // (2 * STATE))),
        whole((rows, 128)),
        whole((rows, 128)),
        whole((rows, 128)),
        pl.BlockSpec((1, 2, rows), lambda p: (p, 0, 0)),
        pl.BlockSpec((1, 128), lambda p: (0, p)),
    ]


def mixer_front_call(inputs, rows):
    f32 = jnp.float32
    tile, whole, specs = mixer_specs(rows)
    return pl.pallas_call(
        front_body,
        grid=(INNER // 128,),
        in_specs=specs,
        out_specs=[tile(lambda p: (0, p)), tile(lambda p: (0, p)), whole((rows, 128))],
        out_shape=[
            jax.ShapeDtypeStruct((rows, INNER), f32),
            jax.ShapeDtypeStruct((rows, INNER), f32),
            jax.ShapeDtypeStruct((rows, 128), f32),
        ],
        scratch_shapes=[pltpu.VMEM((rows, rows), f32), pltpu.VMEM((rows, 2 * STATE), jnp.bfloat16)],
        name="mixer_front",
        cost_estimate=pl.CostEstimate(flops=10**10, bytes_accessed=2 * 10**7, transcendentals=5 * 10**6),
    )(*inputs)


def mixer_back_call(inputs, extra, rows):
    f32, bf = jnp.float32, jnp.bfloat16
    tile, whole, specs = mixer_specs(rows)
    by_pair = tile(lambda p: (0, p))
    return pl.pallas_call(
        back_body,
        grid=(INNER // 128,),
        in_specs=specs
        + [by_pair, by_pair, pl.BlockSpec((1, 128), lambda p: (0, p)), whole((rows, 128)), whole((rows, 128))],
        out_specs=[
            by_pair, by_pair, pl.BlockSpec((8, 128), lambda p: (0, p)), whole((rows, 2 * STATE)),
            whole((8, 2 * STATE)), whole((rows, 128)), whole((64, rows)), whole((rows, 128)),
        ],
        out_shape=[
            jax.ShapeDtypeStruct((rows, INNER), bf),
            jax.ShapeDtypeStruct((rows, INNER), bf),
            jax.ShapeDtypeStruct((8, INNER), f32),
            jax.ShapeDtypeStruct((rows, 2 * STATE), bf),
            jax.ShapeDtypeStruct((8, 2 * STATE), f32),
            jax.ShapeDtypeStruct((rows, 128), f32),
            jax.ShapeDtypeStruct((64, rows), f32),
            jax.ShapeDtypeStruct((rows, 128), f32),
        ],
        scratch_shapes=[
            pltpu.VMEM((rows, rows), f32), pltpu.VMEM((rows, 2 * STATE), bf),
            pltpu.VMEM((rows, rows), f32), pltpu.VMEM((rows, 128), f32),
        ],
        name="mixer_back",
        cost_estimate=pl.CostEstimate(flops=3 * 10**10, bytes_accessed=3 * 10**7, transcendentals=5 * 10**6),
    )(*inputs, *extra)


def picks(slot_row, slots):
    rows = slot_row.shape[1]
    at = lax.broadcasted_iota(jnp.int32, (slots, rows), 0).astype(jnp.float32)
    return at == slot_row


def cot_chunk(cots, g):
    if g < 6:
        return cots[g][...]
    return jnp.concatenate([cots[2 * g - 6][...], cots[2 * g - 5][...]], axis=0)


def experts_body(lines, x_ref, *refs):
    cots, refs = refs[:10], refs[10:]
    experts_step(lines, x_ref, cots, *refs)


def experts_step(
    lines, x_ref, cots, up, down, slot_rows, gates,
    y_out, gin_out, grads, dots,
    xe, gy, gu_grad, hid, gate_cols,
):
    f32, bf = jnp.float32, jnp.bfloat16
    chunks, rows, width = x_ref.shape
    slots = xe.shape[0] // chunks
    hidden = down.shape[1]

    for g in range(chunks):
        p = picks(slot_rows[0, g : g + 1, :], slots)
        one = p.astype(bf)
        at = pl.ds(g * slots, slots)
        xe[at, :] = product(one, x_ref[g]).astype(bf)
        gate = jnp.sum(jnp.where(p, gates[0, g : g + 1, :], 0.0), axis=1, keepdims=True)
        gate_cols[at, :] = jnp.broadcast_to(gate, (slots, 128))
        gy[at, :] = (gate * product(one, cot_chunk(cots, g))).astype(bf)

    tile = 2 * slots

    @pl.loop(0, xe.shape[0] // tile)
    def _(t):
        at = pl.ds(pl.multiple_of(t * tile, tile), tile)
        gu = product(xe[at, :], up[0])
        a, b = gu[:, :hidden], gu[:, hidden:]
        s = sigmoid(a)
        silu = a * s
        h = (silu * b).astype(bf)
        hid[at, :] = h
        gh = product(gy[at, :], down[0], 1, 1)
        gu_grad[at, :hidden] = (gh * b * (s * (1.0 + a * (1.0 - s)))).astype(bf)
        gu_grad[at, hidden:] = (gh * silu).astype(bf)
        y = product(h, down[0]).astype(bf).astype(f32)
        dot = jnp.sum(y * gy[at, :].astype(f32), axis=1, keepdims=True)
        y_out[0, at, :] = (gate_cols[at, :1] * y).astype(bf)
        for i in range(2):
            p = picks(slot_rows[0, pl.ds(2 * t + i, 1), :], slots)
            dots[0, pl.ds(2 * t + i, 1), :] = jnp.sum(
                jnp.where(p, dot[i * slots : (i + 1) * slots, :], 0.0), axis=0, keepdims=True
            )
        gin_out[0, at, :] = product(gu_grad[at, :], up[0], 1, 1).astype(bf)

    cols = grads.shape[2]
    own_up, per = width // lines, hidden // lines
    for n in range(lines):
        base = n * (grads.shape[1] // lines)
        grads[0, base : base + own_up, :] = product(
            xe[:, n * own_up : (n + 1) * own_up], gu_grad[...], 0, 0
        ).astype(bf)
    cut = width - cols
    for n in range(0, lines, 2):
        down_two = product(hid[:, n * per : (n + 2) * per], gy[...], 0, 0).astype(bf)
        for k in range(2):
            base = (n + k) * (grads.shape[1] // lines) + own_up
            part = down_two[k * per : (k + 1) * per, :]
            grads[0, base : base + per, :] = part[:, :cols]
            grads[0, base + per : base + per + per // 2, :cut] = part[: per // 2, cols:]
            grads[0, base + per : base + per + per // 2, cut:] = part[per // 2 :, cols:]


def experts_call(x, cots, up, down, slot_rows, gates, slots, lines):
    f32, bf = jnp.float32, jnp.bfloat16
    chunks, rows, width = x.shape
    held, _, double = up.shape
    total = chunks * slots
    once = pl.Buffered(1)
    each = lambda *shape: pl.BlockSpec((1,) + shape, lambda e: (e, 0, 0))
    keep = lambda *shape: pl.BlockSpec((1,) + shape, lambda e: (e, 0, 0), pipeline_mode=once)
    whole = pl.BlockSpec((chunks, rows, width), lambda e: (0, 0, 0), pipeline_mode=once)
    shape = lambda *s: jax.ShapeDtypeStruct((held,) + s, bf)
    packed = width + double // 2 + double // 4
    return pl.pallas_call(
        partial(experts_body, lines),
        grid=(held,),
        in_specs=[
            whole, *[pl.BlockSpec(c.shape, lambda e: (0, 0), pipeline_mode=once) for c in cots], keep(width, double), keep(double // 2, width), each(chunks, rows), each(chunks, rows),
        ],
        out_specs=[
            each(total, width), each(total, width), each(packed, double), each(chunks, rows),
        ],
        out_shape=[
            shape(total, width), shape(total, width), shape(packed, double),
            jax.ShapeDtypeStruct((held, chunks, rows), f32),
        ],
        scratch_shapes=[
            pltpu.VMEM((total, width), bf), pltpu.VMEM((total, width), bf), pltpu.VMEM((total, double), bf),
            pltpu.VMEM((total, double // 2), bf), pltpu.VMEM((total, 128), f32),
        ],
        name="experts",
        compiler_params=pltpu.CompilerParams(vmem_limit_bytes=62 << 20),
        cost_estimate=pl.CostEstimate(flops=4 * 10**10, bytes_accessed=5 * 10**7, transcendentals=10**6),
    )(x, *cots, up, down, slot_rows, gates)


def join_body(where, x_ref, *refs):
    cots, refs = refs[:10], refs[10:]
    join_step(where, x_ref, cots, *refs)


def join_step(
    where, x_ref, cots, y_ref, gin_ref, slot_rows, up, down, dots,
    y_part, g_part, dot_part, up_grad, down_grad, up_acc, down_acc, cot_ref,
):
    f32, bf = jnp.float32, jnp.bfloat16
    g = pl.program_id(0)

    @pl.when(g == 0)
    def _():
        up_acc[...] = jnp.zeros_like(up_acc)
        down_acc[...] = jnp.zeros_like(down_acc)

    for k in range(8):

        @pl.when(g == k)
        def _(k=k):
            cot_ref[...] = cot_chunk(cots, k)

    x, cot = x_ref[0], cot_ref[...]
    half = down.shape[0]
    gu = product(x, up[...])
    a, b = gu[:, :half], gu[:, half:]
    s = sigmoid(a)
    silu = a * s
    h = (silu * b).astype(bf)
    gh = product(cot, down[...], 1, 1)
    gu_grad = jnp.concatenate(
        [gh * b * (s * (1.0 + a * (1.0 - s))), gh * silu], axis=1
    ).astype(bf)
    up_acc[...] += product(x, gu_grad, 0, 0)
    down_acc[...] += product(h, cot, 0, 0)
    y = product(h, down[...])
    gx = product(gu_grad, up[...], 1, 1)
    for e in range(y_ref.shape[0]):
        one = picks(slot_rows[e, pl.ds(g, 1), :], y_ref.shape[1]).astype(bf)
        y = y + product(one, y_ref[e], 0, 0)
        gx = gx + product(one, gin_ref[e], 0, 0)
    held = y_ref.shape[0]
    lists = jnp.zeros((8, x.shape[0]), f32)
    spot = lax.broadcasted_iota(jnp.int32, lists.shape, 0)
    for e in range(held):
        row = dots[e, pl.ds(g, 1), :]
        high = row.astype(bf).astype(f32)
        lists = jnp.where(spot == e, high, lists)
        lists = jnp.where(spot == held + e, row - high, lists)
    col = lax.broadcasted_iota(jnp.int32, (8, 128), 1)
    spot = lax.broadcasted_iota(jnp.int32, (8, 128), 0)
    first = held * where[0]
    to = (spot < held) & (col == first + spot)
    to = to | ((spot >= held) & (spot < 2 * held) & (col == 8 * held + first + spot - held))
    dot_part[0] = product(lists.astype(bf), to.astype(bf), 0, 0).astype(bf)
    y_part[0] = y.astype(bf)
    g_part[0] = gx.astype(bf)

    @pl.when(g == pl.num_programs(0) - 1)
    def _():
        up_grad[...] = up_acc[...].astype(bf)
        down_grad[...] = down_acc[...].astype(bf)


def join_call(where, x, cots, y, gin, slot_rows, up, down, dots, slots):
    f32, bf = jnp.float32, jnp.bfloat16
    chunks, rows, width = x.shape
    held = y.shape[0]
    chunk = pl.BlockSpec((1, rows, width), lambda g, w: (g, 0, 0))
    placed = pl.BlockSpec((1, rows, width), lambda g, w: (g ^ w[0], 0, 0))
    rows_of = pl.BlockSpec((held, slots, width), lambda g, w: (0, g, 0))
    whole = lambda a: pl.BlockSpec(a.shape, lambda g, w: (0,) * a.ndim)
    return pl.pallas_call(
        join_body,
        grid_spec=pltpu.PrefetchScalarGridSpec(
            num_scalar_prefetch=1,
            grid=(chunks,),
            in_specs=[chunk, *[whole(c) for c in cots], rows_of, rows_of, whole(slot_rows), whole(up), whole(down), whole(dots)],
            out_specs=[
                placed, chunk, pl.BlockSpec((1, rows, 128), lambda g, w: (g, 0, 0)), whole(up), whole(down),
            ],
            scratch_shapes=[
                pltpu.VMEM(up.shape, f32), pltpu.VMEM(down.shape, f32), pltpu.VMEM((rows, width), bf),
            ],
        ),
        out_shape=[
            jax.ShapeDtypeStruct(x.shape, bf), jax.ShapeDtypeStruct(x.shape, bf),
            jax.ShapeDtypeStruct((chunks, rows, 128), bf),
            jax.ShapeDtypeStruct(up.shape, bf), jax.ShapeDtypeStruct(down.shape, bf),
        ],
        name="join",
        compiler_params=pltpu.CompilerParams(vmem_limit_bytes=48 << 20),
        cost_estimate=pl.CostEstimate(flops=10**10, bytes_accessed=4 * 10**7, transcendentals=10**6),
    )(where, x, *cots, y, gin, slot_rows, up, down, dots)


def local_fast(
    tokens, lengths, routes, cotangent, norm_gain, in_weight, conv_weight, conv_bias, dt_bias,
    a_log, d_skip, mix_gain, out_weight, ffn_gain, router_weight, shared_up, shared_down,
    expert_up, expert_down,
):
    bf, f32 = jnp.bfloat16, jnp.float32
    block = tokens.shape[1]
    parts = tokens.shape[0]
    rows = block * parts
    groups = lax.axis_size("dp")
    lines = lax.axis_size("seq")
    held = expert_up.shape[0]
    experts = held * groups
    top = routes.shape[2]
    slots = block * top * 5 // (4 * experts) * parts
    slots = -(-slots // 128) * 128
    place = lax.axis_index("seq")
    group = lax.axis_index("dp")

    def to(a, bit):
        return lax.ppermute(a, "dp", [(i, i ^ bit) for i in range(groups)])

    pad = lambda a, n: jnp.pad(a, ((0, 0), (0, n - a.shape[1])))
    in_blocks, router_blocks, out_blocks, down_line, up_line, x_low, route = gather_rows(
        [in_weight, pad(router_weight, 128), out_weight],
        [in_weight.shape[0] // 3, router_weight.shape[0], out_weight.shape[0] // 2, shared_down.shape[0],
         shared_up.shape[0]],
        [shared_down, shared_up], lines, 2, [tokens, routes], False, 1,
    )
    out_full = out_blocks.reshape(-1, MODEL_WIDTH)
    in_full = in_blocks.reshape(MODEL_WIDTH, -1)
    router_full = router_blocks.reshape(MODEL_WIDTH, -1)[:, :experts]
    down_part = down_line.reshape(-1, MODEL_WIDTH)
    in_full, late_cot = lax.optimization_barrier((in_full, cotangent))
    cot_low = lax.all_to_all(late_cot, "seq", split_axis=0, concat_axis=0, tiled=True)
    width = SFF // groups
    up_cols = up_line.reshape(-1, 2, groups, width).transpose(2, 0, 1, 3).reshape(groups, -1, 2 * width)

    length = lax.dynamic_index_in_dim(lengths, place, 0, False)
    x_low = x_low.reshape(rows, MODEL_WIDTH)
    cot_low = cot_low.reshape(rows, MODEL_WIDTH)
    cotangent_rows = cot_low
    route = route.reshape(rows, top)
    used = jnp.arange(rows) < length
    valid = used.astype(f32)[:, None]
    x_rows = x_low.astype(f32)
    normed, norm_pull = jax.vjp(rms_norm, x_rows, norm_gain)
    normed_low = normed.astype(bf)
    projected = jnp.dot(normed_low, in_full, preferred_element_type=f32).astype(bf)
    before_step = projected[:, INNER + CONV :].astype(f32) + dt_bias
    steps = jax.nn.softplus(before_step)
    rates = -steps * jnp.exp(a_log)
    lower = (jnp.arange(rows)[:, None] >= jnp.arange(rows)[None, :]).astype(f32)
    cumulative = jnp.dot(lower, rates, precision=PRECISE)
    wide = lambda a: jnp.broadcast_to(a[:, :, None], a.shape + (HDIM,)).reshape(a.shape[0], -1)
    lanes = lambda a: jnp.broadcast_to(a, (rows, 128))
    mixer_in = (
        projected, projected, projected, conv_weight, conv_bias[None], conv_weight, conv_bias[None],
        lanes(valid), pad(steps, 128), pad(cumulative, 128), cumulative.T.reshape(HEADS // 2, 2, rows),
        wide(d_skip[None]),
    )
    cot_low = jnp.where(used[:, None], cot_low, 0)
    first_in, cot_own, up_cols = lax.optimization_barrier((mixer_in[0], cot_low, up_cols))
    cut = rows // 2
    cot_x, cot_y = to(cot_own, 2), to(cot_own, 4)
    mixed, gated, squares = mixer_front_call((first_in,) + mixer_in[1:], rows)
    up_part = lax.all_to_all(up_cols, "dp", split_axis=0, concat_axis=0, tiled=True)
    gated, cot_x, cot_y, up_part = lax.optimization_barrier((gated, cot_x, cot_y, up_part))
    up_part = up_part.reshape(MODEL_WIDTH, 2 * width)
    cot_far = (to(cot_x[:cut], 4), to(cot_y[cut:], 2))
    cot_core = [to(a, 1) for a in (cot_own, cot_x, cot_y)]
    scale = lax.rsqrt(jnp.sum(squares, axis=1, keepdims=True) / INNER + EPSILON)
    mix_low = (gated * scale * mix_gain).astype(bf)
    mixer_out = jnp.dot(mix_low, out_full, preferred_element_type=f32)
    hidden = x_rows + mixer_out * valid
    normed_ffn, ffn_pull = jax.vjp(rms_norm, hidden, ffn_gain)
    ffn_low = normed_ffn.astype(bf)
    logits = jnp.dot(ffn_low, router_full, preferred_element_type=f32)
    onehot = (route[:, :, None] == jnp.arange(experts)[None, None, :]).astype(f32)
    chosen = jnp.sum(onehot, axis=1)
    peak = jnp.max(jnp.where(chosen > 0, logits, -jnp.inf), axis=1, keepdims=True)
    raised = jnp.exp(jnp.where(chosen > 0, logits - peak, -jnp.inf))
    probs = raised / jnp.sum(raised, axis=1, keepdims=True)

    ffn_low, cot_far, cot_core = lax.optimization_barrier((ffn_low, cot_far, cot_core))
    cot_far_core = tuple(to(a, 1) for a in cot_far)
    all_rows, all_probs = gather_rows(
        [ffn_low, (probs * valid).T], [64, experts], [], 1, 2, [], True, 2
    )
    all_rows = all_rows[:, 0]
    all_cot = [cot_own, cot_core[0], cot_x, cot_core[1], cot_y, cot_core[2], *cot_far, *cot_far_core]
    mine = group * held + jnp.arange(held)
    gates = lax.dynamic_slice_in_dim(all_probs[:, 0], group * held, held, 1).transpose(1, 0, 2)
    member = gates > 0
    earlier = (jnp.arange(rows)[:, None] < jnp.arange(rows)[None, :]).astype(bf)
    before = jnp.einsum("egt,ts->egs", member.astype(bf), earlier, preferred_element_type=f32)
    slot_rows = jnp.where(member, before, -1.0)
    y_slots, gin_slots, grad_experts, dots = experts_call(
        all_rows, all_cot, expert_up, expert_down, slot_rows, gates, slots, lines
    )
    own_experts = lax.psum_scatter(grad_experts, "seq", scatter_dimension=1, tiled=True)
    y_part, g_part, dots, grad_sup, grad_sdown = join_call(
        group.reshape(1), all_rows, all_cot, y_slots, gin_slots, slot_rows, up_part, down_part, dots, slots
    )
    g_sum, dots = sum_to_owners(
        [g_part.reshape(-1, MODEL_WIDTH), dots.reshape(-1, 128)],
        [384, 128], 1, [MODEL_WIDTH, 128], None, [], (True, True), 3,
    )
    dots = dots[:, :experts] + dots[:, experts : 2 * experts]
    g_sum, y_part = lax.optimization_barrier((g_sum, y_part))
    y_part = lax.all_to_all(y_part, "dp", split_axis=0, concat_axis=0, tiled=True)
    grad_out = cotangent_rows.astype(f32)
    grad_logit = (dots - probs * jnp.sum(dots, axis=1, keepdims=True)).astype(bf)
    grad_router = contract_rows(ffn_low, grad_logit)
    grad_ffn = g_sum + contract_cols(grad_logit, router_full)
    grad_hidden, grad_fgain = ffn_pull(grad_ffn)
    grad_hidden = grad_hidden + grad_out
    grad_mo = (grad_hidden * valid).astype(bf)
    grad_outw = contract_rows(mix_low, grad_mo).astype(bf)
    grad_mix = contract_cols(grad_mo, out_full)
    mean_dot = jnp.sum(grad_mo.astype(f32) * mixer_out, axis=1, keepdims=True) / INNER
    grad_z, grad_in, stats, grad_bc, bc_stats, row_sums, col_sums, step_sums = mixer_back_call(
        mixer_in, (mixed, grad_mix, mix_gain[None], lanes(scale), lanes(mean_dot)), rows
    )
    grad_z, y_part = lax.optimization_barrier((grad_z, y_part))
    grad_rates = jnp.dot(lower.T, row_sums[:, :HEADS] - col_sums[:HEADS].T, precision=PRECISE)
    grad_raw = (step_sums[:, :HEADS] - grad_rates * jnp.exp(a_log)) * jax.nn.sigmoid(before_step)
    grad_al = jnp.sum(grad_rates * rates, axis=0)
    grad_db = jnp.sum(grad_raw, axis=0)
    grad_skip = jnp.sum(stats[1].reshape(HEADS, HDIM), axis=1)
    grad_proj = jnp.concatenate([grad_z, grad_in, grad_bc, grad_raw.astype(bf)], axis=1)
    spare = -PROJ % 128
    grad_inw = contract_rows(normed_low, pad(grad_proj, PROJ + spare)).astype(bf)
    grad_x, grad_ngain = norm_pull(contract_cols(grad_proj, in_full))
    input_grad = (grad_x + grad_hidden).astype(bf)
    grad_router = contract_rows(ffn_low, pad(grad_logit, 128)).astype(bf)

    grad_inw, grad_sup = lax.optimization_barrier((grad_inw, grad_sup))
    y_sum = jnp.sum(y_part.astype(f32), axis=0)
    output = (hidden + valid * y_sum).astype(bf).reshape(tokens.shape)

    heads = jnp.pad(jnp.stack([grad_db, grad_al, grad_skip]), ((0, 5), (0, 256 - HEADS)))
    gains = jnp.pad(jnp.stack([grad_ngain, grad_fgain]), ((0, 6), (0, 0)))
    own_out, own_in, own_router, output, input_grad, sdown, conv_w, conv_b, mix_g, norm_g, ffn_g, heads = sum_to_owners(
        [grad_outw, grad_inw, grad_router], [512, 768, 128], lines, [MODEL_WIDTH, PROJ, experts],
        [stats, bc_stats, gains, heads], [output, input_grad.reshape(tokens.shape), grad_sdown.reshape(lines, -1, MODEL_WIDTH)],
        (False, False, False), 4,
    )
    sup = lax.all_to_all(
        grad_sup.reshape(groups * lines, -1, 2 * width), ("dp", "seq"), split_axis=0, concat_axis=0, tiled=True
    ).astype(f32)
    sup = jnp.sum(sup.reshape(groups, lines, -1, 2 * width), axis=1)
    sup = sup.reshape(groups, -1, 2, width).transpose(1, 2, 0, 3).reshape(-1, 2 * SFF)
    sdown = jnp.sum(sdown.astype(f32), axis=0)
    own_up, per = MODEL_WIDTH // lines, EXPERT_HIDDEN // lines
    rest = own_experts[:, own_up + per :]
    cut = rest.shape[2] // 2
    rest = jnp.concatenate([rest[:, :, :cut], rest[:, :, cut:]], axis=1)
    own_down = jnp.concatenate([own_experts[:, own_up : own_up + per], rest], axis=2)
    return (
        output, input_grad, norm_g.reshape(-1), own_in, conv_w, conv_b.reshape(-1), heads[0, :HEADS], heads[1, :HEADS],
        heads[2, :HEADS], mix_g.reshape(-1), own_out, ffn_g.reshape(-1), own_router, sup, sdown,
        own_experts[:, :own_up].astype(f32), own_down.astype(f32),
    )


def solution(mesh):
    def program(*arrays):
        each = arrays[0].shape[0] == lax.axis_size("seq") == 4 and lax.axis_size("dp") == 8
        return (local_fast if each else local)(*arrays)

    return jax.shard_map(
        program,
        mesh=mesh,
        in_specs=(
            P("dp", "seq", None),
            P("dp"),
            P("dp", "seq", None),
            P("dp", "seq", None),
            P(),
            P(("dp", "seq"), None),
            P(),
            P(),
            P(),
            P(),
            P(),
            P(),
            P(("dp", "seq"), None),
            P(),
            P(("dp", "seq"), None),
            P(("dp", "seq"), None),
            P(("dp", "seq"), None),
            P("dp", None, None),
            P("dp", None, None),
        ),
        out_specs=(
            P("dp", "seq", None),
            P("dp", "seq", None),
            P(),
            P(("dp", "seq"), None),
            P(),
            P(),
            P(),
            P(),
            P(),
            P(),
            P(("dp", "seq"), None),
            P(),
            P(("dp", "seq"), None),
            P(("dp", "seq"), None),
            P(("dp", "seq"), None),
            P("dp", "seq", None),
            P("dp", "seq", None),
        ),
        check_vma=False,
    )
```

```python
from functools import partial

import jax
import jax.numpy as jnp
from jax import lax
from jax.experimental import pallas as pl
from jax.experimental.pallas import tpu as pltpu
from jax.sharding import PartitionSpec as P

MODEL_WIDTH = 1536
INNER = 3072
HEADS = 48
HDIM = 64
STATE = 128
KCONV = 4
EXPERT_HIDDEN = 512
SFF = 1024
MB = 4
CONV = 3328
PROJ = 6448


EPSILON = 1e-05
PRECISE = lax.Precision.HIGHEST
MESH = pl.DeviceIdType.MESH


def from_behind(x, axis, by):
    size = lax.axis_size(axis)
    pairs = [(i, i + by) for i in range(size) if 0 <= i + by < size]
    return lax.ppermute(x, axis, pairs)


def prefix(x, axis, join, neutral):
    place = lax.axis_index(axis)
    gathered = jax.tree.map(
        lambda a, kind: lax.all_gather(a.astype(kind), axis), x, (jnp.bfloat16, jnp.bfloat16)
    )
    state = jax.tree.map(lambda a, e: jnp.zeros_like(a) + jnp.asarray(e, a.dtype), x, neutral)

    def one(step, state):
        return join(
            state,
            jax.tree.map(
                lambda a, own: lax.dynamic_index_in_dim(a, step, 0, False).astype(own.dtype),
                gathered,
                x,
            ),
        )

    return lax.fori_loop(0, place, one, state)


def prefix_2(x, axis, join, neutral):
    count = lax.axis_size(axis)
    place = lax.axis_index(axis)
    ahead = count - 1 - place
    gathered = jax.tree.map(
        lambda a, kind: lax.all_gather(a.astype(kind), axis),
        x,
        jax.tree.map(lambda a: jnp.bfloat16 if a.dtype == jnp.float32 else a.dtype, x),
    )
    state = jax.tree.map(lambda a, e: jnp.zeros_like(a) + jnp.asarray(e, a.dtype), x, neutral)

    def one(step, state):
        source = count - 1 - step
        return join(
            state,
            jax.tree.map(
                lambda a, own: lax.dynamic_index_in_dim(a, source, 0, False).astype(own.dtype),
                gathered,
                x,
            ),
        )

    return lax.fori_loop(0, ahead, one, state)


def rms_norm(values, gain_vec):
    return (
        values * lax.rsqrt(jnp.mean(values * values, axis=-1, keepdims=True) + EPSILON) * gain_vec
    )


def swiglu(values, half_width):
    return jax.nn.silu(values[..., :half_width]) * values[..., half_width:]


def contract_rows(left_mat, right_mat):
    return lax.dot_general(
        left_mat, right_mat, (((0,), (0,)), ((), ())), preferred_element_type=jnp.float32
    )


def contract_cols(left_mat, right_mat):
    return lax.dot_general(
        left_mat, right_mat, (((1,), (1,)), ((), ())), preferred_element_type=jnp.float32
    )


def block_terms(head_in, b_rows, c_rows, step_sizes, a_log):
    log_rates = -step_sizes * jnp.exp(a_log)
    cumulative = jnp.cumsum(log_rates, axis=0)
    block_len = head_in.shape[0]
    lower_tri = jnp.arange(block_len)[:, None] >= jnp.arange(block_len)[None, :]
    spread = jnp.where(
        lower_tri[:, :, None], cumulative[:, None, :] - cumulative[None, :, :], -jnp.inf
    )
    scores = jnp.dot(c_rows, b_rows.T, precision=PRECISE)
    weights = jnp.exp(spread) * scores[:, :, None] * step_sizes[None, :, :]
    local_out = jnp.einsum("tih,ihp->thp", weights, head_in, precision=PRECISE)
    tail_weight = jnp.exp(cumulative[-1][None, :] - cumulative) * step_sizes
    local_state = jnp.einsum("ih,ihp,in->hpn", tail_weight, head_in, b_rows, precision=PRECISE)
    return (cumulative, local_out, local_state, jnp.exp(cumulative[-1]))


def carried_out(c_rows, cumulative, state_in):
    return (
        jnp.einsum("tn,hpn->thp", c_rows, state_in, precision=PRECISE)
        * jnp.exp(cumulative)[:, :, None]
    )


def mixer_front(valid_rows, projected, previous, conv_weight, conv_bias, dt_bias, a_log):
    row_count = projected.shape[0]
    conv_in = projected[:, INNER : INNER + CONV]
    padded = jnp.concatenate([previous, conv_in], axis=0)
    conv_sum = conv_bias + conv_weight[0] * padded[0:row_count]
    for tap_idx in range(1, KCONV):
        conv_sum = conv_sum + conv_weight[tap_idx] * padded[tap_idx : tap_idx + row_count]
    activated = jax.nn.silu(conv_sum) * valid_rows
    head_in = activated[:, :INNER].reshape(row_count, HEADS, HDIM)
    b_rows = activated[:, INNER : INNER + STATE]
    c_rows = activated[:, INNER + STATE :]
    step_sizes = jax.nn.softplus(projected[:, INNER + CONV :] + dt_bias)
    cumulative, local_out, local_state, decay_total = block_terms(
        head_in, b_rows, c_rows, step_sizes, a_log
    )
    return (projected[:, :INNER], head_in, c_rows, cumulative, local_out, local_state, decay_total)


def mixer_tail(gate_z, head_in, c_rows, cumulative, local_out, state_in, d_skip, mix_gain):
    mixed_out = local_out + carried_out(c_rows, cumulative, state_in) + d_skip[:, None] * head_in
    gated_out = mixed_out.reshape(head_in.shape[0], INNER) * jax.nn.silu(gate_z)
    return rms_norm(gated_out, mix_gain)


def link_states(earlier, latter):
    return (earlier[0] * latter[0], latter[1] + latter[0][:, None, None] * earlier[1])


def local(
    tokens,
    lengths,
    routes,
    cotangent,
    norm_gain,
    in_weight,
    conv_weight,
    conv_bias,
    dt_bias,
    a_log,
    d_skip,
    mix_gain,
    out_weight,
    ffn_gain,
    router_weight,
    shared_up,
    shared_down,
    expert_up,
    expert_down,
):
    row_count = tokens.shape[1]
    resident_experts = expert_up.shape[0]
    groups = lax.axis_size("dp")
    experts = resident_experts * groups
    top_count = routes.shape[2]
    capacity = row_count * top_count * 5 // (4 * experts)
    shards = (in_weight, out_weight, router_weight, shared_up, shared_down)
    kept_full = (
        lax.all_gather(shards[0], ("dp", "seq"), axis=0, tiled=True),
        lax.all_gather(shards[1], ("dp", "seq"), axis=0, tiled=True),
        lax.all_gather(shards[2], ("dp", "seq"), axis=0, tiled=True),
        lax.all_gather(shards[3], ("dp", "seq"), axis=0, tiled=True),
        lax.all_gather(shards[4], ("dp", "seq"), axis=0, tiled=True),
    )
    grad_inw = jnp.zeros((MODEL_WIDTH, PROJ), jnp.float32)
    grad_outw = jnp.zeros((INNER, MODEL_WIDTH), jnp.float32)
    grad_router = jnp.zeros((MODEL_WIDTH, experts), jnp.float32)
    grad_sup = jnp.zeros((MODEL_WIDTH, 2 * SFF), jnp.float32)
    grad_sdown = jnp.zeros((SFF, MODEL_WIDTH), jnp.float32)
    expert_upward_grad = jnp.zeros((resident_experts, MODEL_WIDTH, 2 * EXPERT_HIDDEN), jnp.float32)
    grad_edown = jnp.zeros((resident_experts, EXPERT_HIDDEN, MODEL_WIDTH), jnp.float32)
    grad_ngain = jnp.zeros_like(norm_gain)
    grad_cw = jnp.zeros_like(conv_weight)
    grad_cb = jnp.zeros_like(conv_bias)
    grad_db = jnp.zeros_like(dt_bias)
    grad_al = jnp.zeros_like(a_log)
    grad_skip = jnp.zeros_like(d_skip)
    grad_mgain = jnp.zeros_like(mix_gain)
    grad_fgain = jnp.zeros_like(ffn_gain)
    outputs = []
    input_grads = []
    for micro_idx in range(MB):
        in_full, out_full, router_full, up_full, down_full = kept_full
        x_rows = tokens[micro_idx].astype(jnp.float32)
        position = lax.axis_index("seq") * row_count + jnp.arange(row_count)
        valid_rows = (position < lengths[micro_idx]).astype(jnp.float32)[:, None]
        normed, norm_pull = jax.vjp(rms_norm, x_rows, norm_gain)
        normed_low = normed.astype(jnp.bfloat16)
        projected = jnp.dot(normed_low, in_full, preferred_element_type=jnp.float32).astype(
            jnp.bfloat16
        )
        previous = from_behind(projected[row_count - (KCONV - 1) :, INNER : INNER + CONV], "seq", 1)
        front_out, front_pull = jax.vjp(
            partial(mixer_front, valid_rows),
            projected.astype(jnp.float32),
            previous.astype(jnp.float32),
            conv_weight,
            conv_bias,
            dt_bias,
            a_log,
        )
        gate_z, head_in, c_rows, cumulative, local_out, local_state, decay_total = front_out
        identity = (jnp.ones_like(decay_total), jnp.zeros_like(local_state))
        _, state_in = prefix((decay_total, local_state), "seq", link_states, identity)
        normed_mix, tail_pull = jax.vjp(
            mixer_tail, gate_z, head_in, c_rows, cumulative, local_out, state_in, d_skip, mix_gain
        )
        mix_low = normed_mix.astype(jnp.bfloat16)
        mixer_out = jnp.dot(mix_low, out_full, preferred_element_type=jnp.float32)
        hidden = x_rows + mixer_out * valid_rows
        normed_ffn, ffn_pull = jax.vjp(rms_norm, hidden, ffn_gain)
        ffn_low = normed_ffn.astype(jnp.bfloat16)
        logits = jnp.dot(ffn_low, router_full, preferred_element_type=jnp.float32)
        route_row = routes[micro_idx]
        picked = jnp.take_along_axis(logits, route_row, axis=1)
        gate_probs = jax.nn.softmax(picked, axis=-1)
        shared_gu = jnp.dot(ffn_low, up_full, preferred_element_type=jnp.float32)
        shared_act, shared_pull = jax.vjp(partial(swiglu, half_width=SFF), shared_gu)
        shared_h = shared_act.astype(jnp.bfloat16)
        shared_y = jnp.dot(shared_h, down_full, preferred_element_type=jnp.float32)
        flat_route = route_row.reshape(-1)
        member = (flat_route[:, None] == jnp.arange(experts)[None, :]).astype(jnp.int32)
        slot_pos = jnp.sum((jnp.cumsum(member, axis=0) - member) * member, axis=1)
        target = flat_route * capacity + slot_pos
        source = (
            jnp.zeros((experts * capacity,), jnp.int32)
            .at[target]
            .set(jnp.arange(row_count * top_count, dtype=jnp.int32))
        )
        filled = jnp.zeros((experts * capacity, 1), jnp.bfloat16).at[target].set(jnp.bfloat16(1))
        outgoing = (jnp.take(ffn_low, source // top_count, axis=0) * filled).reshape(
            groups, resident_experts, capacity, MODEL_WIDTH
        )
        received_rows = lax.all_to_all(outgoing, "dp", split_axis=0, concat_axis=2, tiled=True)[0]
        expert_gu = jnp.einsum(
            "erd,edf->erf", received_rows, expert_up, preferred_element_type=jnp.float32
        )
        expert_act, expert_pull = jax.vjp(partial(swiglu, half_width=EXPERT_HIDDEN), expert_gu)
        expert_h = expert_act.astype(jnp.bfloat16)
        expert_y = jnp.einsum(
            "erf,efd->erd", expert_h, expert_down, preferred_element_type=jnp.float32
        ).astype(jnp.bfloat16)
        returned = lax.all_to_all(expert_y[None], "dp", split_axis=2, concat_axis=0, tiled=True)
        per_choice = (
            jnp.take(returned.reshape(experts * capacity, MODEL_WIDTH), target, axis=0)
            .reshape(row_count, top_count, MODEL_WIDTH)
            .astype(jnp.float32)
        )
        routed = jnp.einsum("lk,lkd->ld", gate_probs, per_choice, precision=PRECISE)
        outputs.append((hidden + valid_rows * (shared_y + routed)).astype(jnp.bfloat16))
        in_back, out_back, router_back, up_back, down_back = kept_full
        grad_out = cotangent[micro_idx].astype(jnp.float32)
        branch = valid_rows * grad_out
        shared_g = branch.astype(jnp.bfloat16)
        grad_sdown = grad_sdown + contract_rows(shared_h, shared_g)
        grad_sgu = shared_pull(contract_cols(shared_g, down_back))[0].astype(jnp.bfloat16)
        grad_sup = grad_sup + contract_rows(ffn_low, grad_sgu)
        grad_ffn = contract_cols(grad_sgu, up_back)
        grad_choice = (gate_probs[:, :, None] * branch[:, None, :]).astype(jnp.bfloat16)
        grad_gate = jnp.sum(branch[:, None, :] * per_choice, axis=-1)
        grad_pick = gate_probs * (
            grad_gate - jnp.sum(gate_probs * grad_gate, axis=-1, keepdims=True)
        )
        onehot = (route_row[:, :, None] == jnp.arange(experts)[None, None, :]).astype(jnp.float32)
        grad_logit = jnp.einsum("lk,lke->le", grad_pick, onehot, precision=PRECISE).astype(
            jnp.bfloat16
        )
        grad_router = grad_router + contract_rows(ffn_low, grad_logit)
        grad_ffn = grad_ffn + contract_cols(grad_logit, router_back)
        back_out = (
            jnp.take(grad_choice.reshape(row_count * top_count, MODEL_WIDTH), source, axis=0)
            * filled
        ).reshape(groups, resident_experts, capacity, MODEL_WIDTH)
        grad_arrived = lax.all_to_all(back_out, "dp", split_axis=0, concat_axis=2, tiled=True)[0]
        step_edown = jnp.einsum(
            "erf,erd->efd", expert_h, grad_arrived, preferred_element_type=jnp.float32
        )
        grad_eh = jnp.einsum(
            "erd,efd->erf", grad_arrived, expert_down, preferred_element_type=jnp.float32
        )
        expert_gate_up_grad = expert_pull(grad_eh)[0].astype(jnp.bfloat16)
        expert_upward_step = jnp.einsum(
            "tbw,tbj->twj", received_rows, expert_gate_up_grad, preferred_element_type=jnp.float32
        )
        grad_ein = jnp.einsum(
            "erf,edf->erd", expert_gate_up_grad, expert_up, preferred_element_type=jnp.float32
        ).astype(jnp.bfloat16)
        expert_upward_grad = expert_upward_grad + expert_upward_step
        grad_edown = grad_edown + step_edown
        came_back = lax.all_to_all(grad_ein[None], "dp", split_axis=2, concat_axis=0, tiled=True)
        grad_ffn = grad_ffn + jnp.sum(
            jnp.take(came_back.reshape(experts * capacity, MODEL_WIDTH), target, axis=0)
            .reshape(row_count, top_count, MODEL_WIDTH)
            .astype(jnp.float32),
            axis=1,
        )
        grad_hidden, step_fgain = ffn_pull(grad_ffn)
        grad_fgain = grad_fgain + step_fgain
        grad_hidden = grad_hidden + grad_out
        grad_mix_out = (grad_hidden * valid_rows).astype(jnp.bfloat16)
        grad_outw = grad_outw + contract_rows(mix_low, grad_mix_out)
        grad_mix = contract_cols(grad_mix_out, out_back)
        grad_z, grad_head, grad_c, grad_cum, grad_local, grad_state, step_skip, step_mgain = (
            tail_pull(grad_mix)
        )
        grad_skip = grad_skip + step_skip
        grad_mgain = grad_mgain + step_mgain
        _, grad_carry = prefix_2((decay_total, grad_state), "seq", link_states, identity)
        grad_decay = jnp.sum(grad_carry * state_in, axis=(1, 2))
        grad_proj, grad_prev, step_cw, step_cb, step_db, step_al = front_pull(
            (grad_z, grad_head, grad_c, grad_cum, grad_local, grad_carry, grad_decay)
        )
        grad_cw = grad_cw + step_cw
        grad_cb = grad_cb + step_cb
        grad_db = grad_db + step_db
        grad_al = grad_al + step_al
        from_next = from_behind(grad_prev.astype(jnp.bfloat16), "seq", -1).astype(grad_prev.dtype)
        grad_proj = (
            grad_proj.at[row_count - (KCONV - 1) :, INNER : INNER + CONV]
            .add(from_next)
            .astype(jnp.bfloat16)
        )
        grad_inw = grad_inw + contract_rows(normed_low, grad_proj)
        grad_normed = contract_cols(grad_proj, in_back)
        grad_x, step_ngain = norm_pull(grad_normed)
        grad_ngain = grad_ngain + step_ngain
        input_grads.append((grad_x + grad_hidden).astype(jnp.bfloat16))
    weight_grads = (
        lax.psum_scatter(grad_inw, ("dp", "seq"), scatter_dimension=0, tiled=True),
        lax.psum_scatter(grad_outw, ("dp", "seq"), scatter_dimension=0, tiled=True),
        lax.psum_scatter(grad_router, ("dp", "seq"), scatter_dimension=0, tiled=True),
        lax.psum_scatter(grad_sup, ("dp", "seq"), scatter_dimension=0, tiled=True),
        lax.psum_scatter(grad_sdown, ("dp", "seq"), scatter_dimension=0, tiled=True),
    )
    small_sums = lax.psum(
        (grad_ngain, grad_cw, grad_cb, grad_db, grad_al, grad_skip, grad_mgain, grad_fgain),
        ("dp", "seq"),
    )
    expert_sums = (
        lax.psum_scatter(
            expert_upward_grad.astype(jnp.bfloat16), "seq", scatter_dimension=1, tiled=True
        ).astype(jnp.float32),
        lax.psum_scatter(
            grad_edown.astype(jnp.bfloat16), "seq", scatter_dimension=1, tiled=True
        ).astype(jnp.float32),
    )
    return (
        jnp.stack(outputs),
        jnp.stack(input_grads),
        small_sums[0],
        weight_grads[0],
        small_sums[1],
        small_sums[2],
        small_sums[3],
        small_sums[4],
        small_sums[5],
        small_sums[6],
        weight_grads[1],
        small_sums[7],
        weight_grads[2],
        weight_grads[3],
        weight_grads[4],
        expert_sums[0],
        expert_sums[1],
    )


def at_neighbours():
    d = lax.axis_index("dp")
    core, x, y = d % 2, (d // 2) % 2, d // 4
    return d, core, x, y, d + 1 - 2 * core, d + 2 - 4 * x, d + 4 - 8 * y


def meet(devices):
    barrier = pltpu.get_barrier_semaphore()
    for there in devices:
        pl.semaphore_signal(barrier, inc=1, device_id=there, device_id_type=MESH)
    pl.semaphore_wait(barrier, len(devices))


def send(source, target, send_sem, recv_sem, there):
    copy = pltpu.make_async_remote_copy(
        src_ref=source, dst_ref=target, send_sem=send_sem, recv_sem=recv_sem,
        device_id=there, device_id_type=MESH,
    )
    copy.start()
    return copy


def add_into(target, source, high):
    step = 16
    for s in (64, 48, 32):
        if high % s == 0:
            step = s
            break

    @pl.loop(0, high // step)
    def _(i):
        rows = pl.ds(pl.multiple_of(i * step, step), step)
        target[rows, :] = target[rows, :] + source[rows, :]


def swap_start(swaps, landed, line, lines, local_sem, send_sem, recv_sem):
    copies = []
    for n, (a, b) in enumerate(zip(swaps, landed)):
        keep = pltpu.make_async_copy(a.at[line], b.at[line], local_sem.at[n])
        keep.start()
        away = [
            send(a.at[o], b.at[line], send_sem.at[n, k], recv_sem.at[n, k], {"seq": o})
            for k, o in enumerate(lax.rem(line + k, lines) for k in range(1, lines))
        ]
        copies.append((keep, away))
    return copies


def swap_end(copies):
    for keep, away in copies:
        for copy in away:
            copy.wait_recv()
    for keep, away in copies:
        for copy in away:
            copy.wait_send()
        keep.wait()


def swap_sems(count, lines):
    dma = pltpu.SemaphoreType.DMA
    return [dma((count,)), dma((count, lines - 1)), dma((count, lines - 1))]


def sum_body(items, arrays, lines, tiny, moved, relative, *refs):
    count = len(items)
    grads, refs = refs[:arrays], refs[arrays:]
    swaps, refs = refs[:moved], refs[moved:]
    if tiny:
        small_in, refs = refs[:4], refs[4:]
    outs, refs = refs[:arrays], refs[arrays:]
    landed, refs = refs[:moved], refs[moved:]
    if tiny:
        small_out, refs = refs[:6], refs[6:]
    own, refs = refs[:count], refs[count:]
    got, refs = refs[:count], refs[count:]
    from_x, refs = refs[:count], refs[count:]
    from_y, refs = refs[:count], refs[count:]
    last_x, refs = refs[:count], refs[count:]
    last_y, refs = refs[:count], refs[count:]
    if lines > 1:
        from_z, refs = refs[:count], refs[count:]
    (load_sem, send_sem, recv_sem), refs = refs[:3], refs[3:]
    if moved:
        swap_sem, refs = refs[:3], refs[3:]
    if tiny:
        packed, half, t_core, t_x, t_y, t_z, t_back, t_send, t_recv = refs
    d, core, x, y, at_core, at_x, at_y = at_neighbours()
    bits = [(0, 0, 0) if own else (core, x, y) for own in relative]
    own_core = core
    line = lax.axis_index("seq")
    others = [lax.rem(line + k, lines) for k in range(1, lines)]
    beside, across = line + 1 - 2 * (line % 2), lax.rem(line + 2, 4)
    meet([{"dp": at_core}, {"dp": at_x}, {"dp": at_y}] + [{"seq": o} for o in others])
    sent = [[] for _ in items]
    stage = [None] * count
    cross = [None] * count
    close = [None] * count
    along = [None] * count
    loads = [None] * count

    def begin(t):
        a, c0, wide, high = items[t]
        core, x, y = bits[a]
        cols = pl.ds(c0, wide)
        loads[t] = pltpu.make_async_copy(grads[a].at[:, :, core, :, cols], own[t], load_sem.at[t])
        loads[t].start()
        stage[t] = send(
            grads[a].at[:, :, 1 - core, :, cols], got[t], send_sem.at[t, 0], recv_sem.at[t, 0], {"dp": at_core}
        )

    def fold(t):
        a, c0, wide, high = items[t]
        core, x, y = bits[a]
        loads[t].wait()
        stage[t].wait_recv()
        for i in range(2):
            for j in range(2):
                add_into(got[t].at[i, j], own[t].at[i, j], high)
        top, low = pl.ds(0, high // 2), pl.ds(high // 2, high // 2)
        cross[t] = (
            send(got[t].at[:, 1 - x, top, :], from_x[t], send_sem.at[t, 1], recv_sem.at[t, 1], {"dp": at_x}),
            send(got[t].at[1 - y, :, low, :], from_y[t], send_sem.at[t, 2], recv_sem.at[t, 2], {"dp": at_y}),
        )

    def turn(t):
        a, c0, wide, high = items[t]
        core, x, y = bits[a]
        top, low = pl.ds(0, high // 2), pl.ds(high // 2, high // 2)
        cross[t][0].wait_recv()
        for i in range(2):
            add_into(got[t].at[i, x, top, :], from_x[t].at[i], high // 2)
        close_y = send(got[t].at[1 - y, x, top, :], last_y[t], send_sem.at[t, 3], recv_sem.at[t, 3], {"dp": at_y})
        cross[t][1].wait_recv()
        for j in range(2):
            add_into(got[t].at[y, j, low, :], from_y[t].at[j], high // 2)
        close_x = send(got[t].at[y, 1 - x, low, :], last_x[t], send_sem.at[t, 4], recv_sem.at[t, 4], {"dp": at_x})
        close[t] = (close_y, close_x)

    def settle(t):
        a, c0, wide, high = items[t]
        core, x, y = bits[a]
        top, low = pl.ds(0, high // 2), pl.ds(high // 2, high // 2)
        cols = pl.ds(c0, wide)
        close[t][0].wait_recv()
        add_into(got[t].at[y, x, top, :], last_y[t], high // 2)
        close[t][1].wait_recv()
        add_into(got[t].at[y, x, low, :], last_x[t], high // 2)
        if lines == 1:
            show = min(wide, outs[a].shape[1] - c0)
            outs[a][:, c0 : c0 + show] = got[t][y, x, :, :show].astype(jnp.float32)
            return
        each = high // lines
        along[t] = tuple(
            send(
                unit(t, 1 - line % 2 + 2 * k, each), from_z[t].at[k],
                send_sem.at[t, 5 + k], recv_sem.at[t, 5 + k], {"seq": beside},
            )
            for k in range(2)
        )

    def unit(t, u, each):
        core, x, y = bits[items[t][0]]
        return got[t].at[y, x, pl.ds(pl.multiple_of(u * each, 16), each), :]

    def halve(t):
        each = items[t][3] // lines
        for k in range(2):
            along[t][k].wait_recv()
            add_into(unit(t, line % 2 + 2 * k, each), from_z[t].at[k], each)
        along[t] += (
            send(unit(t, across, each), from_z[t].at[2], send_sem.at[t, 7], recv_sem.at[t, 7], {"seq": across}),
        )

    def finish(t):
        a, c0, wide, high = items[t]
        along[t][2].wait_recv()
        total = unit(t, line, high // lines)[...].astype(jnp.float32) + from_z[t][2].astype(jnp.float32)
        show = min(wide, outs[a].shape[1] - c0)
        outs[a][:, c0 : c0 + show] = total[:, :show]

    little = []

    def tiny_step(n):
        if n == 0:
            at = 0
            for part in small_in:
                size = part.shape[1] // 2
                for k in range(2):
                    packed[k, :, at : at + size] = part[:, k * size : (k + 1) * size]
                at += size
            little.append(send(packed.at[1 - own_core], t_core, t_send.at[0], t_recv.at[0], {"dp": at_core}))
        elif n == 1:
            little[0].wait_recv()
            half[0] = packed[own_core] + t_core[...]
            little.append(send(half.at[0], t_x, t_send.at[1], t_recv.at[1], {"dp": at_x}))
        elif n == 2:
            little[1].wait_recv()
            half[1] = half[0] + t_x[...]
            little.append(send(half.at[1], t_y, t_send.at[2], t_recv.at[2], {"dp": at_y}))
        elif n == 3:
            little[2].wait_recv()
            half[2] = half[1] + t_y[...]
            t_z[line] = half[2]
            for k, o in enumerate(others):
                little.append(send(half.at[2], t_z.at[line], t_send.at[3 + k], t_recv.at[3 + k], {"seq": o}))
        elif n == 4:
            for k in range(lines - 1):
                little[3 + k].wait_recv()
            total = t_z[0]
            for k in range(1, lines):
                total = total + t_z[k]
            t_back[own_core] = total
            little.append(
                send(t_back.at[own_core], t_back.at[own_core], t_send.at[7], t_recv.at[7], {"dp": at_core})
            )
        elif n == 5:
            little[-1].wait_recv()
            for copy in little:
                copy.wait_send()
            conv_w, conv_b, mix_g, norm_g, ffn_g, heads = small_out
            at = 0
            spans = []
            for part in small_in:
                size = part.shape[1] // 2
                spans.append((at, size))
                at += size
            for k in range(2):
                at, size = spans[0]
                mix_g[k * size : (k + 1) * size] = t_back[k, 0, at : at + size]
                conv_b[k * size : (k + 1) * size] = t_back[k, 2, at : at + size]
                conv_w[:, k * size : (k + 1) * size] = t_back[k, 3:7, at : at + size]
                at, size = spans[1]
                here = INNER + k * size
                conv_b[here : here + size] = t_back[k, 0, at : at + size]
                conv_w[:, here : here + size] = t_back[k, 1:5, at : at + size]
                at, size = spans[2]
                norm_g[k * size : (k + 1) * size] = t_back[k, 0, at : at + size]
                ffn_g[k * size : (k + 1) * size] = t_back[k, 1, at : at + size]
                at, size = spans[3]
                heads[:, k * size : (k + 1) * size] = t_back[k, :, at : at + size]

    begin(0)
    if tiny:
        tiny_step(0)
    moves = swap_start(swaps, landed, line, lines, *swap_sem) if moved else ()
    for t in range(max(count + 4, 5 if tiny else 0)):
        if t + 1 < count:
            begin(t + 1)
        if t < count:
            fold(t)
        if 0 <= t - 1 < count:
            turn(t - 1)
        if 0 <= t - 2 < count:
            settle(t - 2)
        if lines > 1 and 0 <= t - 3 < count:
            halve(t - 3)
        if lines > 1 and 0 <= t - 4 < count:
            finish(t - 4)
        if tiny and t < 5:
            tiny_step(t + 1)
    swap_end(moves)
    for t in range(count):
        stage[t].wait_send()
        for copy in cross[t] + close[t] + tuple(along[t] or ()):
            copy.wait_send()


def sum_to_owners(grads, widths, lines, shown, small, swaps, relative, identity):
    items, starts = [], [0] * len(grads)
    views = [g.reshape(2, 2, 2, g.shape[0] // 8, g.shape[1]) for g in grads]
    for a, wide in widths:
        items.append((a, starts[a], wide, views[a].shape[3]))
        starts[a] += wide
    assert starts == [g.shape[1] for g in grads]
    tiny = small is not None
    bf = jnp.bfloat16
    scratch = [pltpu.VMEM((2, 2, h, w), bf) for _, _, w, h in items]
    scratch += [pltpu.VMEM((2, 2, h, w), bf) for _, _, w, h in items]
    scratch += [pltpu.VMEM((2, h // 2, w), bf) for _, _, w, h in items] * 2
    scratch += [pltpu.VMEM((h // 2, w), bf) for _, _, w, h in items] * 2
    if lines > 1:
        scratch += [pltpu.VMEM((lines - 1, h // lines, w), bf) for _, _, w, h in items]
    ways = 4 + lines
    scratch += [
        pltpu.SemaphoreType.DMA((len(items),)),
        pltpu.SemaphoreType.DMA((len(items), ways)),
        pltpu.SemaphoreType.DMA((len(items), ways)),
    ]
    out_shape = [
        jax.ShapeDtypeStruct((g.shape[0] // 8 // lines, cols), jnp.float32) for g, cols in zip(grads, shown)
    ]
    ins = list(views)
    in_specs = [pl.BlockSpec(memory_space=pl.ANY)] * len(views)
    out_specs = [pl.BlockSpec(memory_space=pltpu.VMEM)] * len(views)
    if swaps:
        scratch += swap_sems(len(swaps), lines)
        ins += swaps
        in_specs += [pl.BlockSpec(memory_space=pl.ANY)] * len(swaps)
        out_specs += [pl.BlockSpec(memory_space=pl.ANY)] * len(swaps)
        out_shape += [jax.ShapeDtypeStruct(a.shape, a.dtype) for a in swaps]
    if tiny:
        cols = sum(part.shape[1] for part in small) // 2
        part = lambda *lead: pltpu.VMEM(lead + (8, cols), jnp.float32)
        scratch += [part(2), part(3), part(), part(), part(), part(lines), part(2)]
        scratch += [pltpu.SemaphoreType.DMA((8,)), pltpu.SemaphoreType.DMA((8,))]
        ins += small
        in_specs += [pl.BlockSpec(memory_space=pltpu.VMEM)] * 4
        for shape in ((KCONV, CONV), (CONV,), (INNER,), (MODEL_WIDTH,), (MODEL_WIDTH,), (8, 256)):
            out_shape.append(jax.ShapeDtypeStruct(shape, jnp.float32))
            out_specs.append(pl.BlockSpec(memory_space=pltpu.VMEM))
    return pl.pallas_call(
        partial(sum_body, items, len(views), lines, tiny, len(swaps), relative),
        out_shape=out_shape,
        in_specs=in_specs,
        out_specs=out_specs,
        scratch_shapes=scratch,
        name="sum_to_owners_%d" % identity,
        compiler_params=pltpu.CompilerParams(
            collective_id=identity, has_side_effects=True, vmem_limit_bytes=60 << 20
        ),
    )(*ins)


def gather_body(pieces, arrays, flat, lines, ahead, moved, relative, *refs):
    mine, refs = refs[:arrays], refs[arrays:]
    swaps, refs = refs[:moved], refs[moved:]
    full, refs = refs[:arrays], refs[arrays:]
    landed, refs = refs[:moved], refs[moved:]
    keep_sem, send_sem, recv_sem, z_send, z_recv = refs[:5]
    swap_sem = refs[5:]
    d, core, x, y, at_core, at_x, at_y = at_neighbours()
    at_far = at_x + at_y - d
    line = lax.rem(lax.axis_index("seq"), lines)
    hops = [line]
    if lines > 1:
        upper = line // 2
        hops += [line + 1 - 2 * (line % 2), 2 - upper, 3 - 3 * upper]
    meet([{"dp": at_core}, {"dp": at_x}, {"dp": at_y}] + [{"seq": o} for o in hops[1:]])
    blocks = dict(own=d, x=at_x, y=at_y, far=at_far)
    lands = dict(x=d, y=d, core=d, x_y=at_x, x_core=at_x, y_x=at_y, y_core=at_y, far_core=at_far)
    if relative:
        blocks = dict(own=0, x=2, y=4, far=6)
        lands = dict(x=2, y=4, core=1, x_y=6, x_core=3, y_x=6, y_core=5, far_core=7)
    mains = [q for q, piece in enumerate(pieces) if piece[0] < arrays - flat]
    sides = [q for q, piece in enumerate(pieces) if piece[0] >= arrays - flat]
    home = lambda a: blocks["own"] if a < arrays - flat else 0
    keep = []
    for a in range(arrays):
        keep.append(pltpu.make_async_copy(mine[a], full[a].at[home(a), line], keep_sem.at[a]))
        keep[a].start()
    order = [(j, q) for j in range(lines) for q in mains]
    total = len(order)
    out = [[None] * 7 for _ in order]

    def place(j, q, block):
        a, r0, high = pieces[q]
        return full[a].at[block, hops[j], pl.ds(r0, high), :]

    def own_piece(q):
        a, r0, high = pieces[q]
        return mine[a].at[pl.ds(r0, high), :]

    def hop(j, q, sem, to):
        a = pieces[q][0]
        return pltpu.make_async_remote_copy(
            src_ref=own_piece(q) if j == 0 else place(j, q, home(a)),
            dst_ref=place(j, q, home(a)),
            send_sem=z_send.at[q, sem], recv_sem=z_recv.at[q, hops[j]],
            device_id={"seq": to}, device_id_type=MESH,
        )

    def onward(j, q, act):
        o = hops[j]

        @pl.when((o <= line) & (line < lines - 1))
        def _():
            act(hop(j, q, 2 * j, jnp.minimum(line + 1, lines - 1)))

        @pl.when((o >= line) & (line > 0))
        def _():
            act(hop(j, q, 2 * j + 1, jnp.maximum(line - 1, 0)))

    def relay(j, q):
        hop(j, q, 2 * j, line).wait_recv()
        onward(j, q, lambda copy: copy.start())

    def pass_on(i, n, block, lands_at, there):
        j, q = order[i]
        source = own_piece(q) if block is None else place(j, q, block)
        out[i][n] = send(
            source, place(j, q, lands[lands_at]), send_sem.at[i, n], recv_sem.at[i, n], {"dp": there}
        )

    def first(i):
        block = None if order[i][0] == 0 else blocks["own"]
        pass_on(i, 0, block, "x", at_x)
        pass_on(i, 1, block, "y", at_y)
        pass_on(i, 2, block, "core", at_core)

    def second(i):
        out[i][0].wait_recv()
        if sum((i,) + order[i][:1]) % 2 == 0:
            pass_on(i, 5, blocks["x"], "x_y", at_y)
        pass_on(i, 3, blocks["x"], "x_core", at_core)
        out[i][1].wait_recv()
        if sum((i,) + order[i][:1]) % 2 == 1:
            pass_on(i, 5, blocks["y"], "y_x", at_x)
        pass_on(i, 4, blocks["y"], "y_core", at_core)

    def third(i):
        out[i][5].wait_recv()
        pass_on(i, 6, blocks["far"], "far_core", at_core)

    lead = ahead + 2
    if lines > 1:
        for q in mains:
            onward(0, q, lambda copy: copy.start())
    for i in range(min(ahead, total)):
        first(i)
    moves = swap_start(swaps, landed, line, lines, *swap_sem) if moved else ()
    for i in range(total):
        if i + lead < total and order[i + lead][0] > 0:
            relay(*order[i + lead])
        if i % len(mains) == 1:
            j = i // len(mains)
            for q in sides:
                if j == 0:
                    onward(0, q, lambda copy: copy.start())
                else:
                    relay(j, q)
        if i + ahead < total:
            first(i + ahead)
        second(i)
        if i:
            third(i - 1)
    third(total - 1)
    for i in range(total):
        for n in (2, 3, 4, 6):
            out[i][n].wait_recv()
        for copy in out[i]:
            copy.wait_send()
    swap_end(moves)
    if lines > 1:
        for q in range(len(pieces)):
            for j in range(lines):
                onward(j, q, lambda copy: copy.wait_send())
    for copy in keep:
        copy.wait()


def gather_rows(arrays, chunks, flat, lines, ahead, swaps, relative, identity):
    pieces = []
    count = len(arrays) + len(flat)
    for a, (w, chunk) in enumerate(zip(list(arrays) + list(flat), chunks)):
        for r0 in range(0, w.shape[0], chunk):
            pieces.append((a, r0, chunk))
    total = lines * len([p for p in pieces if p[0] < len(arrays)])
    anywhere = pl.BlockSpec(memory_space=pl.ANY)
    return pl.pallas_call(
        partial(gather_body, pieces, count, len(flat), lines, ahead, len(swaps), relative),
        out_shape=[jax.ShapeDtypeStruct((8, lines) + w.shape, w.dtype) for w in arrays]
        + [jax.ShapeDtypeStruct((1, lines) + w.shape, w.dtype) for w in flat]
        + [jax.ShapeDtypeStruct(a.shape, a.dtype) for a in swaps],
        in_specs=[anywhere] * (count + len(swaps)),
        out_specs=[anywhere] * (count + len(swaps)),
        scratch_shapes=[
            pltpu.SemaphoreType.DMA((count,)),
            pltpu.SemaphoreType.DMA((total, 7)),
            pltpu.SemaphoreType.DMA((total, 7)),
            pltpu.SemaphoreType.DMA((len(pieces), 2 * lines)),
            pltpu.SemaphoreType.DMA((len(pieces), lines)),
        ]
        + (swap_sems(len(swaps), lines) if swaps else []),
        name="gather_rows_%d" % identity,
        compiler_params=pltpu.CompilerParams(collective_id=identity, has_side_effects=True),
    )(*arrays, *flat, *swaps)


def sigmoid(v):
    return 1.0 / (1.0 + jnp.exp(-v))


def shifted(v, by):
    if by == 0:
        return v
    rows = v.shape[0]
    at = lax.broadcasted_iota(jnp.int32, v.shape, 0)
    keep = at >= by if by > 0 else at < rows + by
    return jnp.where(keep, pltpu.roll(v, by % rows, 0), 0.0)


def conv_sums(v, taps, bias):
    total = bias
    for k in range(KCONV):
        total = total + taps[k : k + 1, :] * shifted(v, KCONV - 1 - k)
    return total


def conv_back(v, taps, bias, valid, grad):
    conv_sum = conv_sums(v, taps, bias)
    s = sigmoid(conv_sum)
    grad = grad * valid * (s * (1.0 + conv_sum * (1.0 - s)))
    total = taps[KCONV - 1 : KCONV, :] * grad
    for k in range(KCONV - 1):
        total = total + taps[k : k + 1, :] * shifted(grad, k - (KCONV - 1))
    sums = [jnp.sum(grad, axis=0, keepdims=True)]
    for k in range(KCONV):
        sums.append(jnp.sum(grad * shifted(v, KCONV - 1 - k), axis=0, keepdims=True))
    return total, sums


def head_columns(ref, pair):
    v = pltpu.roll(ref[...], lax.rem(128 - 2 * pair, 128), 1)
    return v[:, 0:1], v[:, 1:2]


def over_lanes(columns):
    rows = columns[0].shape[0]
    lane = lax.broadcasted_iota(jnp.int32, (rows, 128), 1)
    return jnp.where(lane < HDIM, columns[0], columns[1])


def lower_left(rows):
    return lax.broadcasted_iota(jnp.int32, (rows, rows), 0) >= lax.broadcasted_iota(
        jnp.int32, (rows, rows), 1
    )


def product(a, b, over_a=1, over_b=0):
    return lax.dot_general(
        a, b, (((over_a,), (over_b,)), ((), ())), preferred_element_type=jnp.float32
    )


def bc_scores(bc_ref, bc_taps, bc_bias, valid, scores, bc_keep):
    conv_sum = conv_sums(bc_ref[...].astype(jnp.float32), bc_taps[...], bc_bias[...])
    bc = conv_sum * sigmoid(conv_sum) * valid[:, :1]
    bc_keep[...] = bc.astype(jnp.bfloat16)
    rows = scores.shape[0]
    g = product(bc_keep[:, STATE:], bc_keep[:, :STATE], 1, 1)
    scores[...] = jnp.where(lower_left(rows), g, 0.0)


def front_body(
    z_ref, x_ref, bc_ref, taps, bias, bc_taps, bc_bias, valid, step, cum, cum_rows, skip,
    mixed_ref, gated_ref, squares, scores, bc_keep,
):
    f32, bf = jnp.float32, jnp.bfloat16

    @pl.when(pl.program_id(0) == 0)
    def _():
        bc_scores(bc_ref, bc_taps, bc_bias, valid, scores, bc_keep)
        squares[...] = jnp.zeros_like(squares)

    rows = x_ref.shape[0]
    half = rows // 2
    conv_sum = conv_sums(x_ref[...].astype(f32), taps[...], bias[...])
    x = conv_sum * sigmoid(conv_sum) * valid[...]
    xs = (x * over_lanes(head_columns(step, pl.program_id(0)))).astype(bf)
    sums = head_columns(cum, pl.program_id(0))
    lane = lax.broadcasted_iota(jnp.int32, (half, 128), 1)
    for r in range(2):
        at, wide = pl.ds(r * half, half), (r + 1) * half
        parts = []
        for h in range(2):
            gap = sums[h][r * half : (r + 1) * half, :] - cum_rows[0, h : h + 1, :wide]
            m = (jnp.exp(jnp.minimum(gap, 0.0)) * scores[at, :wide]).astype(bf)
            parts.append(product(m, xs[:wide, :]))
        mixed = jnp.where(lane < HDIM, parts[0], parts[1]) + skip[...] * x[r * half : (r + 1) * half, :]
        z = z_ref[at, :].astype(f32)
        gated = mixed * (z * sigmoid(z))
        mixed_ref[at, :] = mixed
        gated_ref[at, :] = gated
        squares[at, :] += gated * gated


def back_body(
    z_ref, x_ref, bc_ref, taps, bias, bc_taps, bc_bias, valid, step, cum, cum_rows, skip,
    mixed_ref, grad_ref, gain, scale, mean_dot,
    grad_z, grad_x, stats, grad_bc, bc_stats, row_sums, col_sums, step_sums,
    scores, bc_keep, grad_scores, grad_xs,
):
    f32, bf = jnp.float32, jnp.bfloat16
    pair = pl.program_id(0)

    @pl.when(pair == 0)
    def _():
        bc_scores(bc_ref, bc_taps, bc_bias, valid, scores, bc_keep)
        grad_scores[...] = jnp.zeros_like(grad_scores)
        row_sums[...] = jnp.zeros_like(row_sums)
        col_sums[...] = jnp.zeros_like(col_sums)
        step_sums[...] = jnp.zeros_like(step_sums)

    rows = x_ref.shape[0]
    half = rows // 2
    v = x_ref[...].astype(f32)
    conv_sum = conv_sums(v, taps[...], bias[...])
    x = conv_sum * sigmoid(conv_sum) * valid[...]
    steps = over_lanes(head_columns(step, pair))
    sums = head_columns(cum, pair)
    xs = (x * steps).astype(bf)
    z = z_ref[...].astype(f32)
    s = sigmoid(z)
    silu = z * s
    mixed = mixed_ref[...]
    normal = mixed * silu * scale[...]
    grad = grad_ref[...]
    grad_gated = scale[...] * (grad * gain[...] - normal * mean_dot[...])
    grad_mixed = grad_gated * silu
    grad_z[...] = (grad_gated * mixed * (s * (1.0 + z * (1.0 - s)))).astype(bf)
    lane = lax.broadcasted_iota(jnp.int32, (rows, 128), 1)
    dy = [
        jnp.where(lane < HDIM, grad_mixed, 0.0).astype(bf),
        jnp.where(lane < HDIM, 0.0, grad_mixed).astype(bf),
    ]
    for r in range(2):
        at, wide = pl.ds(r * half, half), (r + 1) * half
        total = None
        for h in range(2):
            head = 2 * pair + h
            g = scores[at, :wide]
            gap = sums[h][r * half : (r + 1) * half, :] - cum_rows[0, h : h + 1, :wide]
            e = jnp.exp(jnp.minimum(gap, 0.0))
            m = (e * g).astype(bf)
            dy_rows = dy[h][r * half : (r + 1) * half, :]
            slope = product(dy_rows, xs[:wide, :], 1, 1) * e
            grad_scores[at, :wide] += slope
            both = (slope * g).astype(bf)
            back = product(m, dy_rows, 0, 0)
            total = back if total is None else total + back
            to_lane = (lax.broadcasted_iota(jnp.int32, (wide, 128), 1) == head).astype(bf)
            row_sums[at, :] += product(both, to_lane)
            to_row = (lax.broadcasted_iota(jnp.int32, (64, half), 0) == head).astype(bf)
            col_sums[:, :wide] += product(to_row, both)
        if r == 0:
            grad_xs[:half, :] = total
        else:
            grad_xs[:half, :] += total[:half, :]
            grad_xs[half:, :] = total[half:, :]
    gxs = grad_xs[...]
    fold = (
        lax.broadcasted_iota(jnp.int32, (128, 128), 1)
        == 2 * pair + lax.broadcasted_iota(jnp.int32, (128, 128), 0) // HDIM
    ).astype(bf)
    step_sums[...] += product((gxs * x).astype(bf), fold)
    gx, parts = conv_back(v, taps[...], bias[...], valid[...], gxs * steps + skip[...] * grad_mixed)
    grad_x[...] = gx.astype(bf)
    stats[0:1, :] = jnp.sum(grad * normal, axis=0, keepdims=True)
    stats[1:2, :] = jnp.sum(grad_mixed * x, axis=0, keepdims=True)
    for k, total in enumerate(parts):
        stats[2 + k : 3 + k, :] = total
    stats[7:8, :] = jnp.zeros((1, 128), f32)

    @pl.when(pair == pl.num_programs(0) - 1)
    def _():
        gs = jnp.where(lower_left(rows), grad_scores[...], 0.0).astype(bf)
        grad_c = product(gs, bc_keep[:, :STATE])
        grad_b = product(gs, bc_keep[:, STATE:], 0, 0)
        ends = ((grad_b, 0), (grad_c, STATE))
        for g, at in ends:
            cols = pl.ds(at, STATE)
            gi, sums = conv_back(
                bc_ref[:, cols].astype(f32), bc_taps[:, cols], bc_bias[:, cols], valid[...], g
            )
            grad_bc[:, cols] = gi.astype(bf)
            for k, total in enumerate(sums):
                bc_stats[k : k + 1, cols] = total
            bc_stats[5:8, cols] = jnp.zeros((3, STATE), f32)


def mixer_specs(rows):
    tile = lambda at: pl.BlockSpec((rows, 128), at)
    whole = lambda shape: pl.BlockSpec(shape, lambda p: (0,) * len(shape))
    pairs = INNER // 128
    return tile, whole, [
        tile(lambda p: (0, p)),
        tile(lambda p: (0, pairs + p)),
        pl.BlockSpec((rows, 2 * STATE), lambda p: (0, 2 * INNER // (2 * STATE))),
        pl.BlockSpec((KCONV, 128), lambda p: (0, p)),
        pl.BlockSpec((1, 128), lambda p: (0, p)),
        pl.BlockSpec((KCONV, 2 * STATE), lambda p: (0, INNER // (2 * STATE))),
        pl.BlockSpec((1, 2 * STATE), lambda p: (0, INNER // (2 * STATE))),
        whole((rows, 128)),
        whole((rows, 128)),
        whole((rows, 128)),
        pl.BlockSpec((1, 2, rows), lambda p: (p, 0, 0)),
        pl.BlockSpec((1, 128), lambda p: (0, p)),
    ]


def mixer_front_call(inputs, rows):
    f32 = jnp.float32
    tile, whole, specs = mixer_specs(rows)
    return pl.pallas_call(
        front_body,
        grid=(INNER // 128,),
        in_specs=specs,
        out_specs=[tile(lambda p: (0, p)), tile(lambda p: (0, p)), whole((rows, 128))],
        out_shape=[
            jax.ShapeDtypeStruct((rows, INNER), f32),
            jax.ShapeDtypeStruct((rows, INNER), f32),
            jax.ShapeDtypeStruct((rows, 128), f32),
        ],
        scratch_shapes=[pltpu.VMEM((rows, rows), f32), pltpu.VMEM((rows, 2 * STATE), jnp.bfloat16)],
        name="mixer_front",
        cost_estimate=pl.CostEstimate(flops=10**10, bytes_accessed=2 * 10**7, transcendentals=5 * 10**6),
    )(*inputs)


def mixer_back_call(inputs, extra, rows):
    f32, bf = jnp.float32, jnp.bfloat16
    tile, whole, specs = mixer_specs(rows)
    by_pair = tile(lambda p: (0, p))
    return pl.pallas_call(
        back_body,
        grid=(INNER // 128,),
        in_specs=specs
        + [by_pair, by_pair, pl.BlockSpec((1, 128), lambda p: (0, p)), whole((rows, 128)), whole((rows, 128))],
        out_specs=[
            by_pair, by_pair, pl.BlockSpec((8, 128), lambda p: (0, p)), whole((rows, 2 * STATE)),
            whole((8, 2 * STATE)), whole((rows, 128)), whole((64, rows)), whole((rows, 128)),
        ],
        out_shape=[
            jax.ShapeDtypeStruct((rows, INNER), bf),
            jax.ShapeDtypeStruct((rows, INNER), bf),
            jax.ShapeDtypeStruct((8, INNER), f32),
            jax.ShapeDtypeStruct((rows, 2 * STATE), bf),
            jax.ShapeDtypeStruct((8, 2 * STATE), f32),
            jax.ShapeDtypeStruct((rows, 128), f32),
            jax.ShapeDtypeStruct((64, rows), f32),
            jax.ShapeDtypeStruct((rows, 128), f32),
        ],
        scratch_shapes=[
            pltpu.VMEM((rows, rows), f32), pltpu.VMEM((rows, 2 * STATE), bf),
            pltpu.VMEM((rows, rows), f32), pltpu.VMEM((rows, 128), f32),
        ],
        name="mixer_back",
        cost_estimate=pl.CostEstimate(flops=3 * 10**10, bytes_accessed=3 * 10**7, transcendentals=5 * 10**6),
    )(*inputs, *extra)


def picks(slot_row, slots):
    rows = slot_row.shape[1]
    at = lax.broadcasted_iota(jnp.int32, (slots, rows), 0).astype(jnp.float32)
    return at == slot_row


def cot_chunk(cots, g):
    if g < 6:
        return cots[g][...]
    return jnp.concatenate([cots[2 * g - 6][...], cots[2 * g - 5][...]], axis=0)


def experts_body(lines, x_ref, *refs):
    cots, refs = refs[:10], refs[10:]
    experts_step(lines, x_ref, cots, *refs)


def experts_step(
    lines, x_ref, cots, up, down, slot_rows, gates,
    y_out, gin_out, grads, dots,
    xe, gy, gu_grad, hid, gate_cols,
):
    f32, bf = jnp.float32, jnp.bfloat16
    chunks, rows, width = x_ref.shape
    slots = xe.shape[0] // chunks
    hidden = down.shape[1]

    for g in range(chunks):
        p = picks(slot_rows[0, g : g + 1, :], slots)
        one = p.astype(bf)
        at = pl.ds(g * slots, slots)
        xe[at, :] = product(one, x_ref[g]).astype(bf)
        gate = jnp.sum(jnp.where(p, gates[0, g : g + 1, :], 0.0), axis=1, keepdims=True)
        gate_cols[at, :] = jnp.broadcast_to(gate, (slots, 128))
        gy[at, :] = (gate * product(one, cot_chunk(cots, g))).astype(bf)

    tile = 2 * slots

    @pl.loop(0, xe.shape[0] // tile)
    def _(t):
        at = pl.ds(pl.multiple_of(t * tile, tile), tile)
        gu = product(xe[at, :], up[0])
        a, b = gu[:, :hidden], gu[:, hidden:]
        s = sigmoid(a)
        silu = a * s
        h = (silu * b).astype(bf)
        hid[at, :] = h
        gh = product(gy[at, :], down[0], 1, 1)
        gu_grad[at, :hidden] = (gh * b * (s * (1.0 + a * (1.0 - s)))).astype(bf)
        gu_grad[at, hidden:] = (gh * silu).astype(bf)
        y = product(h, down[0]).astype(bf).astype(f32)
        dot = jnp.sum(y * gy[at, :].astype(f32), axis=1, keepdims=True)
        y_out[0, at, :] = (gate_cols[at, :1] * y).astype(bf)
        for i in range(2):
            p = picks(slot_rows[0, pl.ds(2 * t + i, 1), :], slots)
            dots[0, pl.ds(2 * t + i, 1), :] = jnp.sum(
                jnp.where(p, dot[i * slots : (i + 1) * slots, :], 0.0), axis=0, keepdims=True
            )
        gin_out[0, at, :] = product(gu_grad[at, :], up[0], 1, 1).astype(bf)

    cols = grads.shape[2]
    own_up, per = width // lines, hidden // lines
    for n in range(lines):
        base = n * (grads.shape[1] // lines)
        grads[0, base : base + own_up, :] = product(
            xe[:, n * own_up : (n + 1) * own_up], gu_grad[...], 0, 0
        ).astype(bf)
    cut = width - cols
    for n in range(0, lines, 2):
        down_two = product(hid[:, n * per : (n + 2) * per], gy[...], 0, 0).astype(bf)
        for k in range(2):
            base = (n + k) * (grads.shape[1] // lines) + own_up
            part = down_two[k * per : (k + 1) * per, :]
            grads[0, base : base + per, :] = part[:, :cols]
            grads[0, base + per : base + per + per // 2, :cut] = part[: per // 2, cols:]
            grads[0, base + per : base + per + per // 2, cut:] = part[per // 2 :, cols:]


def experts_call(x, cots, up, down, slot_rows, gates, slots, lines):
    f32, bf = jnp.float32, jnp.bfloat16
    chunks, rows, width = x.shape
    held, _, double = up.shape
    total = chunks * slots
    once = pl.Buffered(1)
    each = lambda *shape: pl.BlockSpec((1,) + shape, lambda e: (e, 0, 0))
    keep = lambda *shape: pl.BlockSpec((1,) + shape, lambda e: (e, 0, 0), pipeline_mode=once)
    whole = pl.BlockSpec((chunks, rows, width), lambda e: (0, 0, 0), pipeline_mode=once)
    shape = lambda *s: jax.ShapeDtypeStruct((held,) + s, bf)
    packed = width + double // 2 + double // 4
    return pl.pallas_call(
        partial(experts_body, lines),
        grid=(held,),
        in_specs=[
            whole, *[pl.BlockSpec(c.shape, lambda e: (0, 0), pipeline_mode=once) for c in cots], keep(width, double), keep(double // 2, width), each(chunks, rows), each(chunks, rows),
        ],
        out_specs=[
            each(total, width), each(total, width), each(packed, double), each(chunks, rows),
        ],
        out_shape=[
            shape(total, width), shape(total, width), shape(packed, double),
            jax.ShapeDtypeStruct((held, chunks, rows), f32),
        ],
        scratch_shapes=[
            pltpu.VMEM((total, width), bf), pltpu.VMEM((total, width), bf), pltpu.VMEM((total, double), bf),
            pltpu.VMEM((total, double // 2), bf), pltpu.VMEM((total, 128), f32),
        ],
        name="experts",
        compiler_params=pltpu.CompilerParams(vmem_limit_bytes=62 << 20),
        cost_estimate=pl.CostEstimate(flops=4 * 10**10, bytes_accessed=5 * 10**7, transcendentals=10**6),
    )(x, *cots, up, down, slot_rows, gates)


def join_body(where, x_ref, *refs):
    cots, refs = refs[:10], refs[10:]
    join_step(where, x_ref, cots, *refs)


def join_step(
    where, x_ref, cots, y_ref, gin_ref, slot_rows, up, down, dots,
    y_part, g_part, dot_part, up_grad, down_grad, up_acc, down_acc, cot_ref,
):
    f32, bf = jnp.float32, jnp.bfloat16
    g = pl.program_id(0)

    @pl.when(g == 0)
    def _():
        up_acc[...] = jnp.zeros_like(up_acc)
        down_acc[...] = jnp.zeros_like(down_acc)

    for k in range(8):

        @pl.when(g == k)
        def _(k=k):
            cot_ref[...] = cot_chunk(cots, k)

    x, cot = x_ref[0], cot_ref[...]
    half = down.shape[0]
    gu = product(x, up[...])
    a, b = gu[:, :half], gu[:, half:]
    s = sigmoid(a)
    silu = a * s
    h = (silu * b).astype(bf)
    gh = product(cot, down[...], 1, 1)
    gu_grad = jnp.concatenate(
        [gh * b * (s * (1.0 + a * (1.0 - s))), gh * silu], axis=1
    ).astype(bf)
    up_acc[...] += product(x, gu_grad, 0, 0)
    down_acc[...] += product(h, cot, 0, 0)
    y = product(h, down[...])
    gx = product(gu_grad, up[...], 1, 1)
    held, slots, width = y_ref.shape
    one = jnp.concatenate(
        [picks(slot_rows[e, pl.ds(g, 1), :], slots).astype(bf) for e in range(held)], axis=0
    )
    y = y + product(one, y_ref[...].reshape(held * slots, width), 0, 0)
    gx = gx + product(one, gin_ref[...].reshape(held * slots, width), 0, 0)
    lists = jnp.zeros((8, x.shape[0]), f32)
    spot = lax.broadcasted_iota(jnp.int32, lists.shape, 0)
    for e in range(held):
        row = dots[e, pl.ds(g, 1), :]
        high = row.astype(bf).astype(f32)
        lists = jnp.where(spot == e, high, lists)
        lists = jnp.where(spot == held + e, row - high, lists)
    col = lax.broadcasted_iota(jnp.int32, (8, 128), 1)
    spot = lax.broadcasted_iota(jnp.int32, (8, 128), 0)
    first = held * where[0]
    to = (spot < held) & (col == first + spot)
    to = to | ((spot >= held) & (spot < 2 * held) & (col == 8 * held + first + spot - held))
    dot_part[0] = product(lists.astype(bf), to.astype(bf), 0, 0).astype(bf)
    y_part[0] = y.astype(bf)
    g_part[0] = gx.astype(bf)

    @pl.when(g == pl.num_programs(0) - 1)
    def _():
        up_grad[...] = up_acc[...].astype(bf)
        down_grad[...] = down_acc[...].astype(bf)


def join_call(where, x, cots, y, gin, slot_rows, up, down, dots, slots):
    f32, bf = jnp.float32, jnp.bfloat16
    chunks, rows, width = x.shape
    held = y.shape[0]
    chunk = pl.BlockSpec((1, rows, width), lambda g, w: (g, 0, 0))
    placed = pl.BlockSpec((1, rows, width), lambda g, w: (g ^ w[0], 0, 0))
    rows_of = pl.BlockSpec((held, slots, width), lambda g, w: (0, g, 0))
    whole = lambda a: pl.BlockSpec(a.shape, lambda g, w: (0,) * a.ndim)
    return pl.pallas_call(
        join_body,
        grid_spec=pltpu.PrefetchScalarGridSpec(
            num_scalar_prefetch=1,
            grid=(chunks,),
            in_specs=[chunk, *[whole(c) for c in cots], rows_of, rows_of, whole(slot_rows), whole(up), whole(down), whole(dots)],
            out_specs=[
                placed, chunk, pl.BlockSpec((1, rows, 128), lambda g, w: (g, 0, 0)), whole(up), whole(down),
            ],
            scratch_shapes=[
                pltpu.VMEM(up.shape, f32), pltpu.VMEM(down.shape, f32), pltpu.VMEM((rows, width), bf),
            ],
        ),
        out_shape=[
            jax.ShapeDtypeStruct(x.shape, bf), jax.ShapeDtypeStruct(x.shape, bf),
            jax.ShapeDtypeStruct((chunks, rows, 128), bf),
            jax.ShapeDtypeStruct(up.shape, bf), jax.ShapeDtypeStruct(down.shape, bf),
        ],
        name="join",
        compiler_params=pltpu.CompilerParams(vmem_limit_bytes=48 << 20),
        cost_estimate=pl.CostEstimate(flops=10**10, bytes_accessed=4 * 10**7, transcendentals=10**6),
    )(where, x, *cots, y, gin, slot_rows, up, down, dots)


def local_fast(
    tokens, lengths, routes, cotangent, norm_gain, in_weight, conv_weight, conv_bias, dt_bias,
    a_log, d_skip, mix_gain, out_weight, ffn_gain, router_weight, shared_up, shared_down,
    expert_up, expert_down,
):
    bf, f32 = jnp.bfloat16, jnp.float32
    block = tokens.shape[1]
    parts = tokens.shape[0]
    rows = block * parts
    groups = lax.axis_size("dp")
    lines = lax.axis_size("seq")
    held = expert_up.shape[0]
    experts = held * groups
    top = routes.shape[2]
    slots = block * top * 5 // (4 * experts) * parts
    slots = -(-slots // 128) * 128
    place = lax.axis_index("seq")
    group = lax.axis_index("dp")

    def to(a, bit):
        return lax.ppermute(a, "dp", [(i, i ^ bit) for i in range(groups)])

    pad = lambda a, n: jnp.pad(a, ((0, 0), (0, n - a.shape[1])))
    in_blocks, router_blocks, out_blocks, down_line, up_line, x_low, cot_low, route = gather_rows(
        [in_weight, pad(router_weight, 128), out_weight],
        [in_weight.shape[0] // 3, router_weight.shape[0], out_weight.shape[0] // 2, shared_down.shape[0],
         shared_up.shape[0]],
        [shared_down, shared_up], lines, 2, [tokens, cotangent, routes], False, 1,
    )
    out_full = out_blocks.reshape(-1, MODEL_WIDTH)
    in_full = in_blocks.reshape(MODEL_WIDTH, -1)
    router_full = router_blocks.reshape(MODEL_WIDTH, -1)[:, :experts]
    down_part = down_line.reshape(-1, MODEL_WIDTH)
    width = SFF // groups
    up_cols = up_line.reshape(-1, 2, groups, width).transpose(2, 0, 1, 3).reshape(groups, -1, 2 * width)

    length = lax.dynamic_index_in_dim(lengths, place, 0, False)
    x_low = x_low.reshape(rows, MODEL_WIDTH)
    cot_low = cot_low.reshape(rows, MODEL_WIDTH)
    cotangent_rows = cot_low
    route = route.reshape(rows, top)
    used = jnp.arange(rows) < length
    valid = used.astype(f32)[:, None]
    x_rows = x_low.astype(f32)
    normed, norm_pull = jax.vjp(rms_norm, x_rows, norm_gain)
    normed_low = normed.astype(bf)
    projected = jnp.dot(normed_low, in_full, preferred_element_type=f32).astype(bf)
    before_step = projected[:, INNER + CONV :].astype(f32) + dt_bias
    steps = jax.nn.softplus(before_step)
    rates = -steps * jnp.exp(a_log)
    lower = (jnp.arange(rows)[:, None] >= jnp.arange(rows)[None, :]).astype(f32)
    cumulative = jnp.dot(lower, rates, precision=PRECISE)
    wide = lambda a: jnp.broadcast_to(a[:, :, None], a.shape + (HDIM,)).reshape(a.shape[0], -1)
    lanes = lambda a: jnp.broadcast_to(a, (rows, 128))
    mixer_in = (
        projected, projected, projected, conv_weight, conv_bias[None], conv_weight, conv_bias[None],
        lanes(valid), pad(steps, 128), pad(cumulative, 128), cumulative.T.reshape(HEADS // 2, 2, rows),
        wide(d_skip[None]),
    )
    cot_low = jnp.where(used[:, None], cot_low, 0)
    first_in, cot_own, up_cols = lax.optimization_barrier((mixer_in[0], cot_low, up_cols))
    cut = rows // 2
    cot_x, cot_y = to(cot_own, 2), to(cot_own, 4)
    mixed, gated, squares = mixer_front_call((first_in,) + mixer_in[1:], rows)
    up_part = lax.all_to_all(up_cols, "dp", split_axis=0, concat_axis=0, tiled=True)
    gated, cot_x, cot_y, up_part = lax.optimization_barrier((gated, cot_x, cot_y, up_part))
    up_part = up_part.reshape(MODEL_WIDTH, 2 * width)
    cot_far = (to(cot_x[:cut], 4), to(cot_y[cut:], 2))
    cot_core = [to(a, 1) for a in (cot_own, cot_x, cot_y)]
    scale = lax.rsqrt(jnp.sum(squares, axis=1, keepdims=True) / INNER + EPSILON)
    mix_low = (gated * scale * mix_gain).astype(bf)
    mixer_out = jnp.dot(mix_low, out_full, preferred_element_type=f32)
    hidden = x_rows + mixer_out * valid
    normed_ffn, ffn_pull = jax.vjp(rms_norm, hidden, ffn_gain)
    ffn_low = normed_ffn.astype(bf)
    logits = jnp.dot(ffn_low, router_full, preferred_element_type=f32)
    onehot = (route[:, :, None] == jnp.arange(experts)[None, None, :]).astype(f32)
    chosen = jnp.sum(onehot, axis=1)
    peak = jnp.max(jnp.where(chosen > 0, logits, -jnp.inf), axis=1, keepdims=True)
    raised = jnp.exp(jnp.where(chosen > 0, logits - peak, -jnp.inf))
    probs = raised / jnp.sum(raised, axis=1, keepdims=True)

    ffn_low, cot_far, cot_core = lax.optimization_barrier((ffn_low, cot_far, cot_core))
    cot_far_core = tuple(to(a, 1) for a in cot_far)
    all_rows, all_probs = gather_rows(
        [ffn_low, (probs * valid).T], [64, experts], [], 1, 2, [], True, 2
    )
    all_rows = all_rows[:, 0]
    all_cot = [cot_own, cot_core[0], cot_x, cot_core[1], cot_y, cot_core[2], *cot_far, *cot_far_core]
    mine = group * held + jnp.arange(held)
    gates = lax.dynamic_slice_in_dim(all_probs[:, 0], group * held, held, 1).transpose(1, 0, 2)
    member = gates > 0
    earlier = (jnp.arange(rows)[:, None] < jnp.arange(rows)[None, :]).astype(bf)
    before = jnp.einsum("egt,ts->egs", member.astype(bf), earlier, preferred_element_type=f32)
    slot_rows = jnp.where(member, before, -1.0)
    y_slots, gin_slots, grad_experts, dots = experts_call(
        all_rows, all_cot, expert_up, expert_down, slot_rows, gates, slots, lines
    )
    own_experts = lax.psum_scatter(grad_experts, "seq", scatter_dimension=1, tiled=True)
    y_part, g_part, dots, grad_sup, grad_sdown = join_call(
        group.reshape(1), all_rows, all_cot, y_slots, gin_slots, slot_rows, up_part, down_part, dots, slots
    )
    g_sum, dots = sum_to_owners(
        [g_part.reshape(-1, MODEL_WIDTH), dots.reshape(-1, 128)],
        [(0, 384)] * 4 + [(1, 128)], 1, [MODEL_WIDTH, 128], None, [], (True, True), 3,
    )
    dots = dots[:, :experts] + dots[:, experts : 2 * experts]
    g_sum, y_part = lax.optimization_barrier((g_sum, y_part))
    y_part = lax.all_to_all(y_part, "dp", split_axis=0, concat_axis=0, tiled=True)
    grad_out = cotangent_rows.astype(f32)
    grad_logit = (dots - probs * jnp.sum(dots, axis=1, keepdims=True)).astype(bf)
    grad_router = contract_rows(ffn_low, grad_logit)
    grad_ffn = g_sum + contract_cols(grad_logit, router_full)
    grad_hidden, grad_fgain = ffn_pull(grad_ffn)
    grad_hidden = grad_hidden + grad_out
    grad_mo = (grad_hidden * valid).astype(bf)
    grad_mix = contract_cols(grad_mo, out_full)
    mean_dot = jnp.sum(grad_mo.astype(f32) * mixer_out, axis=1, keepdims=True) / INNER
    grad_z, grad_in, stats, grad_bc, bc_stats, row_sums, col_sums, step_sums = mixer_back_call(
        mixer_in, (mixed, grad_mix, mix_gain[None], lanes(scale), lanes(mean_dot)), rows
    )
    grad_rates = jnp.dot(lower.T, row_sums[:, :HEADS] - col_sums[:HEADS].T, precision=PRECISE)
    grad_raw = (step_sums[:, :HEADS] - grad_rates * jnp.exp(a_log)) * jax.nn.sigmoid(before_step)
    grad_al = jnp.sum(grad_rates * rates, axis=0)
    grad_db = jnp.sum(grad_raw, axis=0)
    grad_skip = jnp.sum(stats[1].reshape(HEADS, HDIM), axis=1)
    grad_proj = jnp.concatenate([grad_z, grad_in, grad_bc, grad_raw.astype(bf)], axis=1)
    spare = -PROJ % 128
    wide_proj, late_mo, y_part = lax.optimization_barrier((pad(grad_proj, PROJ + spare), grad_mo, y_part))
    grad_outw = contract_rows(mix_low, late_mo).astype(bf)
    grad_inw = contract_rows(normed_low, wide_proj).astype(bf)
    grad_x, grad_ngain = norm_pull(contract_cols(grad_proj, in_full))
    input_grad = (grad_x + grad_hidden).astype(bf)
    grad_router = contract_rows(ffn_low, pad(grad_logit, 128)).astype(bf)

    grad_inw, grad_sup = lax.optimization_barrier((grad_inw, grad_sup))
    y_sum = jnp.sum(y_part.astype(f32), axis=0)
    output = (hidden + valid * y_sum).astype(bf).reshape(tokens.shape)

    heads = jnp.pad(jnp.stack([grad_db, grad_al, grad_skip]), ((0, 5), (0, 256 - HEADS)))
    gains = jnp.pad(jnp.stack([grad_ngain, grad_fgain]), ((0, 6), (0, 0)))
    own_out, own_in, own_router, output, input_grad, sdown, conv_w, conv_b, mix_g, norm_g, ffn_g, heads = sum_to_owners(
        [grad_outw, grad_inw, grad_router],
        [(0, 512)] * 3 + [(1, 768)] * 8 + [(1, (PROJ + spare) % 768), (2, 128)], lines, [MODEL_WIDTH, PROJ, experts],
        [stats, bc_stats, gains, heads], [output, input_grad.reshape(tokens.shape), grad_sdown.reshape(lines, -1, MODEL_WIDTH)],
        (False, False, False), 4,
    )
    sup = lax.all_to_all(
        grad_sup.reshape(groups * lines, -1, 2 * width), ("dp", "seq"), split_axis=0, concat_axis=0, tiled=True
    ).astype(f32)
    sup = jnp.sum(sup.reshape(groups, lines, -1, 2 * width), axis=1)
    sup = sup.reshape(groups, -1, 2, width).transpose(1, 2, 0, 3).reshape(-1, 2 * SFF)
    sdown = jnp.sum(sdown.astype(f32), axis=0)
    own_up, per = MODEL_WIDTH // lines, EXPERT_HIDDEN // lines
    rest = own_experts[:, own_up + per :]
    cut = rest.shape[2] // 2
    rest = jnp.concatenate([rest[:, :, :cut], rest[:, :, cut:]], axis=1)
    own_down = jnp.concatenate([own_experts[:, own_up : own_up + per], rest], axis=2)
    return (
        output, input_grad, norm_g.reshape(-1), own_in, conv_w, conv_b.reshape(-1), heads[0, :HEADS], heads[1, :HEADS],
        heads[2, :HEADS], mix_g.reshape(-1), own_out, ffn_g.reshape(-1), own_router, sup, sdown,
        own_experts[:, :own_up].astype(f32), own_down.astype(f32),
    )


def solution(mesh):
    def program(*arrays):
        each = arrays[0].shape[0] == lax.axis_size("seq") == 4 and lax.axis_size("dp") == 8
        return (local_fast if each else local)(*arrays)

    return jax.shard_map(
        program,
        mesh=mesh,
        in_specs=(
            P("dp", "seq", None),
            P("dp"),
            P("dp", "seq", None),
            P("dp", "seq", None),
            P(),
            P(("dp", "seq"), None),
            P(),
            P(),
            P(),
            P(),
            P(),
            P(),
            P(("dp", "seq"), None),
            P(),
            P(("dp", "seq"), None),
            P(("dp", "seq"), None),
            P(("dp", "seq"), None),
            P("dp", None, None),
            P("dp", None, None),
        ),
        out_specs=(
            P("dp", "seq", None),
            P("dp", "seq", None),
            P(),
            P(("dp", "seq"), None),
            P(),
            P(),
            P(),
            P(),
            P(),
            P(),
            P(("dp", "seq"), None),
            P(),
            P(("dp", "seq"), None),
            P(("dp", "seq"), None),
            P(("dp", "seq"), None),
            P("dp", "seq", None),
            P("dp", "seq", None),
        ),
        check_vma=False,
    )
```

```python
from functools import partial

import jax
import jax.numpy as jnp
from jax import lax
from jax.experimental import pallas as pl
from jax.experimental.pallas import tpu as pltpu
from jax.sharding import PartitionSpec as P

MODEL_WIDTH = 1536
INNER = 3072
HEADS = 48
HDIM = 64
STATE = 128
KCONV = 4
EXPERT_HIDDEN = 512
SFF = 1024
MB = 4
CONV = 3328
PROJ = 6448


EPSILON = 1e-05
PRECISE = lax.Precision.HIGHEST
MESH = pl.DeviceIdType.MESH


def from_behind(x, axis, by):
    size = lax.axis_size(axis)
    pairs = [(i, i + by) for i in range(size) if 0 <= i + by < size]
    return lax.ppermute(x, axis, pairs)


def prefix(x, axis, join, neutral):
    place = lax.axis_index(axis)
    gathered = jax.tree.map(
        lambda a, kind: lax.all_gather(a.astype(kind), axis), x, (jnp.bfloat16, jnp.bfloat16)
    )
    state = jax.tree.map(lambda a, e: jnp.zeros_like(a) + jnp.asarray(e, a.dtype), x, neutral)

    def one(step, state):
        return join(
            state,
            jax.tree.map(
                lambda a, own: lax.dynamic_index_in_dim(a, step, 0, False).astype(own.dtype),
                gathered,
                x,
            ),
        )

    return lax.fori_loop(0, place, one, state)


def prefix_2(x, axis, join, neutral):
    count = lax.axis_size(axis)
    place = lax.axis_index(axis)
    ahead = count - 1 - place
    gathered = jax.tree.map(
        lambda a, kind: lax.all_gather(a.astype(kind), axis),
        x,
        jax.tree.map(lambda a: jnp.bfloat16 if a.dtype == jnp.float32 else a.dtype, x),
    )
    state = jax.tree.map(lambda a, e: jnp.zeros_like(a) + jnp.asarray(e, a.dtype), x, neutral)

    def one(step, state):
        source = count - 1 - step
        return join(
            state,
            jax.tree.map(
                lambda a, own: lax.dynamic_index_in_dim(a, source, 0, False).astype(own.dtype),
                gathered,
                x,
            ),
        )

    return lax.fori_loop(0, ahead, one, state)


def rms_norm(values, gain_vec):
    return (
        values * lax.rsqrt(jnp.mean(values * values, axis=-1, keepdims=True) + EPSILON) * gain_vec
    )


def swiglu(values, half_width):
    return jax.nn.silu(values[..., :half_width]) * values[..., half_width:]


def contract_rows(left_mat, right_mat):
    return lax.dot_general(
        left_mat, right_mat, (((0,), (0,)), ((), ())), preferred_element_type=jnp.float32
    )


def contract_cols(left_mat, right_mat):
    return lax.dot_general(
        left_mat, right_mat, (((1,), (1,)), ((), ())), preferred_element_type=jnp.float32
    )


def block_terms(head_in, b_rows, c_rows, step_sizes, a_log):
    log_rates = -step_sizes * jnp.exp(a_log)
    cumulative = jnp.cumsum(log_rates, axis=0)
    block_len = head_in.shape[0]
    lower_tri = jnp.arange(block_len)[:, None] >= jnp.arange(block_len)[None, :]
    spread = jnp.where(
        lower_tri[:, :, None], cumulative[:, None, :] - cumulative[None, :, :], -jnp.inf
    )
    scores = jnp.dot(c_rows, b_rows.T, precision=PRECISE)
    weights = jnp.exp(spread) * scores[:, :, None] * step_sizes[None, :, :]
    local_out = jnp.einsum("tih,ihp->thp", weights, head_in, precision=PRECISE)
    tail_weight = jnp.exp(cumulative[-1][None, :] - cumulative) * step_sizes
    local_state = jnp.einsum("ih,ihp,in->hpn", tail_weight, head_in, b_rows, precision=PRECISE)
    return (cumulative, local_out, local_state, jnp.exp(cumulative[-1]))


def carried_out(c_rows, cumulative, state_in):
    return (
        jnp.einsum("tn,hpn->thp", c_rows, state_in, precision=PRECISE)
        * jnp.exp(cumulative)[:, :, None]
    )


def mixer_front(valid_rows, projected, previous, conv_weight, conv_bias, dt_bias, a_log):
    row_count = projected.shape[0]
    conv_in = projected[:, INNER : INNER + CONV]
    padded = jnp.concatenate([previous, conv_in], axis=0)
    conv_sum = conv_bias + conv_weight[0] * padded[0:row_count]
    for tap_idx in range(1, KCONV):
        conv_sum = conv_sum + conv_weight[tap_idx] * padded[tap_idx : tap_idx + row_count]
    activated = jax.nn.silu(conv_sum) * valid_rows
    head_in = activated[:, :INNER].reshape(row_count, HEADS, HDIM)
    b_rows = activated[:, INNER : INNER + STATE]
    c_rows = activated[:, INNER + STATE :]
    step_sizes = jax.nn.softplus(projected[:, INNER + CONV :] + dt_bias)
    cumulative, local_out, local_state, decay_total = block_terms(
        head_in, b_rows, c_rows, step_sizes, a_log
    )
    return (projected[:, :INNER], head_in, c_rows, cumulative, local_out, local_state, decay_total)


def mixer_tail(gate_z, head_in, c_rows, cumulative, local_out, state_in, d_skip, mix_gain):
    mixed_out = local_out + carried_out(c_rows, cumulative, state_in) + d_skip[:, None] * head_in
    gated_out = mixed_out.reshape(head_in.shape[0], INNER) * jax.nn.silu(gate_z)
    return rms_norm(gated_out, mix_gain)


def link_states(earlier, latter):
    return (earlier[0] * latter[0], latter[1] + latter[0][:, None, None] * earlier[1])


def local(
    tokens,
    lengths,
    routes,
    cotangent,
    norm_gain,
    in_weight,
    conv_weight,
    conv_bias,
    dt_bias,
    a_log,
    d_skip,
    mix_gain,
    out_weight,
    ffn_gain,
    router_weight,
    shared_up,
    shared_down,
    expert_up,
    expert_down,
):
    row_count = tokens.shape[1]
    resident_experts = expert_up.shape[0]
    groups = lax.axis_size("dp")
    experts = resident_experts * groups
    top_count = routes.shape[2]
    capacity = row_count * top_count * 5 // (4 * experts)
    shards = (in_weight, out_weight, router_weight, shared_up, shared_down)
    kept_full = (
        lax.all_gather(shards[0], ("dp", "seq"), axis=0, tiled=True),
        lax.all_gather(shards[1], ("dp", "seq"), axis=0, tiled=True),
        lax.all_gather(shards[2], ("dp", "seq"), axis=0, tiled=True),
        lax.all_gather(shards[3], ("dp", "seq"), axis=0, tiled=True),
        lax.all_gather(shards[4], ("dp", "seq"), axis=0, tiled=True),
    )
    grad_inw = jnp.zeros((MODEL_WIDTH, PROJ), jnp.float32)
    grad_outw = jnp.zeros((INNER, MODEL_WIDTH), jnp.float32)
    grad_router = jnp.zeros((MODEL_WIDTH, experts), jnp.float32)
    grad_sup = jnp.zeros((MODEL_WIDTH, 2 * SFF), jnp.float32)
    grad_sdown = jnp.zeros((SFF, MODEL_WIDTH), jnp.float32)
    expert_upward_grad = jnp.zeros((resident_experts, MODEL_WIDTH, 2 * EXPERT_HIDDEN), jnp.float32)
    grad_edown = jnp.zeros((resident_experts, EXPERT_HIDDEN, MODEL_WIDTH), jnp.float32)
    grad_ngain = jnp.zeros_like(norm_gain)
    grad_cw = jnp.zeros_like(conv_weight)
    grad_cb = jnp.zeros_like(conv_bias)
    grad_db = jnp.zeros_like(dt_bias)
    grad_al = jnp.zeros_like(a_log)
    grad_skip = jnp.zeros_like(d_skip)
    grad_mgain = jnp.zeros_like(mix_gain)
    grad_fgain = jnp.zeros_like(ffn_gain)
    outputs = []
    input_grads = []
    for micro_idx in range(MB):
        in_full, out_full, router_full, up_full, down_full = kept_full
        x_rows = tokens[micro_idx].astype(jnp.float32)
        position = lax.axis_index("seq") * row_count + jnp.arange(row_count)
        valid_rows = (position < lengths[micro_idx]).astype(jnp.float32)[:, None]
        normed, norm_pull = jax.vjp(rms_norm, x_rows, norm_gain)
        normed_low = normed.astype(jnp.bfloat16)
        projected = jnp.dot(normed_low, in_full, preferred_element_type=jnp.float32).astype(
            jnp.bfloat16
        )
        previous = from_behind(projected[row_count - (KCONV - 1) :, INNER : INNER + CONV], "seq", 1)
        front_out, front_pull = jax.vjp(
            partial(mixer_front, valid_rows),
            projected.astype(jnp.float32),
            previous.astype(jnp.float32),
            conv_weight,
            conv_bias,
            dt_bias,
            a_log,
        )
        gate_z, head_in, c_rows, cumulative, local_out, local_state, decay_total = front_out
        identity = (jnp.ones_like(decay_total), jnp.zeros_like(local_state))
        _, state_in = prefix((decay_total, local_state), "seq", link_states, identity)
        normed_mix, tail_pull = jax.vjp(
            mixer_tail, gate_z, head_in, c_rows, cumulative, local_out, state_in, d_skip, mix_gain
        )
        mix_low = normed_mix.astype(jnp.bfloat16)
        mixer_out = jnp.dot(mix_low, out_full, preferred_element_type=jnp.float32)
        hidden = x_rows + mixer_out * valid_rows
        normed_ffn, ffn_pull = jax.vjp(rms_norm, hidden, ffn_gain)
        ffn_low = normed_ffn.astype(jnp.bfloat16)
        logits = jnp.dot(ffn_low, router_full, preferred_element_type=jnp.float32)
        route_row = routes[micro_idx]
        picked = jnp.take_along_axis(logits, route_row, axis=1)
        gate_probs = jax.nn.softmax(picked, axis=-1)
        shared_gu = jnp.dot(ffn_low, up_full, preferred_element_type=jnp.float32)
        shared_act, shared_pull = jax.vjp(partial(swiglu, half_width=SFF), shared_gu)
        shared_h = shared_act.astype(jnp.bfloat16)
        shared_y = jnp.dot(shared_h, down_full, preferred_element_type=jnp.float32)
        flat_route = route_row.reshape(-1)
        member = (flat_route[:, None] == jnp.arange(experts)[None, :]).astype(jnp.int32)
        slot_pos = jnp.sum((jnp.cumsum(member, axis=0) - member) * member, axis=1)
        target = flat_route * capacity + slot_pos
        source = (
            jnp.zeros((experts * capacity,), jnp.int32)
            .at[target]
            .set(jnp.arange(row_count * top_count, dtype=jnp.int32))
        )
        filled = jnp.zeros((experts * capacity, 1), jnp.bfloat16).at[target].set(jnp.bfloat16(1))
        outgoing = (jnp.take(ffn_low, source // top_count, axis=0) * filled).reshape(
            groups, resident_experts, capacity, MODEL_WIDTH
        )
        received_rows = lax.all_to_all(outgoing, "dp", split_axis=0, concat_axis=2, tiled=True)[0]
        expert_gu = jnp.einsum(
            "erd,edf->erf", received_rows, expert_up, preferred_element_type=jnp.float32
        )
        expert_act, expert_pull = jax.vjp(partial(swiglu, half_width=EXPERT_HIDDEN), expert_gu)
        expert_h = expert_act.astype(jnp.bfloat16)
        expert_y = jnp.einsum(
            "erf,efd->erd", expert_h, expert_down, preferred_element_type=jnp.float32
        ).astype(jnp.bfloat16)
        returned = lax.all_to_all(expert_y[None], "dp", split_axis=2, concat_axis=0, tiled=True)
        per_choice = (
            jnp.take(returned.reshape(experts * capacity, MODEL_WIDTH), target, axis=0)
            .reshape(row_count, top_count, MODEL_WIDTH)
            .astype(jnp.float32)
        )
        routed = jnp.einsum("lk,lkd->ld", gate_probs, per_choice, precision=PRECISE)
        outputs.append((hidden + valid_rows * (shared_y + routed)).astype(jnp.bfloat16))
        in_back, out_back, router_back, up_back, down_back = kept_full
        grad_out = cotangent[micro_idx].astype(jnp.float32)
        branch = valid_rows * grad_out
        shared_g = branch.astype(jnp.bfloat16)
        grad_sdown = grad_sdown + contract_rows(shared_h, shared_g)
        grad_sgu = shared_pull(contract_cols(shared_g, down_back))[0].astype(jnp.bfloat16)
        grad_sup = grad_sup + contract_rows(ffn_low, grad_sgu)
        grad_ffn = contract_cols(grad_sgu, up_back)
        grad_choice = (gate_probs[:, :, None] * branch[:, None, :]).astype(jnp.bfloat16)
        grad_gate = jnp.sum(branch[:, None, :] * per_choice, axis=-1)
        grad_pick = gate_probs * (
            grad_gate - jnp.sum(gate_probs * grad_gate, axis=-1, keepdims=True)
        )
        onehot = (route_row[:, :, None] == jnp.arange(experts)[None, None, :]).astype(jnp.float32)
        grad_logit = jnp.einsum("lk,lke->le", grad_pick, onehot, precision=PRECISE).astype(
            jnp.bfloat16
        )
        grad_router = grad_router + contract_rows(ffn_low, grad_logit)
        grad_ffn = grad_ffn + contract_cols(grad_logit, router_back)
        back_out = (
            jnp.take(grad_choice.reshape(row_count * top_count, MODEL_WIDTH), source, axis=0)
            * filled
        ).reshape(groups, resident_experts, capacity, MODEL_WIDTH)
        grad_arrived = lax.all_to_all(back_out, "dp", split_axis=0, concat_axis=2, tiled=True)[0]
        step_edown = jnp.einsum(
            "erf,erd->efd", expert_h, grad_arrived, preferred_element_type=jnp.float32
        )
        grad_eh = jnp.einsum(
            "erd,efd->erf", grad_arrived, expert_down, preferred_element_type=jnp.float32
        )
        expert_gate_up_grad = expert_pull(grad_eh)[0].astype(jnp.bfloat16)
        expert_upward_step = jnp.einsum(
            "tbw,tbj->twj", received_rows, expert_gate_up_grad, preferred_element_type=jnp.float32
        )
        grad_ein = jnp.einsum(
            "erf,edf->erd", expert_gate_up_grad, expert_up, preferred_element_type=jnp.float32
        ).astype(jnp.bfloat16)
        expert_upward_grad = expert_upward_grad + expert_upward_step
        grad_edown = grad_edown + step_edown
        came_back = lax.all_to_all(grad_ein[None], "dp", split_axis=2, concat_axis=0, tiled=True)
        grad_ffn = grad_ffn + jnp.sum(
            jnp.take(came_back.reshape(experts * capacity, MODEL_WIDTH), target, axis=0)
            .reshape(row_count, top_count, MODEL_WIDTH)
            .astype(jnp.float32),
            axis=1,
        )
        grad_hidden, step_fgain = ffn_pull(grad_ffn)
        grad_fgain = grad_fgain + step_fgain
        grad_hidden = grad_hidden + grad_out
        grad_mix_out = (grad_hidden * valid_rows).astype(jnp.bfloat16)
        grad_outw = grad_outw + contract_rows(mix_low, grad_mix_out)
        grad_mix = contract_cols(grad_mix_out, out_back)
        grad_z, grad_head, grad_c, grad_cum, grad_local, grad_state, step_skip, step_mgain = (
            tail_pull(grad_mix)
        )
        grad_skip = grad_skip + step_skip
        grad_mgain = grad_mgain + step_mgain
        _, grad_carry = prefix_2((decay_total, grad_state), "seq", link_states, identity)
        grad_decay = jnp.sum(grad_carry * state_in, axis=(1, 2))
        grad_proj, grad_prev, step_cw, step_cb, step_db, step_al = front_pull(
            (grad_z, grad_head, grad_c, grad_cum, grad_local, grad_carry, grad_decay)
        )
        grad_cw = grad_cw + step_cw
        grad_cb = grad_cb + step_cb
        grad_db = grad_db + step_db
        grad_al = grad_al + step_al
        from_next = from_behind(grad_prev.astype(jnp.bfloat16), "seq", -1).astype(grad_prev.dtype)
        grad_proj = (
            grad_proj.at[row_count - (KCONV - 1) :, INNER : INNER + CONV]
            .add(from_next)
            .astype(jnp.bfloat16)
        )
        grad_inw = grad_inw + contract_rows(normed_low, grad_proj)
        grad_normed = contract_cols(grad_proj, in_back)
        grad_x, step_ngain = norm_pull(grad_normed)
        grad_ngain = grad_ngain + step_ngain
        input_grads.append((grad_x + grad_hidden).astype(jnp.bfloat16))
    weight_grads = (
        lax.psum_scatter(grad_inw, ("dp", "seq"), scatter_dimension=0, tiled=True),
        lax.psum_scatter(grad_outw, ("dp", "seq"), scatter_dimension=0, tiled=True),
        lax.psum_scatter(grad_router, ("dp", "seq"), scatter_dimension=0, tiled=True),
        lax.psum_scatter(grad_sup, ("dp", "seq"), scatter_dimension=0, tiled=True),
        lax.psum_scatter(grad_sdown, ("dp", "seq"), scatter_dimension=0, tiled=True),
    )
    small_sums = lax.psum(
        (grad_ngain, grad_cw, grad_cb, grad_db, grad_al, grad_skip, grad_mgain, grad_fgain),
        ("dp", "seq"),
    )
    expert_sums = (
        lax.psum_scatter(
            expert_upward_grad.astype(jnp.bfloat16), "seq", scatter_dimension=1, tiled=True
        ).astype(jnp.float32),
        lax.psum_scatter(
            grad_edown.astype(jnp.bfloat16), "seq", scatter_dimension=1, tiled=True
        ).astype(jnp.float32),
    )
    return (
        jnp.stack(outputs),
        jnp.stack(input_grads),
        small_sums[0],
        weight_grads[0],
        small_sums[1],
        small_sums[2],
        small_sums[3],
        small_sums[4],
        small_sums[5],
        small_sums[6],
        weight_grads[1],
        small_sums[7],
        weight_grads[2],
        weight_grads[3],
        weight_grads[4],
        expert_sums[0],
        expert_sums[1],
    )


def at_neighbours():
    d = lax.axis_index("dp")
    core, x, y = d % 2, (d // 2) % 2, d // 4
    return d, core, x, y, d + 1 - 2 * core, d + 2 - 4 * x, d + 4 - 8 * y


def meet(devices):
    barrier = pltpu.get_barrier_semaphore()
    for there in devices:
        pl.semaphore_signal(barrier, inc=1, device_id=there, device_id_type=MESH)
    pl.semaphore_wait(barrier, len(devices))


def send(source, target, send_sem, recv_sem, there):
    copy = pltpu.make_async_remote_copy(
        src_ref=source, dst_ref=target, send_sem=send_sem, recv_sem=recv_sem,
        device_id=there, device_id_type=MESH,
    )
    copy.start()
    return copy


def add_into(target, source, high):
    step = 16
    for s in (64, 48, 32):
        if high % s == 0:
            step = s
            break

    @pl.loop(0, high // step)
    def _(i):
        rows = pl.ds(pl.multiple_of(i * step, step), step)
        target[rows, :] = target[rows, :] + source[rows, :]


def swap_start(swaps, landed, which, line, lines, local_sem, send_sem, recv_sem):
    copies = []
    for n in which:
        a, b = swaps[n], landed[n]
        keep = pltpu.make_async_copy(a.at[line], b.at[line], local_sem.at[n])
        keep.start()
        away = [
            send(a.at[o], b.at[line], send_sem.at[n, k], recv_sem.at[n, k], {"seq": o})
            for k, o in enumerate(lax.rem(line + k, lines) for k in range(1, lines))
        ]
        copies.append((keep, away))
    return copies


def swap_end(copies):
    for keep, away in copies:
        for copy in away:
            copy.wait_recv()
    for keep, away in copies:
        for copy in away:
            copy.wait_send()
        keep.wait()


def swap_sems(count, lines):
    dma = pltpu.SemaphoreType.DMA
    return [dma((count,)), dma((count, lines - 1)), dma((count, lines - 1))]


def sum_body(items, arrays, lines, tiny, moved, relative, *refs):
    count = len(items)
    grads, refs = refs[:arrays], refs[arrays:]
    swaps, refs = refs[:moved], refs[moved:]
    if tiny:
        small_in, refs = refs[:4], refs[4:]
    outs, refs = refs[:arrays], refs[arrays:]
    landed, refs = refs[:moved], refs[moved:]
    if tiny:
        small_out, refs = refs[:6], refs[6:]
    own, refs = refs[:count], refs[count:]
    got, refs = refs[:count], refs[count:]
    from_x, refs = refs[:count], refs[count:]
    from_y, refs = refs[:count], refs[count:]
    last_x, refs = refs[:count], refs[count:]
    last_y, refs = refs[:count], refs[count:]
    if lines > 1:
        from_z, refs = refs[:count], refs[count:]
    (load_sem, send_sem, recv_sem), refs = refs[:3], refs[3:]
    if moved:
        swap_sem, refs = refs[:3], refs[3:]
    if tiny:
        packed, half, t_core, t_x, t_y, t_z, t_back, t_send, t_recv = refs
    d, core, x, y, at_core, at_x, at_y = at_neighbours()
    bits = [(0, 0, 0) if own else (core, x, y) for own in relative]
    own_core = core
    line = lax.axis_index("seq")
    others = [lax.rem(line + k, lines) for k in range(1, lines)]
    beside, across = line + 1 - 2 * (line % 2), lax.rem(line + 2, 4)
    meet([{"dp": at_core}, {"dp": at_x}, {"dp": at_y}] + [{"seq": o} for o in others])
    sent = [[] for _ in items]
    stage = [None] * count
    cross = [None] * count
    close = [None] * count
    along = [None] * count
    loads = [None] * count

    def begin(t):
        a, c0, wide, high = items[t]
        core, x, y = bits[a]
        cols = pl.ds(c0, wide)
        loads[t] = pltpu.make_async_copy(grads[a].at[:, :, core, :, cols], own[t], load_sem.at[t])
        loads[t].start()
        stage[t] = send(
            grads[a].at[:, :, 1 - core, :, cols], got[t], send_sem.at[t, 0], recv_sem.at[t, 0], {"dp": at_core}
        )

    def fold(t):
        a, c0, wide, high = items[t]
        core, x, y = bits[a]
        loads[t].wait()
        stage[t].wait_recv()
        for i in range(2):
            for j in range(2):
                add_into(got[t].at[i, j], own[t].at[i, j], high)
        top, low = pl.ds(0, high // 2), pl.ds(high // 2, high // 2)
        cross[t] = (
            send(got[t].at[:, 1 - x, top, :], from_x[t], send_sem.at[t, 1], recv_sem.at[t, 1], {"dp": at_x}),
            send(got[t].at[1 - y, :, low, :], from_y[t], send_sem.at[t, 2], recv_sem.at[t, 2], {"dp": at_y}),
        )

    def turn(t):
        a, c0, wide, high = items[t]
        core, x, y = bits[a]
        top, low = pl.ds(0, high // 2), pl.ds(high // 2, high // 2)
        cross[t][0].wait_recv()
        for i in range(2):
            add_into(got[t].at[i, x, top, :], from_x[t].at[i], high // 2)
        close_y = send(got[t].at[1 - y, x, top, :], last_y[t], send_sem.at[t, 3], recv_sem.at[t, 3], {"dp": at_y})
        cross[t][1].wait_recv()
        for j in range(2):
            add_into(got[t].at[y, j, low, :], from_y[t].at[j], high // 2)
        close_x = send(got[t].at[y, 1 - x, low, :], last_x[t], send_sem.at[t, 4], recv_sem.at[t, 4], {"dp": at_x})
        close[t] = (close_y, close_x)

    def settle(t):
        a, c0, wide, high = items[t]
        core, x, y = bits[a]
        top, low = pl.ds(0, high // 2), pl.ds(high // 2, high // 2)
        cols = pl.ds(c0, wide)
        close[t][0].wait_recv()
        add_into(got[t].at[y, x, top, :], last_y[t], high // 2)
        close[t][1].wait_recv()
        add_into(got[t].at[y, x, low, :], last_x[t], high // 2)
        if lines == 1:
            show = min(wide, outs[a].shape[1] - c0)
            outs[a][:, c0 : c0 + show] = got[t][y, x, :, :show].astype(jnp.float32)
            return
        each = high // lines
        along[t] = tuple(
            send(
                unit(t, 1 - line % 2 + 2 * k, each), from_z[t].at[k],
                send_sem.at[t, 5 + k], recv_sem.at[t, 5 + k], {"seq": beside},
            )
            for k in range(2)
        )

    def unit(t, u, each):
        core, x, y = bits[items[t][0]]
        return got[t].at[y, x, pl.ds(pl.multiple_of(u * each, 16), each), :]

    def halve(t):
        each = items[t][3] // lines
        for k in range(2):
            along[t][k].wait_recv()
            add_into(unit(t, line % 2 + 2 * k, each), from_z[t].at[k], each)
        along[t] += (
            send(unit(t, across, each), from_z[t].at[2], send_sem.at[t, 7], recv_sem.at[t, 7], {"seq": across}),
        )

    def finish(t):
        a, c0, wide, high = items[t]
        along[t][2].wait_recv()
        total = unit(t, line, high // lines)[...].astype(jnp.float32) + from_z[t][2].astype(jnp.float32)
        show = min(wide, outs[a].shape[1] - c0)
        outs[a][:, c0 : c0 + show] = total[:, :show]

    little = []

    def tiny_step(n):
        if n == 0:
            at = 0
            for part in small_in:
                size = part.shape[1] // 2
                for k in range(2):
                    packed[k, :, at : at + size] = part[:, k * size : (k + 1) * size]
                at += size
            little.append(send(packed.at[1 - own_core], t_core, t_send.at[0], t_recv.at[0], {"dp": at_core}))
        elif n == 1:
            little[0].wait_recv()
            half[0] = packed[own_core] + t_core[...]
            little.append(send(half.at[0], t_x, t_send.at[1], t_recv.at[1], {"dp": at_x}))
        elif n == 2:
            little[1].wait_recv()
            half[1] = half[0] + t_x[...]
            little.append(send(half.at[1], t_y, t_send.at[2], t_recv.at[2], {"dp": at_y}))
        elif n == 3:
            little[2].wait_recv()
            half[2] = half[1] + t_y[...]
            t_z[line] = half[2]
            for k, o in enumerate(others):
                little.append(send(half.at[2], t_z.at[line], t_send.at[3 + k], t_recv.at[3 + k], {"seq": o}))
        elif n == 4:
            for k in range(lines - 1):
                little[3 + k].wait_recv()
            total = t_z[0]
            for k in range(1, lines):
                total = total + t_z[k]
            t_back[own_core] = total
            little.append(
                send(t_back.at[own_core], t_back.at[own_core], t_send.at[7], t_recv.at[7], {"dp": at_core})
            )
        elif n == 5:
            little[-1].wait_recv()
            for copy in little:
                copy.wait_send()
            conv_w, conv_b, mix_g, norm_g, ffn_g, heads = small_out
            at = 0
            spans = []
            for part in small_in:
                size = part.shape[1] // 2
                spans.append((at, size))
                at += size
            for k in range(2):
                at, size = spans[0]
                mix_g[k * size : (k + 1) * size] = t_back[k, 0, at : at + size]
                conv_b[k * size : (k + 1) * size] = t_back[k, 2, at : at + size]
                conv_w[:, k * size : (k + 1) * size] = t_back[k, 3:7, at : at + size]
                at, size = spans[1]
                here = INNER + k * size
                conv_b[here : here + size] = t_back[k, 0, at : at + size]
                conv_w[:, here : here + size] = t_back[k, 1:5, at : at + size]
                at, size = spans[2]
                norm_g[k * size : (k + 1) * size] = t_back[k, 0, at : at + size]
                ffn_g[k * size : (k + 1) * size] = t_back[k, 1, at : at + size]
                at, size = spans[3]
                heads[:, k * size : (k + 1) * size] = t_back[k, :, at : at + size]

    begin(0)
    if tiny:
        tiny_step(0)
    moves = swap_start(swaps, landed, range(moved), line, lines, *swap_sem) if moved else ()
    for t in range(max(count + 4, 5 if tiny else 0)):
        if t + 1 < count:
            begin(t + 1)
        if t < count:
            fold(t)
        if 0 <= t - 1 < count:
            turn(t - 1)
        if 0 <= t - 2 < count:
            settle(t - 2)
        if lines > 1 and 0 <= t - 3 < count:
            halve(t - 3)
        if lines > 1 and 0 <= t - 4 < count:
            finish(t - 4)
        if tiny and t < 5:
            tiny_step(t + 1)
    swap_end(moves)
    for t in range(count):
        stage[t].wait_send()
        for copy in cross[t] + close[t] + tuple(along[t] or ()):
            copy.wait_send()


def sum_to_owners(grads, widths, lines, shown, small, swaps, relative, identity):
    items, starts = [], [0] * len(grads)
    views = [g.reshape(2, 2, 2, g.shape[0] // 8, g.shape[1]) for g in grads]
    for a, wide in widths:
        items.append((a, starts[a], wide, views[a].shape[3]))
        starts[a] += wide
    assert starts == [g.shape[1] for g in grads]
    tiny = small is not None
    bf = jnp.bfloat16
    scratch = [pltpu.VMEM((2, 2, h, w), bf) for _, _, w, h in items]
    scratch += [pltpu.VMEM((2, 2, h, w), bf) for _, _, w, h in items]
    scratch += [pltpu.VMEM((2, h // 2, w), bf) for _, _, w, h in items] * 2
    scratch += [pltpu.VMEM((h // 2, w), bf) for _, _, w, h in items] * 2
    if lines > 1:
        scratch += [pltpu.VMEM((lines - 1, h // lines, w), bf) for _, _, w, h in items]
    ways = 4 + lines
    scratch += [
        pltpu.SemaphoreType.DMA((len(items),)),
        pltpu.SemaphoreType.DMA((len(items), ways)),
        pltpu.SemaphoreType.DMA((len(items), ways)),
    ]
    out_shape = [
        jax.ShapeDtypeStruct((g.shape[0] // 8 // lines, cols), jnp.float32) for g, cols in zip(grads, shown)
    ]
    ins = list(views)
    in_specs = [pl.BlockSpec(memory_space=pl.ANY)] * len(views)
    out_specs = [pl.BlockSpec(memory_space=pltpu.VMEM)] * len(views)
    if swaps:
        scratch += swap_sems(len(swaps), lines)
        ins += swaps
        in_specs += [pl.BlockSpec(memory_space=pl.ANY)] * len(swaps)
        out_specs += [pl.BlockSpec(memory_space=pl.ANY)] * len(swaps)
        out_shape += [jax.ShapeDtypeStruct(a.shape, a.dtype) for a in swaps]
    if tiny:
        cols = sum(part.shape[1] for part in small) // 2
        part = lambda *lead: pltpu.VMEM(lead + (8, cols), jnp.float32)
        scratch += [part(2), part(3), part(), part(), part(), part(lines), part(2)]
        scratch += [pltpu.SemaphoreType.DMA((8,)), pltpu.SemaphoreType.DMA((8,))]
        ins += small
        in_specs += [pl.BlockSpec(memory_space=pltpu.VMEM)] * 4
        for shape in ((KCONV, CONV), (CONV,), (INNER,), (MODEL_WIDTH,), (MODEL_WIDTH,), (8, 256)):
            out_shape.append(jax.ShapeDtypeStruct(shape, jnp.float32))
            out_specs.append(pl.BlockSpec(memory_space=pltpu.VMEM))
    return pl.pallas_call(
        partial(sum_body, items, len(views), lines, tiny, len(swaps), relative),
        out_shape=out_shape,
        in_specs=in_specs,
        out_specs=out_specs,
        scratch_shapes=scratch,
        name="sum_to_owners_%d" % identity,
        compiler_params=pltpu.CompilerParams(
            collective_id=identity, has_side_effects=True, vmem_limit_bytes=60 << 20
        ),
    )(*ins)


def gather_body(pieces, arrays, flat, lines, ahead, moved, relative, *refs):
    mine, refs = refs[:arrays], refs[arrays:]
    swaps, refs = refs[:moved], refs[moved:]
    full, refs = refs[:arrays], refs[arrays:]
    landed, refs = refs[:moved], refs[moved:]
    keep_sem, send_sem, recv_sem, z_send, z_recv = refs[:5]
    swap_sem = refs[5:]
    d, core, x, y, at_core, at_x, at_y = at_neighbours()
    at_far = at_x + at_y - d
    line = lax.rem(lax.axis_index("seq"), lines)
    hops = [line]
    if lines > 1:
        upper = line // 2
        hops += [line + 1 - 2 * (line % 2), 2 - upper, 3 - 3 * upper]
    meet([{"dp": at_core}, {"dp": at_x}, {"dp": at_y}] + [{"seq": o} for o in hops[1:]])
    blocks = dict(own=d, x=at_x, y=at_y, far=at_far)
    lands = dict(x=d, y=d, core=d, x_y=at_x, x_core=at_x, y_x=at_y, y_core=at_y, far_core=at_far)
    if relative:
        blocks = dict(own=0, x=2, y=4, far=6)
        lands = dict(x=2, y=4, core=1, x_y=6, x_core=3, y_x=6, y_core=5, far_core=7)
    mains = [q for q, piece in enumerate(pieces) if piece[0] < arrays - flat]
    sides = [q for q, piece in enumerate(pieces) if piece[0] >= arrays - flat]
    home = lambda a: blocks["own"] if a < arrays - flat else 0
    keep = []
    for a in range(arrays):
        keep.append(pltpu.make_async_copy(mine[a], full[a].at[home(a), line], keep_sem.at[a]))
        keep[a].start()
    order = [(j, q) for j in range(lines) for q in mains]
    total = len(order)
    out = [[None] * 7 for _ in order]

    def place(j, q, block):
        a, r0, high = pieces[q]
        return full[a].at[block, hops[j], pl.ds(r0, high), :]

    def own_piece(q):
        a, r0, high = pieces[q]
        return mine[a].at[pl.ds(r0, high), :]

    def hop(j, q, sem, to):
        a = pieces[q][0]
        return pltpu.make_async_remote_copy(
            src_ref=own_piece(q) if j == 0 else place(j, q, home(a)),
            dst_ref=place(j, q, home(a)),
            send_sem=z_send.at[q, sem], recv_sem=z_recv.at[q, hops[j]],
            device_id={"seq": to}, device_id_type=MESH,
        )

    def onward(j, q, act):
        o = hops[j]

        @pl.when((o <= line) & (line < lines - 1))
        def _():
            act(hop(j, q, 2 * j, jnp.minimum(line + 1, lines - 1)))

        @pl.when((o >= line) & (line > 0))
        def _():
            act(hop(j, q, 2 * j + 1, jnp.maximum(line - 1, 0)))

    def relay(j, q):
        hop(j, q, 2 * j, line).wait_recv()
        onward(j, q, lambda copy: copy.start())

    def pass_on(i, n, block, lands_at, there):
        j, q = order[i]
        source = own_piece(q) if block is None else place(j, q, block)
        out[i][n] = send(
            source, place(j, q, lands[lands_at]), send_sem.at[i, n], recv_sem.at[i, n], {"dp": there}
        )

    def first(i):
        block = None if order[i][0] == 0 else blocks["own"]
        pass_on(i, 0, block, "x", at_x)
        pass_on(i, 1, block, "y", at_y)
        pass_on(i, 2, block, "core", at_core)

    def second(i):
        out[i][0].wait_recv()
        if sum((i,) + order[i][:1]) % 2 == 0:
            pass_on(i, 5, blocks["x"], "x_y", at_y)
        pass_on(i, 3, blocks["x"], "x_core", at_core)
        out[i][1].wait_recv()
        if sum((i,) + order[i][:1]) % 2 == 1:
            pass_on(i, 5, blocks["y"], "y_x", at_x)
        pass_on(i, 4, blocks["y"], "y_core", at_core)

    def third(i):
        out[i][5].wait_recv()
        pass_on(i, 6, blocks["far"], "far_core", at_core)

    lead = ahead + 2
    if lines > 1:
        for q in mains:
            onward(0, q, lambda copy: copy.start())
    for i in range(min(ahead, total)):
        first(i)
    moves = []
    for i in range(total):
        if moved and i == 2:
            moves = swap_start(swaps, landed, range(moved), line, lines, *swap_sem)
        if i + lead < total and order[i + lead][0] > 0:
            relay(*order[i + lead])
        if i % len(mains) == 1:
            j = i // len(mains)
            for q in sides:
                if j == 0:
                    onward(0, q, lambda copy: copy.start())
                else:
                    relay(j, q)
        if i + ahead < total:
            first(i + ahead)
        second(i)
        if i:
            third(i - 1)
    third(total - 1)
    for i in range(total):
        for n in (2, 3, 4, 6):
            out[i][n].wait_recv()
        for copy in out[i]:
            copy.wait_send()
    swap_end(moves)
    if lines > 1:
        for q in range(len(pieces)):
            for j in range(lines):
                onward(j, q, lambda copy: copy.wait_send())
    for copy in keep:
        copy.wait()


def gather_rows(arrays, chunks, flat, lines, ahead, swaps, relative, identity):
    pieces = []
    count = len(arrays) + len(flat)
    for a, (w, chunk) in enumerate(zip(list(arrays) + list(flat), chunks)):
        for r0 in range(0, w.shape[0], chunk):
            pieces.append((a, r0, chunk))
    total = lines * len([p for p in pieces if p[0] < len(arrays)])
    anywhere = pl.BlockSpec(memory_space=pl.ANY)
    return pl.pallas_call(
        partial(gather_body, pieces, count, len(flat), lines, ahead, len(swaps), relative),
        out_shape=[jax.ShapeDtypeStruct((8, lines) + w.shape, w.dtype) for w in arrays]
        + [jax.ShapeDtypeStruct((1, lines) + w.shape, w.dtype) for w in flat]
        + [jax.ShapeDtypeStruct(a.shape, a.dtype) for a in swaps],
        in_specs=[anywhere] * (count + len(swaps)),
        out_specs=[anywhere] * (count + len(swaps)),
        scratch_shapes=[
            pltpu.SemaphoreType.DMA((count,)),
            pltpu.SemaphoreType.DMA((total, 7)),
            pltpu.SemaphoreType.DMA((total, 7)),
            pltpu.SemaphoreType.DMA((len(pieces), 2 * lines)),
            pltpu.SemaphoreType.DMA((len(pieces), lines)),
        ]
        + (swap_sems(len(swaps), lines) if swaps else []),
        name="gather_rows_%d" % identity,
        compiler_params=pltpu.CompilerParams(collective_id=identity, has_side_effects=True),
    )(*arrays, *flat, *swaps)


def sigmoid(v):
    return 1.0 / (1.0 + jnp.exp(-v))


def shifted(v, by):
    if by == 0:
        return v
    rows = v.shape[0]
    at = lax.broadcasted_iota(jnp.int32, v.shape, 0)
    keep = at >= by if by > 0 else at < rows + by
    return jnp.where(keep, pltpu.roll(v, by % rows, 0), 0.0)


def conv_sums(v, taps, bias):
    total = bias
    for k in range(KCONV):
        total = total + taps[k : k + 1, :] * shifted(v, KCONV - 1 - k)
    return total


def conv_back(v, taps, bias, valid, grad):
    conv_sum = conv_sums(v, taps, bias)
    s = sigmoid(conv_sum)
    grad = grad * valid * (s * (1.0 + conv_sum * (1.0 - s)))
    total = taps[KCONV - 1 : KCONV, :] * grad
    for k in range(KCONV - 1):
        total = total + taps[k : k + 1, :] * shifted(grad, k - (KCONV - 1))
    sums = [jnp.sum(grad, axis=0, keepdims=True)]
    for k in range(KCONV):
        sums.append(jnp.sum(grad * shifted(v, KCONV - 1 - k), axis=0, keepdims=True))
    return total, sums


def head_columns(ref, pair):
    v = pltpu.roll(ref[...], lax.rem(128 - 2 * pair, 128), 1)
    return v[:, 0:1], v[:, 1:2]


def over_lanes(columns):
    rows = columns[0].shape[0]
    lane = lax.broadcasted_iota(jnp.int32, (rows, 128), 1)
    return jnp.where(lane < HDIM, columns[0], columns[1])


def lower_left(rows):
    return lax.broadcasted_iota(jnp.int32, (rows, rows), 0) >= lax.broadcasted_iota(
        jnp.int32, (rows, rows), 1
    )


def product(a, b, over_a=1, over_b=0):
    return lax.dot_general(
        a, b, (((over_a,), (over_b,)), ((), ())), preferred_element_type=jnp.float32
    )


def bc_scores(bc_ref, bc_taps, bc_bias, valid, scores, bc_keep):
    conv_sum = conv_sums(bc_ref[...].astype(jnp.float32), bc_taps[...], bc_bias[...])
    bc = conv_sum * sigmoid(conv_sum) * valid[:, :1]
    bc_keep[...] = bc.astype(jnp.bfloat16)
    rows = scores.shape[0]
    g = product(bc_keep[:, STATE:], bc_keep[:, :STATE], 1, 1)
    scores[...] = jnp.where(lower_left(rows), g, 0.0)


def front_body(
    z_ref, x_ref, bc_ref, taps, bias, bc_taps, bc_bias, valid, step, cum, cum_rows, skip,
    mixed_ref, gated_ref, squares, scores, bc_keep,
):
    f32, bf = jnp.float32, jnp.bfloat16

    @pl.when(pl.program_id(0) == 0)
    def _():
        bc_scores(bc_ref, bc_taps, bc_bias, valid, scores, bc_keep)
        squares[...] = jnp.zeros_like(squares)

    rows = x_ref.shape[0]
    half = rows // 2
    conv_sum = conv_sums(x_ref[...].astype(f32), taps[...], bias[...])
    x = conv_sum * sigmoid(conv_sum) * valid[...]
    xs = (x * over_lanes(head_columns(step, pl.program_id(0)))).astype(bf)
    sums = head_columns(cum, pl.program_id(0))
    lane = lax.broadcasted_iota(jnp.int32, (half, 128), 1)
    for r in range(2):
        at, wide = pl.ds(r * half, half), (r + 1) * half
        parts = []
        for h in range(2):
            gap = sums[h][r * half : (r + 1) * half, :] - cum_rows[0, h : h + 1, :wide]
            m = (jnp.exp(jnp.minimum(gap, 0.0)) * scores[at, :wide]).astype(bf)
            parts.append(product(m, xs[:wide, :]))
        mixed = jnp.where(lane < HDIM, parts[0], parts[1]) + skip[...] * x[r * half : (r + 1) * half, :]
        z = z_ref[at, :].astype(f32)
        gated = mixed * (z * sigmoid(z))
        mixed_ref[at, :] = mixed
        gated_ref[at, :] = gated
        squares[at, :] += gated * gated


def back_body(
    z_ref, x_ref, bc_ref, taps, bias, bc_taps, bc_bias, valid, step, cum, cum_rows, skip,
    mixed_ref, grad_ref, gain, scale, mean_dot,
    grad_z, grad_x, stats, grad_bc, bc_stats, row_sums, col_sums, step_sums,
    scores, bc_keep, grad_scores, grad_xs,
):
    f32, bf = jnp.float32, jnp.bfloat16
    pair = pl.program_id(0)

    @pl.when(pair == 0)
    def _():
        bc_scores(bc_ref, bc_taps, bc_bias, valid, scores, bc_keep)
        grad_scores[...] = jnp.zeros_like(grad_scores)
        row_sums[...] = jnp.zeros_like(row_sums)
        col_sums[...] = jnp.zeros_like(col_sums)
        step_sums[...] = jnp.zeros_like(step_sums)

    rows = x_ref.shape[0]
    half = rows // 2
    v = x_ref[...].astype(f32)
    conv_sum = conv_sums(v, taps[...], bias[...])
    x = conv_sum * sigmoid(conv_sum) * valid[...]
    steps = over_lanes(head_columns(step, pair))
    sums = head_columns(cum, pair)
    xs = (x * steps).astype(bf)
    z = z_ref[...].astype(f32)
    s = sigmoid(z)
    silu = z * s
    mixed = mixed_ref[...]
    normal = mixed * silu * scale[...]
    grad = grad_ref[...]
    grad_gated = scale[...] * (grad * gain[...] - normal * mean_dot[...])
    grad_mixed = grad_gated * silu
    grad_z[...] = (grad_gated * mixed * (s * (1.0 + z * (1.0 - s)))).astype(bf)
    lane = lax.broadcasted_iota(jnp.int32, (rows, 128), 1)
    dy = [
        jnp.where(lane < HDIM, grad_mixed, 0.0).astype(bf),
        jnp.where(lane < HDIM, 0.0, grad_mixed).astype(bf),
    ]
    for r in range(2):
        at, wide = pl.ds(r * half, half), (r + 1) * half
        total = None
        for h in range(2):
            head = 2 * pair + h
            g = scores[at, :wide]
            gap = sums[h][r * half : (r + 1) * half, :] - cum_rows[0, h : h + 1, :wide]
            e = jnp.exp(jnp.minimum(gap, 0.0))
            m = (e * g).astype(bf)
            dy_rows = dy[h][r * half : (r + 1) * half, :]
            slope = product(dy_rows, xs[:wide, :], 1, 1) * e
            grad_scores[at, :wide] += slope
            both = (slope * g).astype(bf)
            back = product(m, dy_rows, 0, 0)
            total = back if total is None else total + back
            to_lane = (lax.broadcasted_iota(jnp.int32, (wide, 128), 1) == head).astype(bf)
            row_sums[at, :] += product(both, to_lane)
            to_row = (lax.broadcasted_iota(jnp.int32, (64, half), 0) == head).astype(bf)
            col_sums[:, :wide] += product(to_row, both)
        if r == 0:
            grad_xs[:half, :] = total
        else:
            grad_xs[:half, :] += total[:half, :]
            grad_xs[half:, :] = total[half:, :]
    gxs = grad_xs[...]
    fold = (
        lax.broadcasted_iota(jnp.int32, (128, 128), 1)
        == 2 * pair + lax.broadcasted_iota(jnp.int32, (128, 128), 0) // HDIM
    ).astype(bf)
    step_sums[...] += product((gxs * x).astype(bf), fold)
    gx, parts = conv_back(v, taps[...], bias[...], valid[...], gxs * steps + skip[...] * grad_mixed)
    grad_x[...] = gx.astype(bf)
    stats[0:1, :] = jnp.sum(grad * normal, axis=0, keepdims=True)
    stats[1:2, :] = jnp.sum(grad_mixed * x, axis=0, keepdims=True)
    for k, total in enumerate(parts):
        stats[2 + k : 3 + k, :] = total
    stats[7:8, :] = jnp.zeros((1, 128), f32)

    @pl.when(pair == pl.num_programs(0) - 1)
    def _():
        gs = jnp.where(lower_left(rows), grad_scores[...], 0.0).astype(bf)
        grad_c = product(gs, bc_keep[:, :STATE])
        grad_b = product(gs, bc_keep[:, STATE:], 0, 0)
        ends = ((grad_b, 0), (grad_c, STATE))
        for g, at in ends:
            cols = pl.ds(at, STATE)
            gi, sums = conv_back(
                bc_ref[:, cols].astype(f32), bc_taps[:, cols], bc_bias[:, cols], valid[...], g
            )
            grad_bc[:, cols] = gi.astype(bf)
            for k, total in enumerate(sums):
                bc_stats[k : k + 1, cols] = total
            bc_stats[5:8, cols] = jnp.zeros((3, STATE), f32)


def mixer_specs(rows):
    tile = lambda at: pl.BlockSpec((rows, 128), at)
    whole = lambda shape: pl.BlockSpec(shape, lambda p: (0,) * len(shape))
    pairs = INNER // 128
    return tile, whole, [
        tile(lambda p: (0, p)),
        tile(lambda p: (0, pairs + p)),
        pl.BlockSpec((rows, 2 * STATE), lambda p: (0, 2 * INNER // (2 * STATE))),
        pl.BlockSpec((KCONV, 128), lambda p: (0, p)),
        pl.BlockSpec((1, 128), lambda p: (0, p)),
        pl.BlockSpec((KCONV, 2 * STATE), lambda p: (0, INNER // (2 * STATE))),
        pl.BlockSpec((1, 2 * STATE), lambda p: (0, INNER // (2 * STATE))),
        whole((rows, 128)),
        whole((rows, 128)),
        whole((rows, 128)),
        pl.BlockSpec((1, 2, rows), lambda p: (p, 0, 0)),
        pl.BlockSpec((1, 128), lambda p: (0, p)),
    ]


def mixer_front_call(inputs, rows):
    f32 = jnp.float32
    tile, whole, specs = mixer_specs(rows)
    return pl.pallas_call(
        front_body,
        grid=(INNER // 128,),
        in_specs=specs,
        out_specs=[tile(lambda p: (0, p)), tile(lambda p: (0, p)), whole((rows, 128))],
        out_shape=[
            jax.ShapeDtypeStruct((rows, INNER), f32),
            jax.ShapeDtypeStruct((rows, INNER), f32),
            jax.ShapeDtypeStruct((rows, 128), f32),
        ],
        scratch_shapes=[pltpu.VMEM((rows, rows), f32), pltpu.VMEM((rows, 2 * STATE), jnp.bfloat16)],
        name="mixer_front",
        cost_estimate=pl.CostEstimate(flops=10**10, bytes_accessed=2 * 10**7, transcendentals=5 * 10**6),
    )(*inputs)


def mixer_back_call(inputs, extra, rows):
    f32, bf = jnp.float32, jnp.bfloat16
    tile, whole, specs = mixer_specs(rows)
    by_pair = tile(lambda p: (0, p))
    return pl.pallas_call(
        back_body,
        grid=(INNER // 128,),
        in_specs=specs
        + [by_pair, by_pair, pl.BlockSpec((1, 128), lambda p: (0, p)), whole((rows, 128)), whole((rows, 128))],
        out_specs=[
            by_pair, by_pair, pl.BlockSpec((8, 128), lambda p: (0, p)), whole((rows, 2 * STATE)),
            whole((8, 2 * STATE)), whole((rows, 128)), whole((64, rows)), whole((rows, 128)),
        ],
        out_shape=[
            jax.ShapeDtypeStruct((rows, INNER), bf),
            jax.ShapeDtypeStruct((rows, INNER), bf),
            jax.ShapeDtypeStruct((8, INNER), f32),
            jax.ShapeDtypeStruct((rows, 2 * STATE), bf),
            jax.ShapeDtypeStruct((8, 2 * STATE), f32),
            jax.ShapeDtypeStruct((rows, 128), f32),
            jax.ShapeDtypeStruct((64, rows), f32),
            jax.ShapeDtypeStruct((rows, 128), f32),
        ],
        scratch_shapes=[
            pltpu.VMEM((rows, rows), f32), pltpu.VMEM((rows, 2 * STATE), bf),
            pltpu.VMEM((rows, rows), f32), pltpu.VMEM((rows, 128), f32),
        ],
        name="mixer_back",
        cost_estimate=pl.CostEstimate(flops=3 * 10**10, bytes_accessed=3 * 10**7, transcendentals=5 * 10**6),
    )(*inputs, *extra)


def picks(slot_row, slots):
    rows = slot_row.shape[1]
    at = lax.broadcasted_iota(jnp.int32, (slots, rows), 0).astype(jnp.float32)
    return at == slot_row


def cot_chunk(cots, g):
    if g < 6:
        return cots[g][...]
    return jnp.concatenate([cots[2 * g - 6][...], cots[2 * g - 5][...]], axis=0)


def experts_body(lines, x_ref, *refs):
    cots, refs = refs[:10], refs[10:]
    experts_step(lines, x_ref, cots, *refs)


def experts_step(
    lines, x_ref, cots, up, down, slot_rows, gates,
    y_out, gin_out, grads, dots,
    xe, gy, gu_grad, hid, gate_cols,
):
    f32, bf = jnp.float32, jnp.bfloat16
    chunks, rows, width = x_ref.shape
    slots = xe.shape[0] // chunks
    hidden = down.shape[1]

    for g in range(chunks):
        p = picks(slot_rows[0, g : g + 1, :], slots)
        one = p.astype(bf)
        at = pl.ds(g * slots, slots)
        xe[at, :] = product(one, x_ref[g]).astype(bf)
        gate = jnp.sum(jnp.where(p, gates[0, g : g + 1, :], 0.0), axis=1, keepdims=True)
        gate_cols[at, :] = jnp.broadcast_to(gate, (slots, 128))
        gy[at, :] = (gate * product(one, cot_chunk(cots, g))).astype(bf)

    tile = 2 * slots

    @pl.loop(0, xe.shape[0] // tile)
    def _(t):
        at = pl.ds(pl.multiple_of(t * tile, tile), tile)
        gu = product(xe[at, :], up[0])
        a, b = gu[:, :hidden], gu[:, hidden:]
        s = sigmoid(a)
        silu = a * s
        h = (silu * b).astype(bf)
        hid[at, :] = h
        gh = product(gy[at, :], down[0], 1, 1)
        gu_grad[at, :hidden] = (gh * b * (s * (1.0 + a * (1.0 - s)))).astype(bf)
        gu_grad[at, hidden:] = (gh * silu).astype(bf)
        y = product(h, down[0]).astype(bf).astype(f32)
        dot = jnp.sum(y * gy[at, :].astype(f32), axis=1, keepdims=True)
        y_out[0, at, :] = (gate_cols[at, :1] * y).astype(bf)
        for i in range(2):
            p = picks(slot_rows[0, pl.ds(2 * t + i, 1), :], slots)
            dots[0, pl.ds(2 * t + i, 1), :] = jnp.sum(
                jnp.where(p, dot[i * slots : (i + 1) * slots, :], 0.0), axis=0, keepdims=True
            )
        gin_out[0, at, :] = product(gu_grad[at, :], up[0], 1, 1).astype(bf)

    cols = grads.shape[2]
    own_up, per = width // lines, hidden // lines
    for n in range(lines):
        base = n * (grads.shape[1] // lines)
        grads[0, base : base + own_up, :] = product(
            xe[:, n * own_up : (n + 1) * own_up], gu_grad[...], 0, 0
        ).astype(bf)
    cut = width - cols
    for n in range(0, lines, 2):
        down_two = product(hid[:, n * per : (n + 2) * per], gy[...], 0, 0).astype(bf)
        for k in range(2):
            base = (n + k) * (grads.shape[1] // lines) + own_up
            part = down_two[k * per : (k + 1) * per, :]
            grads[0, base : base + per, :] = part[:, :cols]
            grads[0, base + per : base + per + per // 2, :cut] = part[: per // 2, cols:]
            grads[0, base + per : base + per + per // 2, cut:] = part[per // 2 :, cols:]


def experts_call(x, cots, up, down, slot_rows, gates, slots, lines):
    f32, bf = jnp.float32, jnp.bfloat16
    chunks, rows, width = x.shape
    held, _, double = up.shape
    total = chunks * slots
    once = pl.Buffered(1)
    each = lambda *shape: pl.BlockSpec((1,) + shape, lambda e: (e, 0, 0))
    keep = lambda *shape: pl.BlockSpec((1,) + shape, lambda e: (e, 0, 0), pipeline_mode=once)
    whole = pl.BlockSpec((chunks, rows, width), lambda e: (0, 0, 0), pipeline_mode=once)
    shape = lambda *s: jax.ShapeDtypeStruct((held,) + s, bf)
    packed = width + double // 2 + double // 4
    return pl.pallas_call(
        partial(experts_body, lines),
        grid=(held,),
        in_specs=[
            whole, *[pl.BlockSpec(c.shape, lambda e: (0, 0), pipeline_mode=once) for c in cots], keep(width, double), keep(double // 2, width), each(chunks, rows), each(chunks, rows),
        ],
        out_specs=[
            each(total, width), each(total, width), each(packed, double), each(chunks, rows),
        ],
        out_shape=[
            shape(total, width), shape(total, width), shape(packed, double),
            jax.ShapeDtypeStruct((held, chunks, rows), f32),
        ],
        scratch_shapes=[
            pltpu.VMEM((total, width), bf), pltpu.VMEM((total, width), bf), pltpu.VMEM((total, double), bf),
            pltpu.VMEM((total, double // 2), bf), pltpu.VMEM((total, 128), f32),
        ],
        name="experts",
        compiler_params=pltpu.CompilerParams(vmem_limit_bytes=62 << 20),
        cost_estimate=pl.CostEstimate(flops=4 * 10**10, bytes_accessed=5 * 10**7, transcendentals=10**6),
    )(x, *cots, up, down, slot_rows, gates)


def join_body(where, x_ref, *refs):
    cots, refs = refs[:10], refs[10:]
    join_step(where, x_ref, cots, *refs)


def join_step(
    where, x_ref, cots, y_ref, gin_ref, slot_rows, up, down, dots,
    y_part, g_part, dot_part, up_grad, down_grad, up_acc, down_acc, cot_ref,
):
    f32, bf = jnp.float32, jnp.bfloat16
    g = pl.program_id(0)

    @pl.when(g == 0)
    def _():
        up_acc[...] = jnp.zeros_like(up_acc)
        down_acc[...] = jnp.zeros_like(down_acc)

    for k in range(8):

        @pl.when(g == k)
        def _(k=k):
            cot_ref[...] = cot_chunk(cots, k)

    x, cot = x_ref[0], cot_ref[...]
    half = down.shape[0]
    gu = product(x, up[...])
    a, b = gu[:, :half], gu[:, half:]
    s = sigmoid(a)
    silu = a * s
    h = (silu * b).astype(bf)
    gh = product(cot, down[...], 1, 1)
    gu_grad = jnp.concatenate(
        [gh * b * (s * (1.0 + a * (1.0 - s))), gh * silu], axis=1
    ).astype(bf)
    up_acc[...] += product(x, gu_grad, 0, 0)
    down_acc[...] += product(h, cot, 0, 0)
    y = product(h, down[...])
    gx = product(gu_grad, up[...], 1, 1)
    held, slots, width = y_ref.shape
    one = jnp.concatenate(
        [picks(slot_rows[e, pl.ds(g, 1), :], slots).astype(bf) for e in range(held)], axis=0
    )
    y = y + product(one, y_ref[...].reshape(held * slots, width), 0, 0)
    gx = gx + product(one, gin_ref[...].reshape(held * slots, width), 0, 0)
    lists = jnp.zeros((8, x.shape[0]), f32)
    spot = lax.broadcasted_iota(jnp.int32, lists.shape, 0)
    for e in range(held):
        row = dots[e, pl.ds(g, 1), :]
        high = row.astype(bf).astype(f32)
        lists = jnp.where(spot == e, high, lists)
        lists = jnp.where(spot == held + e, row - high, lists)
    col = lax.broadcasted_iota(jnp.int32, (8, 128), 1)
    spot = lax.broadcasted_iota(jnp.int32, (8, 128), 0)
    first = held * where[0]
    to = (spot < held) & (col == first + spot)
    to = to | ((spot >= held) & (spot < 2 * held) & (col == 8 * held + first + spot - held))
    dot_part[0] = product(lists.astype(bf), to.astype(bf), 0, 0).astype(bf)
    y_part[0] = y.astype(bf)
    g_part[0] = gx.astype(bf)

    @pl.when(g == pl.num_programs(0) - 1)
    def _():
        up_grad[...] = up_acc[...].astype(bf)
        down_grad[...] = down_acc[...].astype(bf)


def join_call(where, x, cots, y, gin, slot_rows, up, down, dots, slots):
    f32, bf = jnp.float32, jnp.bfloat16
    chunks, rows, width = x.shape
    held = y.shape[0]
    chunk = pl.BlockSpec((1, rows, width), lambda g, w: (g, 0, 0))
    placed = pl.BlockSpec((1, rows, width), lambda g, w: (g ^ w[0], 0, 0))
    rows_of = pl.BlockSpec((held, slots, width), lambda g, w: (0, g, 0))
    whole = lambda a: pl.BlockSpec(a.shape, lambda g, w: (0,) * a.ndim)
    return pl.pallas_call(
        join_body,
        grid_spec=pltpu.PrefetchScalarGridSpec(
            num_scalar_prefetch=1,
            grid=(chunks,),
            in_specs=[chunk, *[whole(c) for c in cots], rows_of, rows_of, whole(slot_rows), whole(up), whole(down), whole(dots)],
            out_specs=[
                placed, chunk, pl.BlockSpec((1, rows, 128), lambda g, w: (g, 0, 0)), whole(up), whole(down),
            ],
            scratch_shapes=[
                pltpu.VMEM(up.shape, f32), pltpu.VMEM(down.shape, f32), pltpu.VMEM((rows, width), bf),
            ],
        ),
        out_shape=[
            jax.ShapeDtypeStruct(x.shape, bf), jax.ShapeDtypeStruct(x.shape, bf),
            jax.ShapeDtypeStruct((chunks, rows, 128), bf),
            jax.ShapeDtypeStruct(up.shape, bf), jax.ShapeDtypeStruct(down.shape, bf),
        ],
        name="join",
        compiler_params=pltpu.CompilerParams(vmem_limit_bytes=48 << 20),
        cost_estimate=pl.CostEstimate(flops=10**10, bytes_accessed=4 * 10**7, transcendentals=10**6),
    )(where, x, *cots, y, gin, slot_rows, up, down, dots)


def local_fast(
    tokens, lengths, routes, cotangent, norm_gain, in_weight, conv_weight, conv_bias, dt_bias,
    a_log, d_skip, mix_gain, out_weight, ffn_gain, router_weight, shared_up, shared_down,
    expert_up, expert_down,
):
    bf, f32 = jnp.bfloat16, jnp.float32
    block = tokens.shape[1]
    parts = tokens.shape[0]
    rows = block * parts
    groups = lax.axis_size("dp")
    lines = lax.axis_size("seq")
    held = expert_up.shape[0]
    experts = held * groups
    top = routes.shape[2]
    slots = block * top * 5 // (4 * experts) * parts
    slots = -(-slots // 128) * 128
    place = lax.axis_index("seq")
    group = lax.axis_index("dp")

    def to(a, bit):
        return lax.ppermute(a, "dp", [(i, i ^ bit) for i in range(groups)])

    pad = lambda a, n: jnp.pad(a, ((0, 0), (0, n - a.shape[1])))
    in_blocks, router_blocks, out_blocks, down_line, up_line, x_low, cot_low, route = gather_rows(
        [in_weight, pad(router_weight, 128), out_weight],
        [in_weight.shape[0] // 3, router_weight.shape[0], out_weight.shape[0] // 2, shared_down.shape[0],
         shared_up.shape[0]],
        [shared_down, shared_up], lines, 2, [tokens, cotangent, routes], False, 1,
    )
    out_full = out_blocks.reshape(-1, MODEL_WIDTH)
    in_full = in_blocks.reshape(MODEL_WIDTH, -1)
    router_full = router_blocks.reshape(MODEL_WIDTH, -1)[:, :experts]
    down_part = down_line.reshape(-1, MODEL_WIDTH)
    width = SFF // groups
    up_cols = up_line.reshape(-1, 2, groups, width).transpose(2, 0, 1, 3).reshape(groups, -1, 2 * width)

    length = lax.dynamic_index_in_dim(lengths, place, 0, False)
    x_low = x_low.reshape(rows, MODEL_WIDTH)
    cot_low = cot_low.reshape(rows, MODEL_WIDTH)
    cotangent_rows = cot_low
    route = route.reshape(rows, top)
    used = jnp.arange(rows) < length
    valid = used.astype(f32)[:, None]
    x_rows = x_low.astype(f32)
    normed, norm_pull = jax.vjp(rms_norm, x_rows, norm_gain)
    normed_low = normed.astype(bf)
    projected = jnp.dot(normed_low, in_full, preferred_element_type=f32).astype(bf)
    before_step = projected[:, INNER + CONV :].astype(f32) + dt_bias
    steps = jax.nn.softplus(before_step)
    rates = -steps * jnp.exp(a_log)
    lower = (jnp.arange(rows)[:, None] >= jnp.arange(rows)[None, :]).astype(f32)
    cumulative = jnp.dot(lower, rates, precision=PRECISE)
    wide = lambda a: jnp.broadcast_to(a[:, :, None], a.shape + (HDIM,)).reshape(a.shape[0], -1)
    lanes = lambda a: jnp.broadcast_to(a, (rows, 128))
    mixer_in = (
        projected, projected, projected, conv_weight, conv_bias[None], conv_weight, conv_bias[None],
        lanes(valid), pad(steps, 128), pad(cumulative, 128), cumulative.T.reshape(HEADS // 2, 2, rows),
        wide(d_skip[None]),
    )
    cot_low = jnp.where(used[:, None], cot_low, 0)
    cut = rows // 2
    cot_own = cot_low
    cot_x, cot_y = to(cot_own, 2), to(cot_own, 4)
    first_in, cot_x, cot_y, up_cols = lax.optimization_barrier((mixer_in[0], cot_x, cot_y, up_cols))
    cot_far = (to(cot_x[:cut], 4), to(cot_y[cut:], 2))
    mixed, gated, squares = mixer_front_call((first_in,) + mixer_in[1:], rows)
    up_part = lax.all_to_all(up_cols, "dp", split_axis=0, concat_axis=0, tiled=True)
    gated, cot_far, up_part = lax.optimization_barrier((gated, cot_far, up_part))
    cot_far_core = tuple(to(a, 1) for a in cot_far)
    up_part = up_part.reshape(MODEL_WIDTH, 2 * width)
    cot_core = [to(a, 1) for a in (cot_own, cot_x, cot_y)]
    scale = lax.rsqrt(jnp.sum(squares, axis=1, keepdims=True) / INNER + EPSILON)
    mix_low = (gated * scale * mix_gain).astype(bf)
    mixer_out = jnp.dot(mix_low, out_full, preferred_element_type=f32)
    hidden = x_rows + mixer_out * valid
    normed_ffn, ffn_pull = jax.vjp(rms_norm, hidden, ffn_gain)
    ffn_low = normed_ffn.astype(bf)
    logits = jnp.dot(ffn_low, router_full, preferred_element_type=f32)
    onehot = (route[:, :, None] == jnp.arange(experts)[None, None, :]).astype(f32)
    chosen = jnp.sum(onehot, axis=1)
    peak = jnp.max(jnp.where(chosen > 0, logits, -jnp.inf), axis=1, keepdims=True)
    raised = jnp.exp(jnp.where(chosen > 0, logits - peak, -jnp.inf))
    probs = raised / jnp.sum(raised, axis=1, keepdims=True)

    ffn_low, cot_far_core, cot_core = lax.optimization_barrier((ffn_low, cot_far_core, cot_core))
    all_rows, all_probs = gather_rows(
        [ffn_low, (probs * valid).T], [64, experts], [], 1, 2, [], True, 2
    )
    all_rows = all_rows[:, 0]
    all_cot = [cot_own, cot_core[0], cot_x, cot_core[1], cot_y, cot_core[2], *cot_far, *cot_far_core]
    mine = group * held + jnp.arange(held)
    gates = lax.dynamic_slice_in_dim(all_probs[:, 0], group * held, held, 1).transpose(1, 0, 2)
    member = gates > 0
    earlier = (jnp.arange(rows)[:, None] < jnp.arange(rows)[None, :]).astype(bf)
    before = jnp.einsum("egt,ts->egs", member.astype(bf), earlier, preferred_element_type=f32)
    slot_rows = jnp.where(member, before, -1.0)
    y_slots, gin_slots, grad_experts, dots = experts_call(
        all_rows, all_cot, expert_up, expert_down, slot_rows, gates, slots, lines
    )
    own_experts = lax.psum_scatter(grad_experts, "seq", scatter_dimension=1, tiled=True)
    y_part, g_part, dots, grad_sup, grad_sdown = join_call(
        group.reshape(1), all_rows, all_cot, y_slots, gin_slots, slot_rows, up_part, down_part, dots, slots
    )
    g_sum, dots = sum_to_owners(
        [g_part.reshape(-1, MODEL_WIDTH), dots.reshape(-1, 128)],
        [(0, 384)] * 4 + [(1, 128)], 1, [MODEL_WIDTH, 128], None, [], (True, True), 3,
    )
    dots = dots[:, :experts] + dots[:, experts : 2 * experts]
    g_sum, y_part = lax.optimization_barrier((g_sum, y_part))
    y_part = lax.all_to_all(y_part, "dp", split_axis=0, concat_axis=0, tiled=True)
    grad_out = cotangent_rows.astype(f32)
    grad_logit = (dots - probs * jnp.sum(dots, axis=1, keepdims=True)).astype(bf)
    grad_router = contract_rows(ffn_low, grad_logit)
    grad_ffn = g_sum + contract_cols(grad_logit, router_full)
    grad_hidden, grad_fgain = ffn_pull(grad_ffn)
    grad_hidden = grad_hidden + grad_out
    grad_mo = (grad_hidden * valid).astype(bf)
    grad_mix = contract_cols(grad_mo, out_full)
    mean_dot = jnp.sum(grad_mo.astype(f32) * mixer_out, axis=1, keepdims=True) / INNER
    grad_z, grad_in, stats, grad_bc, bc_stats, row_sums, col_sums, step_sums = mixer_back_call(
        mixer_in, (mixed, grad_mix, mix_gain[None], lanes(scale), lanes(mean_dot)), rows
    )
    grad_rates = jnp.dot(lower.T, row_sums[:, :HEADS] - col_sums[:HEADS].T, precision=PRECISE)
    grad_raw = (step_sums[:, :HEADS] - grad_rates * jnp.exp(a_log)) * jax.nn.sigmoid(before_step)
    grad_al = jnp.sum(grad_rates * rates, axis=0)
    grad_db = jnp.sum(grad_raw, axis=0)
    grad_skip = jnp.sum(stats[1].reshape(HEADS, HDIM), axis=1)
    grad_proj = jnp.concatenate([grad_z, grad_in, grad_bc, grad_raw.astype(bf)], axis=1)
    spare = -PROJ % 128
    wide_proj, late_mo, y_part = lax.optimization_barrier((pad(grad_proj, PROJ + spare), grad_mo, y_part))
    grad_outw = contract_rows(mix_low, late_mo).astype(bf)
    grad_inw = contract_rows(normed_low, wide_proj).astype(bf)
    grad_x, grad_ngain = norm_pull(contract_cols(grad_proj, in_full))
    input_grad = (grad_x + grad_hidden).astype(bf)
    grad_router = contract_rows(ffn_low, pad(grad_logit, 128)).astype(bf)

    grad_inw, grad_sup = lax.optimization_barrier((grad_inw, grad_sup))
    y_sum = jnp.sum(y_part.astype(f32), axis=0)
    output = (hidden + valid * y_sum).astype(bf).reshape(tokens.shape)

    heads = jnp.pad(jnp.stack([grad_db, grad_al, grad_skip]), ((0, 5), (0, 256 - HEADS)))
    gains = jnp.pad(jnp.stack([grad_ngain, grad_fgain]), ((0, 6), (0, 0)))
    own_out, own_in, own_router, output, input_grad, sdown, conv_w, conv_b, mix_g, norm_g, ffn_g, heads = sum_to_owners(
        [grad_outw, grad_inw, grad_router],
        [(0, 512)] * 3 + [(1, 768)] * 8 + [(1, (PROJ + spare) % 768), (2, 128)], lines, [MODEL_WIDTH, PROJ, experts],
        [stats, bc_stats, gains, heads], [output, input_grad.reshape(tokens.shape), grad_sdown.reshape(lines, -1, MODEL_WIDTH)],
        (False, False, False), 4,
    )
    sup = lax.all_to_all(
        grad_sup.reshape(groups * lines, -1, 2 * width), ("dp", "seq"), split_axis=0, concat_axis=0, tiled=True
    ).astype(f32)
    sup = jnp.sum(sup.reshape(groups, lines, -1, 2 * width), axis=1)
    sup = sup.reshape(groups, -1, 2, width).transpose(1, 2, 0, 3).reshape(-1, 2 * SFF)
    sdown = jnp.sum(sdown.astype(f32), axis=0)
    own_up, per = MODEL_WIDTH // lines, EXPERT_HIDDEN // lines
    rest = own_experts[:, own_up + per :]
    cut = rest.shape[2] // 2
    rest = jnp.concatenate([rest[:, :, :cut], rest[:, :, cut:]], axis=1)
    own_down = jnp.concatenate([own_experts[:, own_up : own_up + per], rest], axis=2)
    return (
        output, input_grad, norm_g.reshape(-1), own_in, conv_w, conv_b.reshape(-1), heads[0, :HEADS], heads[1, :HEADS],
        heads[2, :HEADS], mix_g.reshape(-1), own_out, ffn_g.reshape(-1), own_router, sup, sdown,
        own_experts[:, :own_up].astype(f32), own_down.astype(f32),
    )


def solution(mesh):
    def program(*arrays):
        each = arrays[0].shape[0] == lax.axis_size("seq") == 4 and lax.axis_size("dp") == 8
        return (local_fast if each else local)(*arrays)

    return jax.shard_map(
        program,
        mesh=mesh,
        in_specs=(
            P("dp", "seq", None),
            P("dp"),
            P("dp", "seq", None),
            P("dp", "seq", None),
            P(),
            P(("dp", "seq"), None),
            P(),
            P(),
            P(),
            P(),
            P(),
            P(),
            P(("dp", "seq"), None),
            P(),
            P(("dp", "seq"), None),
            P(("dp", "seq"), None),
            P(("dp", "seq"), None),
            P("dp", None, None),
            P("dp", None, None),
        ),
        out_specs=(
            P("dp", "seq", None),
            P("dp", "seq", None),
            P(),
            P(("dp", "seq"), None),
            P(),
            P(),
            P(),
            P(),
            P(),
            P(),
            P(("dp", "seq"), None),
            P(),
            P(("dp", "seq"), None),
            P(("dp", "seq"), None),
            P(("dp", "seq"), None),
            P("dp", "seq", None),
            P("dp", "seq", None),
        ),
        check_vma=False,
    )
```
